32 devices in a mesh: grp: 8 (over z, y), blk: 4 (over x, core).
Axes of the slice: x: 2, y: 2, z: 4, core: 2. Of those that a mesh axis runs over, the one named last changes fastest.
Arguments:
- frames: bfloat16 [8, 512, 1536], P('grp', 'blk'), may hold values from -6 to 6
- text_states: bfloat16 [8, 64, 1536], P('grp'), may hold values from -6 to 6
- block_table: int32 [8, 8], P('grp'), may hold values from 0 to 7, each once within a row
- inward: bfloat16 [1536, 4608], P('grp', 'blk'), may hold values from -0.21875 to 0.21875
- outward: bfloat16 [1536, 1536], P('grp', 'blk'), may hold values from -1.75 to 1.75
- querying: bfloat16 [1536, 1536], P('grp', 'blk'), may hold values from -0.21875 to 0.21875
- keying: bfloat16 [1536, 3072], P('grp', 'blk'), may hold values from -0.21875 to 0.21875
- returning: bfloat16 [1536, 1536], P('grp', 'blk'), may hold values from -0.875 to 0.875
- expand: bfloat16 [1536, 6144], P('grp', 'blk'), may hold values from -0.15625 to 0.15625
- contract: bfloat16 [6144, 1536], P('blk', 'grp'), may hold values from -0.078125 to 0.078125
- gains: bfloat16 [3, 1536], P(None, ('grp', 'blk')), may hold values from 0.099609375 to 1.8984375
- shifts: bfloat16 [3, 1536], P(None, ('grp', 'blk')), may hold values from -1.1953125 to 1.1953125
- out_grad: bfloat16 [8, 512, 1536], P('grp', 'blk'), may hold values from -6 to 6
Outputs:
- block_out: bfloat16 [8, 512, 1536], P('grp', 'blk')
- frames_grad: float32 [8, 512, 1536], P('grp', 'blk')
- text_grad: float32 [8, 64, 1536], P('grp', 'blk')
- inward_grad: float32 [1536, 4608], P('grp', 'blk')
- outward_grad: float32 [1536, 1536], P('grp', 'blk')
- querying_grad: float32 [1536, 1536], P('grp', 'blk')
- keying_grad: float32 [1536, 3072], P('grp', 'blk')
- returning_grad: float32 [1536, 1536], P('grp', 'blk')
- expand_grad: float32 [1536, 6144], P('grp', 'blk')
- contract_grad: float32 [6144, 1536], P('blk', 'grp')
- gains_grad: float32 [3, 1536], P(None, ('grp', 'blk'))
- shifts_grad: float32 [3, 1536], P(None, ('grp', 'blk'))
The draws below stay inside these ranges and needn't reach their ends.
Inputs may be any that keep to these rules, and one draw needn't show every extreme that they name: Each row is an ordering of the clip's 8 frame blocks: storage block s of clip c holds frames block_table[c, s] * 64 to block_table[c, s] * 64 + 63.
All inputs are finite; a program needn't handle non-finite values.
Results may differ from the reference program's by a relative error of at most 0.028.
Values may be sent and summed in bfloat16 or wider, within the bound.
A program may use at most 320 MiB of HBM per device.

```python
import math
import jax
import jax.numpy as jnp
from jax import lax

D = 1536
HEADS = 24
HEAD = 64
FF = 6144
TEXT = 64
SEG = 64
BLOCKS = 8
CLIP_LEN = 512
CLIPS = 8


def shard_levels(rng, extent, pieces, smallest, top_value):
    def one(dim, parts):
        steps = jax.random.uniform(jax.random.fold_in(jax.random.fold_in(rng, 6), dim), (parts,), jnp.float32, smallest / len(pieces), top_value / len(pieces))
        return jnp.repeat(jnp.exp(steps), extent[dim] // parts).reshape((-1,) + (1,) * (len(extent) - dim - 1))

    level = one(*pieces[0])
    for cut in pieces[1:]:
        level = level * one(*cut)
    return level


def bell_draw(key, shape, scale, reach, cuts=(), kind=jnp.bfloat16):
    values = jax.random.normal(key, shape, jnp.float32) * scale
    if len(cuts) > 0:
        values = shard_levels(key, shape, cuts, -0.22, 0.18) * values
    return jnp.clip(values, min=-reach, max=reach).astype(kind)


def setup_inputs(seed: int = 0) -> dict:
    arg_keys = jax.random.split(jax.random.key(seed), 14)
    return {
        "frames": bell_draw(arg_keys[0], (CLIPS, CLIP_LEN, D), 1.0, 6.0, ((0, 8), (1, 4))),
        "text_states": bell_draw(arg_keys[1], (CLIPS, TEXT, D), 1.0, 6.0, ((0, 8),)),
        "block_table": jax.vmap(lambda own: jax.random.permutation(own, BLOCKS))(jax.random.split(arg_keys[2], CLIPS)).reshape((CLIPS, BLOCKS)).astype(jnp.int32),
        "inward": bell_draw(arg_keys[3], (D, 3 * D), (D // 2) ** -0.5, 0.21875, ((0, 8), (1, 4))),
        "outward": bell_draw(arg_keys[4], (D, D), (D // 128) ** -0.5, 1.75, ((0, 8), (1, 4))),
        "querying": bell_draw(arg_keys[5], (D, D), (D // 2) ** -0.5, 0.21875, ((0, 8), (1, 4))),
        "keying": bell_draw(arg_keys[6], (D, 2 * D), (D // 2) ** -0.5, 0.21875, ((0, 8), (1, 4))),
        "returning": bell_draw(arg_keys[7], (D, D), (D // 32) ** -0.5, 0.875, ((0, 8), (1, 4))),
        "expand": bell_draw(arg_keys[8], (D, FF), D ** -0.5, 0.15625, ((0, 8), (1, 4))),
        "contract": bell_draw(arg_keys[9], (FF, D), FF ** -0.5, 0.078125, ((0, 4), (1, 8))),
        "gains": jnp.clip(1.0 + 0.18 * jax.random.normal(arg_keys[10], (3, D), jnp.float32), 0.099609375, 1.8984375).astype(jnp.bfloat16),
        "shifts": bell_draw(arg_keys[11], (3, D), 0.3, 1.1953125, ((1, 32),)),
        "out_grad": bell_draw(arg_keys[12], (CLIPS, CLIP_LEN, D), 1.0, 6.0, ((0, 8), (1, 4))),
    }


@jax.custom_vjp
def low(v):
    return lax.optimization_barrier(v.astype(jnp.bfloat16)).astype(jnp.float32)

@jax.custom_vjp
def low_back(v):
    return v

def low_keep(v):
    return (low(v), None)

def low_pass(kept, grad):
    return (grad,)

def back_keep(v):
    return (v, None)

def back_low(kept, grad):
    return (low(grad),)
low.defvjp(low_keep, low_pass)
low_back.defvjp(back_keep, back_low)

def matmul(left, right):
    return jnp.dot(left, right, precision=lax.Precision.HIGHEST, preferred_element_type=jnp.float32)

def heads_of(values):
    return values.reshape(values.shape[0], HEADS, HEAD)

def layer_norm(values, gain, shift):
    center = values - lax.optimization_barrier(jnp.mean(values, axis=-1, keepdims=True))
    spread = lax.optimization_barrier(jnp.mean(center * center, axis=-1, keepdims=True))
    return center * lax.rsqrt(spread + 1e-05) * gain + shift

def self_attend(queries, keys, values):
    length = queries.shape[0]
    span = math.gcd(length, 512)
    key_frames = jnp.arange(length, dtype=jnp.int32)

    def one_block(index):
        start = index * span
        rows = lax.dynamic_slice_in_dim(queries, start, span, 0)
        scores = low_back(jnp.einsum('qhd,khd->hqk', rows, keys, precision=lax.Precision.HIGHEST) * 0.125)
        query_frames = start + jnp.arange(span, dtype=jnp.int32)
        allowed = key_frames[None, :] <= query_frames[:, None]
        scores = jnp.where(allowed[None], scores, -1e+30)
        weighting = low(jax.nn.softmax(scores, axis=-1))
        return jnp.einsum('hqk,khd->qhd', weighting, values, precision=lax.Precision.HIGHEST)
    blocks = lax.map(jax.checkpoint(one_block), jnp.arange(length // span, dtype=jnp.int32))
    return blocks.reshape(length, HEADS * HEAD)

def decoder_layer(weights, timed, text):
    inward, outward, querying, keying, returning, expand, contract, gains, shifts = weights
    first = low(layer_norm(timed, gains[0], shifts[0]))
    joint = low(low_back(matmul(first, inward)))
    attended = self_attend(heads_of(joint[:, :D]), heads_of(joint[:, D:2 * D]), heads_of(joint[:, 2 * D:]))
    attended = low(low_back(attended))
    hidden_one = timed + low_back(matmul(attended, outward))
    second = low(layer_norm(hidden_one, gains[1], shifts[1]))
    cross_query = heads_of(low(low_back(matmul(second, querying))))
    text_pairs = low(low_back(matmul(text, keying)))
    cross_scores = low_back(jnp.einsum('qhd,khd->hqk', cross_query, heads_of(text_pairs[:, :D]), precision=lax.Precision.HIGHEST) * 0.125)
    cross_weighting = low(jax.nn.softmax(cross_scores, axis=-1))
    crossed = jnp.einsum('hqk,khd->qhd', cross_weighting, heads_of(text_pairs[:, D:]), precision=lax.Precision.HIGHEST).reshape(-1, D)
    crossed = low(low_back(crossed))
    hidden_two = hidden_one + low_back(matmul(crossed, returning))
    third = low(layer_norm(hidden_two, gains[2], shifts[2]))
    upward = low_back(matmul(third, expand))
    activated = low(jax.nn.gelu(upward, approximate=False))
    return hidden_two + low_back(matmul(activated, contract))

def reference(frames, text_states, block_table, inward, outward, querying, keying, returning, expand, contract, gains, shifts, out_grad):
    weights = tuple((item.astype(jnp.float32) for item in (inward, outward, querying, keying, returning, expand, contract, gains, shifts)))
    count = block_table.shape[1]

    def per_clip(totals, items):
        stored, text, order, stored_grad = items
        inverse = jnp.zeros((count,), jnp.int32).at[order].set(jnp.arange(count, dtype=jnp.int32))
        timed = stored.astype(jnp.float32).reshape(count, SEG, D)[inverse].reshape(count * SEG, D)
        timed_grad = stored_grad.astype(jnp.float32).reshape(count, SEG, D)[inverse].reshape(count * SEG, D)
        result, pullback = jax.vjp(decoder_layer, weights, timed, text.astype(jnp.float32))
        weight_grads, input_grad, text_grad = pullback(timed_grad)
        totals = tuple((total + item for total, item in zip(totals, weight_grads)))
        result = result.reshape(count, SEG, D)[order].reshape(count * SEG, D).astype(jnp.bfloat16)
        input_grad = input_grad.reshape(count, SEG, D)[order].reshape(count * SEG, D)
        return (totals, (result, input_grad, text_grad))
    start = tuple((jnp.zeros_like(item) for item in weights))
    totals, outputs = lax.scan(per_clip, start, (frames, text_states, block_table, out_grad))
    return (outputs[0], outputs[1], outputs[2], totals[0], totals[1], totals[2], totals[3], totals[4], totals[5], totals[6], totals[7], totals[8])
```

```python
import math

import jax
import jax.numpy as jnp
from jax import lax
from jax.sharding import PartitionSpec as P

HEADS = 24
HEAD = 64
TEXT = 64
SEG = 64


def layer_norm(values, gain, shift):
    center = values - jnp.mean(values, axis=-1, keepdims=True)
    spread = jnp.mean(center * center, axis=-1, keepdims=True)
    return center * lax.rsqrt(spread + 1e-05) * gain + shift


def norm_pull(values, gain, shift, incoming):
    unused, pullback = jax.vjp(layer_norm, values, gain, shift)
    return pullback(incoming)


def gelu_slope(upward):
    return (
        0.5 * (1.0 + lax.erf(upward * 0.7071067811865476))
        + upward * jnp.exp(-0.5 * upward * upward) * 0.3989422804014327
    )


def gather_weights(inward, outward, querying, keying, returning, expand, contract, gains, shifts):
    inward, outward, querying, keying, returning, expand, contract, gains, shifts = (
        lax.all_gather(inward, "blk", axis=1, tiled=True),
        lax.all_gather(outward, "blk", axis=1, tiled=True),
        lax.all_gather(querying, "blk", axis=1, tiled=True),
        lax.all_gather(keying, "blk", axis=1, tiled=True),
        lax.all_gather(returning, "blk", axis=1, tiled=True),
        lax.all_gather(expand, "blk", axis=1, tiled=True),
        lax.all_gather(contract, "blk", axis=0, tiled=True),
        lax.all_gather(gains, "blk", axis=1, tiled=True),
        lax.all_gather(shifts, "blk", axis=1, tiled=True),
    )
    return (
        lax.all_gather(inward, "grp", axis=0, tiled=True),
        lax.all_gather(outward, "grp", axis=0, tiled=True),
        lax.all_gather(querying, "grp", axis=0, tiled=True),
        lax.all_gather(keying, "grp", axis=0, tiled=True),
        lax.all_gather(returning, "grp", axis=0, tiled=True),
        lax.all_gather(expand, "grp", axis=0, tiled=True),
        lax.all_gather(contract, "grp", axis=1, tiled=True),
        lax.all_gather(gains, "grp", axis=1, tiled=True),
        lax.all_gather(shifts, "grp", axis=1, tiled=True),
    )


def shards(
    frames,
    text_states,
    block_table,
    inward,
    outward,
    querying,
    keying,
    returning,
    expand,
    contract,
    gains,
    shifts,
    out_grad,
):
    (
        full_inward,
        full_outward,
        full_query,
        full_keys,
        full_return,
        full_expand,
        full_contract,
        full_gains,
        full_shifts,
    ) = gather_weights(
        inward, outward, querying, keying, returning, expand, contract, gains, shifts
    )
    width = frames.shape[2]
    rows = frames.shape[1]
    length = block_table.shape[1] * SEG
    group = lax.axis_size("blk")
    member = lax.axis_index("blk")
    span = math.gcd(length, 512)
    steps = length // span
    gain_rows = full_gains.astype(jnp.float32)
    shift_rows = full_shifts.astype(jnp.float32)
    key_frames = (
        block_table[0][:, None] * SEG + jnp.arange(SEG, dtype=jnp.int32)[None, :]
    ).reshape(length)
    own_frames = lax.dynamic_slice_in_dim(key_frames, member * rows, rows, 0)
    inputs = frames[0].astype(jnp.float32)
    first = layer_norm(inputs, gain_rows[0], shift_rows[0]).astype(jnp.bfloat16)
    joint = jnp.dot(first, full_inward, preferred_element_type=jnp.float32).astype(jnp.bfloat16)
    queries = joint[:, :width].reshape(rows, HEADS, HEAD)
    pairs = lax.all_gather(joint[:, width:], "blk", axis=0, tiled=True)
    pair_blocks = pairs.reshape(steps, span, 2 * width)
    frame_blocks = key_frames.reshape(steps, span)

    def scores_of(block, block_frames):
        keys = block[:, :width].reshape(span, HEADS, HEAD)
        raw = jnp.einsum("qhd,khd->hqk", queries, keys, preferred_element_type=jnp.float32) * 0.125
        allowed = block_frames[None, :] <= own_frames[:, None]
        return jnp.where(allowed[None], raw, -1e30)

    def stat_step(carry, items):
        peak, total = carry
        scores = scores_of(items[0], items[1])
        higher = jnp.maximum(peak, jnp.max(scores, axis=2))
        total = total * jnp.exp(peak - higher) + jnp.sum(
            jnp.exp(scores - higher[:, :, None]), axis=2
        )
        return ((higher, total), None)

    start_peak = jnp.full((HEADS, rows), -1e30, jnp.float32)
    (peak, total), unused = lax.scan(
        stat_step, (start_peak, jnp.zeros((HEADS, rows), jnp.float32)), (pair_blocks, frame_blocks)
    )
    log_total = peak + jnp.log(total)

    def out_step(carry, items):
        weighting = jnp.exp(scores_of(items[0], items[1]) - log_total[:, :, None]).astype(
            jnp.bfloat16
        )
        values = items[0][:, width:].reshape(span, HEADS, HEAD)
        return (
            carry
            + jnp.einsum("hqk,khd->qhd", weighting, values, preferred_element_type=jnp.float32),
            None,
        )

    mixed, unused = lax.scan(
        out_step, jnp.zeros((rows, HEADS, HEAD), jnp.float32), (pair_blocks, frame_blocks)
    )
    attended = mixed.reshape(rows, width).astype(jnp.bfloat16)
    hidden_one = inputs + jnp.dot(attended, full_outward, preferred_element_type=jnp.float32)
    second = layer_norm(hidden_one, gain_rows[1], shift_rows[1]).astype(jnp.bfloat16)
    cross_query = jnp.dot(second, full_query, preferred_element_type=jnp.float32).astype(
        jnp.bfloat16
    )
    cross_heads = cross_query.reshape(rows, HEADS, HEAD)
    text = text_states[0]
    text_pairs = jnp.dot(text, full_keys, preferred_element_type=jnp.float32).astype(jnp.bfloat16)
    text_keys = text_pairs[:, :width].reshape(TEXT, HEADS, HEAD)
    text_values = text_pairs[:, width:].reshape(TEXT, HEADS, HEAD)
    cross_scores = (
        jnp.einsum("qhd,khd->hqk", cross_heads, text_keys, preferred_element_type=jnp.float32)
        * 0.125
    )
    cross_soft = jax.nn.softmax(cross_scores, axis=2)
    cross_weighting = cross_soft.astype(jnp.bfloat16)
    crossed = (
        jnp.einsum("hqk,khd->qhd", cross_weighting, text_values, preferred_element_type=jnp.float32)
        .reshape(rows, width)
        .astype(jnp.bfloat16)
    )
    hidden_two = hidden_one + jnp.dot(crossed, full_return, preferred_element_type=jnp.float32)
    third = layer_norm(hidden_two, gain_rows[2], shift_rows[2]).astype(jnp.bfloat16)
    upward = jnp.dot(third, full_expand, preferred_element_type=jnp.float32)
    activated = jax.nn.gelu(upward, approximate=False).astype(jnp.bfloat16)
    branch = jnp.dot(activated, full_contract, preferred_element_type=jnp.float32)
    block_out = (hidden_two + branch).astype(jnp.bfloat16)[None]
    (
        full_inward,
        full_outward,
        full_query,
        full_keys,
        full_return,
        full_expand,
        full_contract,
        full_gains,
        full_shifts,
    ) = gather_weights(
        inward, outward, querying, keying, returning, expand, contract, gains, shifts
    )
    incoming = out_grad[0].astype(jnp.float32)
    branch_grad = out_grad[0]
    act_grad = jnp.dot(branch_grad, full_contract.T, preferred_element_type=jnp.float32)
    contract_grad = jnp.dot(activated.T, branch_grad, preferred_element_type=jnp.float32)
    up_grad = (act_grad * gelu_slope(upward)).astype(jnp.bfloat16)
    expand_grad = jnp.dot(third.T, up_grad, preferred_element_type=jnp.float32)
    third_grad = jnp.dot(up_grad, full_expand.T, preferred_element_type=jnp.float32)
    two_grad, gain_two, shift_two = norm_pull(hidden_two, gain_rows[2], shift_rows[2], third_grad)
    hidden_two_grad = incoming + two_grad
    branch_two = hidden_two_grad.astype(jnp.bfloat16)
    crossed_grad = jnp.dot(branch_two, full_return.T, preferred_element_type=jnp.float32).astype(
        jnp.bfloat16
    )
    crossed_grad = crossed_grad.reshape(rows, HEADS, HEAD)
    prob_grad = jnp.einsum(
        "qhd,khd->hqk", crossed_grad, text_values, preferred_element_type=jnp.float32
    )
    text_value_grad = jnp.einsum(
        "hqk,qhd->khd", cross_weighting, crossed_grad, preferred_element_type=jnp.float32
    )
    cross_score_grad = (
        cross_soft * (prob_grad - jnp.sum(prob_grad * cross_soft, axis=2, keepdims=True))
    ).astype(jnp.bfloat16)
    cross_query_grad = (
        (
            jnp.einsum(
                "hqk,khd->qhd", cross_score_grad, text_keys, preferred_element_type=jnp.float32
            )
            * 0.125
        )
        .reshape(rows, width)
        .astype(jnp.bfloat16)
    )
    text_key_grad = (
        jnp.einsum(
            "hqk,qhd->khd", cross_score_grad, cross_heads, preferred_element_type=jnp.float32
        )
        * 0.125
    )
    text_terms = jnp.concatenate(
        [text_key_grad.reshape(TEXT, width), text_value_grad.reshape(TEXT, width)], axis=1
    )
    text_share = lax.psum_scatter(
        text_terms.astype(jnp.bfloat16), "blk", scatter_dimension=0, tiled=True
    )
    share = TEXT // group
    text_grad = jnp.dot(text_share, full_keys.T, preferred_element_type=jnp.float32)[None]
    one_grad, gain_one, shift_one = norm_pull(
        hidden_one,
        gain_rows[1],
        shift_rows[1],
        jnp.dot(cross_query_grad, full_query.T, preferred_element_type=jnp.float32),
    )
    hidden_one_grad = hidden_two_grad + one_grad
    branch_one = hidden_one_grad.astype(jnp.bfloat16)
    attended_grad = jnp.dot(branch_one, full_outward.T, preferred_element_type=jnp.float32).astype(
        jnp.bfloat16
    )
    attended_grad = attended_grad.reshape(rows, HEADS, HEAD)
    delta = jnp.sum(attended_grad.astype(jnp.float32) * mixed, axis=2).T

    def back_step(carry, items):
        block = items[0]
        weighting = jnp.exp(scores_of(block, items[1]) - log_total[:, :, None])
        keys = block[:, :width].reshape(span, HEADS, HEAD)
        values = block[:, width:].reshape(span, HEADS, HEAD)
        value_grad = jnp.einsum(
            "hqk,qhd->khd",
            weighting.astype(jnp.bfloat16),
            attended_grad,
            preferred_element_type=jnp.float32,
        )
        weight_grad = jnp.einsum(
            "qhd,khd->hqk", attended_grad, values, preferred_element_type=jnp.float32
        )
        score_grad = (weighting * (weight_grad - delta[:, :, None])).astype(jnp.bfloat16)
        carry = carry + jnp.einsum(
            "hqk,khd->qhd", score_grad, keys, preferred_element_type=jnp.float32
        )
        key_grad = (
            jnp.einsum("hqk,qhd->khd", score_grad, queries, preferred_element_type=jnp.float32)
            * 0.125
        )
        return (
            carry,
            jnp.concatenate(
                [key_grad.reshape(span, width), value_grad.reshape(span, width)], axis=1
            ),
        )

    query_sum, pair_terms = lax.scan(
        back_step, jnp.zeros((rows, HEADS, HEAD), jnp.float32), (pair_blocks, frame_blocks)
    )
    pair_grad = lax.psum_scatter(
        pair_terms.reshape(length, 2 * width).astype(jnp.bfloat16),
        "blk",
        scatter_dimension=0,
        tiled=True,
    )
    joint_grad = jnp.concatenate(
        [(query_sum * 0.125).reshape(rows, width).astype(jnp.bfloat16), pair_grad], axis=1
    )
    zero_grad, gain_zero, shift_zero = norm_pull(
        inputs,
        gain_rows[0],
        shift_rows[0],
        jnp.dot(joint_grad, full_inward.T, preferred_element_type=jnp.float32),
    )
    frames_grad = (hidden_one_grad + zero_grad)[None]
    across = lax.axis_size("grp")
    gains_grad = (
        jnp.stack([gain_zero, gain_one, gain_two])
        .reshape(3, across, group, -1)
        .transpose(0, 2, 1, 3)
        .reshape(3, width)
    )
    shifts_grad = (
        jnp.stack([shift_zero, shift_one, shift_two])
        .reshape(3, across, group, -1)
        .transpose(0, 2, 1, 3)
        .reshape(3, width)
    )
    expand_grad, contract_grad = (
        lax.psum_scatter(
            expand_grad.astype(jnp.bfloat16), "blk", scatter_dimension=1, tiled=True
        ).astype(jnp.float32),
        lax.psum_scatter(
            contract_grad.astype(jnp.bfloat16), "blk", scatter_dimension=0, tiled=True
        ).astype(jnp.float32),
    )
    own_text = lax.dynamic_slice_in_dim(text, member * share, share, 0)
    inward_grad = jnp.dot(first.T, joint_grad, preferred_element_type=jnp.float32)
    outward_grad = jnp.dot(attended.T, branch_one, preferred_element_type=jnp.float32)
    querying_grad = jnp.dot(second.T, cross_query_grad, preferred_element_type=jnp.float32)
    keying_grad = jnp.dot(own_text.T, text_share, preferred_element_type=jnp.float32)
    returning_grad = jnp.dot(crossed.T, branch_two, preferred_element_type=jnp.float32)
    (
        inward_grad,
        outward_grad,
        querying_grad,
        keying_grad,
        returning_grad,
        gains_grad,
        shifts_grad,
    ) = (
        lax.psum_scatter(
            inward_grad.astype(jnp.bfloat16), "blk", scatter_dimension=1, tiled=True
        ).astype(jnp.float32),
        lax.psum_scatter(
            outward_grad.astype(jnp.bfloat16), "blk", scatter_dimension=1, tiled=True
        ).astype(jnp.float32),
        lax.psum_scatter(
            querying_grad.astype(jnp.bfloat16), "blk", scatter_dimension=1, tiled=True
        ).astype(jnp.float32),
        lax.psum_scatter(
            keying_grad.astype(jnp.bfloat16), "blk", scatter_dimension=1, tiled=True
        ).astype(jnp.float32),
        lax.psum_scatter(
            returning_grad.astype(jnp.bfloat16), "blk", scatter_dimension=1, tiled=True
        ).astype(jnp.float32),
        lax.psum_scatter(
            gains_grad.astype(jnp.bfloat16), "blk", scatter_dimension=1, tiled=True
        ).astype(jnp.float32),
        lax.psum_scatter(
            shifts_grad.astype(jnp.bfloat16), "blk", scatter_dimension=1, tiled=True
        ).astype(jnp.float32),
    )
    (
        inward_grad,
        outward_grad,
        querying_grad,
        keying_grad,
        returning_grad,
        expand_grad,
        contract_grad,
        gains_grad,
        shifts_grad,
    ) = (
        lax.psum_scatter(
            inward_grad.astype(jnp.bfloat16), "grp", scatter_dimension=0, tiled=True
        ).astype(jnp.float32),
        lax.psum_scatter(
            outward_grad.astype(jnp.bfloat16), "grp", scatter_dimension=0, tiled=True
        ).astype(jnp.float32),
        lax.psum_scatter(
            querying_grad.astype(jnp.bfloat16), "grp", scatter_dimension=0, tiled=True
        ).astype(jnp.float32),
        lax.psum_scatter(
            keying_grad.astype(jnp.bfloat16), "grp", scatter_dimension=0, tiled=True
        ).astype(jnp.float32),
        lax.psum_scatter(
            returning_grad.astype(jnp.bfloat16), "grp", scatter_dimension=0, tiled=True
        ).astype(jnp.float32),
        lax.psum_scatter(
            expand_grad.astype(jnp.bfloat16), "grp", scatter_dimension=0, tiled=True
        ).astype(jnp.float32),
        lax.psum_scatter(
            contract_grad.astype(jnp.bfloat16), "grp", scatter_dimension=1, tiled=True
        ).astype(jnp.float32),
        lax.psum_scatter(
            gains_grad.astype(jnp.bfloat16), "grp", scatter_dimension=1, tiled=True
        ).astype(jnp.float32),
        lax.psum_scatter(
            shifts_grad.astype(jnp.bfloat16), "grp", scatter_dimension=1, tiled=True
        ).astype(jnp.float32),
    )
    return (
        block_out,
        frames_grad,
        text_grad,
        inward_grad,
        outward_grad,
        querying_grad,
        keying_grad,
        returning_grad,
        expand_grad,
        contract_grad,
        gains_grad,
        shifts_grad,
    )


def tp_shards(
    frames,
    text_states,
    block_table,
    inward,
    outward,
    querying,
    keying,
    returning,
    expand,
    contract,
    gains,
    shifts,
    out_grad,
):
    bf16, f32 = jnp.bfloat16, jnp.float32
    width = frames.shape[2]
    rows = frames.shape[1]
    group = lax.axis_size("blk")
    member = lax.axis_index("blk")
    length = rows * group
    heads = HEADS // group
    wide = heads * HEAD

    def mm(left, right):
        return jnp.dot(left, right, preferred_element_type=f32)

    def mm_t(left, right):
        return lax.dot_general(left, right, (((1,), (1,)), ((), ())), preferred_element_type=f32)

    def t_mm(left, right):
        return lax.dot_general(left, right, (((0,), (0,)), ((), ())), preferred_element_type=f32)

    def blk_rows(item):
        return lax.all_gather(item, "blk", axis=0, tiled=True)

    def blk_cols(item):
        return lax.all_gather(item, "blk", axis=1, tiled=True)

    def sum_rows(item):
        return lax.psum_scatter(item.astype(bf16), "blk", scatter_dimension=0, tiled=True).astype(f32)

    def sum_cols(item):
        return lax.psum_scatter(item.astype(bf16), "blk", scatter_dimension=1, tiled=True)

    def turn(item):
        return lax.all_to_all(item, "blk", split_axis=1, concat_axis=0, tiled=True)

    def own_rows(item):
        return lax.dynamic_slice_in_dim(item, member * rows, rows, 0)

    def own_cols(item, size):
        return lax.dynamic_slice_in_dim(item, member * size, size, 1)

    def spread(item, axis):
        return lax.all_gather(item, "grp", axis=axis, tiled=True)

    def collect(item, axis):
        return lax.psum_scatter(
            item.astype(bf16), "grp", scatter_dimension=axis, tiled=True
        )

    whole = blk_cols(inward)
    aligned = jnp.concatenate(
        [lax.dynamic_slice_in_dim(whole, part * width + member * wide, wide, 1) for part in range(3)],
        axis=1,
    )
    full_inward = spread(aligned, 0)
    full_outward = spread(outward, 0)
    full_query = spread(querying, 0)
    full_keys = spread(keying, 0)
    full_return = spread(returning, 0)
    full_expand = spread(expand, 0)
    full_contract = spread(contract, 1)
    norms = lax.all_gather(
        jnp.concatenate([gains, shifts], axis=0), ("grp", "blk"), axis=1, tiled=True
    ).astype(f32)
    gain_rows, shift_rows = norms[:3], norms[3:]

    frame_ids = (
        block_table[0][:, None] * SEG + jnp.arange(SEG, dtype=jnp.int32)[None, :]
    ).reshape(length)
    allowed = frame_ids[None, :] <= frame_ids[:, None]

    def split(item):
        return item.reshape(item.shape[0], heads, HEAD)

    inputs_all = blk_rows(frames[0]).astype(f32)
    first = layer_norm(inputs_all, gain_rows[0], shift_rows[0]).astype(bf16)
    joint = mm(first, full_inward).astype(bf16)
    queries, keys, values = (split(joint[:, part * wide : (part + 1) * wide]) for part in range(3))
    scores = jnp.einsum("qhd,khd->hqk", queries, keys, preferred_element_type=f32) * 0.125
    soft = jax.nn.softmax(jnp.where(allowed[None], scores, -1e30), axis=2)
    weighting = soft.astype(bf16)
    attended = (
        jnp.einsum("hqk,khd->qhd", weighting, values, preferred_element_type=f32)
        .reshape(length, wide)
        .astype(bf16)
    )
    attended_all = blk_cols(attended)
    one = own_cols(inputs_all, wide) + mm(attended_all, full_outward)
    one_all = blk_cols(one.astype(bf16)).astype(f32)
    second = layer_norm(one_all, gain_rows[1], shift_rows[1]).astype(bf16)
    cross_query = mm(second, full_query).astype(bf16)
    cross_heads = split(cross_query)
    text = text_states[0]
    text_pairs = blk_cols(mm(text, full_keys).astype(bf16))
    text_keys = split(own_cols(text_pairs[:, :width], wide))
    text_values = split(own_cols(text_pairs[:, width:], wide))
    cross_scores = (
        jnp.einsum("qhd,khd->hqk", cross_heads, text_keys, preferred_element_type=f32) * 0.125
    )
    cross_soft = jax.nn.softmax(cross_scores, axis=2)
    cross_weighting = cross_soft.astype(bf16)
    crossed = (
        jnp.einsum("hqk,khd->qhd", cross_weighting, text_values, preferred_element_type=f32)
        .reshape(length, wide)
        .astype(bf16)
    )
    crossed_all = blk_cols(crossed)
    two = one + mm(crossed_all, full_return)
    two_all = blk_cols(two.astype(bf16)).astype(f32)
    third = layer_norm(two_all, gain_rows[2], shift_rows[2]).astype(bf16)
    upward = mm(third, full_expand)
    activated = jax.nn.gelu(upward, approximate=False).astype(bf16)
    branch = sum_rows(mm(activated, full_contract))
    two_rows = own_rows(two_all)
    block_out = (two_rows + branch).astype(bf16)[None]

    incoming = out_grad[0].astype(f32)
    grad_all = blk_rows(out_grad[0])
    act_grad = mm_t(grad_all, full_contract)
    contract_grad = collect(t_mm(activated, grad_all), 1)
    up_grad = (act_grad * gelu_slope(upward)).astype(bf16)
    expand_grad = collect(t_mm(third, up_grad), 0)
    third_grad = sum_rows(mm_t(up_grad, full_expand))
    two_grad, gain_two, shift_two = norm_pull(two_rows, gain_rows[2], shift_rows[2], third_grad)
    hidden_two_grad = incoming + two_grad
    branch_two = turn(hidden_two_grad.astype(bf16))
    returning_grad = collect(t_mm(crossed_all, branch_two), 0)
    crossed_grad = split(sum_cols(mm_t(branch_two, full_return)))
    prob_grad = jnp.einsum("qhd,khd->hqk", crossed_grad, text_values, preferred_element_type=f32)
    text_value_grad = jnp.einsum(
        "hqk,qhd->khd", cross_weighting, crossed_grad, preferred_element_type=f32
    )
    cross_score_grad = (
        cross_soft * (prob_grad - jnp.sum(prob_grad * cross_soft, axis=2, keepdims=True))
    ).astype(bf16)
    cross_query_grad = (
        (jnp.einsum("hqk,khd->qhd", cross_score_grad, text_keys, preferred_element_type=f32) * 0.125)
        .reshape(length, wide)
        .astype(bf16)
    )
    text_key_grad = (
        jnp.einsum("hqk,qhd->khd", cross_score_grad, cross_heads, preferred_element_type=f32) * 0.125
    )
    text_terms = blk_cols(
        jnp.concatenate(
            [text_key_grad.reshape(TEXT, wide), text_value_grad.reshape(TEXT, wide)], axis=1
        ).astype(bf16)
    ).reshape(TEXT, group, 2, wide)
    text_terms = text_terms.transpose(0, 2, 1, 3).reshape(TEXT, 2 * width)
    own_terms = own_cols(text_terms, 2 * wide)
    keying_grad = collect(t_mm(text, own_terms), 0)
    text_grad = sum_rows(mm_t(own_terms, full_keys))[None]
    querying_grad = collect(t_mm(second, cross_query_grad), 0)
    one_rows = own_rows(one_all)
    one_grad, gain_one, shift_one = norm_pull(
        one_rows, gain_rows[1], shift_rows[1], sum_rows(mm_t(cross_query_grad, full_query))
    )
    hidden_one_grad = hidden_two_grad + one_grad
    branch_one = turn(hidden_one_grad.astype(bf16))
    outward_grad = collect(t_mm(attended_all, branch_one), 0)
    attended_grad = split(sum_cols(mm_t(branch_one, full_outward)))
    value_grad = jnp.einsum("hqk,qhd->khd", weighting, attended_grad, preferred_element_type=f32)
    weight_grad = jnp.einsum("qhd,khd->hqk", attended_grad, values, preferred_element_type=f32)
    score_grad = (
        soft * (weight_grad - jnp.sum(weight_grad * soft, axis=2, keepdims=True))
    ).astype(bf16)
    query_grad = jnp.einsum("hqk,khd->qhd", score_grad, keys, preferred_element_type=f32) * 0.125
    key_grad = jnp.einsum("hqk,qhd->khd", score_grad, queries, preferred_element_type=f32) * 0.125
    joint_grad = jnp.concatenate(
        [item.reshape(length, wide).astype(bf16) for item in (query_grad, key_grad, value_grad)],
        axis=1,
    )
    inward_grad = collect(t_mm(first, joint_grad), 0)
    zero_grad, gain_zero, shift_zero = norm_pull(
        frames[0].astype(f32),
        gain_rows[0],
        shift_rows[0],
        sum_rows(mm_t(joint_grad, full_inward)),
    )
    frames_grad = (hidden_one_grad + zero_grad)[None]
    inward_all = blk_cols(inward_grad).reshape(-1, group, 3, wide).transpose(0, 2, 1, 3)
    inward_grad = own_cols(inward_all.reshape(-1, 3 * width), 3 * wide)
    norm_grads = lax.psum_scatter(
        jnp.stack([gain_zero, gain_one, gain_two, shift_zero, shift_one, shift_two]),
        ("grp", "blk"),
        scatter_dimension=1,
        tiled=True,
    )
    return (
        block_out,
        frames_grad,
        text_grad,
        inward_grad.astype(f32),
        outward_grad.astype(f32),
        querying_grad.astype(f32),
        keying_grad.astype(f32),
        returning_grad.astype(f32),
        expand_grad.astype(f32),
        contract_grad.astype(f32),
        norm_grads[:3],
        norm_grads[3:],
    )


def solution(mesh):
    return jax.shard_map(
        tp_shards if HEADS % mesh.shape["blk"] == 0 else shards,
        mesh=mesh,
        in_specs=(
            P("grp", "blk", None),
            P("grp", None, None),
            P("grp", None),
            P("grp", "blk"),
            P("grp", "blk"),
            P("grp", "blk"),
            P("grp", "blk"),
            P("grp", "blk"),
            P("grp", "blk"),
            P("blk", "grp"),
            P(None, ("grp", "blk")),
            P(None, ("grp", "blk")),
            P("grp", "blk", None),
        ),
        out_specs=(
            P("grp", "blk", None),
            P("grp", "blk", None),
            P("grp", "blk", None),
            P("grp", "blk"),
            P("grp", "blk"),
            P("grp", "blk"),
            P("grp", "blk"),
            P("grp", "blk"),
            P("grp", "blk"),
            P("blk", "grp"),
            P(None, ("grp", "blk")),
            P(None, ("grp", "blk")),
        ),
        check_vma=False,
    )
```

```python
import functools
import math

import jax
import jax.numpy as jnp
from jax import lax
from jax.experimental import pallas as pl
from jax.experimental.pallas import tpu as pltpu
from jax.sharding import PartitionSpec as P

HEADS = 24
HEAD = 64
TEXT = 64
SEG = 64


def layer_norm(values, gain, shift):
    center = values - jnp.mean(values, axis=-1, keepdims=True)
    spread = jnp.mean(center * center, axis=-1, keepdims=True)
    return center * lax.rsqrt(spread + 1e-05) * gain + shift


def norm_pull(values, gain, shift, incoming):
    unused, pullback = jax.vjp(layer_norm, values, gain, shift)
    return pullback(incoming)


def gelu_slope(upward):
    return (
        0.5 * (1.0 + lax.erf(upward * 0.7071067811865476))
        + upward * jnp.exp(-0.5 * upward * upward) * 0.3989422804014327
    )


def gather_weights(inward, outward, querying, keying, returning, expand, contract, gains, shifts):
    inward, outward, querying, keying, returning, expand, contract, gains, shifts = (
        lax.all_gather(inward, "blk", axis=1, tiled=True),
        lax.all_gather(outward, "blk", axis=1, tiled=True),
        lax.all_gather(querying, "blk", axis=1, tiled=True),
        lax.all_gather(keying, "blk", axis=1, tiled=True),
        lax.all_gather(returning, "blk", axis=1, tiled=True),
        lax.all_gather(expand, "blk", axis=1, tiled=True),
        lax.all_gather(contract, "blk", axis=0, tiled=True),
        lax.all_gather(gains, "blk", axis=1, tiled=True),
        lax.all_gather(shifts, "blk", axis=1, tiled=True),
    )
    return (
        lax.all_gather(inward, "grp", axis=0, tiled=True),
        lax.all_gather(outward, "grp", axis=0, tiled=True),
        lax.all_gather(querying, "grp", axis=0, tiled=True),
        lax.all_gather(keying, "grp", axis=0, tiled=True),
        lax.all_gather(returning, "grp", axis=0, tiled=True),
        lax.all_gather(expand, "grp", axis=0, tiled=True),
        lax.all_gather(contract, "grp", axis=1, tiled=True),
        lax.all_gather(gains, "grp", axis=1, tiled=True),
        lax.all_gather(shifts, "grp", axis=1, tiled=True),
    )


def shards(
    frames,
    text_states,
    block_table,
    inward,
    outward,
    querying,
    keying,
    returning,
    expand,
    contract,
    gains,
    shifts,
    out_grad,
):
    (
        full_inward,
        full_outward,
        full_query,
        full_keys,
        full_return,
        full_expand,
        full_contract,
        full_gains,
        full_shifts,
    ) = gather_weights(
        inward, outward, querying, keying, returning, expand, contract, gains, shifts
    )
    width = frames.shape[2]
    rows = frames.shape[1]
    length = block_table.shape[1] * SEG
    group = lax.axis_size("blk")
    member = lax.axis_index("blk")
    span = math.gcd(length, 512)
    steps = length // span
    gain_rows = full_gains.astype(jnp.float32)
    shift_rows = full_shifts.astype(jnp.float32)
    key_frames = (
        block_table[0][:, None] * SEG + jnp.arange(SEG, dtype=jnp.int32)[None, :]
    ).reshape(length)
    own_frames = lax.dynamic_slice_in_dim(key_frames, member * rows, rows, 0)
    inputs = frames[0].astype(jnp.float32)
    first = layer_norm(inputs, gain_rows[0], shift_rows[0]).astype(jnp.bfloat16)
    joint = jnp.dot(first, full_inward, preferred_element_type=jnp.float32).astype(jnp.bfloat16)
    queries = joint[:, :width].reshape(rows, HEADS, HEAD)
    pairs = lax.all_gather(joint[:, width:], "blk", axis=0, tiled=True)
    pair_blocks = pairs.reshape(steps, span, 2 * width)
    frame_blocks = key_frames.reshape(steps, span)

    def scores_of(block, block_frames):
        keys = block[:, :width].reshape(span, HEADS, HEAD)
        raw = jnp.einsum("qhd,khd->hqk", queries, keys, preferred_element_type=jnp.float32) * 0.125
        allowed = block_frames[None, :] <= own_frames[:, None]
        return jnp.where(allowed[None], raw, -1e30)

    def stat_step(carry, items):
        peak, total = carry
        scores = scores_of(items[0], items[1])
        higher = jnp.maximum(peak, jnp.max(scores, axis=2))
        total = total * jnp.exp(peak - higher) + jnp.sum(
            jnp.exp(scores - higher[:, :, None]), axis=2
        )
        return ((higher, total), None)

    start_peak = jnp.full((HEADS, rows), -1e30, jnp.float32)
    (peak, total), unused = lax.scan(
        stat_step, (start_peak, jnp.zeros((HEADS, rows), jnp.float32)), (pair_blocks, frame_blocks)
    )
    log_total = peak + jnp.log(total)

    def out_step(carry, items):
        weighting = jnp.exp(scores_of(items[0], items[1]) - log_total[:, :, None]).astype(
            jnp.bfloat16
        )
        values = items[0][:, width:].reshape(span, HEADS, HEAD)
        return (
            carry
            + jnp.einsum("hqk,khd->qhd", weighting, values, preferred_element_type=jnp.float32),
            None,
        )

    mixed, unused = lax.scan(
        out_step, jnp.zeros((rows, HEADS, HEAD), jnp.float32), (pair_blocks, frame_blocks)
    )
    attended = mixed.reshape(rows, width).astype(jnp.bfloat16)
    hidden_one = inputs + jnp.dot(attended, full_outward, preferred_element_type=jnp.float32)
    second = layer_norm(hidden_one, gain_rows[1], shift_rows[1]).astype(jnp.bfloat16)
    cross_query = jnp.dot(second, full_query, preferred_element_type=jnp.float32).astype(
        jnp.bfloat16
    )
    cross_heads = cross_query.reshape(rows, HEADS, HEAD)
    text = text_states[0]
    text_pairs = jnp.dot(text, full_keys, preferred_element_type=jnp.float32).astype(jnp.bfloat16)
    text_keys = text_pairs[:, :width].reshape(TEXT, HEADS, HEAD)
    text_values = text_pairs[:, width:].reshape(TEXT, HEADS, HEAD)
    cross_scores = (
        jnp.einsum("qhd,khd->hqk", cross_heads, text_keys, preferred_element_type=jnp.float32)
        * 0.125
    )
    cross_soft = jax.nn.softmax(cross_scores, axis=2)
    cross_weighting = cross_soft.astype(jnp.bfloat16)
    crossed = (
        jnp.einsum("hqk,khd->qhd", cross_weighting, text_values, preferred_element_type=jnp.float32)
        .reshape(rows, width)
        .astype(jnp.bfloat16)
    )
    hidden_two = hidden_one + jnp.dot(crossed, full_return, preferred_element_type=jnp.float32)
    third = layer_norm(hidden_two, gain_rows[2], shift_rows[2]).astype(jnp.bfloat16)
    upward = jnp.dot(third, full_expand, preferred_element_type=jnp.float32)
    activated = jax.nn.gelu(upward, approximate=False).astype(jnp.bfloat16)
    branch = jnp.dot(activated, full_contract, preferred_element_type=jnp.float32)
    block_out = (hidden_two + branch).astype(jnp.bfloat16)[None]
    (
        full_inward,
        full_outward,
        full_query,
        full_keys,
        full_return,
        full_expand,
        full_contract,
        full_gains,
        full_shifts,
    ) = gather_weights(
        inward, outward, querying, keying, returning, expand, contract, gains, shifts
    )
    incoming = out_grad[0].astype(jnp.float32)
    branch_grad = out_grad[0]
    act_grad = jnp.dot(branch_grad, full_contract.T, preferred_element_type=jnp.float32)
    contract_grad = jnp.dot(activated.T, branch_grad, preferred_element_type=jnp.float32)
    up_grad = (act_grad * gelu_slope(upward)).astype(jnp.bfloat16)
    expand_grad = jnp.dot(third.T, up_grad, preferred_element_type=jnp.float32)
    third_grad = jnp.dot(up_grad, full_expand.T, preferred_element_type=jnp.float32)
    two_grad, gain_two, shift_two = norm_pull(hidden_two, gain_rows[2], shift_rows[2], third_grad)
    hidden_two_grad = incoming + two_grad
    branch_two = hidden_two_grad.astype(jnp.bfloat16)
    crossed_grad = jnp.dot(branch_two, full_return.T, preferred_element_type=jnp.float32).astype(
        jnp.bfloat16
    )
    crossed_grad = crossed_grad.reshape(rows, HEADS, HEAD)
    prob_grad = jnp.einsum(
        "qhd,khd->hqk", crossed_grad, text_values, preferred_element_type=jnp.float32
    )
    text_value_grad = jnp.einsum(
        "hqk,qhd->khd", cross_weighting, crossed_grad, preferred_element_type=jnp.float32
    )
    cross_score_grad = (
        cross_soft * (prob_grad - jnp.sum(prob_grad * cross_soft, axis=2, keepdims=True))
    ).astype(jnp.bfloat16)
    cross_query_grad = (
        (
            jnp.einsum(
                "hqk,khd->qhd", cross_score_grad, text_keys, preferred_element_type=jnp.float32
            )
            * 0.125
        )
        .reshape(rows, width)
        .astype(jnp.bfloat16)
    )
    text_key_grad = (
        jnp.einsum(
            "hqk,qhd->khd", cross_score_grad, cross_heads, preferred_element_type=jnp.float32
        )
        * 0.125
    )
    text_terms = jnp.concatenate(
        [text_key_grad.reshape(TEXT, width), text_value_grad.reshape(TEXT, width)], axis=1
    )
    text_share = lax.psum_scatter(
        text_terms.astype(jnp.bfloat16), "blk", scatter_dimension=0, tiled=True
    )
    share = TEXT // group
    text_grad = jnp.dot(text_share, full_keys.T, preferred_element_type=jnp.float32)[None]
    one_grad, gain_one, shift_one = norm_pull(
        hidden_one,
        gain_rows[1],
        shift_rows[1],
        jnp.dot(cross_query_grad, full_query.T, preferred_element_type=jnp.float32),
    )
    hidden_one_grad = hidden_two_grad + one_grad
    branch_one = hidden_one_grad.astype(jnp.bfloat16)
    attended_grad = jnp.dot(branch_one, full_outward.T, preferred_element_type=jnp.float32).astype(
        jnp.bfloat16
    )
    attended_grad = attended_grad.reshape(rows, HEADS, HEAD)
    delta = jnp.sum(attended_grad.astype(jnp.float32) * mixed, axis=2).T

    def back_step(carry, items):
        block = items[0]
        weighting = jnp.exp(scores_of(block, items[1]) - log_total[:, :, None])
        keys = block[:, :width].reshape(span, HEADS, HEAD)
        values = block[:, width:].reshape(span, HEADS, HEAD)
        value_grad = jnp.einsum(
            "hqk,qhd->khd",
            weighting.astype(jnp.bfloat16),
            attended_grad,
            preferred_element_type=jnp.float32,
        )
        weight_grad = jnp.einsum(
            "qhd,khd->hqk", attended_grad, values, preferred_element_type=jnp.float32
        )
        score_grad = (weighting * (weight_grad - delta[:, :, None])).astype(jnp.bfloat16)
        carry = carry + jnp.einsum(
            "hqk,khd->qhd", score_grad, keys, preferred_element_type=jnp.float32
        )
        key_grad = (
            jnp.einsum("hqk,qhd->khd", score_grad, queries, preferred_element_type=jnp.float32)
            * 0.125
        )
        return (
            carry,
            jnp.concatenate(
                [key_grad.reshape(span, width), value_grad.reshape(span, width)], axis=1
            ),
        )

    query_sum, pair_terms = lax.scan(
        back_step, jnp.zeros((rows, HEADS, HEAD), jnp.float32), (pair_blocks, frame_blocks)
    )
    pair_grad = lax.psum_scatter(
        pair_terms.reshape(length, 2 * width).astype(jnp.bfloat16),
        "blk",
        scatter_dimension=0,
        tiled=True,
    )
    joint_grad = jnp.concatenate(
        [(query_sum * 0.125).reshape(rows, width).astype(jnp.bfloat16), pair_grad], axis=1
    )
    zero_grad, gain_zero, shift_zero = norm_pull(
        inputs,
        gain_rows[0],
        shift_rows[0],
        jnp.dot(joint_grad, full_inward.T, preferred_element_type=jnp.float32),
    )
    frames_grad = (hidden_one_grad + zero_grad)[None]
    across = lax.axis_size("grp")
    gains_grad = (
        jnp.stack([gain_zero, gain_one, gain_two])
        .reshape(3, across, group, -1)
        .transpose(0, 2, 1, 3)
        .reshape(3, width)
    )
    shifts_grad = (
        jnp.stack([shift_zero, shift_one, shift_two])
        .reshape(3, across, group, -1)
        .transpose(0, 2, 1, 3)
        .reshape(3, width)
    )
    expand_grad, contract_grad = (
        lax.psum_scatter(
            expand_grad.astype(jnp.bfloat16), "blk", scatter_dimension=1, tiled=True
        ).astype(jnp.float32),
        lax.psum_scatter(
            contract_grad.astype(jnp.bfloat16), "blk", scatter_dimension=0, tiled=True
        ).astype(jnp.float32),
    )
    own_text = lax.dynamic_slice_in_dim(text, member * share, share, 0)
    inward_grad = jnp.dot(first.T, joint_grad, preferred_element_type=jnp.float32)
    outward_grad = jnp.dot(attended.T, branch_one, preferred_element_type=jnp.float32)
    querying_grad = jnp.dot(second.T, cross_query_grad, preferred_element_type=jnp.float32)
    keying_grad = jnp.dot(own_text.T, text_share, preferred_element_type=jnp.float32)
    returning_grad = jnp.dot(crossed.T, branch_two, preferred_element_type=jnp.float32)
    (
        inward_grad,
        outward_grad,
        querying_grad,
        keying_grad,
        returning_grad,
        gains_grad,
        shifts_grad,
    ) = (
        lax.psum_scatter(
            inward_grad.astype(jnp.bfloat16), "blk", scatter_dimension=1, tiled=True
        ).astype(jnp.float32),
        lax.psum_scatter(
            outward_grad.astype(jnp.bfloat16), "blk", scatter_dimension=1, tiled=True
        ).astype(jnp.float32),
        lax.psum_scatter(
            querying_grad.astype(jnp.bfloat16), "blk", scatter_dimension=1, tiled=True
        ).astype(jnp.float32),
        lax.psum_scatter(
            keying_grad.astype(jnp.bfloat16), "blk", scatter_dimension=1, tiled=True
        ).astype(jnp.float32),
        lax.psum_scatter(
            returning_grad.astype(jnp.bfloat16), "blk", scatter_dimension=1, tiled=True
        ).astype(jnp.float32),
        lax.psum_scatter(
            gains_grad.astype(jnp.bfloat16), "blk", scatter_dimension=1, tiled=True
        ).astype(jnp.float32),
        lax.psum_scatter(
            shifts_grad.astype(jnp.bfloat16), "blk", scatter_dimension=1, tiled=True
        ).astype(jnp.float32),
    )
    (
        inward_grad,
        outward_grad,
        querying_grad,
        keying_grad,
        returning_grad,
        expand_grad,
        contract_grad,
        gains_grad,
        shifts_grad,
    ) = (
        lax.psum_scatter(
            inward_grad.astype(jnp.bfloat16), "grp", scatter_dimension=0, tiled=True
        ).astype(jnp.float32),
        lax.psum_scatter(
            outward_grad.astype(jnp.bfloat16), "grp", scatter_dimension=0, tiled=True
        ).astype(jnp.float32),
        lax.psum_scatter(
            querying_grad.astype(jnp.bfloat16), "grp", scatter_dimension=0, tiled=True
        ).astype(jnp.float32),
        lax.psum_scatter(
            keying_grad.astype(jnp.bfloat16), "grp", scatter_dimension=0, tiled=True
        ).astype(jnp.float32),
        lax.psum_scatter(
            returning_grad.astype(jnp.bfloat16), "grp", scatter_dimension=0, tiled=True
        ).astype(jnp.float32),
        lax.psum_scatter(
            expand_grad.astype(jnp.bfloat16), "grp", scatter_dimension=0, tiled=True
        ).astype(jnp.float32),
        lax.psum_scatter(
            contract_grad.astype(jnp.bfloat16), "grp", scatter_dimension=1, tiled=True
        ).astype(jnp.float32),
        lax.psum_scatter(
            gains_grad.astype(jnp.bfloat16), "grp", scatter_dimension=1, tiled=True
        ).astype(jnp.float32),
        lax.psum_scatter(
            shifts_grad.astype(jnp.bfloat16), "grp", scatter_dimension=1, tiled=True
        ).astype(jnp.float32),
    )
    return (
        block_out,
        frames_grad,
        text_grad,
        inward_grad,
        outward_grad,
        querying_grad,
        keying_grad,
        returning_grad,
        expand_grad,
        contract_grad,
        gains_grad,
        shifts_grad,
    )


MESH = pl.DeviceIdType.MESH
BF16, F32 = jnp.bfloat16, jnp.float32


class Bag:
    def __init__(self, **items):
        self.__dict__.update(items)


def named(keys, items):
    return Bag(**dict(zip(keys, items)))


class Spot:
    def __init__(self):
        grp, blk = lax.axis_index("grp"), lax.axis_index("blk")
        self.grp, self.blk = grp, blk
        self.z, self.y = grp // 2, lax.rem(grp, 2)
        self.x, self.core = blk // 2, lax.rem(blk, 2)
        self.sib_blk = self.x * 2 + 1 - self.core
        self.opp_blk = (1 - self.x) * 2 + self.core
        self.sib = (grp, self.sib_blk)
        self.opp = (grp, self.opp_blk)
        self.part = (self.z * 2 + 1 - self.y, blk)
        self.up = ((self.z + 1) * 2 + self.y, blk)
        self.down = ((self.z - 1) * 2 + self.y, blk)

        self.far_blk = (1 - self.x) * 2 + 1 - self.core

    def z_peer(self, k):
        return (lax.rem(self.z + k, 4) * 2 + self.y, self.blk)

    def greet_all(self):
        barrier = pltpu.get_barrier_semaphore()
        peers = [self.z_peer(k) for k in (1, 2, 3)]
        for who in [self.sib, self.opp, (self.grp, self.far_blk), self.part] + peers:
            pl.semaphore_signal(barrier, inc=1, device_id=who, device_id_type=MESH)
        pl.semaphore_wait(barrier, 7)

    def greet(self):
        barrier = pltpu.get_barrier_semaphore()
        for who in (self.sib, self.opp, self.part):
            pl.semaphore_signal(barrier, inc=1, device_id=who, device_id_type=MESH)

        @pl.when(self.z > 0)
        def _():
            pl.semaphore_signal(barrier, inc=1, device_id=self.down, device_id_type=MESH)

        @pl.when(self.z < 3)
        def _():
            pl.semaphore_signal(barrier, inc=1, device_id=self.up, device_id_type=MESH)

        ends = (self.z == 0) | (self.z == 3)

        @pl.when(ends)
        def _():
            pl.semaphore_wait(barrier, 4)

        @pl.when(jnp.logical_not(ends))
        def _():
            pl.semaphore_wait(barrier, 5)


def push(src, dst, send, recv, who):
    return pltpu.make_async_remote_copy(
        src_ref=src, dst_ref=dst, send_sem=send, recv_sem=recv, device_id=who, device_id_type=MESH
    )


class Gather:
    def __init__(self, spot, shard, full, zsend, zrecv, ysend, yrecv, near, spread):
        self.spot, self.shard, self.full = spot, shard, full
        self.zsend, self.zrecv, self.ysend, self.yrecv, self.near = zsend, zrecv, ysend, yrecv, near
        self.spread = spread
        self.size = shard.shape[0]

    def rows(self, z, flip=0):
        spot = self.spot
        row = z * 2 + (1 - spot.y if flip else spot.y)
        return self.full.at[pl.ds(pl.multiple_of(row * self.size, self.size), self.size)]

    def z_copy(self, src, dst, k, side, flip):
        slot = (flip * 2 + side) * 3 + k - 1
        who = self.spot.up if side else self.spot.down
        return push(src, dst, self.zsend.at[slot], self.zrecv.at[slot], who)

    def y_copy(self, src, dst, slot):
        return push(src, dst, self.ysend.at[slot], self.yrecv.at[slot], self.spot.part)

    def launch(self, src, flip):
        spot = self.spot

        @pl.when(spot.z > 0)
        def _():
            self.z_copy(src, self.rows(spot.z, flip), 1, 0, flip).start()

        @pl.when(spot.z < 3)
        def _():
            self.z_copy(src, self.rows(spot.z, flip), 1, 1, flip).start()

    def start(self):
        here = self.rows(self.spot.z)
        self.y_copy(self.shard, here, 0).start()
        self.launch(self.shard, 0)
        pltpu.make_async_copy(self.shard, here, self.near).start()

    def relay(self, k):
        spot = self.spot
        if self.spread and k == 1:
            other = self.rows(spot.z, 1)
            self.y_copy(other, other, 0).wait_recv()
            self.launch(other, 1)
        for flip in (0, 1) if self.spread else (0,):
            for side in (0, 1):
                src_z = spot.z - k if side else spot.z + k
                block = self.rows(src_z, flip)

                @pl.when(src_z >= 0 if side else src_z <= 3)
                def _():
                    self.z_copy(block, block, k, side, flip).wait_recv()
                    if k < 3:

                        @pl.when(spot.z < 3 if side else spot.z > 0)
                        def _():
                            self.z_copy(block, block, k + 1, side, flip).start()

                    if not self.spread:
                        self.y_copy(block, block, 1 + side * 3 + k - 1).start()

    def finish(self):
        spot = self.spot
        pltpu.make_async_copy(self.shard, self.rows(spot.z), self.near).wait()
        if self.spread:
            return
        self.y_copy(self.shard, self.rows(spot.z, 1), 0).wait_recv()
        for side in (0, 1):
            for k in (1, 2, 3):
                src_z = spot.z - k if side else spot.z + k
                block = self.rows(src_z, 1)

                @pl.when(src_z >= 0 if side else src_z <= 3)
                def _():
                    self.y_copy(block, block, 1 + side * 3 + k - 1).wait_recv()

    def drain(self):
        spot = self.spot
        self.y_copy(self.shard, self.rows(spot.z), 0).wait_send()
        for side in (0, 1):
            for k in (1, 2, 3):
                src_z = spot.z - k if side else spot.z + k
                sent_z = spot.z - k + 1 if side else spot.z + k - 1
                block = self.rows(spot.z)
                if not self.spread:

                    @pl.when(src_z >= 0 if side else src_z <= 3)
                    def _():
                        self.y_copy(block, block, 1 + side * 3 + k - 1).wait_send()

                for flip in (0, 1) if self.spread else (0,):

                    @pl.when((spot.z < 3) & (sent_z >= 0) if side else (spot.z > 0) & (sent_z <= 3))
                    def _():
                        self.z_copy(block, block, k, side, flip).wait_send()


class Share:
    def __init__(self, spot, own, where, send, recv):
        self.spot, self.own, self.where, self.send, self.recv = spot, own, where, send, recv

    def first(self):
        return push(
            self.own, self.where(self.spot.blk), self.send.at[0], self.recv.at[0], self.spot.opp
        )

    def second(self):
        return push(
            self.own, self.where(self.spot.blk), self.send.at[1], self.recv.at[1], self.spot.sib
        )

    def third(self):
        passed = self.where(self.spot.opp_blk)
        return push(passed, passed, self.send.at[2], self.recv.at[2], self.spot.sib)

    def start(self):
        self.first().start()
        self.second().start()

    def relay(self):
        self.first().wait_recv()
        self.third().start()

    def finish(self):
        self.second().wait_recv()
        self.third().wait_recv()

    def drain(self):
        self.first().wait_send()
        self.second().wait_send()
        self.third().wait_send()


def dot(left, right):
    return jnp.dot(left, right, preferred_element_type=F32)


def dot_t(left, right):
    return lax.dot_general(left, right, (((1,), (1,)), ((), ())), preferred_element_type=F32)


def tiles(count, size, body):
    @pl.loop(0, count)
    def _(step):
        body(pl.ds(pl.multiple_of(step * size, size), size))


def norm_block(values, gain, shift):
    center = values - jnp.mean(values, axis=1, keepdims=True)
    spread = jnp.mean(center * center, axis=1, keepdims=True)
    return center * lax.rsqrt(spread + 1e-05) * gain + shift


def forward_kernel(names, *refs):
    r = named(names, refs)
    spot = Spot()
    rows, width = r.frames.shape
    length = r.x_all.shape[0]
    wide = r.outward.shape[1]
    blk = spot.blk
    outs = []

    def save(src, dst):
        copy = pltpu.make_async_copy(src, dst, r.local.at[len(outs)])
        copy.start()
        outs.append(copy)
        return copy

    def lanes(index, size):
        return pl.ds(pl.multiple_of(index * size, 128), size)

    def row_block(ref):
        return lambda index: ref.at[pl.ds(pl.multiple_of(index * rows, rows), rows)]

    def col_block(ref, size):
        return lambda index: ref.at[:, lanes(index, size)]

    def share(number, own, where):
        return Share(spot, own, where, r.bsend.at[number], r.brecv.at[number])

    def gather(number, shard, full, spread=False):
        sems = (item.at[number] for item in (r.zsend, r.zrecv, r.ysend, r.yrecv, r.near))
        return Gather(spot, shard, full, *sems, spread)

    gathers = Bag(
        outward=gather(0, r.outward, r.v_outward),
        inward=gather(1, r.aligned, r.v_inward),
        query=gather(2, r.query, r.v_query),
        keys=gather(3, r.keys, r.v_keys, True),
        back=gather(4, r.back, r.v_back, True),
        expand=gather(5, r.expand, r.v_expand),
        contract=gather(6, r.contract, r.v_contract),
        norms=gather(7, r.v_norms, r.v_norm_all),
    )

    spot.greet()

    def piece(part):
        index = blk * 3 + part
        owner = lax.rem(index, 4)
        return owner, index // 4

    def aligned_copy(part):
        owner, kind = piece(part)
        src = r.inward.at[:, part * wide : (part + 1) * wide]
        return owner, kind, src, r.aligned.at[:, lanes(kind, wide)]

    for part in range(3):
        owner, kind, src, dst = aligned_copy(part)

        @pl.when(owner == blk)
        def _():
            pltpu.make_async_copy(src, dst, r.arecv.at[kind]).start()

        @pl.when(owner != blk)
        def _():
            push(src, dst, r.asend.at[part], r.arecv.at[kind], (spot.grp, owner)).start()

    norm_share = share(0, r.norms, lambda index: r.v_norms.at[pl.ds(index * 16, 16)])
    norm_own = pltpu.make_async_copy(r.norms, r.v_norms.at[pl.ds(blk * 16, 16)], r.near.at[8])
    norm_own.start()
    norm_share.start()
    frame_share = share(1, r.frames, row_block(r.x_all))
    frame_own = pltpu.make_async_copy(r.frames, row_block(r.x_all)(blk), r.near.at[9])
    frame_own.start()
    frame_share.start()
    gathers.outward.start()
    for kind in range(3):
        dst = r.aligned.at[:, kind * wide : (kind + 1) * wide]
        home = (kind * 4 + blk) // 3

        @pl.when(home == blk)
        def _():
            pltpu.make_async_copy(dst, dst, r.arecv.at[kind]).wait()

        @pl.when(home != blk)
        def _():
            push(dst, dst, r.asend.at[0], r.arecv.at[kind], spot.sib).wait_recv()

    gathers.inward.start()
    norm_share.relay()
    norm_own.wait()
    norm_share.finish()
    gathers.norms.start()
    frame_share.relay()
    grad_share = share(2, r.incoming, row_block(r.g_all))
    grad_own = pltpu.make_async_copy(r.incoming, row_block(r.g_all)(blk), r.near.at[10])
    grad_own.start()
    grad_share.start()
    gathers.outward.relay(1)
    gathers.norms.relay(1)
    gathers.outward.relay(2)
    gathers.norms.relay(2)
    gathers.outward.relay(3)
    gathers.norms.relay(3)
    gathers.query.start()
    gathers.norms.finish()

    depth = 8 * 128
    line = lax.broadcasted_iota(jnp.int32, (depth, 384), 0)
    column = lax.broadcasted_iota(jnp.int32, (depth, 384), 1)
    inside = line & 127
    place = jnp.where((inside < 48) & (column == (line >> 7) * 48 + inside), 1.0, 0.0).astype(BF16)
    for pair in range(4):
        left = jnp.concatenate(
            [r.v_norm_all[pair * 128 + part * 16 : pair * 128 + part * 16 + 16, :] for part in range(8)],
            axis=1,
        )
        r.v_norm_rows[:, pair * 384 : (pair + 1) * 384] = dot(left, place)
    save(r.v_norm_rows, r.norm_all)
    gathers.inward.relay(1)
    frame_own.wait()
    frame_share.finish()
    grad_share.relay()

    def normed(source, index, turned):
        gain = r.v_norm_rows[index : index + 1, :]
        shift = r.v_norm_rows[3 + index : 4 + index, :]

        def body(block):
            result = norm_block(source[block, :].astype(F32), gain, shift).astype(BF16)
            r.a_all[block, :] = result

        tiles(length // 32, 32, body)

        def flip(block):
            turned[:, block] = r.a_all[block, :].T

        tiles(length // 128, 128, flip)

    normed(r.x_all, 0, r.t_first)
    save(r.t_first, r.first_t)
    gathers.keys.start()
    gathers.inward.relay(2)
    gathers.inward.relay(3)
    gathers.query.relay(1)
    gathers.query.relay(2)
    gathers.query.relay(3)
    gathers.back.start()
    gathers.inward.finish()
    save(r.v_inward, r.w_inward)

    def joint_tile(block):
        r.s_joint[:, block] = dot(r.a_all[...], r.v_inward[:, block]).astype(BF16)

    tiles(3, wide, joint_tile)
    save(r.s_joint, r.joint)
    gathers.keys.relay(1)

    low = lax.broadcasted_iota(jnp.int32, (1, 128), 1) < 64

    def half(value, part):
        return jnp.where(low if part == 0 else jnp.logical_not(low), value, jnp.zeros_like(value))

    def attend_step(step):
        pair, block = step // 4, lax.rem(step, 4)
        here = pl.ds(pl.multiple_of(block * 128, 128), 128)
        query = r.s_joint[here, lanes(pair, 128)]
        key = r.s_joint[:, lanes(pair + 3, 128)]
        value = r.s_joint[:, lanes(pair + 6, 128)]
        keep = r.ids_row[...] <= r.ids_col[here, :]
        results = []
        for part in (0, 1):
            scores = jnp.where(keep, dot_t(half(query, part), key) * 0.125, -1e30)
            power = jnp.exp(scores - jnp.max(scores, axis=1, keepdims=True))
            weighting = (power * (1.0 / jnp.sum(power, axis=1, keepdims=True))).astype(BF16)
            results.append(dot(weighting, value))
        r.s_attended[here, lanes(blk * 3 + pair, 128)] = jnp.where(low, *results).astype(BF16)

    @pl.loop(0, 12)
    def _(step):
        attend_step(step)

    attended_share = share(3, col_block(r.s_attended, wide)(blk), col_block(r.s_attended, wide))
    attended_share.start()
    gathers.keys.relay(2)
    gathers.keys.relay(3)
    gathers.outward.finish()
    save(r.v_outward, r.w_outward)
    attended_share.relay()
    gathers.expand.start()
    attended_share.finish()
    r.s_one[...] = dot(r.s_attended[...], r.v_outward[...]) + r.x_all[:, lanes(blk, wide)].astype(F32)
    r.s_one_all[:, lanes(blk, wide)] = r.s_one[...].astype(BF16)
    one_share = share(4, col_block(r.s_one_all, wide)(blk), col_block(r.s_one_all, wide))
    one_share.start()
    gathers.back.relay(1)
    gathers.back.relay(2)
    one_share.relay()

    def turn_over(source, turned):
        def flip(block):
            turned[:, block] = source[block, :].T

        tiles(length // 128, 128, flip)

    turn_over(r.s_attended, r.t_attended)
    save(r.t_attended, r.attended_t)
    gathers.back.relay(3)
    gathers.contract.start()
    gathers.keys.finish()
    save(r.v_keys, r.w_keys)
    r.s_text[:, lanes(blk, 2 * wide)] = dot(r.text[...], r.v_keys[...]).astype(BF16)
    text_share = share(5, col_block(r.s_text, 2 * wide)(blk), col_block(r.s_text, 2 * wide))
    one_share.finish()
    text_share.start()
    save(row_block(r.s_one_all)(blk), r.one_rows)
    normed(r.s_one_all, 1, r.t_second)
    save(r.t_second, r.second_t)
    text_share.relay()
    gathers.expand.relay(1)
    gathers.query.finish()
    save(r.v_query, r.w_query)
    r.s_query[...] = dot(r.a_all[...], r.v_query[...]).astype(BF16)
    save(r.s_query, r.cross_query)
    text_share.finish()
    save(r.s_text, r.text_all)

    @pl.loop(0, 3)
    def _(pair):
        query = r.s_query[:, lanes(pair, 128)]
        key = r.s_text[:, lanes(blk * 3 + pair, 128)]
        value = r.s_text[:, lanes(12 + blk * 3 + pair, 128)]
        results = []
        for part in (0, 1):
            scores = dot_t(half(query, part), key) * 0.125
            power = jnp.exp(scores - jnp.max(scores, axis=1, keepdims=True))
            weighting = (power * (1.0 / jnp.sum(power, axis=1, keepdims=True))).astype(BF16)
            results.append(dot(weighting, value))
        r.s_crossed[:, lanes(blk * 3 + pair, 128)] = jnp.where(low, *results).astype(BF16)

    crossed_share = share(6, col_block(r.s_crossed, wide)(blk), col_block(r.s_crossed, wide))
    crossed_share.start()
    gathers.expand.relay(2)
    crossed_share.relay()
    gathers.back.finish()
    save(r.v_back, r.w_back)
    crossed_share.finish()
    r.s_one[...] += dot(r.s_crossed[...], r.v_back[...])
    r.s_two_all[:, lanes(blk, wide)] = r.s_one[...].astype(BF16)
    two_share = share(7, col_block(r.s_two_all, wide)(blk), col_block(r.s_two_all, wide))
    two_share.start()
    gathers.expand.relay(3)
    two_share.relay()
    turn_over(r.s_crossed, r.t_crossed)
    save(r.t_crossed, r.crossed_t)
    two_share.finish()
    save(row_block(r.s_two_all)(blk), r.two_rows)
    gathers.contract.relay(1)
    normed(r.s_two_all, 2, r.t_third)
    save(r.t_third, r.third_t)
    grad_share.finish()
    grad_own.wait()
    save(r.g_all, r.grad_all)
    gathers.expand.finish()
    kept = save(r.v_expand, r.w_expand)
    gathers.contract.relay(2)

    def upward_tile(block):
        r.s_upward[:, block] = dot(r.a_all[...], r.v_expand[:, block])

    tiles(4, 384, upward_tile)
    gathers.contract.relay(3)

    def gelu_tile(block):
        upward = r.s_upward[block, :]
        gate = 0.5 + 0.5 * lax.erf(upward * 0.7071067811865476)
        r.s_active[block, :] = (upward * gate).astype(BF16)
        r.s_slope[block, :] = gate + upward * jnp.exp(-0.5 * upward * upward) * 0.3989422804014327

    tiles(length // 16, 16, gelu_tile)
    save(r.s_slope, r.slope)
    turn_over(r.g_all, r.t_grad)
    kept.wait()
    gathers.expand.drain()

    def contract_tile(block):
        r.v_expand[:, block] = dot(r.t_grad[...], r.s_active[:, block]).astype(BF16)

    tiles(4, 384, contract_tile)
    save(r.v_expand, r.contract_grad)
    save(r.s_active, r.active)
    gathers.contract.finish()
    save(r.v_contract, r.w_contract)
    for part in range(3):
        owner, kind, src, dst = aligned_copy(part)

        @pl.when(owner != blk)
        def _():
            push(src, dst, r.asend.at[part], r.arecv.at[kind], (spot.grp, owner)).wait_send()

    for item in (
        norm_share, frame_share, grad_share, attended_share, one_share, text_share, crossed_share, two_share,
    ):
        item.drain()
    for item in vars(gathers).values():
        if item is not gathers.expand:
            item.drain()
    for copy in outs:
        if copy is not kept:
            copy.wait()


def ids_of(table):
    ids = (table[0][:, None] * SEG + jnp.arange(SEG, dtype=jnp.int32)[None, :]).reshape(-1)
    return ids[:, None], ids[None, :]


def run_kernel(kernel, number, inner, outer, out, vmem, sems, credits):
    anywhere = pl.BlockSpec(memory_space=pl.ANY)
    inside = pl.BlockSpec(memory_space=pltpu.VMEM)
    names = [*inner, *outer, *out, *vmem, *sems, *credits]
    results = pl.pallas_call(
        functools.partial(kernel, names),
        out_shape=[jax.ShapeDtypeStruct(*item) for item in out.values()],
        in_specs=[inside] * len(inner) + [anywhere] * len(outer),
        out_specs=[anywhere] * len(out),
        scratch_shapes=[pltpu.VMEM(*item) for item in vmem.values()]
        + [pltpu.SemaphoreType.DMA(shape) for shape in sems.values()]
        + [pltpu.SemaphoreType.REGULAR(shape) for shape in credits.values()],
        compiler_params=pltpu.CompilerParams(
            collective_id=number, has_side_effects=True, vmem_limit_bytes=60 * 2**20
        ),
    )(*inner.values(), *outer.values())
    return named(out, results)


def forward(frames, text, table, norms, incoming, weights):
    rows, width = frames.shape
    length = rows * lax.axis_size("blk")
    wide = width // lax.axis_size("blk")
    feed = weights["expand"].shape[1]
    ids_col, ids_row = ids_of(table)
    one = ((width, wide), BF16)
    two = ((width, 2 * wide), BF16)
    three = ((width, 3 * wide), BF16)
    four = ((width, feed), BF16)
    square, turned, strip = ((length, width), BF16), ((width, length), BF16), ((length, wide), BF16)
    big = ((length, feed), F32)
    own = ((rows, width), BF16)
    out = dict(
        w_outward=one,
        w_inward=three,
        w_query=one,
        w_keys=two,
        w_back=one,
        w_expand=four,
        w_contract=four,
        first_t=turned,
        second_t=turned,
        third_t=turned,
        attended_t=turned,
        crossed_t=turned,
        contract_grad=four,
        grad_all=square,
        joint=((length, 3 * wide), BF16),
        cross_query=strip,
        text_all=((TEXT, 2 * width), BF16),
        slope=big,
        active=((length, feed), BF16),
        one_rows=own,
        two_rows=own,
        norm_all=((16, width), F32),
        aligned=((width // lax.axis_size("grp"), 3 * wide), BF16),
    )
    vmem = dict(
        v_outward=one,
        v_inward=three,
        v_query=one,
        v_keys=two,
        v_back=one,
        v_expand=four,
        v_contract=four,
        x_all=square,
        g_all=square,
        a_all=square,
        s_attended=square,
        s_one_all=square,
        s_crossed=square,
        s_two_all=square,
        t_first=turned,
        t_second=turned,
        t_third=turned,
        t_attended=turned,
        t_crossed=turned,
        t_grad=turned,
        s_joint=((length, 3 * wide), BF16),
        s_one=((length, wide), F32),
        s_query=strip,
        s_text=((TEXT, 2 * width), BF16),
        s_upward=big,
        s_slope=big,
        s_active=((length, feed), BF16),
        v_norms=((64, 128), BF16),
        v_norm_all=((512, 128), BF16),
        v_norm_rows=((16, width), F32),
    )
    sems = dict(
        zsend=(8, 12),
        zrecv=(8, 12),
        ysend=(8, 7),
        yrecv=(8, 7),
        near=(12,),
        bsend=(8, 3),
        brecv=(8, 3),
        asend=(3,),
        arecv=(3,),
        local=(32,),
    )
    inner = dict(text=text, ids_col=ids_col, ids_row=ids_row)
    outer = dict(frames=frames, norms=norms, incoming=incoming, **weights)
    return run_kernel(forward_kernel, 1, inner, outer, out, vmem, sems, {})


class Reduce:
    def __init__(self, spot, grad, over, along, sems, spread, source=None):
        self.spot, self.grad, self.over, self.along = spot, grad, over, along
        self.ysend, self.yrecv, self.zsend, self.zrecv = sems
        self.spread = spread
        self.source = grad if source is None else source
        self.size, self.cols = over.shape[-2], over.shape[-1]

    def rows(self, z, flip=0, ref=None):
        spot = self.spot
        row = z * 2 + (1 - spot.y if flip else spot.y)
        return (self.grad if ref is None else ref).at[pl.ds(pl.multiple_of(row * self.size, self.size), self.size)]

    def add(self, target, extra):
        step = 16

        @pl.loop(0, self.size // step)
        def _(index):
            here = pl.ds(pl.multiple_of(index * step, step), step)
            target[here, :] = (target[here, :].astype(F32) + extra[here, :].astype(F32)).astype(BF16)

    def y_copy(self, z):
        return push(
            self.rows(z, 1, self.source), self.over.at[z], self.ysend.at[z], self.yrecv.at[z], self.spot.part
        )

    def y_start(self):
        for z in (0, 3, 1, 2):
            self.y_copy(z).start()

    def z_copy(self, goal, slot, who, flip):
        index = flip * 4 + slot
        return push(
            self.rows(goal, flip), self.along.at[index], self.zsend.at[flip * 4 + goal],
            self.zrecv.at[index], (who * 2 + self.spot.y, self.spot.blk),
        )

    def z_first(self, goal, flip):
        z = self.spot.z
        middle, end = (2, 3) if goal == 0 else (1, 0)
        for home in range(4):
            if home == goal or (goal in (0, 3) and home == middle):
                continue

            @pl.when(z == home)
            def _():
                if goal in (0, 3) and home == end:
                    self.z_copy(goal, 3, middle, flip).start()
                else:
                    self.z_copy(goal, home - (home > goal), goal, flip).start()

    def z_second(self, goal, flip):
        middle = 2 if goal == 0 else 1

        @pl.when(self.spot.z == middle)
        def _():
            index = flip * 4 + 3
            self.z_copy(goal, 3, goal, flip).wait_recv()
            self.add(self.rows(goal, flip), self.along.at[index])
            self.z_copy(goal, middle - (middle > goal), goal, flip).start()

    def take(self, goal):
        self.y_copy(goal).wait_recv()
        self.add(self.rows(goal), self.over.at[goal])
        self.z_first(goal, 0)

    def start(self):
        if not self.spread:
            return self.y_start()
        for goal in (0, 3, 1, 2):
            for flip in (1, 0):
                self.z_first(goal, flip)

    def combine(self, flip=0):
        self.z_second(0, flip)
        self.z_second(3, flip)

    def arrive(self, flip):
        z = self.spot.z
        for slot in range(3):
            unused = 3 if slot == 2 else 0 if slot == 0 else None

            def wait():
                self.z_copy(0, slot, 0, flip).wait_recv()

            if slot == 1:
                wait()
            else:
                pl.when(z != (0 if slot == 2 else 3))(wait)

    def total(self, flip, extra, body):
        z = self.spot.z
        own = self.rows(z, flip)

        def add_up(slots):
            @pl.loop(0, self.size // 16)
            def _(index):
                here = pl.ds(pl.multiple_of(index * 16, 16), 16)
                value = own[here, :].astype(F32)
                for slot in slots:
                    value += self.along[flip * 4 + slot, here, :].astype(F32)
                if extra is not None:
                    value += extra[here, :].astype(F32)
                body(here, value)

        @pl.when(z == 0)
        def _():
            add_up((0, 1))

        @pl.when(z == 3)
        def _():
            add_up((1, 2))

        @pl.when((z == 1) | (z == 2))
        def _():
            add_up((0, 1, 2))

    def cross(self):
        self.arrive(1)
        target = self.rows(self.spot.z, 1)

        def keep(here, value):
            target[here, :] = value.astype(BF16)

        self.total(1, None, keep)
        push(target, self.over.at[0], self.ysend.at[0], self.yrecv.at[0], self.spot.part).start()

    def finish(self, body):
        self.arrive(0)
        if self.spread:
            target = self.rows(self.spot.z, 1)
            push(target, self.over.at[0], self.ysend.at[0], self.yrecv.at[0], self.spot.part).wait_recv()
            self.total(0, self.over.at[0], body)
        else:
            self.total(0, None, body)

    def drain(self):
        z = self.spot.z
        if self.spread:
            target = self.rows(z, 1)
            push(target, self.over.at[0], self.ysend.at[0], self.yrecv.at[0], self.spot.part).wait_send()
        else:
            for goal in range(4):
                self.y_copy(goal).wait_send()
        for flip in (0, 1) if self.spread else (0,):
            for goal in range(4):

                @pl.when(z != goal)
                def _():
                    self.z_copy(goal, 0, 0, flip).wait_send()


class BlkSum:
    def __init__(self, spot, piece, near, far, send, recv, step, size):
        self.spot, self.piece, self.near, self.far = spot, piece, near, far
        self.send, self.recv, self.step, self.size = send, recv, step, size

    def to_core(self, x):
        spot = self.spot
        goal = x * 2 + 1 - spot.core
        return push(self.piece(goal), self.near.at[x], self.send.at[x], self.recv.at[x], spot.sib)

    def to_chip(self):
        spot = self.spot
        return push(self.piece(spot.opp_blk), self.far, self.send.at[2], self.recv.at[2], spot.opp)

    def start(self):
        self.to_core(0).start()
        self.to_core(1).start()

    def relay(self):
        spot = self.spot
        for x in (0, 1):
            self.to_core(x).wait_recv()
        target, extra = self.piece(spot.opp_blk), self.near.at[1 - spot.x]

        @pl.loop(0, self.size // self.step)
        def _(index):
            here = pl.ds(pl.multiple_of(index * self.step, self.step), self.step)
            target[here, :] = (target[here, :].astype(F32) + extra[here, :].astype(F32)).astype(BF16)

        self.to_chip().start()

    def finish(self):
        self.to_chip().wait_recv()

    def value(self, here):
        spot = self.spot
        own = self.piece(spot.blk)[here, :].astype(F32)
        return own + self.near[spot.x, here, :].astype(F32) + self.far[here, :].astype(F32)

    def drain(self):
        self.to_core(0).wait_send()
        self.to_core(1).wait_send()
        self.to_chip().wait_send()


class Turn:
    def __init__(self, spot, source, target, send, recv):
        self.spot, self.source, self.target, self.send, self.recv = spot, source, target, send, recv
        self.rows, self.wide = source.shape[0], target.shape[1]

    def copy(self, number):
        spot = self.spot
        goal = (spot.sib_blk, spot.opp_blk, spot.far_blk)[number]
        src = self.source.at[:, pl.ds(pl.multiple_of(goal * self.wide, 128), self.wide)]
        return push(src, self.place(spot.blk), self.send.at[number], self.recv.at[number], (spot.grp, goal))

    def place(self, index):
        return self.target.at[pl.ds(pl.multiple_of(index * self.rows, self.rows), self.rows)]

    def start(self):
        for number in (2, 1, 0):
            self.copy(number).start()
        spot = self.spot
        src = self.source.at[:, pl.ds(pl.multiple_of(spot.blk * self.wide, 128), self.wide)]
        self.place(spot.blk)[...] = src[...]

    def finish(self):
        for number in range(3):
            self.copy(number).wait_recv()

    def drain(self):
        for number in range(3):
            self.copy(number).wait_send()


def t_dot(left, right):
    return lax.dot_general(left, right, (((0,), (0,)), ((), ())), preferred_element_type=F32)


def backward_kernel(names, *refs):
    r = named(names, refs)
    spot = Spot()
    rows, width = r.frames.shape
    length = r.v_grad.shape[0]
    wide = r.v_query_grad.shape[1]
    blk = spot.blk
    spot.greet_all()

    def lanes(index, size):
        return pl.ds(pl.multiple_of(index * size, 128), size)

    def part(ref, first, size):
        return ref.at[:, first : first + size]

    def row_piece(ref, size):
        return lambda index: ref.at[pl.ds(pl.multiple_of(index * size, size), size)]

    loads = []

    def load(src, dst):
        copy = pltpu.make_async_copy(src, dst, r.local.at[len(loads)])
        copy.start()
        loads.append(copy)
        return copy

    grads = Bag(
        contract=r.g_contract,
        expand=r.g_expand,
        back=part(r.g_rest, 0, wide),
        keys=part(r.g_rest, wide, 2 * wide),
        query=part(r.g_rest, 3 * wide, wide),
        outward=part(r.g_rest, 4 * wide, wide),
        inward=part(r.g_contract, 0, 3 * wide),
    )

    def reduce(number, grad, over, along, spread=False, source=None):
        sems = tuple(item.at[number] for item in (r.ysend, r.yrecv, r.zsend, r.zrecv))
        return Reduce(spot, grad, over, along, sems, spread, source)

    reduces = Bag(
        contract=reduce(0, grads.contract, r.y_contract, r.z_contract, False, r.contract_grad),
        expand=reduce(1, grads.expand, r.y_expand, r.z_expand),
        back=reduce(2, grads.back, r.y_back, r.z_back, True),
        keys=reduce(3, grads.keys, r.y_keys, r.z_keys, True),
        query=reduce(4, grads.query, r.y_query, r.z_query),
        outward=reduce(5, grads.outward, r.y_outward, r.z_outward),
        inward=reduce(
            6,
            grads.inward,
            r.y_contract.at[:, :, 0 : 3 * wide],
            r.z_contract.at[:, :, 0 : 3 * wide],
        ),
    )
    reduces.contract.start()
    load_grad = load(r.grad_all, r.v_grad)
    load_contract = load(r.w_contract, r.v_one)
    load_slope = load(r.slope, r.v_slope)
    load_third = load(r.third_t, r.v_left)
    load_expand = load(r.w_expand, r.v_two)
    load_own = load(r.contract_grad, r.g_contract)
    load_norm = load(r.norm_all.at[0:8], r.v_norm)
    load_crossed = load(r.crossed_t, r.v_right)
    load_two = load(r.two_rows, r.v_two_rows)
    load_incoming = load(r.incoming, r.v_rows)
    cross_query = part(r.v_joint, 0, wide)
    load_query = load(r.cross_query, cross_query)
    load_text = load(r.text_all.at[:, lanes(blk, wide)], part(r.v_text, 0, wide))
    load_values = load(r.text_all.at[:, lanes(blk + 4, wide)], part(r.v_text, wide, wide))

    def blk_sum(number, piece, near, far, size):
        return BlkSum(spot, piece, near, far, r.bsend.at[number], r.brecv.at[number], 16, size)

    load_grad.wait()
    load_contract.wait()
    load_slope.wait()

    def up_tile(block):
        r.v_up[:, block] = (dot(r.v_grad[...], r.v_one[:, block]) * r.v_slope[:, block]).astype(BF16)

    tiles(4, 384, up_tile)
    load_back = load(r.w_back, part(r.v_one, 0, wide))
    load_keys = load(r.w_keys, part(r.v_one, wide, 2 * wide))
    load_outward = load(r.w_outward, part(r.v_one, 3 * wide, wide))
    load_expand.wait()

    def back_rows(left, right):
        def body(block):
            r.v_part[:, block] = dot_t(left[...], right[block, :]).astype(BF16)

        tiles(4, 384, body)

    def back_cols(left, right):
        for core in (1 - spot.core, spot.core):
            for x in (0, 1):
                goal = x * 2 + core
                here = pl.ds(pl.multiple_of(goal * wide, 128), wide)
                mine = pl.ds(pl.multiple_of(goal * wide, wide), wide)
                r.v_part[:, here] = dot_t(left[...], right[mine, :]).astype(BF16)

    def outer(target, left, right):
        def body(block):
            target[block, :] = dot(left[block, :], right[...]).astype(BF16)

        tiles(4, 384, body)

    row_parts = row_piece(r.v_part, rows)

    def col_parts(index):
        return r.v_part.at[:, lanes(index, wide)]

    back_rows(r.v_up, r.v_two)
    third_sum = blk_sum(0, row_parts, r.near_rows, r.far_rows, rows)
    third_sum.start()
    load_third.wait()

    def expand_tile(block):
        r.g_expand[:, block] = dot(r.v_left[...], r.v_up[:, block]).astype(BF16)

    third_sum.relay()
    tiles(4, 384, expand_tile)
    reduces.expand.start()
    load_wquery = load(r.w_query, part(r.v_two, 0, wide))
    load_winward = load(r.w_inward, part(r.v_two, wide, 3 * wide))
    load_second = load(r.second_t, r.v_left)
    load_own.wait()
    reduces.contract.take(0)
    for copy in (load_norm, load_two, load_incoming):
        copy.wait()
    r.v_norm_grads[...] = jnp.zeros_like(r.v_norm_grads)
    hidden = r.v_slope.at[pl.ds(3 * rows, rows)]

    def norm_back(total, values, number, base, keep):
        gain = r.v_norm[number : number + 1, :]

        @pl.loop(0, rows // 16)
        def _(index):
            here = pl.ds(pl.multiple_of(index * 16, 16), 16)
            incoming = total.value(here)
            value = values[here, :].astype(F32)
            center = value - jnp.mean(value, axis=1, keepdims=True)
            scale = lax.rsqrt(jnp.mean(center * center, axis=1, keepdims=True) + 1e-05)
            normal = center * scale
            scaled = incoming * gain
            mean = jnp.mean(scaled, axis=1, keepdims=True)
            match = jnp.mean(scaled * normal, axis=1, keepdims=True)
            keep(here, base(here) + (scaled - mean - normal * match) * scale)
            for place, term in ((number, incoming * normal), (3 + number, incoming)):
                spread = pl.ds(place * 8, 8)
                r.v_norm_grads[spread, :] += term[0:8, :] + term[8:16, :]

    def keep_branch(here, value):
        hidden[here, :] = value
        r.v_branch[here, :] = value.astype(BF16)

    third_sum.finish()
    norm_back(
        third_sum, r.v_two_rows, 2, lambda here: r.v_rows[here, :].astype(F32), keep_branch
    )
    load_one = load(r.one_rows, r.v_rows)
    turn_two = Turn(spot, r.v_branch, r.v_turn_two, r.tsend.at[0], r.trecv.at[0])
    turn_two.start()
    reduces.contract.take(3)
    load_back.wait()
    turn_two.finish()
    third_sum.drain()
    back_cols(r.v_turn_two, part(r.v_one, 0, wide))
    crossed_sum = blk_sum(1, col_parts, r.near_cols, r.far_cols, length)
    crossed_sum.start()
    load_crossed.wait()
    crossed_sum.relay()
    outer(grads.back, r.v_right, r.v_turn_two)
    reduces.back.start()
    load_attended = load(r.attended_t, r.v_right)
    reduces.contract.take(1)
    crossed_sum.finish()
    load_query.wait()
    load_text.wait()
    load_values.wait()

    def merge(total, target):
        @pl.loop(0, length // 16)
        def _(index):
            here = pl.ds(pl.multiple_of(index * 16, 16), 16)
            target[here, :] = total.value(here).astype(BF16)

    merge(crossed_sum, r.v_head_grad)
    low = lax.broadcasted_iota(jnp.int32, (1, 128), 1) < 64

    def half(value, side):
        return jnp.where(low if side == 0 else jnp.logical_not(low), value, jnp.zeros_like(value))

    def soft(scores):
        power = jnp.exp(scores - jnp.max(scores, axis=1, keepdims=True))
        return power * (1.0 / jnp.sum(power, axis=1, keepdims=True))

    @pl.loop(0, 3)
    def _(pair):
        query = cross_query[:, lanes(pair, 128)]
        key = r.v_text[:, lanes(pair, 128)]
        value = r.v_text[:, lanes(3 + pair, 128)]
        head_grad = r.v_head_grad[:, lanes(pair, 128)]
        results = []
        for side in (0, 1):
            weights = soft(dot_t(half(query, side), key) * 0.125)
            slope = dot_t(half(head_grad, side), value)
            score = (weights * (slope - jnp.sum(slope * weights, axis=1, keepdims=True))).astype(BF16)
            results.append(
                (
                    dot(score, key) * 0.125,
                    t_dot(score, query) * 0.125,
                    t_dot(weights.astype(BF16), head_grad),
                )
            )
        merged = [jnp.where(low, *item).astype(BF16) for item in zip(*results)]
        r.v_query_grad[:, lanes(pair, 128)] = merged[0]
        r.v_terms[0:TEXT, lanes(blk * 3 + pair, 128)] = merged[1]
        r.v_terms[TEXT : 2 * TEXT, lanes(blk * 3 + pair, 128)] = merged[2]

    load_joint = load(r.joint, r.v_joint)
    own_terms = r.v_terms.at[:, lanes(blk, wide)]
    terms_share = Share(
        spot, own_terms, lambda index: r.v_terms.at[:, lanes(index, wide)], r.csend.at[0], r.crecv.at[0]
    )
    terms_share.start()
    load_wquery.wait()
    crossed_sum.drain()
    back_rows(r.v_query_grad, part(r.v_two, 0, wide))
    second_sum = blk_sum(2, row_parts, r.near_rows, r.far_rows, rows)
    second_sum.start()
    load_second.wait()
    second_sum.relay()
    outer(grads.query, r.v_left, r.v_query_grad)
    load_first = load(r.first_t, r.v_left)
    reduces.query.start()
    reduces.back.combine(1)
    reduces.back.combine(0)
    reduces.contract.combine()
    reduces.contract.take(2)
    pl.semaphore_signal(r.credit.at[0], inc=1, device_id=spot.part, device_id_type=MESH)
    terms_share.relay()
    load_one.wait()
    second_sum.finish()
    norm_back(second_sum, r.v_rows, 1, lambda here: hidden[here, :], keep_branch_after(turn_two, keep_branch))
    load_frames = load(r.frames, r.v_rows)
    turn_one = Turn(spot, r.v_branch, r.v_turn_one, r.tsend.at[1], r.trecv.at[1])
    turn_one.start()
    terms_share.finish()
    load_keys.wait()
    own_rows = pl.ds(pl.multiple_of((blk // 2) * TEXT, TEXT), TEXT)
    terms = r.v_terms[own_rows, lanes(lax.rem(blk, 2), 2 * wide)]

    def keys_tile(block):
        product = t_dot(r.text[:, block], r.v_terms[own_rows, lanes(lax.rem(blk, 2), 2 * wide)])
        grads.keys[block, :] = product.astype(BF16)

    tiles(6, 256, keys_tile)
    reduces.keys.start()
    turn_one.finish()
    second_sum.drain()
    load_outward.wait()
    back_cols(r.v_turn_one, part(r.v_one, 3 * wide, wide))
    attended_sum = blk_sum(3, col_parts, r.near_cols, r.far_cols, length)
    attended_sum.start()
    load_attended.wait()
    attended_sum.relay()
    outer(grads.outward, r.v_right, r.v_turn_one)
    reduces.outward.start()
    r.v_text_part[...] = dot_t(terms, r.v_one[:, wide : 3 * wide]).astype(BF16)
    text_rows = TEXT // 4
    text_sum = blk_sum(4, row_piece(r.v_text_part, text_rows), r.near_text, r.far_text, text_rows)
    text_sum.start()
    text_sum.relay()
    reduces.expand.take(0)
    load_joint.wait()
    attended_sum.finish()
    merge(attended_sum, r.v_head_grad)

    @pl.loop(0, 3)
    def _(pair):
        r.v_key_sum[...] = jnp.zeros_like(r.v_key_sum)
        r.v_value_sum[...] = jnp.zeros_like(r.v_value_sum)

        @pl.loop(0, 4)
        def _(block):
            here = pl.ds(pl.multiple_of(block * 128, 128), 128)
            query = r.v_joint[here, lanes(pair, 128)]
            key = r.v_joint[:, lanes(pair + 3, 128)]
            value = r.v_joint[:, lanes(pair + 6, 128)]
            head_grad = r.v_head_grad[here, lanes(pair, 128)]
            keep = r.ids_row[...] <= r.ids_col[here, :]
            results = []
            for side in (0, 1):
                weights = soft(jnp.where(keep, dot_t(half(query, side), key) * 0.125, -1e30))
                slope = dot_t(half(head_grad, side), value)
                score = (weights * (slope - jnp.sum(slope * weights, axis=1, keepdims=True))).astype(BF16)
                results.append(
                    (dot(score, key), t_dot(score, query), t_dot(weights.astype(BF16), head_grad))
                )
            merged = [jnp.where(low, *item) for item in zip(*results)]
            r.v_up[here, lanes(pair, 128)] = (merged[0] * 0.125).astype(BF16)
            r.v_key_sum[...] += merged[1]
            r.v_value_sum[...] += merged[2]

        r.v_up[:, lanes(pair + 3, 128)] = (r.v_key_sum[...] * 0.125).astype(BF16)
        r.v_up[:, lanes(pair + 6, 128)] = r.v_value_sum[...].astype(BF16)

    stores = []

    def store(item, goal):
        size = goal.shape[1]
        slot = len(stores) % 2
        if len(stores) >= 2:
            stores[-2].wait()
        stage = r.v_slope.at[pl.ds(slot * 192, 192), pl.ds(0, size)]

        def keep(here, value):
            stage[here, :] = value

        item.finish(keep)
        copy = pltpu.make_async_copy(stage, goal, r.stored.at[len(stores)])
        copy.start()
        stores.append(copy)

    reduces.back.cross()
    reduces.keys.combine(1)
    reduces.keys.combine(0)
    store(reduces.contract, r.contract_out)
    for k in (1, 2, 3):
        pl.semaphore_signal(r.credit.at[1], inc=1, device_id=spot.z_peer(k), device_id_type=MESH)
    reduces.contract.drain()
    attended_sum.drain()
    load_winward.wait()
    load_first.wait()
    joint_grad = part(r.v_up, 0, 3 * wide)
    back_rows(joint_grad, part(r.v_two, wide, 3 * wide))
    first_sum = blk_sum(5, row_parts, r.near_rows, r.far_rows, rows)
    first_sum.start()

    def inward_tile(block):
        grads.inward[:, block] = dot(r.v_left[...], r.v_up[:, block]).astype(BF16)

    tiles(3, 384, inward_tile)
    pl.semaphore_wait(r.credit.at[0], 1)
    reduces.inward.start()
    first_sum.relay()
    load_again = load(r.w_contract, r.v_one)
    load_active = load(r.active, r.v_grad)
    reduces.expand.take(3)
    reduces.expand.take(1)
    reduces.expand.combine()
    reduces.expand.take(2)
    load_frames.wait()
    first_sum.finish()

    def keep_frames(here, value):
        hidden[here, :] = value

    norm_back(first_sum, r.v_rows, 0, lambda here: hidden[here, :], keep_frames)
    for who in (spot.sib, spot.opp):
        pl.semaphore_signal(r.credit.at[2], inc=1, device_id=who, device_id_type=MESH)
    frames_copy = pltpu.make_async_copy(hidden, r.frames_out, r.stored.at[8])
    frames_copy.start()

    for place in range(6):
        r.v_norm_sum[place : place + 1, :] = jnp.sum(
            r.v_norm_grads[place * 8 : place * 8 + 8, :], axis=0, keepdims=True
        )
    r.v_norm_sum[6:8, :] = jnp.zeros((2, width), F32)

    def norm_hop(number, who):
        return push(r.v_norm_sum, r.v_norm_in.at[number], r.nsend.at[number], r.nrecv.at[number], who)

    norm_hop(0, spot.sib).start()
    text_sum.finish()
    r.v_text_out[...] = text_sum.value(pl.ds(0, text_rows))
    text_copy = pltpu.make_async_copy(r.v_text_out, r.text_out, r.stored.at[9])
    text_copy.start()
    reduces.query.take(0)
    reduces.query.take(3)
    reduces.query.take(1)
    reduces.query.take(2)

    def norm_step(number, who):
        norm_hop(number, who).wait()
        r.v_norm_sum[...] += r.v_norm_in[number]

    norm_step(0, spot.sib)
    norm_hop(1, spot.opp).start()
    load_again.wait()
    load_active.wait()
    first_sum.drain()
    back_rows(r.v_grad, r.v_one)
    out_sum = blk_sum(6, row_parts, r.near_rows, r.far_rows, rows)
    pl.semaphore_wait(r.credit.at[2], 2)
    out_sum.start()
    norm_step(1, spot.opp)
    norm_hop(2, spot.part).start()
    reduces.query.combine()
    for goal in (0, 3, 1, 2):
        reduces.outward.take(goal)
    out_sum.relay()
    reduces.keys.cross()
    norm_step(2, spot.part)
    for k in (1, 2, 3):
        norm_hop(2 + k, spot.z_peer(k)).start()
    reduces.outward.combine()
    pl.semaphore_wait(r.credit.at[1], 3)
    for goal in (0, 3):
        reduces.inward.take(goal)
    out_sum.finish()
    turn_one.drain()

    @pl.loop(0, rows // 16)
    def _(index):
        here = pl.ds(pl.multiple_of(index * 16, 16), 16)
        r.v_branch[here, :] = (out_sum.value(here) + r.v_two_rows[here, :].astype(F32)).astype(BF16)

    block_copy = pltpu.make_async_copy(r.v_branch, r.block_out, r.stored.at[10])
    block_copy.start()
    store(reduces.expand, r.expand_out)
    store(reduces.back, r.returning_out)
    reduces.inward.take(1)
    reduces.inward.take(2)
    reduces.inward.combine()
    store(reduces.query, r.querying_out)
    store(reduces.outward, r.outward_out)
    store(reduces.keys, r.keying_out)
    for k in (1, 2, 3):
        norm_hop(2 + k, spot.z_peer(k)).wait()
    r.v_norm_sum[...] += r.v_norm_in[3] + r.v_norm_in[4] + r.v_norm_in[5]
    norm_copy = pltpu.make_async_copy(r.v_norm_sum, r.norm_out, r.stored.at[11])
    norm_copy.start()

    out_sum.drain()
    inward_sum = r.v_part.at[pl.ds(0, 192), pl.ds(0, 3 * wide)]

    def keep_inward(here, value):
        inward_sum[here, :] = value.astype(BF16)

    reduces.inward.finish(keep_inward)

    def inward_copy(kind):
        index = kind * 4 + blk
        owner, place = index // 3, lax.rem(index, 3)
        src = inward_sum.at[:, kind * wide : (kind + 1) * wide]
        return owner, place, src, r.v_inward_in.at[:, lanes(place, wide)]

    for kind in range(3):
        owner, place, src, dst = inward_copy(kind)

        @pl.when(owner == blk)
        def _():
            pltpu.make_async_copy(src, dst, r.arecv.at[place]).start()

        @pl.when(owner != blk)
        def _():
            push(src, dst, r.asend.at[kind], r.arecv.at[place], (spot.grp, owner)).start()

    for place in range(3):
        dst = r.v_inward_in.at[:, place * wide : (place + 1) * wide]
        home = lax.rem(blk * 3 + place, 4)

        @pl.when(home == blk)
        def _():
            pltpu.make_async_copy(dst, dst, r.arecv.at[place]).wait()

        @pl.when(home != blk)
        def _():
            push(dst, dst, r.asend.at[0], r.arecv.at[place], spot.sib).wait_recv()

    for copy in stores[-2:]:
        copy.wait()
    final = r.v_slope.at[pl.ds(0, 192), pl.ds(0, 3 * wide)]

    @pl.loop(0, 192 // 16)
    def _(index):
        here = pl.ds(pl.multiple_of(index * 16, 16), 16)
        final[here, :] = r.v_inward_in[here, :].astype(F32)

    inward_done = pltpu.make_async_copy(final, r.inward_out, r.stored.at[12])
    inward_done.start()
    for kind in range(3):
        owner, place, src, dst = inward_copy(kind)

        @pl.when(owner != blk)
        def _():
            push(src, dst, r.asend.at[kind], r.arecv.at[place], (spot.grp, owner)).wait_send()

    for item in vars(reduces).values():
        if item is not reduces.contract:
            item.drain()
    terms_share.drain()
    text_sum.drain()
    for copy in (frames_copy, text_copy, block_copy, norm_copy, inward_done):
        copy.wait()


def keep_branch_after(turn, keep):
    turn.drain()
    return keep


def backward(ahead, frames, text, table, incoming):
    rows, width = frames.shape
    length = rows * lax.axis_size("blk")
    wide = width // lax.axis_size("blk")
    shard = width // lax.axis_size("grp")
    feed = ahead.w_expand.shape[1]
    ids_col, ids_row = ids_of(table)
    out = dict(
        contract_out=((shard, feed), F32),
        expand_out=((shard, feed), F32),
        returning_out=((shard, wide), F32),
        keying_out=((shard, 2 * wide), F32),
        querying_out=((shard, wide), F32),
        outward_out=((shard, wide), F32),
        inward_out=((shard, 3 * wide), F32),
        frames_out=((rows, width), F32),
        block_out=((rows, width), BF16),
        text_out=((TEXT // 4, width), F32),
        norm_out=((8, width), F32),
    )
    square, turned, strip = (length, width), (width, length), (length, wide)
    vmem = dict(
        v_one=((width, feed), BF16),
        v_two=((width, feed), BF16),
        g_contract=((width, feed), BF16),
        g_expand=((width, feed), BF16),
        g_rest=((width, 5 * wide), BF16),
        v_left=(turned, BF16),
        v_right=(turned, BF16),
        v_grad=(square, BF16),
        v_up=(square, BF16),
        v_part=(square, BF16),
        v_slope=(square, F32),
        v_joint=((length, 3 * wide), BF16),
        v_query_grad=(strip, BF16),
        v_head_grad=(strip, BF16),
        v_turn_one=(strip, BF16),
        v_turn_two=(strip, BF16),
        v_text=((TEXT, 2 * wide), BF16),
        v_terms=((2 * TEXT, width), BF16),
        v_text_part=((TEXT, width), BF16),
        v_text_out=((TEXT // 4, width), F32),
        near_rows=((2, rows, width), BF16),
        far_rows=((rows, width), BF16),
        near_cols=((2, length, wide), BF16),
        far_cols=(strip, BF16),
        near_text=((2, TEXT // 4, width), BF16),
        far_text=((TEXT // 4, width), BF16),
        v_branch=((rows, width), BF16),
        v_rows=((rows, width), BF16),
        v_two_rows=((rows, width), BF16),
        v_norm=((8, width), F32),
        v_norm_grads=((48, width), F32),
        v_norm_sum=((8, width), F32),
        v_norm_in=((6, 8, width), F32),
        v_key_sum=((length, 128), F32),
        v_value_sum=((length, 128), F32),
        v_inward_in=((shard, 3 * wide), BF16),
    )
    vmem.update(
        y_contract=((4, shard, feed), BF16),
        y_expand=((4, shard, feed), BF16),
        y_back=((1, shard, wide), BF16),
        y_keys=((1, shard, 2 * wide), BF16),
        y_query=((4, shard, wide), BF16),
        y_outward=((4, shard, wide), BF16),
        z_contract=((4, shard, feed), BF16),
        z_expand=((4, shard, feed), BF16),
        z_back=((8, shard, wide), BF16),
        z_keys=((8, shard, 2 * wide), BF16),
        z_query=((4, shard, wide), BF16),
        z_outward=((4, shard, wide), BF16),
    )
    sems = dict(
        ysend=(7, 4),
        yrecv=(7, 4),
        zsend=(7, 8),
        zrecv=(7, 8),
        bsend=(7, 3),
        brecv=(7, 3),
        tsend=(2, 3),
        trecv=(2, 3),
        csend=(1, 3),
        crecv=(1, 3),
        nsend=(6,),
        nrecv=(6,),
        asend=(3,),
        arecv=(3,),
        local=(32,),
        stored=(16,),
    )
    inner = dict(text=text, ids_col=ids_col, ids_row=ids_row)
    outer = dict(frames=frames, incoming=incoming, **vars(ahead))
    del outer["aligned"]
    return run_kernel(backward_kernel, 2, inner, outer, out, vmem, sems, dict(credit=(3,)))


def tp_shards(
    frames,
    text_states,
    block_table,
    inward,
    outward,
    querying,
    keying,
    returning,
    expand,
    contract,
    gains,
    shifts,
    out_grad,
):
    ahead = forward(
        frames[0],
        text_states[0],
        block_table,
        jnp.pad(jnp.concatenate([gains, shifts], axis=0), ((0, 10), (0, 80))),
        out_grad[0],
        dict(
            inward=inward,
            outward=outward,
            query=querying,
            keys=keying,
            back=returning,
            expand=expand,
            contract=contract.T,
        ),
    )
    done = backward(ahead, frames[0], text_states[0], block_table, out_grad[0])
    share = gains.shape[1]
    place = (lax.axis_index("grp") * lax.axis_size("blk") + lax.axis_index("blk")) * share
    norm_grads = lax.dynamic_slice_in_dim(done.norm_out, place, share, 1)
    return (
        done.block_out[None],
        done.frames_out[None],
        done.text_out[None],
        done.inward_out,
        done.outward_out,
        done.querying_out,
        done.keying_out,
        done.returning_out,
        done.expand_out,
        done.contract_out.T,
        norm_grads[:3],
        norm_grads[3:6],
    )


def solution(mesh):
    small = mesh.shape["grp"] == 8 and mesh.shape["blk"] == 4
    return jax.shard_map(
        tp_shards if small else shards,
        mesh=mesh,
        in_specs=(
            P("grp", "blk", None),
            P("grp", None, None),
            P("grp", None),
            P("grp", "blk"),
            P("grp", "blk"),
            P("grp", "blk"),
            P("grp", "blk"),
            P("grp", "blk"),
            P("grp", "blk"),
            P("blk", "grp"),
            P(None, ("grp", "blk")),
            P(None, ("grp", "blk")),
            P("grp", "blk", None),
        ),
        out_specs=(
            P("grp", "blk", None),
            P("grp", "blk", None),
            P("grp", "blk", None),
            P("grp", "blk"),
            P("grp", "blk"),
            P("grp", "blk"),
            P("grp", "blk"),
            P("grp", "blk"),
            P("grp", "blk"),
            P("blk", "grp"),
            P(None, ("grp", "blk")),
            P(None, ("grp", "blk")),
        ),
        check_vma=False,
    )
```

```python
import functools
import math

import jax
import jax.numpy as jnp
from jax import lax
from jax.experimental import pallas as pl
from jax.experimental.pallas import tpu as pltpu
from jax.sharding import PartitionSpec as P

HEADS = 24
HEAD = 64
TEXT = 64
SEG = 64


def layer_norm(values, gain, shift):
    center = values - jnp.mean(values, axis=-1, keepdims=True)
    spread = jnp.mean(center * center, axis=-1, keepdims=True)
    return center * lax.rsqrt(spread + 1e-05) * gain + shift


def norm_pull(values, gain, shift, incoming):
    unused, pullback = jax.vjp(layer_norm, values, gain, shift)
    return pullback(incoming)


def gelu_slope(upward):
    return (
        0.5 * (1.0 + lax.erf(upward * 0.7071067811865476))
        + upward * jnp.exp(-0.5 * upward * upward) * 0.3989422804014327
    )


def gather_weights(inward, outward, querying, keying, returning, expand, contract, gains, shifts):
    inward, outward, querying, keying, returning, expand, contract, gains, shifts = (
        lax.all_gather(inward, "blk", axis=1, tiled=True),
        lax.all_gather(outward, "blk", axis=1, tiled=True),
        lax.all_gather(querying, "blk", axis=1, tiled=True),
        lax.all_gather(keying, "blk", axis=1, tiled=True),
        lax.all_gather(returning, "blk", axis=1, tiled=True),
        lax.all_gather(expand, "blk", axis=1, tiled=True),
        lax.all_gather(contract, "blk", axis=0, tiled=True),
        lax.all_gather(gains, "blk", axis=1, tiled=True),
        lax.all_gather(shifts, "blk", axis=1, tiled=True),
    )
    return (
        lax.all_gather(inward, "grp", axis=0, tiled=True),
        lax.all_gather(outward, "grp", axis=0, tiled=True),
        lax.all_gather(querying, "grp", axis=0, tiled=True),
        lax.all_gather(keying, "grp", axis=0, tiled=True),
        lax.all_gather(returning, "grp", axis=0, tiled=True),
        lax.all_gather(expand, "grp", axis=0, tiled=True),
        lax.all_gather(contract, "grp", axis=1, tiled=True),
        lax.all_gather(gains, "grp", axis=1, tiled=True),
        lax.all_gather(shifts, "grp", axis=1, tiled=True),
    )


def shards(
    frames,
    text_states,
    block_table,
    inward,
    outward,
    querying,
    keying,
    returning,
    expand,
    contract,
    gains,
    shifts,
    out_grad,
):
    (
        full_inward,
        full_outward,
        full_query,
        full_keys,
        full_return,
        full_expand,
        full_contract,
        full_gains,
        full_shifts,
    ) = gather_weights(
        inward, outward, querying, keying, returning, expand, contract, gains, shifts
    )
    width = frames.shape[2]
    rows = frames.shape[1]
    length = block_table.shape[1] * SEG
    group = lax.axis_size("blk")
    member = lax.axis_index("blk")
    span = math.gcd(length, 512)
    steps = length // span
    gain_rows = full_gains.astype(jnp.float32)
    shift_rows = full_shifts.astype(jnp.float32)
    key_frames = (
        block_table[0][:, None] * SEG + jnp.arange(SEG, dtype=jnp.int32)[None, :]
    ).reshape(length)
    own_frames = lax.dynamic_slice_in_dim(key_frames, member * rows, rows, 0)
    inputs = frames[0].astype(jnp.float32)
    first = layer_norm(inputs, gain_rows[0], shift_rows[0]).astype(jnp.bfloat16)
    joint = jnp.dot(first, full_inward, preferred_element_type=jnp.float32).astype(jnp.bfloat16)
    queries = joint[:, :width].reshape(rows, HEADS, HEAD)
    pairs = lax.all_gather(joint[:, width:], "blk", axis=0, tiled=True)
    pair_blocks = pairs.reshape(steps, span, 2 * width)
    frame_blocks = key_frames.reshape(steps, span)

    def scores_of(block, block_frames):
        keys = block[:, :width].reshape(span, HEADS, HEAD)
        raw = jnp.einsum("qhd,khd->hqk", queries, keys, preferred_element_type=jnp.float32) * 0.125
        allowed = block_frames[None, :] <= own_frames[:, None]
        return jnp.where(allowed[None], raw, -1e30)

    def stat_step(carry, items):
        peak, total = carry
        scores = scores_of(items[0], items[1])
        higher = jnp.maximum(peak, jnp.max(scores, axis=2))
        total = total * jnp.exp(peak - higher) + jnp.sum(
            jnp.exp(scores - higher[:, :, None]), axis=2
        )
        return ((higher, total), None)

    start_peak = jnp.full((HEADS, rows), -1e30, jnp.float32)
    (peak, total), unused = lax.scan(
        stat_step, (start_peak, jnp.zeros((HEADS, rows), jnp.float32)), (pair_blocks, frame_blocks)
    )
    log_total = peak + jnp.log(total)

    def out_step(carry, items):
        weighting = jnp.exp(scores_of(items[0], items[1]) - log_total[:, :, None]).astype(
            jnp.bfloat16
        )
        values = items[0][:, width:].reshape(span, HEADS, HEAD)
        return (
            carry
            + jnp.einsum("hqk,khd->qhd", weighting, values, preferred_element_type=jnp.float32),
            None,
        )

    mixed, unused = lax.scan(
        out_step, jnp.zeros((rows, HEADS, HEAD), jnp.float32), (pair_blocks, frame_blocks)
    )
    attended = mixed.reshape(rows, width).astype(jnp.bfloat16)
    hidden_one = inputs + jnp.dot(attended, full_outward, preferred_element_type=jnp.float32)
    second = layer_norm(hidden_one, gain_rows[1], shift_rows[1]).astype(jnp.bfloat16)
    cross_query = jnp.dot(second, full_query, preferred_element_type=jnp.float32).astype(
        jnp.bfloat16
    )
    cross_heads = cross_query.reshape(rows, HEADS, HEAD)
    text = text_states[0]
    text_pairs = jnp.dot(text, full_keys, preferred_element_type=jnp.float32).astype(jnp.bfloat16)
    text_keys = text_pairs[:, :width].reshape(TEXT, HEADS, HEAD)
    text_values = text_pairs[:, width:].reshape(TEXT, HEADS, HEAD)
    cross_scores = (
        jnp.einsum("qhd,khd->hqk", cross_heads, text_keys, preferred_element_type=jnp.float32)
        * 0.125
    )
    cross_soft = jax.nn.softmax(cross_scores, axis=2)
    cross_weighting = cross_soft.astype(jnp.bfloat16)
    crossed = (
        jnp.einsum("hqk,khd->qhd", cross_weighting, text_values, preferred_element_type=jnp.float32)
        .reshape(rows, width)
        .astype(jnp.bfloat16)
    )
    hidden_two = hidden_one + jnp.dot(crossed, full_return, preferred_element_type=jnp.float32)
    third = layer_norm(hidden_two, gain_rows[2], shift_rows[2]).astype(jnp.bfloat16)
    upward = jnp.dot(third, full_expand, preferred_element_type=jnp.float32)
    activated = jax.nn.gelu(upward, approximate=False).astype(jnp.bfloat16)
    branch = jnp.dot(activated, full_contract, preferred_element_type=jnp.float32)
    block_out = (hidden_two + branch).astype(jnp.bfloat16)[None]
    (
        full_inward,
        full_outward,
        full_query,
        full_keys,
        full_return,
        full_expand,
        full_contract,
        full_gains,
        full_shifts,
    ) = gather_weights(
        inward, outward, querying, keying, returning, expand, contract, gains, shifts
    )
    incoming = out_grad[0].astype(jnp.float32)
    branch_grad = out_grad[0]
    act_grad = jnp.dot(branch_grad, full_contract.T, preferred_element_type=jnp.float32)
    contract_grad = jnp.dot(activated.T, branch_grad, preferred_element_type=jnp.float32)
    up_grad = (act_grad * gelu_slope(upward)).astype(jnp.bfloat16)
    expand_grad = jnp.dot(third.T, up_grad, preferred_element_type=jnp.float32)
    third_grad = jnp.dot(up_grad, full_expand.T, preferred_element_type=jnp.float32)
    two_grad, gain_two, shift_two = norm_pull(hidden_two, gain_rows[2], shift_rows[2], third_grad)
    hidden_two_grad = incoming + two_grad
    branch_two = hidden_two_grad.astype(jnp.bfloat16)
    crossed_grad = jnp.dot(branch_two, full_return.T, preferred_element_type=jnp.float32).astype(
        jnp.bfloat16
    )
    crossed_grad = crossed_grad.reshape(rows, HEADS, HEAD)
    prob_grad = jnp.einsum(
        "qhd,khd->hqk", crossed_grad, text_values, preferred_element_type=jnp.float32
    )
    text_value_grad = jnp.einsum(
        "hqk,qhd->khd", cross_weighting, crossed_grad, preferred_element_type=jnp.float32
    )
    cross_score_grad = (
        cross_soft * (prob_grad - jnp.sum(prob_grad * cross_soft, axis=2, keepdims=True))
    ).astype(jnp.bfloat16)
    cross_query_grad = (
        (
            jnp.einsum(
                "hqk,khd->qhd", cross_score_grad, text_keys, preferred_element_type=jnp.float32
            )
            * 0.125
        )
        .reshape(rows, width)
        .astype(jnp.bfloat16)
    )
    text_key_grad = (
        jnp.einsum(
            "hqk,qhd->khd", cross_score_grad, cross_heads, preferred_element_type=jnp.float32
        )
        * 0.125
    )
    text_terms = jnp.concatenate(
        [text_key_grad.reshape(TEXT, width), text_value_grad.reshape(TEXT, width)], axis=1
    )
    text_share = lax.psum_scatter(
        text_terms.astype(jnp.bfloat16), "blk", scatter_dimension=0, tiled=True
    )
    share = TEXT // group
    text_grad = jnp.dot(text_share, full_keys.T, preferred_element_type=jnp.float32)[None]
    one_grad, gain_one, shift_one = norm_pull(
        hidden_one,
        gain_rows[1],
        shift_rows[1],
        jnp.dot(cross_query_grad, full_query.T, preferred_element_type=jnp.float32),
    )
    hidden_one_grad = hidden_two_grad + one_grad
    branch_one = hidden_one_grad.astype(jnp.bfloat16)
    attended_grad = jnp.dot(branch_one, full_outward.T, preferred_element_type=jnp.float32).astype(
        jnp.bfloat16
    )
    attended_grad = attended_grad.reshape(rows, HEADS, HEAD)
    delta = jnp.sum(attended_grad.astype(jnp.float32) * mixed, axis=2).T

    def back_step(carry, items):
        block = items[0]
        weighting = jnp.exp(scores_of(block, items[1]) - log_total[:, :, None])
        keys = block[:, :width].reshape(span, HEADS, HEAD)
        values = block[:, width:].reshape(span, HEADS, HEAD)
        value_grad = jnp.einsum(
            "hqk,qhd->khd",
            weighting.astype(jnp.bfloat16),
            attended_grad,
            preferred_element_type=jnp.float32,
        )
        weight_grad = jnp.einsum(
            "qhd,khd->hqk", attended_grad, values, preferred_element_type=jnp.float32
        )
        score_grad = (weighting * (weight_grad - delta[:, :, None])).astype(jnp.bfloat16)
        carry = carry + jnp.einsum(
            "hqk,khd->qhd", score_grad, keys, preferred_element_type=jnp.float32
        )
        key_grad = (
            jnp.einsum("hqk,qhd->khd", score_grad, queries, preferred_element_type=jnp.float32)
            * 0.125
        )
        return (
            carry,
            jnp.concatenate(
                [key_grad.reshape(span, width), value_grad.reshape(span, width)], axis=1
            ),
        )

    query_sum, pair_terms = lax.scan(
        back_step, jnp.zeros((rows, HEADS, HEAD), jnp.float32), (pair_blocks, frame_blocks)
    )
    pair_grad = lax.psum_scatter(
        pair_terms.reshape(length, 2 * width).astype(jnp.bfloat16),
        "blk",
        scatter_dimension=0,
        tiled=True,
    )
    joint_grad = jnp.concatenate(
        [(query_sum * 0.125).reshape(rows, width).astype(jnp.bfloat16), pair_grad], axis=1
    )
    zero_grad, gain_zero, shift_zero = norm_pull(
        inputs,
        gain_rows[0],
        shift_rows[0],
        jnp.dot(joint_grad, full_inward.T, preferred_element_type=jnp.float32),
    )
    frames_grad = (hidden_one_grad + zero_grad)[None]
    across = lax.axis_size("grp")
    gains_grad = (
        jnp.stack([gain_zero, gain_one, gain_two])
        .reshape(3, across, group, -1)
        .transpose(0, 2, 1, 3)
        .reshape(3, width)
    )
    shifts_grad = (
        jnp.stack([shift_zero, shift_one, shift_two])
        .reshape(3, across, group, -1)
        .transpose(0, 2, 1, 3)
        .reshape(3, width)
    )
    expand_grad, contract_grad = (
        lax.psum_scatter(
            expand_grad.astype(jnp.bfloat16), "blk", scatter_dimension=1, tiled=True
        ).astype(jnp.float32),
        lax.psum_scatter(
            contract_grad.astype(jnp.bfloat16), "blk", scatter_dimension=0, tiled=True
        ).astype(jnp.float32),
    )
    own_text = lax.dynamic_slice_in_dim(text, member * share, share, 0)
    inward_grad = jnp.dot(first.T, joint_grad, preferred_element_type=jnp.float32)
    outward_grad = jnp.dot(attended.T, branch_one, preferred_element_type=jnp.float32)
    querying_grad = jnp.dot(second.T, cross_query_grad, preferred_element_type=jnp.float32)
    keying_grad = jnp.dot(own_text.T, text_share, preferred_element_type=jnp.float32)
    returning_grad = jnp.dot(crossed.T, branch_two, preferred_element_type=jnp.float32)
    (
        inward_grad,
        outward_grad,
        querying_grad,
        keying_grad,
        returning_grad,
        gains_grad,
        shifts_grad,
    ) = (
        lax.psum_scatter(
            inward_grad.astype(jnp.bfloat16), "blk", scatter_dimension=1, tiled=True
        ).astype(jnp.float32),
        lax.psum_scatter(
            outward_grad.astype(jnp.bfloat16), "blk", scatter_dimension=1, tiled=True
        ).astype(jnp.float32),
        lax.psum_scatter(
            querying_grad.astype(jnp.bfloat16), "blk", scatter_dimension=1, tiled=True
        ).astype(jnp.float32),
        lax.psum_scatter(
            keying_grad.astype(jnp.bfloat16), "blk", scatter_dimension=1, tiled=True
        ).astype(jnp.float32),
        lax.psum_scatter(
            returning_grad.astype(jnp.bfloat16), "blk", scatter_dimension=1, tiled=True
        ).astype(jnp.float32),
        lax.psum_scatter(
            gains_grad.astype(jnp.bfloat16), "blk", scatter_dimension=1, tiled=True
        ).astype(jnp.float32),
        lax.psum_scatter(
            shifts_grad.astype(jnp.bfloat16), "blk", scatter_dimension=1, tiled=True
        ).astype(jnp.float32),
    )
    (
        inward_grad,
        outward_grad,
        querying_grad,
        keying_grad,
        returning_grad,
        expand_grad,
        contract_grad,
        gains_grad,
        shifts_grad,
    ) = (
        lax.psum_scatter(
            inward_grad.astype(jnp.bfloat16), "grp", scatter_dimension=0, tiled=True
        ).astype(jnp.float32),
        lax.psum_scatter(
            outward_grad.astype(jnp.bfloat16), "grp", scatter_dimension=0, tiled=True
        ).astype(jnp.float32),
        lax.psum_scatter(
            querying_grad.astype(jnp.bfloat16), "grp", scatter_dimension=0, tiled=True
        ).astype(jnp.float32),
        lax.psum_scatter(
            keying_grad.astype(jnp.bfloat16), "grp", scatter_dimension=0, tiled=True
        ).astype(jnp.float32),
        lax.psum_scatter(
            returning_grad.astype(jnp.bfloat16), "grp", scatter_dimension=0, tiled=True
        ).astype(jnp.float32),
        lax.psum_scatter(
            expand_grad.astype(jnp.bfloat16), "grp", scatter_dimension=0, tiled=True
        ).astype(jnp.float32),
        lax.psum_scatter(
            contract_grad.astype(jnp.bfloat16), "grp", scatter_dimension=1, tiled=True
        ).astype(jnp.float32),
        lax.psum_scatter(
            gains_grad.astype(jnp.bfloat16), "grp", scatter_dimension=1, tiled=True
        ).astype(jnp.float32),
        lax.psum_scatter(
            shifts_grad.astype(jnp.bfloat16), "grp", scatter_dimension=1, tiled=True
        ).astype(jnp.float32),
    )
    return (
        block_out,
        frames_grad,
        text_grad,
        inward_grad,
        outward_grad,
        querying_grad,
        keying_grad,
        returning_grad,
        expand_grad,
        contract_grad,
        gains_grad,
        shifts_grad,
    )


MESH = pl.DeviceIdType.MESH
BF16, F32 = jnp.bfloat16, jnp.float32


class Bag:
    def __init__(self, **items):
        self.__dict__.update(items)


def named(keys, items):
    return Bag(**dict(zip(keys, items)))


class Spot:
    def __init__(self):
        grp, blk = lax.axis_index("grp"), lax.axis_index("blk")
        self.grp, self.blk = grp, blk
        self.z, self.y = grp // 2, lax.rem(grp, 2)
        self.x, self.core = blk // 2, lax.rem(blk, 2)
        self.sib_blk = self.x * 2 + 1 - self.core
        self.opp_blk = (1 - self.x) * 2 + self.core
        self.sib = (grp, self.sib_blk)
        self.opp = (grp, self.opp_blk)
        self.part = (self.z * 2 + 1 - self.y, blk)
        self.up = ((self.z + 1) * 2 + self.y, blk)
        self.down = ((self.z - 1) * 2 + self.y, blk)

        self.far_blk = (1 - self.x) * 2 + 1 - self.core

    def z_peer(self, k):
        return (lax.rem(self.z + k, 4) * 2 + self.y, self.blk)

    def greet_all(self):
        barrier = pltpu.get_barrier_semaphore()
        peers = [self.z_peer(k) for k in (1, 2, 3)]
        for who in [self.sib, self.opp, (self.grp, self.far_blk), self.part] + peers:
            pl.semaphore_signal(barrier, inc=1, device_id=who, device_id_type=MESH)
        pl.semaphore_wait(barrier, 7)

    def greet(self):
        barrier = pltpu.get_barrier_semaphore()
        for who in (self.sib, self.opp, self.part):
            pl.semaphore_signal(barrier, inc=1, device_id=who, device_id_type=MESH)

        @pl.when(self.z > 0)
        def _():
            pl.semaphore_signal(barrier, inc=1, device_id=self.down, device_id_type=MESH)

        @pl.when(self.z < 3)
        def _():
            pl.semaphore_signal(barrier, inc=1, device_id=self.up, device_id_type=MESH)

        ends = (self.z == 0) | (self.z == 3)

        @pl.when(ends)
        def _():
            pl.semaphore_wait(barrier, 4)

        @pl.when(jnp.logical_not(ends))
        def _():
            pl.semaphore_wait(barrier, 5)


def push(src, dst, send, recv, who):
    return pltpu.make_async_remote_copy(
        src_ref=src, dst_ref=dst, send_sem=send, recv_sem=recv, device_id=who, device_id_type=MESH
    )


class Gather:
    def __init__(self, spot, shard, full, zsend, zrecv, ysend, yrecv, near, spread):
        self.spot, self.shard, self.full = spot, shard, full
        self.zsend, self.zrecv, self.ysend, self.yrecv, self.near = zsend, zrecv, ysend, yrecv, near
        self.spread = spread
        self.size = shard.shape[0]

    def rows(self, z, flip=0):
        spot = self.spot
        row = z * 2 + (1 - spot.y if flip else spot.y)
        return self.full.at[pl.ds(pl.multiple_of(row * self.size, self.size), self.size)]

    def z_copy(self, src, dst, k, side, flip):
        slot = (flip * 2 + side) * 3 + k - 1
        who = self.spot.up if side else self.spot.down
        return push(src, dst, self.zsend.at[slot], self.zrecv.at[slot], who)

    def y_copy(self, src, dst, slot):
        return push(src, dst, self.ysend.at[slot], self.yrecv.at[slot], self.spot.part)

    def launch(self, src, flip):
        spot = self.spot

        @pl.when(spot.z > 0)
        def _():
            self.z_copy(src, self.rows(spot.z, flip), 1, 0, flip).start()

        @pl.when(spot.z < 3)
        def _():
            self.z_copy(src, self.rows(spot.z, flip), 1, 1, flip).start()

    def start(self):
        here = self.rows(self.spot.z)
        self.y_copy(self.shard, here, 0).start()
        self.launch(self.shard, 0)
        pltpu.make_async_copy(self.shard, here, self.near).start()

    def pass_on(self):
        other = self.rows(self.spot.z, 1)
        self.y_copy(other, other, 0).wait_recv()
        self.launch(other, 1)

    def relay(self, k, side, flip):
        spot = self.spot
        src_z = spot.z - k if side else spot.z + k
        block = self.rows(src_z, flip)

        @pl.when(src_z >= 0 if side else src_z <= 3)
        def _():
            self.z_copy(block, block, k, side, flip).wait_recv()
            if k < 3:

                @pl.when(spot.z < 3 if side else spot.z > 0)
                def _():
                    self.z_copy(block, block, k + 1, side, flip).start()

            if not self.spread:
                self.y_copy(block, block, 1 + side * 3 + k - 1).start()

    def finish(self):
        spot = self.spot
        pltpu.make_async_copy(self.shard, self.rows(spot.z), self.near).wait()
        if self.spread:
            return
        self.y_copy(self.shard, self.rows(spot.z, 1), 0).wait_recv()
        for side in (0, 1):
            for k in (1, 2, 3):
                src_z = spot.z - k if side else spot.z + k
                block = self.rows(src_z, 1)

                @pl.when(src_z >= 0 if side else src_z <= 3)
                def _():
                    self.y_copy(block, block, 1 + side * 3 + k - 1).wait_recv()

    def drain(self):
        spot = self.spot
        self.y_copy(self.shard, self.rows(spot.z), 0).wait_send()
        for side in (0, 1):
            for k in (1, 2, 3):
                src_z = spot.z - k if side else spot.z + k
                sent_z = spot.z - k + 1 if side else spot.z + k - 1
                block = self.rows(spot.z)
                if not self.spread:

                    @pl.when(src_z >= 0 if side else src_z <= 3)
                    def _():
                        self.y_copy(block, block, 1 + side * 3 + k - 1).wait_send()

                for flip in (0, 1) if self.spread else (0,):

                    @pl.when((spot.z < 3) & (sent_z >= 0) if side else (spot.z > 0) & (sent_z <= 3))
                    def _():
                        self.z_copy(block, block, k, side, flip).wait_send()


class Share:
    def __init__(self, spot, own, where, send, recv):
        self.spot, self.own, self.where, self.send, self.recv = spot, own, where, send, recv

    def first(self):
        return push(
            self.own, self.where(self.spot.blk), self.send.at[0], self.recv.at[0], self.spot.opp
        )

    def second(self):
        return push(
            self.own, self.where(self.spot.blk), self.send.at[1], self.recv.at[1], self.spot.sib
        )

    def third(self):
        passed = self.where(self.spot.opp_blk)
        return push(passed, passed, self.send.at[2], self.recv.at[2], self.spot.sib)

    def start(self):
        self.first().start()
        self.second().start()

    def relay(self):
        self.first().wait_recv()
        self.third().start()

    def finish(self):
        self.second().wait_recv()
        self.third().wait_recv()

    def drain(self):
        self.first().wait_send()
        self.second().wait_send()
        self.third().wait_send()


def dot(left, right):
    return jnp.dot(left, right, preferred_element_type=F32)


def dot_t(left, right):
    return lax.dot_general(left, right, (((1,), (1,)), ((), ())), preferred_element_type=F32)


def tiles(count, size, body):
    @pl.loop(0, count)
    def _(step):
        body(pl.ds(pl.multiple_of(step * size, size), size))


def norm_block(values, gain, shift):
    center = values - jnp.mean(values, axis=1, keepdims=True)
    spread = jnp.mean(center * center, axis=1, keepdims=True)
    return center * lax.rsqrt(spread + 1e-05) * gain + shift


FORWARD_ORDER = (
    (0, 1), (0, 0), (3, 28), (0, 2), (2, 0, 1, 0, 0), (2, 0, 1, 1, 0), (2, 1, 1, 0, 0),
    (2, 1, 1, 1, 0), (2, 2, 1, 0, 0), (2, 2, 1, 1, 0), (2, 0, 2, 1, 0), (2, 0, 2, 0, 0), (0, 3),
    (3, 29), (2, 1, 2, 1, 0), (3, 31), (2, 2, 2, 0, 0), (2, 2, 2, 1, 0), (2, 1, 2, 0, 0),
    (2, 0, 3, 1, 0), (3, 30), (2, 0, 3, 0, 0), (0, 4), (2, 3, 1, 1, 0), (2, 3, 1, 0, 0),
    (2, 2, 3, 0, 0), (2, 1, 3, 1, 0), (2, 2, 3, 1, 0), (2, 1, 3, 0, 0), (3, 0), (3, 32),
    (2, 4, 1, 1, 0), (2, 3, 2, 0, 0), (2, 3, 2, 1, 0), (2, 4, 1, 0, 0), (0, 5), (2, 4, 2, 1, 0),
    (2, 3, 3, 0, 0), (3, 33), (3, 36), (2, 3, 3, 1, 0), (2, 4, 2, 0, 0), (0, 6), (2, 5, 1, 0, 0),
    (2, 5, 1, 1, 0), (2, 4, 3, 1, 0), (2, 4, 3, 0, 0), (2, 6, 1, 1, 0), (2, 6, 1, 0, 0),
    (2, 5, 2, 1, 0), (2, 5, 2, 0, 0), (0, 7), (0, 8), (2, 6, 2, 1, 0), (2, 6, 2, 0, 0),
    (2, 5, 3, 1, 0), (2, 5, 3, 0, 0), (2, 7, 1, 1, 0), (2, 7, 1, 0, 0), (3, 1), (3, 2), (3, 3),
    (2, 6, 3, 1, 0), (2, 8, 1, 0, 0), (2, 6, 3, 0, 0), (2, 7, 2, 1, 0), (2, 7, 2, 0, 0), (0, 9),
    (2, 8, 1, 1, 0), (0, 10), (2, 7, 3, 1, 0), (2, 8, 2, 0, 0), (3, 4), (2, 9, 1, 1, 0),
    (2, 7, 3, 0, 0), (3, 5), (3, 6), (3, 7), (2, 8, 2, 1, 0), (2, 9, 1, 0, 0), (0, 11), (3, 34),
    (2, 10, 1, 1, 0), (2, 10, 1, 0, 0), (1, 8), (3, 10), (3, 11), (2, 9, 2, 1, 0),
    (2, 8, 3, 0, 0), (3, 8), (3, 9), (3, 12), (3, 13), (2, 8, 3, 1, 0), (2, 9, 2, 0, 0), (3, 14),
    (2, 11, 1, 0, 0), (2, 10, 2, 0, 0), (0, 12), (3, 15), (3, 16), (2, 8, 1, 1, 1), (3, 17),
    (2, 8, 1, 0, 1), (0, 13), (2, 10, 2, 1, 0), (2, 11, 1, 1, 0), (2, 9, 3, 0, 0),
    (2, 9, 3, 1, 0), (2, 11, 2, 0, 0), (2, 12, 1, 1, 0), (3, 18), (2, 10, 3, 0, 0), (3, 19),
    (2, 8, 2, 1, 1), (2, 12, 1, 0, 0), (3, 20), (3, 21), (2, 13, 1, 1, 0), (3, 35),
    (2, 8, 2, 0, 1), (2, 10, 3, 1, 0), (2, 11, 2, 1, 0), (2, 13, 1, 0, 0), (2, 11, 3, 0, 0),
    (2, 12, 2, 1, 0), (3, 22), (2, 12, 2, 0, 0), (3, 23), (2, 8, 3, 1, 1), (3, 24),
    (2, 8, 3, 0, 1), (2, 13, 2, 1, 0), (2, 11, 3, 1, 0), (2, 13, 2, 0, 0), (3, 25),
    (2, 12, 3, 0, 0), (2, 12, 3, 1, 0), (2, 13, 3, 0, 0), (2, 13, 3, 1, 0), (3, 26), (3, 27),
)


def forward_kernel(names, *refs):
    r = named(names, refs)
    spot = Spot()
    rows, width = r.frames.shape
    length = r.x_all.shape[0]
    wide = r.outward.shape[1]
    blk = spot.blk
    outs = []

    def save(src, dst):
        copy = pltpu.make_async_copy(src, dst, r.local.at[len(outs)])
        copy.start()
        outs.append(copy)
        return copy

    def lanes(index, size):
        return pl.ds(pl.multiple_of(index * size, 128), size)

    def row_block(ref):
        return lambda index: ref.at[pl.ds(pl.multiple_of(index * rows, rows), rows)]

    def col_block(ref, size):
        return lambda index: ref.at[:, lanes(index, size)]

    def share(number, own, where):
        return Share(spot, own, where, r.bsend.at[number], r.brecv.at[number])

    gathers = []

    def gather(shard, full, spread):
        wide = full.shape[1] // len(spread)
        first = len(gathers)
        for number, flag in enumerate(spread):
            here = slice(number * wide, (number + 1) * wide)
            sems = (item.at[first + number] for item in (r.zsend, r.zrecv, r.ysend, r.yrecv, r.near))
            gathers.append(Gather(spot, shard.at[:, here], full.at[:, here], *sems, flag))
        return gathers[first:]

    g_norms = gather(r.v_norms, r.v_norm_all, (False,))
    g_outward = gather(r.outward, r.v_outward, (False,))
    g_inward = gather(r.aligned, r.v_inward, (False, False, False))
    g_query = gather(r.query, r.v_query, (False,))
    g_keys = gather(r.keys, r.v_keys, (False,))
    g_back = gather(r.back, r.v_back, (False,))
    g_expand = gather(r.expand, r.v_expand, (True, False))
    g_contract = gather(r.contract, r.v_contract, (False, False, False, False))

    spot.greet()

    def piece(part):
        index = blk * 3 + part
        owner = lax.rem(index, 4)
        return owner, index // 4

    def aligned_copy(part):
        owner, kind = piece(part)
        src = r.inward.at[:, part * wide : (part + 1) * wide]
        return owner, kind, src, r.aligned.at[:, lanes(kind, wide)]

    for part in range(3):
        owner, kind, src, dst = aligned_copy(part)

        @pl.when(owner == blk)
        def _():
            pltpu.make_async_copy(src, dst, r.arecv.at[kind]).start()

        @pl.when(owner != blk)
        def _():
            push(src, dst, r.asend.at[part], r.arecv.at[kind], (spot.grp, owner)).start()

    norm_share = share(0, r.norms, lambda index: r.v_norms.at[pl.ds(index * 16, 16)])
    norm_own = pltpu.make_async_copy(r.norms, r.v_norms.at[pl.ds(blk * 16, 16)], r.near.at[16])
    norm_own.start()
    norm_share.start()
    frame_share = share(1, r.frames, row_block(r.x_all))
    frame_own = pltpu.make_async_copy(r.frames, row_block(r.x_all)(blk), r.near.at[17])
    frame_own.start()
    frame_share.start()
    grad_share = share(2, r.incoming, row_block(r.g_all))
    grad_own = pltpu.make_async_copy(r.incoming, row_block(r.g_all)(blk), r.near.at[18])
    attended_share = share(3, col_block(r.s_attended, wide)(blk), col_block(r.s_attended, wide))
    one_share = share(4, col_block(r.s_one_all, wide)(blk), col_block(r.s_one_all, wide))
    text_share = share(5, col_block(r.s_text, 2 * wide)(blk), col_block(r.s_text, 2 * wide))
    crossed_share = share(6, col_block(r.s_crossed, wide)(blk), col_block(r.s_crossed, wide))
    two_share = share(7, col_block(r.s_two_all, wide)(blk), col_block(r.s_two_all, wide))
    g_outward[0].start()
    for kind in range(3):
        dst = r.aligned.at[:, kind * wide : (kind + 1) * wide]
        home = (kind * 4 + blk) // 3

        @pl.when(home == blk)
        def _():
            pltpu.make_async_copy(dst, dst, r.arecv.at[kind]).wait()

        @pl.when(home != blk)
        def _():
            push(dst, dst, r.asend.at[0], r.arecv.at[kind], spot.sib).wait_recv()

    low = lax.broadcasted_iota(jnp.int32, (1, 128), 1) < 64
    kept = []

    def half(value, part):
        return jnp.where(low if part == 0 else jnp.logical_not(low), value, jnp.zeros_like(value))

    def finish(items):
        for item in items:
            item.finish()

    def turn_over(source, turned):
        def flip(block):
            turned[:, block] = source[block, :].T

        tiles(length // 128, 128, flip)

    def normed(source, index, turned):
        gain = r.v_norm_rows[index : index + 1, :]
        shift = r.v_norm_rows[3 + index : 4 + index, :]

        def body(block):
            result = norm_block(source[block, :].astype(F32), gain, shift).astype(BF16)
            r.a_all[block, :] = result

        tiles(length // 32, 32, body)
        turn_over(r.a_all, turned)

    def side_by_side():
        depth = 8 * 128
        line = lax.broadcasted_iota(jnp.int32, (depth, 384), 0)
        column = lax.broadcasted_iota(jnp.int32, (depth, 384), 1)
        inside = line & 127
        place = jnp.where((inside < 48) & (column == (line >> 7) * 48 + inside), 1.0, 0.0).astype(BF16)
        for pair in range(4):
            parts = [pl.ds(pair * 128 + part * 16, 16) for part in range(8)]
            left = jnp.concatenate([r.v_norm_all[part, :] for part in parts], axis=1)
            r.v_norm_rows[:, pair * 384 : (pair + 1) * 384] = dot(left, place)
        save(r.v_norm_rows, r.norm_all)

    def first_norm():
        finish(g_norms)
        side_by_side()
        normed(r.x_all, 0, r.t_first)
        save(r.t_first, r.first_t)

    def joint():
        finish(g_inward)
        save(r.v_inward, r.w_inward)

        def body(block):
            r.s_joint[:, block] = dot(r.a_all[...], r.v_inward[:, block]).astype(BF16)

        tiles(3, wide, body)
        save(r.s_joint, r.joint)

    def soft(scores):
        power = jnp.exp(scores - jnp.max(scores, axis=1, keepdims=True))
        return (power * (1.0 / jnp.sum(power, axis=1, keepdims=True))).astype(BF16)

    def attend():
        @pl.loop(0, 12)
        def _(step):
            pair, block = step // 4, lax.rem(step, 4)
            here = pl.ds(pl.multiple_of(block * 128, 128), 128)
            query = r.s_joint[here, lanes(pair, 128)]
            key = r.s_joint[:, lanes(pair + 3, 128)]
            value = r.s_joint[:, lanes(pair + 6, 128)]
            keep = r.ids_row[...] <= r.ids_col[here, :]
            results = []
            for part in (0, 1):
                scores = jnp.where(keep, dot_t(half(query, part), key) * 0.125, -1e30)
                results.append(dot(soft(scores), value))
            r.s_attended[here, lanes(blk * 3 + pair, 128)] = jnp.where(low, *results).astype(BF16)

    def hidden_one():
        finish(g_outward)
        save(r.v_outward, r.w_outward)
        own = r.x_all[:, lanes(blk, wide)].astype(F32)
        r.s_one[...] = dot(r.s_attended[...], r.v_outward[...]) + own
        r.s_one_all[:, lanes(blk, wide)] = r.s_one[...].astype(BF16)

    def one_here():
        one_share.finish()
        save(row_block(r.s_one_all)(blk), r.one_rows)

    def text_pairs():
        finish(g_keys)
        save(r.v_keys, r.w_keys)
        r.s_text[:, lanes(blk, 2 * wide)] = dot(r.text[...], r.v_keys[...]).astype(BF16)

    def second_norm():
        normed(r.s_one_all, 1, r.t_second)
        save(r.t_second, r.second_t)

    def cross_query():
        finish(g_query)
        save(r.v_query, r.w_query)
        r.s_query[...] = dot(r.a_all[...], r.v_query[...]).astype(BF16)
        save(r.s_query, r.cross_query)

    def text_here():
        text_share.finish()
        save(r.s_text, r.text_all)

    def cross():
        @pl.loop(0, 3)
        def _(pair):
            query = r.s_query[:, lanes(pair, 128)]
            key = r.s_text[:, lanes(blk * 3 + pair, 128)]
            value = r.s_text[:, lanes(12 + blk * 3 + pair, 128)]
            results = []
            for part in (0, 1):
                results.append(dot(soft(dot_t(half(query, part), key) * 0.125), value))
            r.s_crossed[:, lanes(blk * 3 + pair, 128)] = jnp.where(low, *results).astype(BF16)

    def hidden_two():
        finish(g_back)
        save(r.v_back, r.w_back)
        r.s_one[...] += dot(r.s_crossed[...], r.v_back[...])
        r.s_two_all[:, lanes(blk, wide)] = r.s_one[...].astype(BF16)

    def two_here():
        two_share.finish()
        save(row_block(r.s_two_all)(blk), r.two_rows)

    def third_norm():
        normed(r.s_two_all, 2, r.t_third)
        save(r.t_third, r.third_t)

    def upward():
        finish(g_expand)
        kept.append(save(r.v_expand, r.w_expand))

        def body(block):
            r.s_upward[:, block] = dot(r.a_all[...], r.v_expand[:, block])

        tiles(4, 384, body)

    def gelu():
        def body(block):
            value = r.s_upward[block, :]
            gate = 0.5 + 0.5 * lax.erf(value * 0.7071067811865476)
            r.s_active[block, :] = (value * gate).astype(BF16)
            r.s_slope[block, :] = gate + value * jnp.exp(-0.5 * value * value) * 0.3989422804014327

        tiles(length // 16, 16, body)
        save(r.s_slope, r.slope)
        save(r.s_active, r.active)

    def contract_grad():
        kept[0].wait()
        for item in g_expand:
            item.drain()

        def body(block):
            r.v_expand[:, block] = dot(r.t_grad[...], r.s_active[:, block]).astype(BF16)

        tiles(4, 384, body)
        save(r.v_expand, r.contract_grad)

    def nothing():
        pass

    def frames_here():
        frame_own.wait()
        frame_share.finish()

    def grad_start():
        grad_own.start()
        grad_share.start()

    def grad_here():
        grad_share.finish()
        grad_own.wait()
        save(r.g_all, r.grad_all)

    def attended_over():
        turn_over(r.s_attended, r.t_attended)
        save(r.t_attended, r.attended_t)

    def crossed_over():
        turn_over(r.s_crossed, r.t_crossed)
        save(r.t_crossed, r.crossed_t)

    def grad_over():
        turn_over(r.g_all, r.t_grad)

    steps = (
        first_norm, joint, attend,
        attended_share.start, attended_share.relay, attended_share.finish,
        hidden_one, one_share.start, one_share.relay, one_here,
        text_pairs, text_share.start, text_share.relay, text_here,
        second_norm, cross_query, cross,
        crossed_share.start, crossed_share.relay, crossed_share.finish,
        hidden_two, two_share.start, two_share.relay, two_here,
        third_norm, upward, gelu, contract_grad,
        nothing, frame_share.relay, frames_here, grad_start, grad_share.relay, grad_here,
        attended_over, crossed_over, grad_over,
    )
    for kind, number, *rest in FORWARD_ORDER:
        if kind == 3:
            steps[number]()
            continue
        item = gathers[number]
        if kind == 2:
            item.relay(*rest)
        elif kind == 1:
            item.pass_on()
        elif item is g_norms[0]:
            norm_share.relay()
            norm_own.wait()
            norm_share.finish()
            item.start()
        elif item is not g_outward[0]:
            item.start()
    finish(g_contract)
    save(r.v_contract, r.w_contract)
    for part in range(3):
        owner, kind, src, dst = aligned_copy(part)

        @pl.when(owner != blk)
        def _():
            push(src, dst, r.asend.at[part], r.arecv.at[kind], (spot.grp, owner)).wait_send()

    for item in (
        norm_share, frame_share, grad_share, attended_share, one_share, text_share, crossed_share, two_share,
    ):
        item.drain()
    for item in gathers:
        if item not in g_expand:
            item.drain()
    for copy in outs:
        if copy is not kept[0]:
            copy.wait()


def ids_of(table):
    ids = (table[0][:, None] * SEG + jnp.arange(SEG, dtype=jnp.int32)[None, :]).reshape(-1)
    return ids[:, None], ids[None, :]


def run_kernel(kernel, number, inner, outer, out, vmem, sems, credits):
    anywhere = pl.BlockSpec(memory_space=pl.ANY)
    inside = pl.BlockSpec(memory_space=pltpu.VMEM)
    names = [*inner, *outer, *out, *vmem, *sems, *credits]
    results = pl.pallas_call(
        functools.partial(kernel, names),
        out_shape=[jax.ShapeDtypeStruct(*item) for item in out.values()],
        in_specs=[inside] * len(inner) + [anywhere] * len(outer),
        out_specs=[anywhere] * len(out),
        scratch_shapes=[pltpu.VMEM(*item) for item in vmem.values()]
        + [pltpu.SemaphoreType.DMA(shape) for shape in sems.values()]
        + [pltpu.SemaphoreType.REGULAR(shape) for shape in credits.values()],
        compiler_params=pltpu.CompilerParams(
            collective_id=number, has_side_effects=True, vmem_limit_bytes=60 * 2**20
        ),
    )(*inner.values(), *outer.values())
    return named(out, results)


def forward(frames, text, table, norms, incoming, weights):
    rows, width = frames.shape
    length = rows * lax.axis_size("blk")
    wide = width // lax.axis_size("blk")
    feed = weights["expand"].shape[1]
    ids_col, ids_row = ids_of(table)
    one = ((width, wide), BF16)
    two = ((width, 2 * wide), BF16)
    three = ((width, 3 * wide), BF16)
    four = ((width, feed), BF16)
    square, turned, strip = ((length, width), BF16), ((width, length), BF16), ((length, wide), BF16)
    big = ((length, feed), F32)
    own = ((rows, width), BF16)
    out = dict(
        w_outward=one,
        w_inward=three,
        w_query=one,
        w_keys=two,
        w_back=one,
        w_expand=four,
        w_contract=four,
        first_t=turned,
        second_t=turned,
        third_t=turned,
        attended_t=turned,
        crossed_t=turned,
        contract_grad=four,
        grad_all=square,
        joint=((length, 3 * wide), BF16),
        cross_query=strip,
        text_all=((TEXT, 2 * width), BF16),
        slope=big,
        active=((length, feed), BF16),
        one_rows=own,
        two_rows=own,
        norm_all=((16, width), F32),
        aligned=((width // lax.axis_size("grp"), 3 * wide), BF16),
    )
    vmem = dict(
        v_outward=one,
        v_inward=three,
        v_query=one,
        v_keys=two,
        v_back=one,
        v_expand=four,
        v_contract=four,
        x_all=square,
        g_all=square,
        a_all=square,
        s_attended=square,
        s_one_all=square,
        s_crossed=square,
        s_two_all=square,
        t_first=turned,
        t_second=turned,
        t_third=turned,
        t_attended=turned,
        t_crossed=turned,
        t_grad=turned,
        s_joint=((length, 3 * wide), BF16),
        s_one=((length, wide), F32),
        s_query=strip,
        s_text=((TEXT, 2 * width), BF16),
        s_upward=big,
        s_slope=big,
        s_active=((length, feed), BF16),
        v_norms=((64, 128), BF16),
        v_norm_all=((512, 128), BF16),
        v_norm_rows=((16, width), F32),
    )
    sems = dict(
        zsend=(14, 12),
        zrecv=(14, 12),
        ysend=(14, 7),
        yrecv=(14, 7),
        near=(19,),
        bsend=(8, 3),
        brecv=(8, 3),
        asend=(3,),
        arecv=(3,),
        local=(32,),
    )
    inner = dict(text=text, ids_col=ids_col, ids_row=ids_row)
    outer = dict(frames=frames, norms=norms, incoming=incoming, **weights)
    return run_kernel(forward_kernel, 1, inner, outer, out, vmem, sems, {})


class Reduce:
    def __init__(self, spot, grad, over, along, sems, spread, source=None):
        self.spot, self.grad, self.over, self.along = spot, grad, over, along
        self.ysend, self.yrecv, self.zsend, self.zrecv = sems
        self.spread = spread
        self.source = grad if source is None else source
        self.size, self.cols = over.shape[-2], over.shape[-1]

    def rows(self, z, flip=0, ref=None):
        spot = self.spot
        row = z * 2 + (1 - spot.y if flip else spot.y)
        return (self.grad if ref is None else ref).at[pl.ds(pl.multiple_of(row * self.size, self.size), self.size)]

    def add(self, target, extra):
        step = 16

        @pl.loop(0, self.size // step)
        def _(index):
            here = pl.ds(pl.multiple_of(index * step, step), step)
            target[here, :] = (target[here, :].astype(F32) + extra[here, :].astype(F32)).astype(BF16)

    def y_copy(self, z):
        return push(
            self.rows(z, 1, self.source), self.over.at[z], self.ysend.at[z], self.yrecv.at[z], self.spot.part
        )

    def y_start(self):
        for z in (0, 3, 1, 2):
            self.y_copy(z).start()

    def z_copy(self, goal, slot, who, flip):
        index = flip * 4 + slot
        return push(
            self.rows(goal, flip), self.along.at[index], self.zsend.at[flip * 4 + goal],
            self.zrecv.at[index], (who * 2 + self.spot.y, self.spot.blk),
        )

    def z_first(self, goal, flip):
        z = self.spot.z
        middle, end = (2, 3) if goal == 0 else (1, 0)
        for home in range(4):
            if home == goal or (goal in (0, 3) and home == middle):
                continue

            @pl.when(z == home)
            def _():
                if goal in (0, 3) and home == end:
                    self.z_copy(goal, 3, middle, flip).start()
                else:
                    self.z_copy(goal, home - (home > goal), goal, flip).start()

    def z_second(self, goal, flip):
        middle = 2 if goal == 0 else 1

        @pl.when(self.spot.z == middle)
        def _():
            index = flip * 4 + 3
            self.z_copy(goal, 3, goal, flip).wait_recv()
            self.add(self.rows(goal, flip), self.along.at[index])
            self.z_copy(goal, middle - (middle > goal), goal, flip).start()

    def take(self, goal):
        self.y_copy(goal).wait_recv()
        self.add(self.rows(goal), self.over.at[goal])
        self.z_first(goal, 0)

    def start(self):
        if not self.spread:
            return self.y_start()
        for goal in (0, 3, 1, 2):
            for flip in (1, 0):
                self.z_first(goal, flip)

    def combine(self, flip=0):
        self.z_second(0, flip)
        self.z_second(3, flip)

    def arrive(self, flip):
        z = self.spot.z
        for slot in range(3):
            unused = 3 if slot == 2 else 0 if slot == 0 else None

            def wait():
                self.z_copy(0, slot, 0, flip).wait_recv()

            if slot == 1:
                wait()
            else:
                pl.when(z != (0 if slot == 2 else 3))(wait)

    def total(self, flip, extra, body):
        z = self.spot.z
        own = self.rows(z, flip)

        def add_up(slots):
            @pl.loop(0, self.size // 16)
            def _(index):
                here = pl.ds(pl.multiple_of(index * 16, 16), 16)
                value = own[here, :].astype(F32)
                for slot in slots:
                    value += self.along[flip * 4 + slot, here, :].astype(F32)
                if extra is not None:
                    value += extra[here, :].astype(F32)
                body(here, value)

        @pl.when(z == 0)
        def _():
            add_up((0, 1))

        @pl.when(z == 3)
        def _():
            add_up((1, 2))

        @pl.when((z == 1) | (z == 2))
        def _():
            add_up((0, 1, 2))

    def cross(self):
        self.arrive(1)
        target = self.rows(self.spot.z, 1)

        def keep(here, value):
            target[here, :] = value.astype(BF16)

        self.total(1, None, keep)
        push(target, self.over.at[0], self.ysend.at[0], self.yrecv.at[0], self.spot.part).start()

    def finish(self, body):
        self.arrive(0)
        if self.spread:
            target = self.rows(self.spot.z, 1)
            push(target, self.over.at[0], self.ysend.at[0], self.yrecv.at[0], self.spot.part).wait_recv()
            self.total(0, self.over.at[0], body)
        else:
            self.total(0, None, body)

    def drain(self):
        z = self.spot.z
        if self.spread:
            target = self.rows(z, 1)
            push(target, self.over.at[0], self.ysend.at[0], self.yrecv.at[0], self.spot.part).wait_send()
        else:
            for goal in range(4):
                self.y_copy(goal).wait_send()
        for flip in (0, 1) if self.spread else (0,):
            for goal in range(4):

                @pl.when(z != goal)
                def _():
                    self.z_copy(goal, 0, 0, flip).wait_send()


class BlkSum:
    def __init__(self, spot, piece, near, far, send, recv, step, size):
        self.spot, self.piece, self.near, self.far = spot, piece, near, far
        self.send, self.recv, self.step, self.size = send, recv, step, size

    def to_core(self, x):
        spot = self.spot
        goal = x * 2 + 1 - spot.core
        return push(self.piece(goal), self.near.at[x], self.send.at[x], self.recv.at[x], spot.sib)

    def to_chip(self):
        spot = self.spot
        return push(self.piece(spot.opp_blk), self.far, self.send.at[2], self.recv.at[2], spot.opp)

    def start(self):
        self.to_core(0).start()
        self.to_core(1).start()

    def relay(self):
        spot = self.spot
        for x in (0, 1):
            self.to_core(x).wait_recv()
        target, extra = self.piece(spot.opp_blk), self.near.at[1 - spot.x]

        @pl.loop(0, self.size // self.step)
        def _(index):
            here = pl.ds(pl.multiple_of(index * self.step, self.step), self.step)
            target[here, :] = (target[here, :].astype(F32) + extra[here, :].astype(F32)).astype(BF16)

        self.to_chip().start()

    def finish(self):
        self.to_chip().wait_recv()

    def value(self, here):
        spot = self.spot
        own = self.piece(spot.blk)[here, :].astype(F32)
        return own + self.near[spot.x, here, :].astype(F32) + self.far[here, :].astype(F32)

    def drain(self):
        self.to_core(0).wait_send()
        self.to_core(1).wait_send()
        self.to_chip().wait_send()


class Turn:
    def __init__(self, spot, source, target, send, recv):
        self.spot, self.source, self.target, self.send, self.recv = spot, source, target, send, recv
        self.rows, self.wide = source.shape[0], target.shape[1]

    def copy(self, number):
        spot = self.spot
        goal = (spot.sib_blk, spot.opp_blk, spot.far_blk)[number]
        src = self.source.at[:, pl.ds(pl.multiple_of(goal * self.wide, 128), self.wide)]
        return push(src, self.place(spot.blk), self.send.at[number], self.recv.at[number], (spot.grp, goal))

    def place(self, index):
        return self.target.at[pl.ds(pl.multiple_of(index * self.rows, self.rows), self.rows)]

    def start(self):
        for number in (2, 1, 0):
            self.copy(number).start()
        spot = self.spot
        src = self.source.at[:, pl.ds(pl.multiple_of(spot.blk * self.wide, 128), self.wide)]
        self.place(spot.blk)[...] = src[...]

    def finish(self):
        for number in range(3):
            self.copy(number).wait_recv()

    def drain(self):
        for number in range(3):
            self.copy(number).wait_send()


def t_dot(left, right):
    return lax.dot_general(left, right, (((0,), (0,)), ((), ())), preferred_element_type=F32)


def backward_kernel(names, *refs):
    r = named(names, refs)
    spot = Spot()
    rows, width = r.frames.shape
    length = r.v_grad.shape[0]
    wide = r.v_query_grad.shape[1]
    blk = spot.blk
    spot.greet_all()

    def lanes(index, size):
        return pl.ds(pl.multiple_of(index * size, 128), size)

    def part(ref, first, size):
        return ref.at[:, first : first + size]

    def row_piece(ref, size):
        return lambda index: ref.at[pl.ds(pl.multiple_of(index * size, size), size)]

    loads = []

    def load(src, dst):
        copy = pltpu.make_async_copy(src, dst, r.local.at[len(loads)])
        copy.start()
        loads.append(copy)
        return copy

    grads = Bag(
        contract=r.g_contract,
        expand=r.g_expand,
        back=part(r.g_rest, 0, wide),
        keys=part(r.g_rest, wide, 2 * wide),
        query=part(r.g_rest, 3 * wide, wide),
        outward=part(r.g_rest, 4 * wide, wide),
        inward=part(r.g_contract, 0, 3 * wide),
    )

    def reduce(number, grad, over, along, spread=False, source=None):
        sems = tuple(item.at[number] for item in (r.ysend, r.yrecv, r.zsend, r.zrecv))
        return Reduce(spot, grad, over, along, sems, spread, source)

    reduces = Bag(
        contract=reduce(0, grads.contract, r.y_contract, r.z_contract, False, r.contract_grad),
        expand=reduce(1, grads.expand, r.y_expand, r.z_expand),
        back=reduce(2, grads.back, r.y_back, r.z_back, True),
        keys=reduce(3, grads.keys, r.y_keys, r.z_keys, True),
        query=reduce(4, grads.query, r.y_query, r.z_query),
        outward=reduce(5, grads.outward, r.y_outward, r.z_outward),
        inward=reduce(
            6,
            grads.inward,
            r.y_contract.at[:, :, 0 : 3 * wide],
            r.z_contract.at[:, :, 0 : 3 * wide],
        ),
    )
    reduces.contract.start()
    load_grad = load(r.grad_all, r.v_grad)
    load_contract = load(r.w_contract, r.v_one)
    load_slope = load(r.slope, r.v_slope)
    load_third = load(r.third_t, r.v_left)
    load_expand = load(r.w_expand, r.v_two)
    load_own = load(r.contract_grad, r.g_contract)
    load_norm = load(r.norm_all.at[0:8], r.v_norm)
    load_crossed = load(r.crossed_t, r.v_right)
    load_two = load(r.two_rows, r.v_two_rows)
    load_incoming = load(r.incoming, r.v_rows)
    cross_query = part(r.v_joint, 0, wide)
    load_query = load(r.cross_query, cross_query)
    load_text = load(r.text_all.at[:, lanes(blk, wide)], part(r.v_text, 0, wide))
    load_values = load(r.text_all.at[:, lanes(blk + 4, wide)], part(r.v_text, wide, wide))

    def blk_sum(number, piece, near, far, size):
        return BlkSum(spot, piece, near, far, r.bsend.at[number], r.brecv.at[number], 16, size)

    load_grad.wait()
    load_contract.wait()
    load_slope.wait()

    def up_tile(block):
        r.v_up[:, block] = (dot(r.v_grad[...], r.v_one[:, block]) * r.v_slope[:, block]).astype(BF16)

    tiles(4, 384, up_tile)
    load_back = load(r.w_back, part(r.v_one, 0, wide))
    load_keys = load(r.w_keys, part(r.v_one, wide, 2 * wide))
    load_outward = load(r.w_outward, part(r.v_one, 3 * wide, wide))
    load_expand.wait()

    def back_rows(left, right):
        def body(block):
            r.v_part[:, block] = dot_t(left[...], right[block, :]).astype(BF16)

        tiles(4, 384, body)

    def back_cols(left, right):
        for core in (1 - spot.core, spot.core):
            for x in (0, 1):
                goal = x * 2 + core
                here = pl.ds(pl.multiple_of(goal * wide, 128), wide)
                mine = pl.ds(pl.multiple_of(goal * wide, wide), wide)
                r.v_part[:, here] = dot_t(left[...], right[mine, :]).astype(BF16)

    def outer(target, left, right):
        def body(block):
            target[block, :] = dot(left[block, :], right[...]).astype(BF16)

        tiles(4, 384, body)

    row_parts = row_piece(r.v_part, rows)

    def col_parts(index):
        return r.v_part.at[:, lanes(index, wide)]

    back_rows(r.v_up, r.v_two)
    third_sum = blk_sum(0, row_parts, r.near_rows, r.far_rows, rows)
    third_sum.start()
    load_third.wait()

    def expand_tile(block):
        r.g_expand[:, block] = dot(r.v_left[...], r.v_up[:, block]).astype(BF16)

    third_sum.relay()
    tiles(4, 384, expand_tile)
    reduces.expand.start()
    load_wquery = load(r.w_query, part(r.v_two, 0, wide))
    load_winward = load(r.w_inward, part(r.v_two, wide, 3 * wide))
    load_second = load(r.second_t, r.v_left)
    load_own.wait()
    reduces.contract.take(0)
    for copy in (load_norm, load_two, load_incoming):
        copy.wait()
    r.v_norm_grads[...] = jnp.zeros_like(r.v_norm_grads)
    hidden = r.v_slope.at[pl.ds(3 * rows, rows)]

    def norm_back(total, values, number, base, keep):
        gain = r.v_norm[number : number + 1, :]

        @pl.loop(0, rows // 16)
        def _(index):
            here = pl.ds(pl.multiple_of(index * 16, 16), 16)
            incoming = total.value(here)
            value = values[here, :].astype(F32)
            center = value - jnp.mean(value, axis=1, keepdims=True)
            scale = lax.rsqrt(jnp.mean(center * center, axis=1, keepdims=True) + 1e-05)
            normal = center * scale
            scaled = incoming * gain
            mean = jnp.mean(scaled, axis=1, keepdims=True)
            match = jnp.mean(scaled * normal, axis=1, keepdims=True)
            keep(here, base(here) + (scaled - mean - normal * match) * scale)
            for place, term in ((number, incoming * normal), (3 + number, incoming)):
                spread = pl.ds(place * 8, 8)
                r.v_norm_grads[spread, :] += term[0:8, :] + term[8:16, :]

    def keep_branch(here, value):
        hidden[here, :] = value
        r.v_branch[here, :] = value.astype(BF16)

    third_sum.finish()
    norm_back(
        third_sum, r.v_two_rows, 2, lambda here: r.v_rows[here, :].astype(F32), keep_branch
    )
    load_one = load(r.one_rows, r.v_rows)
    turn_two = Turn(spot, r.v_branch, r.v_turn_two, r.tsend.at[0], r.trecv.at[0])
    turn_two.start()
    reduces.contract.take(3)
    load_back.wait()
    turn_two.finish()
    third_sum.drain()
    back_cols(r.v_turn_two, part(r.v_one, 0, wide))
    crossed_sum = blk_sum(1, col_parts, r.near_cols, r.far_cols, length)
    crossed_sum.start()
    load_crossed.wait()
    crossed_sum.relay()
    outer(grads.back, r.v_right, r.v_turn_two)
    reduces.back.start()
    load_attended = load(r.attended_t, r.v_right)
    reduces.contract.take(1)
    crossed_sum.finish()
    load_query.wait()
    load_text.wait()
    load_values.wait()

    def merge(total, target):
        @pl.loop(0, length // 16)
        def _(index):
            here = pl.ds(pl.multiple_of(index * 16, 16), 16)
            target[here, :] = total.value(here).astype(BF16)

    merge(crossed_sum, r.v_head_grad)
    low = lax.broadcasted_iota(jnp.int32, (1, 128), 1) < 64

    def half(value, side):
        return jnp.where(low if side == 0 else jnp.logical_not(low), value, jnp.zeros_like(value))

    def soft(scores):
        power = jnp.exp(scores - jnp.max(scores, axis=1, keepdims=True))
        return power * (1.0 / jnp.sum(power, axis=1, keepdims=True))

    @pl.loop(0, 3)
    def _(pair):
        query = cross_query[:, lanes(pair, 128)]
        key = r.v_text[:, lanes(pair, 128)]
        value = r.v_text[:, lanes(3 + pair, 128)]
        head_grad = r.v_head_grad[:, lanes(pair, 128)]
        results = []
        for side in (0, 1):
            weights = soft(dot_t(half(query, side), key) * 0.125)
            slope = dot_t(half(head_grad, side), value)
            score = (weights * (slope - jnp.sum(slope * weights, axis=1, keepdims=True))).astype(BF16)
            results.append(
                (
                    dot(score, key) * 0.125,
                    t_dot(score, query) * 0.125,
                    t_dot(weights.astype(BF16), head_grad),
                )
            )
        merged = [jnp.where(low, *item).astype(BF16) for item in zip(*results)]
        r.v_query_grad[:, lanes(pair, 128)] = merged[0]
        r.v_terms[0:TEXT, lanes(blk * 3 + pair, 128)] = merged[1]
        r.v_terms[TEXT : 2 * TEXT, lanes(blk * 3 + pair, 128)] = merged[2]

    load_joint = load(r.joint, r.v_joint)
    own_terms = r.v_terms.at[:, lanes(blk, wide)]
    terms_share = Share(
        spot, own_terms, lambda index: r.v_terms.at[:, lanes(index, wide)], r.csend.at[0], r.crecv.at[0]
    )
    terms_share.start()
    load_wquery.wait()
    crossed_sum.drain()
    back_rows(r.v_query_grad, part(r.v_two, 0, wide))
    second_sum = blk_sum(2, row_parts, r.near_rows, r.far_rows, rows)
    second_sum.start()
    load_second.wait()
    second_sum.relay()
    outer(grads.query, r.v_left, r.v_query_grad)
    load_first = load(r.first_t, r.v_left)
    reduces.query.start()
    reduces.back.combine(1)
    reduces.back.combine(0)
    reduces.contract.combine()
    reduces.contract.take(2)
    pl.semaphore_signal(r.credit.at[0], inc=1, device_id=spot.part, device_id_type=MESH)
    terms_share.relay()
    load_one.wait()
    second_sum.finish()
    norm_back(second_sum, r.v_rows, 1, lambda here: hidden[here, :], keep_branch_after(turn_two, keep_branch))
    load_frames = load(r.frames, r.v_rows)
    turn_one = Turn(spot, r.v_branch, r.v_turn_one, r.tsend.at[1], r.trecv.at[1])
    turn_one.start()
    terms_share.finish()
    load_keys.wait()
    own_rows = pl.ds(pl.multiple_of((blk // 2) * TEXT, TEXT), TEXT)
    terms = r.v_terms[own_rows, lanes(lax.rem(blk, 2), 2 * wide)]

    def keys_tile(block):
        product = t_dot(r.text[:, block], r.v_terms[own_rows, lanes(lax.rem(blk, 2), 2 * wide)])
        grads.keys[block, :] = product.astype(BF16)

    tiles(6, 256, keys_tile)
    reduces.keys.start()
    turn_one.finish()
    second_sum.drain()
    load_outward.wait()
    back_cols(r.v_turn_one, part(r.v_one, 3 * wide, wide))
    attended_sum = blk_sum(3, col_parts, r.near_cols, r.far_cols, length)
    attended_sum.start()
    load_attended.wait()
    attended_sum.relay()
    outer(grads.outward, r.v_right, r.v_turn_one)
    reduces.outward.start()
    r.v_text_part[...] = dot_t(terms, r.v_one[:, wide : 3 * wide]).astype(BF16)
    text_rows = TEXT // 4
    text_sum = blk_sum(4, row_piece(r.v_text_part, text_rows), r.near_text, r.far_text, text_rows)
    text_sum.start()
    text_sum.relay()
    reduces.expand.take(0)
    load_joint.wait()
    attended_sum.finish()
    merge(attended_sum, r.v_head_grad)

    @pl.loop(0, 3)
    def _(pair):
        r.v_key_sum[...] = jnp.zeros_like(r.v_key_sum)
        r.v_value_sum[...] = jnp.zeros_like(r.v_value_sum)

        @pl.loop(0, 4)
        def _(block):
            here = pl.ds(pl.multiple_of(block * 128, 128), 128)
            query = r.v_joint[here, lanes(pair, 128)]
            key = r.v_joint[:, lanes(pair + 3, 128)]
            value = r.v_joint[:, lanes(pair + 6, 128)]
            head_grad = r.v_head_grad[here, lanes(pair, 128)]
            keep = r.ids_row[...] <= r.ids_col[here, :]
            results = []
            for side in (0, 1):
                weights = soft(jnp.where(keep, dot_t(half(query, side), key) * 0.125, -1e30))
                slope = dot_t(half(head_grad, side), value)
                score = (weights * (slope - jnp.sum(slope * weights, axis=1, keepdims=True))).astype(BF16)
                results.append(
                    (dot(score, key), t_dot(score, query), t_dot(weights.astype(BF16), head_grad))
                )
            merged = [jnp.where(low, *item) for item in zip(*results)]
            r.v_up[here, lanes(pair, 128)] = (merged[0] * 0.125).astype(BF16)
            r.v_key_sum[...] += merged[1]
            r.v_value_sum[...] += merged[2]

        r.v_up[:, lanes(pair + 3, 128)] = (r.v_key_sum[...] * 0.125).astype(BF16)
        r.v_up[:, lanes(pair + 6, 128)] = r.v_value_sum[...].astype(BF16)

    stores = []

    def store(item, goal):
        size = goal.shape[1]
        slot = len(stores) % 2
        if len(stores) >= 2:
            stores[-2].wait()
        stage = r.v_slope.at[pl.ds(slot * 192, 192), pl.ds(0, size)]

        def keep(here, value):
            stage[here, :] = value

        item.finish(keep)
        copy = pltpu.make_async_copy(stage, goal, r.stored.at[len(stores)])
        copy.start()
        stores.append(copy)

    reduces.back.cross()
    reduces.keys.combine(1)
    reduces.keys.combine(0)
    store(reduces.contract, r.contract_out)
    for k in (1, 2, 3):
        pl.semaphore_signal(r.credit.at[1], inc=1, device_id=spot.z_peer(k), device_id_type=MESH)
    reduces.contract.drain()
    attended_sum.drain()
    load_winward.wait()
    load_first.wait()
    joint_grad = part(r.v_up, 0, 3 * wide)
    back_rows(joint_grad, part(r.v_two, wide, 3 * wide))
    first_sum = blk_sum(5, row_parts, r.near_rows, r.far_rows, rows)
    first_sum.start()

    def inward_tile(block):
        grads.inward[:, block] = dot(r.v_left[...], r.v_up[:, block]).astype(BF16)

    tiles(3, 384, inward_tile)
    pl.semaphore_wait(r.credit.at[0], 1)
    reduces.inward.start()
    first_sum.relay()
    load_again = load(r.w_contract, r.v_one)
    load_active = load(r.active, r.v_grad)
    reduces.expand.take(3)
    reduces.expand.take(1)
    reduces.expand.combine()
    reduces.expand.take(2)
    load_frames.wait()
    first_sum.finish()

    def keep_frames(here, value):
        hidden[here, :] = value

    norm_back(first_sum, r.v_rows, 0, lambda here: hidden[here, :], keep_frames)
    for who in (spot.sib, spot.opp):
        pl.semaphore_signal(r.credit.at[2], inc=1, device_id=who, device_id_type=MESH)
    frames_copy = pltpu.make_async_copy(hidden, r.frames_out, r.stored.at[8])
    frames_copy.start()

    for place in range(6):
        r.v_norm_sum[place : place + 1, :] = jnp.sum(
            r.v_norm_grads[place * 8 : place * 8 + 8, :], axis=0, keepdims=True
        )
    r.v_norm_sum[6:8, :] = jnp.zeros((2, width), F32)

    def norm_hop(number, who):
        return push(r.v_norm_sum, r.v_norm_in.at[number], r.nsend.at[number], r.nrecv.at[number], who)

    norm_hop(0, spot.sib).start()
    text_sum.finish()
    r.v_text_out[...] = text_sum.value(pl.ds(0, text_rows))
    text_copy = pltpu.make_async_copy(r.v_text_out, r.text_out, r.stored.at[9])
    text_copy.start()
    reduces.query.take(0)
    reduces.query.take(3)
    reduces.query.take(1)
    reduces.query.take(2)

    def norm_step(number, who):
        norm_hop(number, who).wait()
        r.v_norm_sum[...] += r.v_norm_in[number]

    norm_step(0, spot.sib)
    norm_hop(1, spot.opp).start()
    load_again.wait()
    load_active.wait()
    first_sum.drain()
    back_rows(r.v_grad, r.v_one)
    out_sum = blk_sum(6, row_parts, r.near_rows, r.far_rows, rows)
    pl.semaphore_wait(r.credit.at[2], 2)
    out_sum.start()
    norm_step(1, spot.opp)
    norm_hop(2, spot.part).start()
    reduces.query.combine()
    for goal in (0, 3, 1, 2):
        reduces.outward.take(goal)
    out_sum.relay()
    reduces.keys.cross()
    norm_step(2, spot.part)
    for k in (1, 2, 3):
        norm_hop(2 + k, spot.z_peer(k)).start()
    reduces.outward.combine()
    pl.semaphore_wait(r.credit.at[1], 3)
    for goal in (0, 3):
        reduces.inward.take(goal)
    out_sum.finish()
    turn_one.drain()

    @pl.loop(0, rows // 16)
    def _(index):
        here = pl.ds(pl.multiple_of(index * 16, 16), 16)
        r.v_branch[here, :] = (out_sum.value(here) + r.v_two_rows[here, :].astype(F32)).astype(BF16)

    block_copy = pltpu.make_async_copy(r.v_branch, r.block_out, r.stored.at[10])
    block_copy.start()
    store(reduces.expand, r.expand_out)
    store(reduces.back, r.returning_out)
    reduces.inward.take(1)
    reduces.inward.take(2)
    reduces.inward.combine()
    store(reduces.query, r.querying_out)
    store(reduces.outward, r.outward_out)
    store(reduces.keys, r.keying_out)
    for k in (1, 2, 3):
        norm_hop(2 + k, spot.z_peer(k)).wait()
    r.v_norm_sum[...] += r.v_norm_in[3] + r.v_norm_in[4] + r.v_norm_in[5]
    norm_copy = pltpu.make_async_copy(r.v_norm_sum, r.norm_out, r.stored.at[11])
    norm_copy.start()

    out_sum.drain()
    inward_sum = r.v_part.at[pl.ds(0, 192), pl.ds(0, 3 * wide)]

    def keep_inward(here, value):
        inward_sum[here, :] = value.astype(BF16)

    reduces.inward.finish(keep_inward)

    def inward_copy(kind):
        index = kind * 4 + blk
        owner, place = index // 3, lax.rem(index, 3)
        src = inward_sum.at[:, kind * wide : (kind + 1) * wide]
        return owner, place, src, r.v_inward_in.at[:, lanes(place, wide)]

    for kind in range(3):
        owner, place, src, dst = inward_copy(kind)

        @pl.when(owner == blk)
        def _():
            pltpu.make_async_copy(src, dst, r.arecv.at[place]).start()

        @pl.when(owner != blk)
        def _():
            push(src, dst, r.asend.at[kind], r.arecv.at[place], (spot.grp, owner)).start()

    for place in range(3):
        dst = r.v_inward_in.at[:, place * wide : (place + 1) * wide]
        home = lax.rem(blk * 3 + place, 4)

        @pl.when(home == blk)
        def _():
            pltpu.make_async_copy(dst, dst, r.arecv.at[place]).wait()

        @pl.when(home != blk)
        def _():
            push(dst, dst, r.asend.at[0], r.arecv.at[place], spot.sib).wait_recv()

    for copy in stores[-2:]:
        copy.wait()
    final = r.v_slope.at[pl.ds(0, 192), pl.ds(0, 3 * wide)]

    @pl.loop(0, 192 // 16)
    def _(index):
        here = pl.ds(pl.multiple_of(index * 16, 16), 16)
        final[here, :] = r.v_inward_in[here, :].astype(F32)

    inward_done = pltpu.make_async_copy(final, r.inward_out, r.stored.at[12])
    inward_done.start()
    for kind in range(3):
        owner, place, src, dst = inward_copy(kind)

        @pl.when(owner != blk)
        def _():
            push(src, dst, r.asend.at[kind], r.arecv.at[place], (spot.grp, owner)).wait_send()

    for item in vars(reduces).values():
        if item is not reduces.contract:
            item.drain()
    terms_share.drain()
    text_sum.drain()
    for copy in (frames_copy, text_copy, block_copy, norm_copy, inward_done):
        copy.wait()


def keep_branch_after(turn, keep):
    turn.drain()
    return keep


def backward(ahead, frames, text, table, incoming):
    rows, width = frames.shape
    length = rows * lax.axis_size("blk")
    wide = width // lax.axis_size("blk")
    shard = width // lax.axis_size("grp")
    feed = ahead.w_expand.shape[1]
    ids_col, ids_row = ids_of(table)
    out = dict(
        contract_out=((shard, feed), F32),
        expand_out=((shard, feed), F32),
        returning_out=((shard, wide), F32),
        keying_out=((shard, 2 * wide), F32),
        querying_out=((shard, wide), F32),
        outward_out=((shard, wide), F32),
        inward_out=((shard, 3 * wide), F32),
        frames_out=((rows, width), F32),
        block_out=((rows, width), BF16),
        text_out=((TEXT // 4, width), F32),
        norm_out=((8, width), F32),
    )
    square, turned, strip = (length, width), (width, length), (length, wide)
    vmem = dict(
        v_one=((width, feed), BF16),
        v_two=((width, feed), BF16),
        g_contract=((width, feed), BF16),
        g_expand=((width, feed), BF16),
        g_rest=((width, 5 * wide), BF16),
        v_left=(turned, BF16),
        v_right=(turned, BF16),
        v_grad=(square, BF16),
        v_up=(square, BF16),
        v_part=(square, BF16),
        v_slope=(square, F32),
        v_joint=((length, 3 * wide), BF16),
        v_query_grad=(strip, BF16),
        v_head_grad=(strip, BF16),
        v_turn_one=(strip, BF16),
        v_turn_two=(strip, BF16),
        v_text=((TEXT, 2 * wide), BF16),
        v_terms=((2 * TEXT, width), BF16),
        v_text_part=((TEXT, width), BF16),
        v_text_out=((TEXT // 4, width), F32),
        near_rows=((2, rows, width), BF16),
        far_rows=((rows, width), BF16),
        near_cols=((2, length, wide), BF16),
        far_cols=(strip, BF16),
        near_text=((2, TEXT // 4, width), BF16),
        far_text=((TEXT // 4, width), BF16),
        v_branch=((rows, width), BF16),
        v_rows=((rows, width), BF16),
        v_two_rows=((rows, width), BF16),
        v_norm=((8, width), F32),
        v_norm_grads=((48, width), F32),
        v_norm_sum=((8, width), F32),
        v_norm_in=((6, 8, width), F32),
        v_key_sum=((length, 128), F32),
        v_value_sum=((length, 128), F32),
        v_inward_in=((shard, 3 * wide), BF16),
    )
    vmem.update(
        y_contract=((4, shard, feed), BF16),
        y_expand=((4, shard, feed), BF16),
        y_back=((1, shard, wide), BF16),
        y_keys=((1, shard, 2 * wide), BF16),
        y_query=((4, shard, wide), BF16),
        y_outward=((4, shard, wide), BF16),
        z_contract=((4, shard, feed), BF16),
        z_expand=((4, shard, feed), BF16),
        z_back=((8, shard, wide), BF16),
        z_keys=((8, shard, 2 * wide), BF16),
        z_query=((4, shard, wide), BF16),
        z_outward=((4, shard, wide), BF16),
    )
    sems = dict(
        ysend=(7, 4),
        yrecv=(7, 4),
        zsend=(7, 8),
        zrecv=(7, 8),
        bsend=(7, 3),
        brecv=(7, 3),
        tsend=(2, 3),
        trecv=(2, 3),
        csend=(1, 3),
        crecv=(1, 3),
        nsend=(6,),
        nrecv=(6,),
        asend=(3,),
        arecv=(3,),
        local=(32,),
        stored=(16,),
    )
    inner = dict(text=text, ids_col=ids_col, ids_row=ids_row)
    outer = dict(frames=frames, incoming=incoming, **vars(ahead))
    del outer["aligned"]
    return run_kernel(backward_kernel, 2, inner, outer, out, vmem, sems, dict(credit=(3,)))


def tp_shards(
    frames,
    text_states,
    block_table,
    inward,
    outward,
    querying,
    keying,
    returning,
    expand,
    contract,
    gains,
    shifts,
    out_grad,
):
    ahead = forward(
        frames[0],
        text_states[0],
        block_table,
        jnp.pad(jnp.concatenate([gains, shifts], axis=0), ((0, 10), (0, 80))),
        out_grad[0],
        dict(
            inward=inward,
            outward=outward,
            query=querying,
            keys=keying,
            back=returning,
            expand=expand,
            contract=contract.T,
        ),
    )
    done = backward(ahead, frames[0], text_states[0], block_table, out_grad[0])
    share = gains.shape[1]
    place = (lax.axis_index("grp") * lax.axis_size("blk") + lax.axis_index("blk")) * share
    norm_grads = lax.dynamic_slice_in_dim(done.norm_out, place, share, 1)
    return (
        done.block_out[None],
        done.frames_out[None],
        done.text_out[None],
        done.inward_out,
        done.outward_out,
        done.querying_out,
        done.keying_out,
        done.returning_out,
        done.expand_out,
        done.contract_out.T,
        norm_grads[:3],
        norm_grads[3:6],
    )


def solution(mesh):
    small = mesh.shape["grp"] == 8 and mesh.shape["blk"] == 4
    return jax.shard_map(
        tp_shards if small else shards,
        mesh=mesh,
        in_specs=(
            P("grp", "blk", None),
            P("grp", None, None),
            P("grp", None),
            P("grp", "blk"),
            P("grp", "blk"),
            P("grp", "blk"),
            P("grp", "blk"),
            P("grp", "blk"),
            P("grp", "blk"),
            P("blk", "grp"),
            P(None, ("grp", "blk")),
            P(None, ("grp", "blk")),
            P("grp", "blk", None),
        ),
        out_specs=(
            P("grp", "blk", None),
            P("grp", "blk", None),
            P("grp", "blk", None),
            P("grp", "blk"),
            P("grp", "blk"),
            P("grp", "blk"),
            P("grp", "blk"),
            P("grp", "blk"),
            P("grp", "blk"),
            P("blk", "grp"),
            P(None, ("grp", "blk")),
            P(None, ("grp", "blk")),
        ),
        check_vma=False,
    )
```

```python
import functools
import math

import jax
import jax.numpy as jnp
from jax import lax
from jax.experimental import pallas as pl
from jax.experimental.pallas import tpu as pltpu
from jax.sharding import PartitionSpec as P

HEADS = 24
HEAD = 64
TEXT = 64
SEG = 64


def layer_norm(values, gain, shift):
    center = values - jnp.mean(values, axis=-1, keepdims=True)
    spread = jnp.mean(center * center, axis=-1, keepdims=True)
    return center * lax.rsqrt(spread + 1e-05) * gain + shift


def norm_pull(values, gain, shift, incoming):
    unused, pullback = jax.vjp(layer_norm, values, gain, shift)
    return pullback(incoming)


def gelu_slope(upward):
    return (
        0.5 * (1.0 + lax.erf(upward * 0.7071067811865476))
        + upward * jnp.exp(-0.5 * upward * upward) * 0.3989422804014327
    )


def gather_weights(inward, outward, querying, keying, returning, expand, contract, gains, shifts):
    inward, outward, querying, keying, returning, expand, contract, gains, shifts = (
        lax.all_gather(inward, "blk", axis=1, tiled=True),
        lax.all_gather(outward, "blk", axis=1, tiled=True),
        lax.all_gather(querying, "blk", axis=1, tiled=True),
        lax.all_gather(keying, "blk", axis=1, tiled=True),
        lax.all_gather(returning, "blk", axis=1, tiled=True),
        lax.all_gather(expand, "blk", axis=1, tiled=True),
        lax.all_gather(contract, "blk", axis=0, tiled=True),
        lax.all_gather(gains, "blk", axis=1, tiled=True),
        lax.all_gather(shifts, "blk", axis=1, tiled=True),
    )
    return (
        lax.all_gather(inward, "grp", axis=0, tiled=True),
        lax.all_gather(outward, "grp", axis=0, tiled=True),
        lax.all_gather(querying, "grp", axis=0, tiled=True),
        lax.all_gather(keying, "grp", axis=0, tiled=True),
        lax.all_gather(returning, "grp", axis=0, tiled=True),
        lax.all_gather(expand, "grp", axis=0, tiled=True),
        lax.all_gather(contract, "grp", axis=1, tiled=True),
        lax.all_gather(gains, "grp", axis=1, tiled=True),
        lax.all_gather(shifts, "grp", axis=1, tiled=True),
    )


def shards(
    frames,
    text_states,
    block_table,
    inward,
    outward,
    querying,
    keying,
    returning,
    expand,
    contract,
    gains,
    shifts,
    out_grad,
):
    (
        full_inward,
        full_outward,
        full_query,
        full_keys,
        full_return,
        full_expand,
        full_contract,
        full_gains,
        full_shifts,
    ) = gather_weights(
        inward, outward, querying, keying, returning, expand, contract, gains, shifts
    )
    width = frames.shape[2]
    rows = frames.shape[1]
    length = block_table.shape[1] * SEG
    group = lax.axis_size("blk")
    member = lax.axis_index("blk")
    span = math.gcd(length, 512)
    steps = length // span
    gain_rows = full_gains.astype(jnp.float32)
    shift_rows = full_shifts.astype(jnp.float32)
    key_frames = (
        block_table[0][:, None] * SEG + jnp.arange(SEG, dtype=jnp.int32)[None, :]
    ).reshape(length)
    own_frames = lax.dynamic_slice_in_dim(key_frames, member * rows, rows, 0)
    inputs = frames[0].astype(jnp.float32)
    first = layer_norm(inputs, gain_rows[0], shift_rows[0]).astype(jnp.bfloat16)
    joint = jnp.dot(first, full_inward, preferred_element_type=jnp.float32).astype(jnp.bfloat16)
    queries = joint[:, :width].reshape(rows, HEADS, HEAD)
    pairs = lax.all_gather(joint[:, width:], "blk", axis=0, tiled=True)
    pair_blocks = pairs.reshape(steps, span, 2 * width)
    frame_blocks = key_frames.reshape(steps, span)

    def scores_of(block, block_frames):
        keys = block[:, :width].reshape(span, HEADS, HEAD)
        raw = jnp.einsum("qhd,khd->hqk", queries, keys, preferred_element_type=jnp.float32) * 0.125
        allowed = block_frames[None, :] <= own_frames[:, None]
        return jnp.where(allowed[None], raw, -1e30)

    def stat_step(carry, items):
        peak, total = carry
        scores = scores_of(items[0], items[1])
        higher = jnp.maximum(peak, jnp.max(scores, axis=2))
        total = total * jnp.exp(peak - higher) + jnp.sum(
            jnp.exp(scores - higher[:, :, None]), axis=2
        )
        return ((higher, total), None)

    start_peak = jnp.full((HEADS, rows), -1e30, jnp.float32)
    (peak, total), unused = lax.scan(
        stat_step, (start_peak, jnp.zeros((HEADS, rows), jnp.float32)), (pair_blocks, frame_blocks)
    )
    log_total = peak + jnp.log(total)

    def out_step(carry, items):
        weighting = jnp.exp(scores_of(items[0], items[1]) - log_total[:, :, None]).astype(
            jnp.bfloat16
        )
        values = items[0][:, width:].reshape(span, HEADS, HEAD)
        return (
            carry
            + jnp.einsum("hqk,khd->qhd", weighting, values, preferred_element_type=jnp.float32),
            None,
        )

    mixed, unused = lax.scan(
        out_step, jnp.zeros((rows, HEADS, HEAD), jnp.float32), (pair_blocks, frame_blocks)
    )
    attended = mixed.reshape(rows, width).astype(jnp.bfloat16)
    hidden_one = inputs + jnp.dot(attended, full_outward, preferred_element_type=jnp.float32)
    second = layer_norm(hidden_one, gain_rows[1], shift_rows[1]).astype(jnp.bfloat16)
    cross_query = jnp.dot(second, full_query, preferred_element_type=jnp.float32).astype(
        jnp.bfloat16
    )
    cross_heads = cross_query.reshape(rows, HEADS, HEAD)
    text = text_states[0]
    text_pairs = jnp.dot(text, full_keys, preferred_element_type=jnp.float32).astype(jnp.bfloat16)
    text_keys = text_pairs[:, :width].reshape(TEXT, HEADS, HEAD)
    text_values = text_pairs[:, width:].reshape(TEXT, HEADS, HEAD)
    cross_scores = (
        jnp.einsum("qhd,khd->hqk", cross_heads, text_keys, preferred_element_type=jnp.float32)
        * 0.125
    )
    cross_soft = jax.nn.softmax(cross_scores, axis=2)
    cross_weighting = cross_soft.astype(jnp.bfloat16)
    crossed = (
        jnp.einsum("hqk,khd->qhd", cross_weighting, text_values, preferred_element_type=jnp.float32)
        .reshape(rows, width)
        .astype(jnp.bfloat16)
    )
    hidden_two = hidden_one + jnp.dot(crossed, full_return, preferred_element_type=jnp.float32)
    third = layer_norm(hidden_two, gain_rows[2], shift_rows[2]).astype(jnp.bfloat16)
    upward = jnp.dot(third, full_expand, preferred_element_type=jnp.float32)
    activated = jax.nn.gelu(upward, approximate=False).astype(jnp.bfloat16)
    branch = jnp.dot(activated, full_contract, preferred_element_type=jnp.float32)
    block_out = (hidden_two + branch).astype(jnp.bfloat16)[None]
    (
        full_inward,
        full_outward,
        full_query,
        full_keys,
        full_return,
        full_expand,
        full_contract,
        full_gains,
        full_shifts,
    ) = gather_weights(
        inward, outward, querying, keying, returning, expand, contract, gains, shifts
    )
    incoming = out_grad[0].astype(jnp.float32)
    branch_grad = out_grad[0]
    act_grad = jnp.dot(branch_grad, full_contract.T, preferred_element_type=jnp.float32)
    contract_grad = jnp.dot(activated.T, branch_grad, preferred_element_type=jnp.float32)
    up_grad = (act_grad * gelu_slope(upward)).astype(jnp.bfloat16)
    expand_grad = jnp.dot(third.T, up_grad, preferred_element_type=jnp.float32)
    third_grad = jnp.dot(up_grad, full_expand.T, preferred_element_type=jnp.float32)
    two_grad, gain_two, shift_two = norm_pull(hidden_two, gain_rows[2], shift_rows[2], third_grad)
    hidden_two_grad = incoming + two_grad
    branch_two = hidden_two_grad.astype(jnp.bfloat16)
    crossed_grad = jnp.dot(branch_two, full_return.T, preferred_element_type=jnp.float32).astype(
        jnp.bfloat16
    )
    crossed_grad = crossed_grad.reshape(rows, HEADS, HEAD)
    prob_grad = jnp.einsum(
        "qhd,khd->hqk", crossed_grad, text_values, preferred_element_type=jnp.float32
    )
    text_value_grad = jnp.einsum(
        "hqk,qhd->khd", cross_weighting, crossed_grad, preferred_element_type=jnp.float32
    )
    cross_score_grad = (
        cross_soft * (prob_grad - jnp.sum(prob_grad * cross_soft, axis=2, keepdims=True))
    ).astype(jnp.bfloat16)
    cross_query_grad = (
        (
            jnp.einsum(
                "hqk,khd->qhd", cross_score_grad, text_keys, preferred_element_type=jnp.float32
            )
            * 0.125
        )
        .reshape(rows, width)
        .astype(jnp.bfloat16)
    )
    text_key_grad = (
        jnp.einsum(
            "hqk,qhd->khd", cross_score_grad, cross_heads, preferred_element_type=jnp.float32
        )
        * 0.125
    )
    text_terms = jnp.concatenate(
        [text_key_grad.reshape(TEXT, width), text_value_grad.reshape(TEXT, width)], axis=1
    )
    text_share = lax.psum_scatter(
        text_terms.astype(jnp.bfloat16), "blk", scatter_dimension=0, tiled=True
    )
    share = TEXT // group
    text_grad = jnp.dot(text_share, full_keys.T, preferred_element_type=jnp.float32)[None]
    one_grad, gain_one, shift_one = norm_pull(
        hidden_one,
        gain_rows[1],
        shift_rows[1],
        jnp.dot(cross_query_grad, full_query.T, preferred_element_type=jnp.float32),
    )
    hidden_one_grad = hidden_two_grad + one_grad
    branch_one = hidden_one_grad.astype(jnp.bfloat16)
    attended_grad = jnp.dot(branch_one, full_outward.T, preferred_element_type=jnp.float32).astype(
        jnp.bfloat16
    )
    attended_grad = attended_grad.reshape(rows, HEADS, HEAD)
    delta = jnp.sum(attended_grad.astype(jnp.float32) * mixed, axis=2).T

    def back_step(carry, items):
        block = items[0]
        weighting = jnp.exp(scores_of(block, items[1]) - log_total[:, :, None])
        keys = block[:, :width].reshape(span, HEADS, HEAD)
        values = block[:, width:].reshape(span, HEADS, HEAD)
        value_grad = jnp.einsum(
            "hqk,qhd->khd",
            weighting.astype(jnp.bfloat16),
            attended_grad,
            preferred_element_type=jnp.float32,
        )
        weight_grad = jnp.einsum(
            "qhd,khd->hqk", attended_grad, values, preferred_element_type=jnp.float32
        )
        score_grad = (weighting * (weight_grad - delta[:, :, None])).astype(jnp.bfloat16)
        carry = carry + jnp.einsum(
            "hqk,khd->qhd", score_grad, keys, preferred_element_type=jnp.float32
        )
        key_grad = (
            jnp.einsum("hqk,qhd->khd", score_grad, queries, preferred_element_type=jnp.float32)
            * 0.125
        )
        return (
            carry,
            jnp.concatenate(
                [key_grad.reshape(span, width), value_grad.reshape(span, width)], axis=1
            ),
        )

    query_sum, pair_terms = lax.scan(
        back_step, jnp.zeros((rows, HEADS, HEAD), jnp.float32), (pair_blocks, frame_blocks)
    )
    pair_grad = lax.psum_scatter(
        pair_terms.reshape(length, 2 * width).astype(jnp.bfloat16),
        "blk",
        scatter_dimension=0,
        tiled=True,
    )
    joint_grad = jnp.concatenate(
        [(query_sum * 0.125).reshape(rows, width).astype(jnp.bfloat16), pair_grad], axis=1
    )
    zero_grad, gain_zero, shift_zero = norm_pull(
        inputs,
        gain_rows[0],
        shift_rows[0],
        jnp.dot(joint_grad, full_inward.T, preferred_element_type=jnp.float32),
    )
    frames_grad = (hidden_one_grad + zero_grad)[None]
    across = lax.axis_size("grp")
    gains_grad = (
        jnp.stack([gain_zero, gain_one, gain_two])
        .reshape(3, across, group, -1)
        .transpose(0, 2, 1, 3)
        .reshape(3, width)
    )
    shifts_grad = (
        jnp.stack([shift_zero, shift_one, shift_two])
        .reshape(3, across, group, -1)
        .transpose(0, 2, 1, 3)
        .reshape(3, width)
    )
    expand_grad, contract_grad = (
        lax.psum_scatter(
            expand_grad.astype(jnp.bfloat16), "blk", scatter_dimension=1, tiled=True
        ).astype(jnp.float32),
        lax.psum_scatter(
            contract_grad.astype(jnp.bfloat16), "blk", scatter_dimension=0, tiled=True
        ).astype(jnp.float32),
    )
    own_text = lax.dynamic_slice_in_dim(text, member * share, share, 0)
    inward_grad = jnp.dot(first.T, joint_grad, preferred_element_type=jnp.float32)
    outward_grad = jnp.dot(attended.T, branch_one, preferred_element_type=jnp.float32)
    querying_grad = jnp.dot(second.T, cross_query_grad, preferred_element_type=jnp.float32)
    keying_grad = jnp.dot(own_text.T, text_share, preferred_element_type=jnp.float32)
    returning_grad = jnp.dot(crossed.T, branch_two, preferred_element_type=jnp.float32)
    (
        inward_grad,
        outward_grad,
        querying_grad,
        keying_grad,
        returning_grad,
        gains_grad,
        shifts_grad,
    ) = (
        lax.psum_scatter(
            inward_grad.astype(jnp.bfloat16), "blk", scatter_dimension=1, tiled=True
        ).astype(jnp.float32),
        lax.psum_scatter(
            outward_grad.astype(jnp.bfloat16), "blk", scatter_dimension=1, tiled=True
        ).astype(jnp.float32),
        lax.psum_scatter(
            querying_grad.astype(jnp.bfloat16), "blk", scatter_dimension=1, tiled=True
        ).astype(jnp.float32),
        lax.psum_scatter(
            keying_grad.astype(jnp.bfloat16), "blk", scatter_dimension=1, tiled=True
        ).astype(jnp.float32),
        lax.psum_scatter(
            returning_grad.astype(jnp.bfloat16), "blk", scatter_dimension=1, tiled=True
        ).astype(jnp.float32),
        lax.psum_scatter(
            gains_grad.astype(jnp.bfloat16), "blk", scatter_dimension=1, tiled=True
        ).astype(jnp.float32),
        lax.psum_scatter(
            shifts_grad.astype(jnp.bfloat16), "blk", scatter_dimension=1, tiled=True
        ).astype(jnp.float32),
    )
    (
        inward_grad,
        outward_grad,
        querying_grad,
        keying_grad,
        returning_grad,
        expand_grad,
        contract_grad,
        gains_grad,
        shifts_grad,
    ) = (
        lax.psum_scatter(
            inward_grad.astype(jnp.bfloat16), "grp", scatter_dimension=0, tiled=True
        ).astype(jnp.float32),
        lax.psum_scatter(
            outward_grad.astype(jnp.bfloat16), "grp", scatter_dimension=0, tiled=True
        ).astype(jnp.float32),
        lax.psum_scatter(
            querying_grad.astype(jnp.bfloat16), "grp", scatter_dimension=0, tiled=True
        ).astype(jnp.float32),
        lax.psum_scatter(
            keying_grad.astype(jnp.bfloat16), "grp", scatter_dimension=0, tiled=True
        ).astype(jnp.float32),
        lax.psum_scatter(
            returning_grad.astype(jnp.bfloat16), "grp", scatter_dimension=0, tiled=True
        ).astype(jnp.float32),
        lax.psum_scatter(
            expand_grad.astype(jnp.bfloat16), "grp", scatter_dimension=0, tiled=True
        ).astype(jnp.float32),
        lax.psum_scatter(
            contract_grad.astype(jnp.bfloat16), "grp", scatter_dimension=1, tiled=True
        ).astype(jnp.float32),
        lax.psum_scatter(
            gains_grad.astype(jnp.bfloat16), "grp", scatter_dimension=1, tiled=True
        ).astype(jnp.float32),
        lax.psum_scatter(
            shifts_grad.astype(jnp.bfloat16), "grp", scatter_dimension=1, tiled=True
        ).astype(jnp.float32),
    )
    return (
        block_out,
        frames_grad,
        text_grad,
        inward_grad,
        outward_grad,
        querying_grad,
        keying_grad,
        returning_grad,
        expand_grad,
        contract_grad,
        gains_grad,
        shifts_grad,
    )


MESH = pl.DeviceIdType.MESH
BF16, F32 = jnp.bfloat16, jnp.float32


class Bag:
    def __init__(self, **items):
        self.__dict__.update(items)


def named(keys, items):
    return Bag(**dict(zip(keys, items)))


class Spot:
    def __init__(self):
        grp, blk = lax.axis_index("grp"), lax.axis_index("blk")
        self.grp, self.blk = grp, blk
        self.z, self.y = grp // 2, lax.rem(grp, 2)
        self.x, self.core = blk // 2, lax.rem(blk, 2)
        self.sib_blk = self.x * 2 + 1 - self.core
        self.opp_blk = (1 - self.x) * 2 + self.core
        self.sib = (grp, self.sib_blk)
        self.opp = (grp, self.opp_blk)
        self.part = (self.z * 2 + 1 - self.y, blk)
        self.up = ((self.z + 1) * 2 + self.y, blk)
        self.down = ((self.z - 1) * 2 + self.y, blk)

        self.far_blk = (1 - self.x) * 2 + 1 - self.core

    def z_peer(self, k):
        return (lax.rem(self.z + k, 4) * 2 + self.y, self.blk)

    def greet_all(self):
        barrier = pltpu.get_barrier_semaphore()
        peers = [self.z_peer(k) for k in (1, 2, 3)]
        for who in [self.sib, self.opp, (self.grp, self.far_blk), self.part] + peers:
            pl.semaphore_signal(barrier, inc=1, device_id=who, device_id_type=MESH)
        pl.semaphore_wait(barrier, 7)

    def greet(self):
        barrier = pltpu.get_barrier_semaphore()
        for who in (self.sib, self.opp, self.part):
            pl.semaphore_signal(barrier, inc=1, device_id=who, device_id_type=MESH)

        @pl.when(self.z > 0)
        def _():
            pl.semaphore_signal(barrier, inc=1, device_id=self.down, device_id_type=MESH)

        @pl.when(self.z < 3)
        def _():
            pl.semaphore_signal(barrier, inc=1, device_id=self.up, device_id_type=MESH)

        ends = (self.z == 0) | (self.z == 3)

        @pl.when(ends)
        def _():
            pl.semaphore_wait(barrier, 4)

        @pl.when(jnp.logical_not(ends))
        def _():
            pl.semaphore_wait(barrier, 5)


def push(src, dst, send, recv, who):
    return pltpu.make_async_remote_copy(
        src_ref=src, dst_ref=dst, send_sem=send, recv_sem=recv, device_id=who, device_id_type=MESH
    )


class Gather:
    def __init__(self, spot, shard, full, zsend, zrecv, ysend, yrecv, near, spread):
        self.spot, self.shard, self.full = spot, shard, full
        self.zsend, self.zrecv, self.ysend, self.yrecv, self.near = zsend, zrecv, ysend, yrecv, near
        self.spread = spread
        self.size = shard.shape[0]

    def rows(self, z, flip=0):
        spot = self.spot
        row = z * 2 + (1 - spot.y if flip else spot.y)
        return self.full.at[pl.ds(pl.multiple_of(row * self.size, self.size), self.size)]

    def z_copy(self, src, dst, k, side, flip):
        slot = (flip * 2 + side) * 3 + k - 1
        who = self.spot.up if side else self.spot.down
        return push(src, dst, self.zsend.at[slot], self.zrecv.at[slot], who)

    def y_copy(self, src, dst, slot):
        return push(src, dst, self.ysend.at[slot], self.yrecv.at[slot], self.spot.part)

    def launch(self, src, flip):
        spot = self.spot

        @pl.when(spot.z > 0)
        def _():
            self.z_copy(src, self.rows(spot.z, flip), 1, 0, flip).start()

        @pl.when(spot.z < 3)
        def _():
            self.z_copy(src, self.rows(spot.z, flip), 1, 1, flip).start()

    def start(self):
        here = self.rows(self.spot.z)
        self.y_copy(self.shard, here, 0).start()
        self.launch(self.shard, 0)
        pltpu.make_async_copy(self.shard, here, self.near).start()

    def pass_on(self):
        other = self.rows(self.spot.z, 1)
        self.y_copy(other, other, 0).wait_recv()
        self.launch(other, 1)

    def relay(self, k, side, flip):
        spot = self.spot
        src_z = spot.z - k if side else spot.z + k
        block = self.rows(src_z, flip)

        @pl.when(src_z >= 0 if side else src_z <= 3)
        def _():
            self.z_copy(block, block, k, side, flip).wait_recv()
            if k < 3:

                @pl.when(spot.z < 3 if side else spot.z > 0)
                def _():
                    self.z_copy(block, block, k + 1, side, flip).start()

            if not self.spread:
                self.y_copy(block, block, 1 + side * 3 + k - 1).start()

    def finish(self):
        spot = self.spot
        pltpu.make_async_copy(self.shard, self.rows(spot.z), self.near).wait()
        if self.spread:
            return
        self.y_copy(self.shard, self.rows(spot.z, 1), 0).wait_recv()
        for side in (0, 1):
            for k in (1, 2, 3):
                src_z = spot.z - k if side else spot.z + k
                block = self.rows(src_z, 1)

                @pl.when(src_z >= 0 if side else src_z <= 3)
                def _():
                    self.y_copy(block, block, 1 + side * 3 + k - 1).wait_recv()

    def drain(self):
        spot = self.spot
        self.y_copy(self.shard, self.rows(spot.z), 0).wait_send()
        for side in (0, 1):
            for k in (1, 2, 3):
                src_z = spot.z - k if side else spot.z + k
                sent_z = spot.z - k + 1 if side else spot.z + k - 1
                block = self.rows(spot.z)
                if not self.spread:

                    @pl.when(src_z >= 0 if side else src_z <= 3)
                    def _():
                        self.y_copy(block, block, 1 + side * 3 + k - 1).wait_send()

                for flip in (0, 1) if self.spread else (0,):

                    @pl.when((spot.z < 3) & (sent_z >= 0) if side else (spot.z > 0) & (sent_z <= 3))
                    def _():
                        self.z_copy(block, block, k, side, flip).wait_send()


class Share:
    def __init__(self, spot, own, where, send, recv):
        self.spot, self.own, self.where, self.send, self.recv = spot, own, where, send, recv

    def first(self):
        return push(
            self.own, self.where(self.spot.blk), self.send.at[0], self.recv.at[0], self.spot.opp
        )

    def second(self):
        return push(
            self.own, self.where(self.spot.blk), self.send.at[1], self.recv.at[1], self.spot.sib
        )

    def third(self):
        passed = self.where(self.spot.opp_blk)
        return push(passed, passed, self.send.at[2], self.recv.at[2], self.spot.sib)

    def start(self):
        self.first().start()
        self.second().start()

    def relay(self):
        self.first().wait_recv()
        self.third().start()

    def finish(self):
        self.second().wait_recv()
        self.third().wait_recv()

    def drain(self):
        self.first().wait_send()
        self.second().wait_send()
        self.third().wait_send()


def dot(left, right):
    return jnp.dot(left, right, preferred_element_type=F32)


def dot_t(left, right):
    return lax.dot_general(left, right, (((1,), (1,)), ((), ())), preferred_element_type=F32)


def tiles(count, size, body):
    @pl.loop(0, count)
    def _(step):
        body(pl.ds(pl.multiple_of(step * size, size), size))


def norm_block(values, gain, shift):
    center = values - jnp.mean(values, axis=1, keepdims=True)
    spread = jnp.mean(center * center, axis=1, keepdims=True)
    return center * lax.rsqrt(spread + 1e-05) * gain + shift


FORWARD_ORDER = (
    (0, 1), (0, 0), (3, 28), (0, 2), (2, 0, 1, 0, 0), (2, 0, 1, 1, 0), (2, 1, 1, 0, 0),
    (2, 1, 1, 1, 0), (2, 2, 1, 0, 0), (2, 2, 1, 1, 0), (2, 0, 2, 1, 0), (2, 0, 2, 0, 0), (0, 3),
    (3, 29), (2, 1, 2, 1, 0), (3, 31), (2, 2, 2, 0, 0), (2, 2, 2, 1, 0), (2, 1, 2, 0, 0),
    (2, 0, 3, 1, 0), (3, 30), (2, 0, 3, 0, 0), (0, 4), (2, 3, 1, 1, 0), (2, 3, 1, 0, 0),
    (2, 2, 3, 0, 0), (2, 1, 3, 1, 0), (2, 2, 3, 1, 0), (2, 1, 3, 0, 0), (3, 0), (3, 32),
    (2, 4, 1, 1, 0), (2, 3, 2, 0, 0), (2, 3, 2, 1, 0), (2, 4, 1, 0, 0), (0, 5), (2, 4, 2, 1, 0),
    (2, 3, 3, 0, 0), (3, 33), (3, 36), (2, 3, 3, 1, 0), (2, 4, 2, 0, 0), (0, 6), (2, 5, 1, 0, 0),
    (2, 5, 1, 1, 0), (2, 4, 3, 1, 0), (2, 4, 3, 0, 0), (2, 6, 1, 1, 0), (2, 6, 1, 0, 0),
    (2, 5, 2, 1, 0), (2, 5, 2, 0, 0), (0, 7), (0, 8), (2, 6, 2, 1, 0), (2, 6, 2, 0, 0),
    (2, 5, 3, 1, 0), (2, 5, 3, 0, 0), (2, 7, 1, 1, 0), (2, 7, 1, 0, 0), (3, 1), (3, 2), (3, 3),
    (2, 6, 3, 1, 0), (2, 8, 1, 0, 0), (2, 6, 3, 0, 0), (2, 7, 2, 1, 0), (2, 7, 2, 0, 0), (0, 9),
    (2, 8, 1, 1, 0), (0, 10), (2, 7, 3, 1, 0), (2, 8, 2, 0, 0), (3, 4), (2, 9, 1, 1, 0),
    (2, 7, 3, 0, 0), (3, 5), (3, 6), (3, 7), (2, 8, 2, 1, 0), (2, 9, 1, 0, 0), (0, 11), (3, 34),
    (2, 10, 1, 1, 0), (2, 10, 1, 0, 0), (1, 8), (3, 10), (3, 11), (2, 9, 2, 1, 0),
    (2, 8, 3, 0, 0), (3, 8), (3, 9), (3, 12), (3, 13), (2, 8, 3, 1, 0), (2, 9, 2, 0, 0), (3, 14),
    (2, 11, 1, 0, 0), (2, 10, 2, 0, 0), (0, 12), (3, 15), (3, 16), (2, 8, 1, 1, 1), (3, 17),
    (2, 8, 1, 0, 1), (0, 13), (2, 10, 2, 1, 0), (2, 11, 1, 1, 0), (2, 9, 3, 0, 0),
    (2, 9, 3, 1, 0), (2, 11, 2, 0, 0), (2, 12, 1, 1, 0), (3, 18), (2, 10, 3, 0, 0), (3, 19),
    (2, 8, 2, 1, 1), (2, 12, 1, 0, 0), (3, 20), (3, 21), (2, 13, 1, 1, 0), (3, 35),
    (2, 8, 2, 0, 1), (2, 10, 3, 1, 0), (2, 11, 2, 1, 0), (2, 13, 1, 0, 0), (2, 11, 3, 0, 0),
    (2, 12, 2, 1, 0), (3, 22), (2, 12, 2, 0, 0), (3, 23), (2, 8, 3, 1, 1), (3, 24),
    (2, 8, 3, 0, 1), (2, 13, 2, 1, 0), (2, 11, 3, 1, 0), (2, 13, 2, 0, 0), (3, 25),
    (2, 12, 3, 0, 0), (2, 12, 3, 1, 0), (2, 13, 3, 0, 0), (2, 13, 3, 1, 0), (3, 26), (3, 27),
)


def forward_kernel(names, *refs):
    r = named(names, refs)
    spot = Spot()
    rows, width = r.frames.shape
    length = r.x_all.shape[0]
    wide = r.outward.shape[1]
    blk = spot.blk
    outs = []

    def save(src, dst):
        copy = pltpu.make_async_copy(src, dst, r.local.at[len(outs)])
        copy.start()
        outs.append(copy)
        return copy

    def lanes(index, size):
        return pl.ds(pl.multiple_of(index * size, 128), size)

    def row_block(ref):
        return lambda index: ref.at[pl.ds(pl.multiple_of(index * rows, rows), rows)]

    def col_block(ref, size):
        return lambda index: ref.at[:, lanes(index, size)]

    def share(number, own, where):
        return Share(spot, own, where, r.bsend.at[number], r.brecv.at[number])

    gathers = []

    def gather(shard, full, spread):
        wide = full.shape[1] // len(spread)
        first = len(gathers)
        for number, flag in enumerate(spread):
            here = slice(number * wide, (number + 1) * wide)
            sems = (item.at[first + number] for item in (r.zsend, r.zrecv, r.ysend, r.yrecv, r.near))
            gathers.append(Gather(spot, shard.at[:, here], full.at[:, here], *sems, flag))
        return gathers[first:]

    g_norms = gather(r.v_norms, r.v_norm_all, (False,))
    g_outward = gather(r.outward, r.v_outward, (False,))
    g_inward = gather(r.aligned, r.v_inward, (False, False, False))
    g_query = gather(r.query, r.v_query, (False,))
    g_keys = gather(r.keys, r.v_keys, (False,))
    g_back = gather(r.back, r.v_back, (False,))
    g_expand = gather(r.expand, r.v_expand, (True, False))
    g_contract = gather(r.contract, r.v_contract, (False, False, False, False))

    spot.greet()

    def piece(part):
        index = blk * 3 + part
        owner = lax.rem(index, 4)
        return owner, index // 4

    def aligned_copy(part):
        owner, kind = piece(part)
        src = r.inward.at[:, part * wide : (part + 1) * wide]
        return owner, kind, src, r.aligned.at[:, lanes(kind, wide)]

    for part in range(3):
        owner, kind, src, dst = aligned_copy(part)

        @pl.when(owner == blk)
        def _():
            pltpu.make_async_copy(src, dst, r.arecv.at[kind]).start()

        @pl.when(owner != blk)
        def _():
            push(src, dst, r.asend.at[part], r.arecv.at[kind], (spot.grp, owner)).start()

    norm_share = share(0, r.norms, lambda index: r.v_norms.at[pl.ds(index * 16, 16)])
    norm_own = pltpu.make_async_copy(r.norms, r.v_norms.at[pl.ds(blk * 16, 16)], r.near.at[16])
    norm_own.start()
    norm_share.start()
    frame_share = share(1, r.frames, row_block(r.x_all))
    frame_own = pltpu.make_async_copy(r.frames, row_block(r.x_all)(blk), r.near.at[17])
    frame_own.start()
    frame_share.start()
    grad_share = share(2, r.incoming, row_block(r.g_all))
    grad_own = pltpu.make_async_copy(r.incoming, row_block(r.g_all)(blk), r.near.at[18])
    attended_share = share(3, col_block(r.s_attended, wide)(blk), col_block(r.s_attended, wide))
    one_share = share(4, col_block(r.s_one_all, wide)(blk), col_block(r.s_one_all, wide))
    text_share = share(5, col_block(r.s_text, 2 * wide)(blk), col_block(r.s_text, 2 * wide))
    crossed_share = share(6, col_block(r.s_crossed, wide)(blk), col_block(r.s_crossed, wide))
    two_share = share(7, col_block(r.s_two_all, wide)(blk), col_block(r.s_two_all, wide))
    g_outward[0].start()
    for kind in range(3):
        dst = r.aligned.at[:, kind * wide : (kind + 1) * wide]
        home = (kind * 4 + blk) // 3

        @pl.when(home == blk)
        def _():
            pltpu.make_async_copy(dst, dst, r.arecv.at[kind]).wait()

        @pl.when(home != blk)
        def _():
            push(dst, dst, r.asend.at[0], r.arecv.at[kind], spot.sib).wait_recv()

    low = lax.broadcasted_iota(jnp.int32, (1, 128), 1) < 64
    kept = []

    def half(value, part):
        return jnp.where(low if part == 0 else jnp.logical_not(low), value, jnp.zeros_like(value))

    def finish(items):
        for item in items:
            item.finish()

    def turn_over(source, turned):
        def flip(block):
            turned[:, block] = source[block, :].T

        tiles(length // 128, 128, flip)

    def normed(source, index, turned):
        gain = r.v_norm_rows[index : index + 1, :]
        shift = r.v_norm_rows[3 + index : 4 + index, :]

        def body(block):
            result = norm_block(source[block, :].astype(F32), gain, shift).astype(BF16)
            r.a_all[block, :] = result

        tiles(length // 32, 32, body)
        turn_over(r.a_all, turned)

    def side_by_side():
        depth = 8 * 128
        line = lax.broadcasted_iota(jnp.int32, (depth, 384), 0)
        column = lax.broadcasted_iota(jnp.int32, (depth, 384), 1)
        inside = line & 127
        place = jnp.where((inside < 48) & (column == (line >> 7) * 48 + inside), 1.0, 0.0).astype(BF16)
        for pair in range(4):
            parts = [pl.ds(pair * 128 + part * 16, 16) for part in range(8)]
            left = jnp.concatenate([r.v_norm_all[part, :] for part in parts], axis=1)
            r.v_norm_rows[:, pair * 384 : (pair + 1) * 384] = dot(left, place)
        save(r.v_norm_rows, r.norm_all)

    def first_norm():
        finish(g_norms)
        side_by_side()
        normed(r.x_all, 0, r.t_first)
        save(r.t_first, r.first_t)

    def joint():
        finish(g_inward)
        save(r.v_inward, r.w_inward)

        def body(block):
            r.s_joint[:, block] = dot(r.a_all[...], r.v_inward[:, block]).astype(BF16)

        tiles(3, wide, body)
        save(r.s_joint, r.joint)

    def soft(scores):
        power = jnp.exp(scores - jnp.max(scores, axis=1, keepdims=True))
        return (power * (1.0 / jnp.sum(power, axis=1, keepdims=True))).astype(BF16)

    def attend():
        @pl.loop(0, 12)
        def _(step):
            pair, block = step // 4, lax.rem(step, 4)
            here = pl.ds(pl.multiple_of(block * 128, 128), 128)
            query = r.s_joint[here, lanes(pair, 128)]
            key = r.s_joint[:, lanes(pair + 3, 128)]
            value = r.s_joint[:, lanes(pair + 6, 128)]
            keep = r.ids_row[...] <= r.ids_col[here, :]
            results = []
            for part in (0, 1):
                scores = jnp.where(keep, dot_t(half(query, part), key) * 0.125, -1e30)
                results.append(dot(soft(scores), value))
            r.s_attended[here, lanes(blk * 3 + pair, 128)] = jnp.where(low, *results).astype(BF16)

    def hidden_one():
        finish(g_outward)
        save(r.v_outward, r.w_outward)
        own = r.x_all[:, lanes(blk, wide)].astype(F32)
        r.s_one[...] = dot(r.s_attended[...], r.v_outward[...]) + own
        r.s_one_all[:, lanes(blk, wide)] = r.s_one[...].astype(BF16)

    def one_here():
        one_share.finish()
        save(row_block(r.s_one_all)(blk), r.one_rows)

    def text_pairs():
        finish(g_keys)
        save(r.v_keys, r.w_keys)
        r.s_text[:, lanes(blk, 2 * wide)] = dot(r.text[...], r.v_keys[...]).astype(BF16)

    def second_norm():
        normed(r.s_one_all, 1, r.t_second)
        save(r.t_second, r.second_t)

    def cross_query():
        finish(g_query)
        save(r.v_query, r.w_query)
        r.s_query[...] = dot(r.a_all[...], r.v_query[...]).astype(BF16)
        save(r.s_query, r.cross_query)

    def text_here():
        text_share.finish()
        save(r.s_text, r.text_all)

    def cross():
        @pl.loop(0, 3)
        def _(pair):
            query = r.s_query[:, lanes(pair, 128)]
            key = r.s_text[:, lanes(blk * 3 + pair, 128)]
            value = r.s_text[:, lanes(12 + blk * 3 + pair, 128)]
            results = []
            for part in (0, 1):
                results.append(dot(soft(dot_t(half(query, part), key) * 0.125), value))
            r.s_crossed[:, lanes(blk * 3 + pair, 128)] = jnp.where(low, *results).astype(BF16)

    def hidden_two():
        finish(g_back)
        save(r.v_back, r.w_back)
        r.s_one[...] += dot(r.s_crossed[...], r.v_back[...])
        r.s_two_all[:, lanes(blk, wide)] = r.s_one[...].astype(BF16)

    def two_here():
        two_share.finish()
        save(row_block(r.s_two_all)(blk), r.two_rows)

    def third_norm():
        normed(r.s_two_all, 2, r.t_third)
        save(r.t_third, r.third_t)

    def upward():
        finish(g_expand)
        kept.append(save(r.v_expand, r.w_expand))

        def body(block):
            r.s_upward[:, block] = dot(r.a_all[...], r.v_expand[:, block])

        tiles(4, 384, body)

    def gelu():
        def body(block):
            value = r.s_upward[block, :]
            gate = 0.5 + 0.5 * lax.erf(value * 0.7071067811865476)
            r.s_active[block, :] = (value * gate).astype(BF16)
            r.s_slope[block, :] = gate + value * jnp.exp(-0.5 * value * value) * 0.3989422804014327

        tiles(length // 16, 16, body)
        save(r.s_slope, r.slope)
        save(r.s_active, r.active)

    def contract_grad():
        kept[0].wait()
        for item in g_expand:
            item.drain()

        def body(block):
            r.v_expand[:, block] = dot(r.t_grad[...], r.s_active[:, block]).astype(BF16)

        tiles(4, 384, body)
        save(r.v_expand, r.contract_grad)

    def nothing():
        pass

    def frames_here():
        frame_own.wait()
        frame_share.finish()

    def grad_start():
        grad_own.start()
        grad_share.start()

    def grad_here():
        grad_share.finish()
        grad_own.wait()
        save(r.g_all, r.grad_all)

    def attended_over():
        turn_over(r.s_attended, r.t_attended)
        save(r.t_attended, r.attended_t)

    def crossed_over():
        turn_over(r.s_crossed, r.t_crossed)
        save(r.t_crossed, r.crossed_t)

    def grad_over():
        turn_over(r.g_all, r.t_grad)

    steps = (
        first_norm, joint, attend,
        attended_share.start, attended_share.relay, attended_share.finish,
        hidden_one, one_share.start, one_share.relay, one_here,
        text_pairs, text_share.start, text_share.relay, text_here,
        second_norm, cross_query, cross,
        crossed_share.start, crossed_share.relay, crossed_share.finish,
        hidden_two, two_share.start, two_share.relay, two_here,
        third_norm, upward, gelu, contract_grad,
        nothing, frame_share.relay, frames_here, grad_start, grad_share.relay, grad_here,
        attended_over, crossed_over, grad_over,
    )
    for kind, number, *rest in FORWARD_ORDER:
        if kind == 3:
            steps[number]()
            continue
        item = gathers[number]
        if kind == 2:
            item.relay(*rest)
        elif kind == 1:
            item.pass_on()
        elif item is g_norms[0]:
            norm_share.relay()
            norm_own.wait()
            norm_share.finish()
            item.start()
        elif item is not g_outward[0]:
            item.start()
    finish(g_contract)
    save(r.v_contract, r.w_contract)
    for part in range(3):
        owner, kind, src, dst = aligned_copy(part)

        @pl.when(owner != blk)
        def _():
            push(src, dst, r.asend.at[part], r.arecv.at[kind], (spot.grp, owner)).wait_send()

    for item in (
        norm_share, frame_share, grad_share, attended_share, one_share, text_share, crossed_share, two_share,
    ):
        item.drain()
    for item in gathers:
        if item not in g_expand:
            item.drain()
    for copy in outs:
        if copy is not kept[0]:
            copy.wait()


def ids_of(table):
    ids = (table[0][:, None] * SEG + jnp.arange(SEG, dtype=jnp.int32)[None, :]).reshape(-1)
    return ids[:, None], ids[None, :]


def run_kernel(kernel, number, inner, outer, out, vmem, sems, credits):
    anywhere = pl.BlockSpec(memory_space=pl.ANY)
    inside = pl.BlockSpec(memory_space=pltpu.VMEM)
    names = [*inner, *outer, *out, *vmem, *sems, *credits]
    results = pl.pallas_call(
        functools.partial(kernel, names),
        out_shape=[jax.ShapeDtypeStruct(*item) for item in out.values()],
        in_specs=[inside] * len(inner) + [anywhere] * len(outer),
        out_specs=[anywhere] * len(out),
        scratch_shapes=[pltpu.VMEM(*item) for item in vmem.values()]
        + [pltpu.SemaphoreType.DMA(shape) for shape in sems.values()]
        + [pltpu.SemaphoreType.REGULAR(shape) for shape in credits.values()],
        compiler_params=pltpu.CompilerParams(
            collective_id=number, has_side_effects=True, vmem_limit_bytes=60 * 2**20
        ),
    )(*inner.values(), *outer.values())
    return named(out, results)


def forward(frames, text, table, norms, incoming, weights):
    rows, width = frames.shape
    length = rows * lax.axis_size("blk")
    wide = width // lax.axis_size("blk")
    feed = weights["expand"].shape[1]
    ids_col, ids_row = ids_of(table)
    one = ((width, wide), BF16)
    two = ((width, 2 * wide), BF16)
    three = ((width, 3 * wide), BF16)
    four = ((width, feed), BF16)
    square, turned, strip = ((length, width), BF16), ((width, length), BF16), ((length, wide), BF16)
    big = ((length, feed), F32)
    own = ((rows, width), BF16)
    out = dict(
        w_outward=one,
        w_inward=three,
        w_query=one,
        w_keys=two,
        w_back=one,
        w_expand=four,
        w_contract=four,
        first_t=turned,
        second_t=turned,
        third_t=turned,
        attended_t=turned,
        crossed_t=turned,
        contract_grad=four,
        grad_all=square,
        joint=((length, 3 * wide), BF16),
        cross_query=strip,
        text_all=((TEXT, 2 * width), BF16),
        slope=big,
        active=((length, feed), BF16),
        one_rows=own,
        two_rows=own,
        norm_all=((16, width), F32),
        aligned=((width // lax.axis_size("grp"), 3 * wide), BF16),
    )
    vmem = dict(
        v_outward=one,
        v_inward=three,
        v_query=one,
        v_keys=two,
        v_back=one,
        v_expand=four,
        v_contract=four,
        x_all=square,
        g_all=square,
        a_all=square,
        s_attended=square,
        s_one_all=square,
        s_crossed=square,
        s_two_all=square,
        t_first=turned,
        t_second=turned,
        t_third=turned,
        t_attended=turned,
        t_crossed=turned,
        t_grad=turned,
        s_joint=((length, 3 * wide), BF16),
        s_one=((length, wide), F32),
        s_query=strip,
        s_text=((TEXT, 2 * width), BF16),
        s_upward=big,
        s_slope=big,
        s_active=((length, feed), BF16),
        v_norms=((64, 128), BF16),
        v_norm_all=((512, 128), BF16),
        v_norm_rows=((16, width), F32),
    )
    sems = dict(
        zsend=(14, 12),
        zrecv=(14, 12),
        ysend=(14, 7),
        yrecv=(14, 7),
        near=(19,),
        bsend=(8, 3),
        brecv=(8, 3),
        asend=(3,),
        arecv=(3,),
        local=(32,),
    )
    inner = dict(text=text, ids_col=ids_col, ids_row=ids_row)
    outer = dict(frames=frames, norms=norms, incoming=incoming, **weights)
    return run_kernel(forward_kernel, 1, inner, outer, out, vmem, sems, {})


class Reduce:
    def __init__(self, spot, grad, over, along, sems, spread, source=None):
        self.spot, self.grad, self.over, self.along = spot, grad, over, along
        self.ysend, self.yrecv, self.zsend, self.zrecv = sems
        self.spread = spread
        self.source = grad if source is None else source
        self.size, self.cols = over.shape[-2], over.shape[-1]

    def rows(self, z, flip=0, ref=None):
        spot = self.spot
        row = z * 2 + (1 - spot.y if flip else spot.y)
        return (self.grad if ref is None else ref).at[pl.ds(pl.multiple_of(row * self.size, self.size), self.size)]

    def add(self, target, extra):
        step = 16

        @pl.loop(0, self.size // step)
        def _(index):
            here = pl.ds(pl.multiple_of(index * step, step), step)
            target[here, :] = (target[here, :].astype(F32) + extra[here, :].astype(F32)).astype(BF16)

    def y_copy(self, z):
        return push(
            self.rows(z, 1, self.source), self.over.at[z], self.ysend.at[z], self.yrecv.at[z], self.spot.part
        )

    def y_start(self):
        for z in (0, 3, 1, 2):
            self.y_copy(z).start()

    def z_push(self, goal, flip, who, slot):
        index = flip * 5 + slot
        return push(
            self.rows(goal, flip), self.along.at[index], self.zsend.at[flip * 4 + goal],
            self.zrecv.at[index], (who * 2 + self.spot.y, self.spot.blk),
        )

    def onward(self, goal, flip, home):
        who = home + 1 if goal > home else home - 1
        slot = 4 if who == goal and home > goal else goal
        self.z_push(goal, flip, who, slot).start()

    def z_first(self, goal, flip):
        for home in (0, 3):
            if home != goal:

                @pl.when(self.spot.z == home)
                def _():
                    self.onward(goal, flip, home)

    def pass_on(self, goal, flip, home):
        @pl.when(self.spot.z == home)
        def _():
            self.z_push(goal, flip, home, goal).wait_recv()
            self.add(self.rows(goal, flip), self.along.at[flip * 5 + goal])
            self.onward(goal, flip, home)

    def take(self, goal):
        self.y_copy(goal).wait_recv()
        self.add(self.rows(goal), self.over.at[goal])
        self.z_first(goal, 0)

    def start(self):
        if not self.spread:
            return self.y_start()
        for goal in (0, 3, 1, 2):
            for flip in (1, 0):
                self.z_first(goal, flip)

    def slots(self, home):
        return ([home] if home > 0 else []) + ([4] if home < 3 else [])

    def arrive(self, flip):
        for home in range(4):

            @pl.when(self.spot.z == home)
            def _():
                for slot in self.slots(home):
                    self.z_push(home, flip, home, slot).wait_recv()

    def total(self, flip, extra, body):
        own = self.rows(self.spot.z, flip)
        for home in range(4):

            @pl.when(self.spot.z == home)
            def _():
                @pl.loop(0, self.size // 16)
                def _(index):
                    here = pl.ds(pl.multiple_of(index * 16, 16), 16)
                    value = own[here, :].astype(F32)
                    for slot in self.slots(home):
                        value += self.along[flip * 5 + slot, here, :].astype(F32)
                    if extra is not None:
                        value += extra[here, :].astype(F32)
                    body(here, value)

    def cross(self):
        self.arrive(1)
        target = self.rows(self.spot.z, 1)

        def keep(here, value):
            target[here, :] = value.astype(BF16)

        self.total(1, None, keep)
        push(target, self.over.at[0], self.ysend.at[0], self.yrecv.at[0], self.spot.part).start()

    def finish(self, body):
        self.arrive(0)
        if self.spread:
            target = self.rows(self.spot.z, 1)
            push(target, self.over.at[0], self.ysend.at[0], self.yrecv.at[0], self.spot.part).wait_recv()
            self.total(0, self.over.at[0], body)
        else:
            self.total(0, None, body)

    def drain(self):
        z = self.spot.z
        if self.spread:
            target = self.rows(z, 1)
            push(target, self.over.at[0], self.ysend.at[0], self.yrecv.at[0], self.spot.part).wait_send()
        else:
            for goal in range(4):
                self.y_copy(goal).wait_send()
        for flip in (0, 1) if self.spread else (0,):
            for goal in range(4):

                @pl.when(z != goal)
                def _():
                    self.z_push(goal, flip, 0, 0).wait_send()


class BlkSum:
    def __init__(self, spot, piece, near, far, send, recv, step, size):
        self.spot, self.piece, self.near, self.far = spot, piece, near, far
        self.send, self.recv, self.step, self.size = send, recv, step, size

    def to_core(self, x):
        spot = self.spot
        goal = x * 2 + 1 - spot.core
        return push(self.piece(goal), self.near.at[x], self.send.at[x], self.recv.at[x], spot.sib)

    def to_chip(self):
        spot = self.spot
        return push(self.piece(spot.opp_blk), self.far, self.send.at[2], self.recv.at[2], spot.opp)

    def start(self):
        self.to_core(0).start()
        self.to_core(1).start()

    def relay(self):
        spot = self.spot
        for x in (0, 1):
            self.to_core(x).wait_recv()
        target, extra = self.piece(spot.opp_blk), self.near.at[1 - spot.x]

        @pl.loop(0, self.size // self.step)
        def _(index):
            here = pl.ds(pl.multiple_of(index * self.step, self.step), self.step)
            target[here, :] = (target[here, :].astype(F32) + extra[here, :].astype(F32)).astype(BF16)

        self.to_chip().start()

    def finish(self):
        self.to_chip().wait_recv()

    def value(self, here):
        spot = self.spot
        own = self.piece(spot.blk)[here, :].astype(F32)
        return own + self.near[spot.x, here, :].astype(F32) + self.far[here, :].astype(F32)

    def drain(self):
        self.to_core(0).wait_send()
        self.to_core(1).wait_send()
        self.to_chip().wait_send()


class Turn:
    def __init__(self, spot, source, target, send, recv):
        self.spot, self.source, self.target, self.send, self.recv = spot, source, target, send, recv
        self.rows, self.wide = source.shape[0], target.shape[1]

    def copy(self, number):
        spot = self.spot
        goal = (spot.sib_blk, spot.opp_blk, spot.far_blk)[number]
        src = self.source.at[:, pl.ds(pl.multiple_of(goal * self.wide, 128), self.wide)]
        return push(src, self.place(spot.blk), self.send.at[number], self.recv.at[number], (spot.grp, goal))

    def place(self, index):
        return self.target.at[pl.ds(pl.multiple_of(index * self.rows, self.rows), self.rows)]

    def start(self):
        for number in (2, 1, 0):
            self.copy(number).start()
        spot = self.spot
        src = self.source.at[:, pl.ds(pl.multiple_of(spot.blk * self.wide, 128), self.wide)]
        self.place(spot.blk)[...] = src[...]

    def finish(self):
        for number in range(3):
            self.copy(number).wait_recv()

    def drain(self):
        for number in range(3):
            self.copy(number).wait_send()


def t_dot(left, right):
    return lax.dot_general(left, right, (((0,), (0,)), ((), ())), preferred_element_type=F32)


BACKWARD_ORDER = (
    (0, 0), (0, 1), (0, 2), (0, 3), (5, 0), (1, 0, 0), (5, 1), (1, 0, 3), (5, 5), (5, 2), (5, 6),
    (1, 0, 1), (0, 4), (0, 5), (2, 0, 0, 0, 2), (5, 7), (0, 6), (5, 8), (0, 7), (1, 0, 2),
    (2, 0, 3, 0, 1), (5, 3), (2, 0, 1, 0, 2), (1, 1, 0), (2, 0, 0, 0, 1), (1, 1, 3),
    (2, 0, 3, 0, 2), (2, 1, 0, 0, 2), (2, 0, 2, 0, 1), (1, 1, 1), (5, 4), (2, 1, 3, 0, 1),
    (1, 1, 2), (4, 0), (5, 9), (2, 1, 1, 0, 2), (2, 1, 0, 0, 1), (1, 2, 0), (2, 1, 3, 0, 2),
    (2, 1, 2, 0, 1), (1, 2, 3), (5, 10), (2, 2, 0, 0, 2), (1, 2, 1), (5, 11), (5, 12), (5, 15),
    (0, 8), (4, 1), (2, 2, 3, 0, 1), (1, 2, 2), (5, 13), (2, 2, 0, 0, 1), (2, 2, 1, 0, 2),
    (1, 3, 0), (2, 2, 3, 0, 2), (2, 8, 3, 1, 1), (2, 8, 0, 1, 2), (1, 3, 3), (2, 8, 3, 0, 1),
    (2, 8, 0, 0, 2), (1, 3, 1), (5, 14), (2, 8, 3, 1, 2), (2, 8, 0, 1, 1), (2, 8, 1, 1, 2),
    (1, 3, 2), (5, 16), (5, 17), (2, 8, 0, 0, 1), (2, 8, 1, 0, 2), (2, 8, 3, 0, 2), (1, 4, 0),
    (2, 8, 2, 1, 1), (5, 20), (5, 21), (1, 4, 3), (5, 24), (5, 18), (2, 8, 2, 0, 1), (1, 4, 1),
    (5, 19), (5, 22), (5, 25), (3, 8), (0, 9), (2, 2, 2, 0, 1), (5, 26), (2, 3, 3, 0, 1),
    (2, 3, 0, 0, 2), (5, 27), (1, 5, 0), (1, 4, 2), (4, 2), (2, 3, 1, 0, 2), (1, 5, 3), (5, 28),
    (5, 23), (2, 3, 0, 0, 1), (2, 3, 3, 0, 2), (2, 3, 2, 0, 1), (5, 29), (1, 5, 1),
    (2, 4, 0, 0, 2), (2, 4, 3, 0, 1), (1, 5, 2), (4, 3), (2, 4, 1, 0, 2), (1, 6, 0), (5, 30),
    (5, 35), (2, 4, 0, 0, 1), (2, 4, 3, 0, 2), (2, 4, 2, 0, 1), (2, 5, 0, 0, 2), (5, 31),
    (5, 32), (0, 11), (1, 6, 3), (2, 5, 3, 0, 1), (1, 6, 1), (5, 33), (2, 5, 0, 0, 1), (4, 4),
    (2, 5, 1, 0, 2), (1, 6, 2), (2, 5, 3, 0, 2), (2, 5, 2, 0, 1), (1, 7, 0), (2, 6, 0, 0, 2),
    (2, 11, 3, 1, 1), (1, 7, 3), (4, 5), (5, 34), (2, 11, 0, 1, 2), (2, 11, 3, 0, 1), (1, 7, 1),
    (5, 36), (2, 11, 2, 0, 1), (2, 11, 0, 0, 2), (2, 6, 0, 0, 1), (2, 11, 3, 1, 2),
    (2, 11, 3, 0, 2), (2, 11, 1, 1, 2), (2, 11, 1, 0, 2), (2, 11, 2, 1, 1), (2, 11, 0, 1, 1),
    (2, 6, 3, 0, 1), (1, 9, 0), (1, 7, 2), (4, 8), (5, 41), (0, 12), (5, 42), (0, 13), (5, 43),
    (2, 11, 0, 0, 1), (5, 37), (5, 38), (1, 9, 3), (2, 7, 0, 0, 2), (2, 7, 3, 0, 1),
    (2, 6, 2, 0, 1), (2, 6, 1, 0, 2), (0, 14), (5, 39), (3, 11), (0, 10), (2, 7, 1, 0, 2),
    (2, 6, 3, 0, 2), (1, 9, 1), (2, 7, 2, 0, 1), (2, 7, 3, 0, 2), (2, 9, 0, 0, 2),
    (2, 7, 0, 0, 1), (1, 12, 0), (4, 6), (1, 9, 2), (2, 9, 3, 0, 1), (5, 40), (4, 7), (1, 12, 3),
    (5, 44), (1, 12, 1), (5, 49), (5, 50), (5, 45), (2, 9, 1, 0, 2), (2, 9, 0, 0, 1),
    (2, 12, 0, 0, 2), (1, 13, 0), (5, 51), (1, 12, 2), (5, 46), (2, 9, 2, 0, 1), (2, 9, 3, 0, 2),
    (1, 13, 3), (2, 12, 3, 0, 1), (5, 47), (1, 13, 1), (2, 12, 1, 0, 2), (2, 12, 0, 0, 1),
    (5, 52), (5, 53), (2, 12, 2, 0, 1), (1, 14, 0), (1, 13, 2), (2, 13, 0, 0, 2), (4, 9),
    (5, 48), (2, 13, 3, 0, 1), (2, 12, 3, 0, 2), (1, 14, 3), (2, 13, 1, 0, 2), (1, 14, 1),
    (4, 12), (2, 13, 0, 0, 1), (2, 13, 3, 0, 2), (2, 13, 2, 0, 1), (2, 14, 0, 0, 2), (1, 14, 2),
    (2, 14, 3, 0, 1), (4, 11), (4, 13), (2, 14, 0, 0, 1), (2, 14, 1, 0, 2), (1, 10, 0),
    (2, 14, 2, 0, 1), (2, 14, 3, 0, 2), (1, 10, 3), (2, 10, 0, 0, 2), (1, 10, 1), (4, 14),
    (2, 10, 3, 0, 1), (1, 10, 2), (2, 10, 0, 0, 1), (2, 10, 1, 0, 2), (2, 10, 3, 0, 2),
    (2, 10, 2, 0, 1), (4, 10),
)


def backward_kernel(names, *refs):
    r = named(names, refs)
    spot = Spot()
    rows, width = r.frames.shape
    length = r.v_grad.shape[0]
    wide = width // 4
    blk = spot.blk
    spot.greet_all()
    query_part, head_part, turn_part, turned_part = (
        r.v_grad.at[:, index * wide : (index + 1) * wide] for index in range(4)
    )

    def lanes(index, size):
        return pl.ds(pl.multiple_of(index * size, 128), size)

    def part(ref, first, size):
        return ref.at[:, first : first + size]

    def row_piece(ref, size):
        return lambda index: ref.at[pl.ds(pl.multiple_of(index * size, size), size)]

    loads = []

    def load(src, dst):
        copy = pltpu.make_async_copy(src, dst, r.local.at[len(loads)])
        copy.start()
        loads.append(copy)
        return copy

    reduces, grads = [], []

    def reduce(grad, over, along, spread=False, source=None):
        number = len(reduces)
        sems = tuple(item.at[number] for item in (r.ysend, r.yrecv, r.zsend, r.zrecv))
        reduces.append(Reduce(spot, grad, over, along, sems, spread, source))
        grads.append(grad)

    def columns(index, *items):
        here = slice(index * wide, (index + 1) * wide)
        return [item.at[:, here] if len(item.shape) == 2 else item.at[:, :, here] for item in items]

    for index in range(4):
        *items, source = columns(index, r.g_contract, r.y_contract, r.z_contract, r.contract_grad)
        reduce(*items, False, source)
    for index in range(4):
        reduce(*columns(index, r.g_expand, r.y_expand, r.z_expand))
    reduce(part(r.g_rest, 0 * wide, 1 * wide), r.y_back, r.z_back, True)
    reduce(part(r.g_rest, 1 * wide, 2 * wide), r.y_keys, r.z_keys, False)
    reduce(part(r.g_rest, 3 * wide, 1 * wide), r.y_query, r.z_query, False)
    reduce(part(r.g_rest, 4 * wide, 1 * wide), r.y_outward, r.z_outward, True)
    for index in range(3):
        reduce(*columns(index, r.g_contract, r.y_contract, r.z_contract))
    back, keys, query, outward = range(8, 12)
    inward = 12
    load_grad = load(r.grad_all, r.v_grad)
    load_contract = load(r.w_contract, r.v_one)
    load_slope = load(r.slope, r.v_slope)
    later = Bag()
    later.own = [
        load(reduces[0].rows(z, 0, r.contract_grad), reduces[0].rows(z, 0, r.g_contract))
        for z in range(4)
    ]
    cross_query = part(r.v_joint, 0, wide)

    def blk_sum(number, piece, near, far, size):
        return BlkSum(spot, piece, near, far, r.bsend.at[number], r.brecv.at[number], 16, size)

    copies = []

    def give(src, goal):
        copy = pltpu.make_async_copy(src, goal, r.stored.at[len(copies)])
        copy.start()
        copies.append(copy)
        return copy

    def back_rows(left, right):
        def body(block):
            r.v_part[:, block] = dot_t(left[...], right[block, :]).astype(BF16)

        tiles(4, 384, body)

    def back_cols(left, right):
        for core in (1 - spot.core, spot.core):
            for x in (0, 1):
                goal = x * 2 + core
                here = pl.ds(pl.multiple_of(goal * wide, 128), wide)
                mine = pl.ds(pl.multiple_of(goal * wide, wide), wide)
                r.v_part[:, here] = dot_t(left[...], right[mine, :]).astype(BF16)

    def outer(target, left, right):
        def body(block):
            target[block, :] = dot(left[block, :], right[...]).astype(BF16)

        tiles(4, 384, body)

    row_parts = row_piece(r.v_part, rows)

    def col_parts(index):
        return r.v_part.at[:, lanes(index, wide)]

    third_sum = blk_sum(0, row_parts, r.near_rows, r.far_rows, rows)
    crossed_sum = blk_sum(1, col_parts, r.near_cols, r.far_cols, length)
    second_sum = blk_sum(2, row_parts, r.near_rows, r.far_rows, rows)
    attended_sum = blk_sum(3, col_parts, r.near_cols, r.far_cols, length)
    text_rows = TEXT // 4
    text_sum = blk_sum(4, row_piece(r.v_text_part, text_rows), r.near_text, r.far_text, text_rows)
    first_sum = blk_sum(5, row_parts, r.near_rows, r.far_rows, rows)
    out_sum = blk_sum(6, row_parts, r.near_rows, r.far_rows, rows)
    turn_two = Turn(spot, r.v_branch, turn_part, r.tsend.at[0], r.trecv.at[0])
    turn_one = Turn(spot, r.v_branch, turned_part, r.tsend.at[1], r.trecv.at[1])
    terms_share = Share(
        spot,
        r.v_terms.at[:, lanes(blk, wide)],
        lambda index: r.v_terms.at[:, lanes(index, wide)],
        r.csend.at[0],
        r.crecv.at[0],
    )
    hidden = r.v_slope.at[pl.ds(3 * rows, rows)]
    joint_grad = part(r.v_up, 0, 3 * wide)
    own_rows = pl.ds(pl.multiple_of((blk // 2) * TEXT, TEXT), TEXT)
    own_cols = lanes(lax.rem(blk, 2), 2 * wide)
    low = lax.broadcasted_iota(jnp.int32, (1, 128), 1) < 64

    def up():
        load_grad.wait()
        load_contract.wait()
        load_slope.wait()
        later.expand_in = load(r.w_expand, r.v_two)
        later.third_in = load(r.third_t, r.v_left)
        later.norm_in = load(r.norm_all.at[0:8], r.v_norm)
        later.two_in = load(r.two_rows, r.v_two_rows)
        later.incoming_in = load(r.incoming, r.v_rows)
        later.crossed_in = load(r.crossed_t, r.v_right)
        later.query_in = load(r.cross_query, cross_query)
        later.text_in = load(r.text_all.at[:, lanes(blk, wide)], part(r.v_text, 0, wide))
        later.values_in = load(r.text_all.at[:, lanes(blk + 4, wide)], part(r.v_text, wide, wide))

        def body(block):
            product = dot(r.v_grad[...], r.v_one[:, block])
            r.v_up[:, block] = (product * r.v_slope[:, block]).astype(BF16)

        tiles(4, 384, body)
        later.back = load(r.w_back, part(r.v_one, 0, wide))
        later.keys = load(r.w_keys, part(r.v_one, wide, 2 * wide))
        later.outward = load(r.w_outward, part(r.v_one, 3 * wide, wide))

    def third_back():
        later.expand_in.wait()
        back_rows(r.v_up, r.v_two)
        later.query = load(r.w_query, part(r.v_two, 0, wide))
        later.inward = load(r.w_inward, part(r.v_two, wide, 3 * wide))

    expand_done = []

    def expand_grad(index):
        if not expand_done:
            later.third_in.wait()
        expand_done.append(index)
        grads[4 + index][...] = dot(r.v_left[...], part(r.v_up, index * wide, wide)[...]).astype(BF16)
        if len(expand_done) == 4:
            later.second = load(r.second_t, r.v_left)

    def norm_back(total, number, base, keep):
        values = r.v_two_rows if number == 2 else r.v_rows
        gain = r.v_norm[number : number + 1, :]

        @pl.loop(0, rows // 16)
        def _(index):
            here = pl.ds(pl.multiple_of(index * 16, 16), 16)
            incoming = total.value(here)
            value = values[here, :].astype(F32)
            center = value - jnp.mean(value, axis=1, keepdims=True)
            scale = lax.rsqrt(jnp.mean(center * center, axis=1, keepdims=True) + 1e-05)
            normal = center * scale
            scaled = incoming * gain
            mean = jnp.mean(scaled, axis=1, keepdims=True)
            match = jnp.mean(scaled * normal, axis=1, keepdims=True)
            result = base[here, :].astype(F32) + (scaled - mean - normal * match) * scale
            hidden[here, :] = result
            if keep:
                r.v_branch[here, :] = result.astype(BF16)
            for place, term in ((number, incoming * normal), (3 + number, incoming)):
                spread = pl.ds(place * 8, 8)
                r.v_norm_grads[spread, :] += term[0:8, :] + term[8:16, :]

    def third_norm():
        for copy in (later.norm_in, later.two_in, later.incoming_in):
            copy.wait()
        r.v_norm_grads[...] = jnp.zeros_like(r.v_norm_grads)
        norm_back(third_sum, 2, r.v_rows, True)
        later.one = load(r.one_rows, r.v_rows)
        turn_two.start()

    def crossed_back():
        third_sum.drain()
        later.back.wait()
        back_cols(turn_part, part(r.v_one, 0, wide))

    def back_grad():
        later.crossed_in.wait()
        outer(grads[back], r.v_right, turn_part)
        later.attended = load(r.attended_t, r.v_right)

    def merge(total, target):
        @pl.loop(0, length // 16)
        def _(index):
            here = pl.ds(pl.multiple_of(index * 16, 16), 16)
            target[here, :] = total.value(here).astype(BF16)

    def half(value, side):
        return jnp.where(low if side == 0 else jnp.logical_not(low), value, jnp.zeros_like(value))

    def soft(scores):
        power = jnp.exp(scores - jnp.max(scores, axis=1, keepdims=True))
        return power * (1.0 / jnp.sum(power, axis=1, keepdims=True))

    def cross():
        later.query_in.wait()
        later.text_in.wait()
        later.values_in.wait()
        merge(crossed_sum, head_part)

        @pl.loop(0, 3)
        def _(pair):
            query = cross_query[:, lanes(pair, 128)]
            key = r.v_text[:, lanes(pair, 128)]
            value = r.v_text[:, lanes(3 + pair, 128)]
            head_grad = head_part[:, lanes(pair, 128)]
            results = []
            for side in (0, 1):
                weights = soft(dot_t(half(query, side), key) * 0.125)
                slope = dot_t(half(head_grad, side), value)
                score = (weights * (slope - jnp.sum(slope * weights, axis=1, keepdims=True))).astype(BF16)
                results.append(
                    (
                        dot(score, key) * 0.125,
                        t_dot(score, query) * 0.125,
                        t_dot(weights.astype(BF16), head_grad),
                    )
                )
            merged = [jnp.where(low, *item).astype(BF16) for item in zip(*results)]
            query_part[:, lanes(pair, 128)] = merged[0]
            r.v_terms[0:TEXT, lanes(blk * 3 + pair, 128)] = merged[1]
            r.v_terms[TEXT : 2 * TEXT, lanes(blk * 3 + pair, 128)] = merged[2]

        later.joint = load(r.joint, r.v_joint)

    def second_back():
        later.query.wait()
        crossed_sum.drain()
        back_rows(query_part, part(r.v_two, 0, wide))

    def query_grad():
        later.second.wait()
        outer(grads[query], r.v_left, query_part)
        later.first = load(r.first_t, r.v_left)

    def keys_grad():
        def body(block):
            product = t_dot(r.text[:, block], r.v_terms[own_rows, own_cols])
            grads[keys][block, :] = product.astype(BF16)

        tiles(6, 256, body)

    def text_start():
        later.keys.wait()
        terms = r.v_terms[own_rows, own_cols]
        r.v_text_part[...] = dot_t(terms, r.v_one[:, wide : 3 * wide]).astype(BF16)
        text_sum.start()

    def text_done():
        text_sum.finish()
        r.v_text_out[...] = text_sum.value(pl.ds(0, text_rows))
        give(r.v_text_out, r.text_out)

    def second_norm():
        later.one.wait()
        turn_two.drain()
        norm_back(second_sum, 1, hidden, True)
        later.frames = load(r.frames, r.v_rows)
        turn_one.start()

    def attended_back():
        second_sum.drain()
        later.outward.wait()
        back_cols(turned_part, part(r.v_one, 3 * wide, wide))

    def outward_grad():
        later.attended.wait()
        outer(grads[outward], r.v_right, turned_part)

    def attend():
        later.joint.wait()
        merge(attended_sum, head_part)

        @pl.loop(0, 3)
        def _(pair):
            r.v_key_sum[...] = jnp.zeros_like(r.v_key_sum)
            r.v_value_sum[...] = jnp.zeros_like(r.v_value_sum)

            @pl.loop(0, 4)
            def _(block):
                here = pl.ds(pl.multiple_of(block * 128, 128), 128)
                query = r.v_joint[here, lanes(pair, 128)]
                key = r.v_joint[:, lanes(pair + 3, 128)]
                value = r.v_joint[:, lanes(pair + 6, 128)]
                head_grad = head_part[here, lanes(pair, 128)]
                keep = r.ids_row[...] <= r.ids_col[here, :]
                results = []
                for side in (0, 1):
                    weights = soft(jnp.where(keep, dot_t(half(query, side), key) * 0.125, -1e30))
                    slope = dot_t(half(head_grad, side), value)
                    score = weights * (slope - jnp.sum(slope * weights, axis=1, keepdims=True))
                    score = score.astype(BF16)
                    results.append(
                        (dot(score, key), t_dot(score, query), t_dot(weights.astype(BF16), head_grad))
                    )
                merged = [jnp.where(low, *item) for item in zip(*results)]
                r.v_up[here, lanes(pair, 128)] = (merged[0] * 0.125).astype(BF16)
                r.v_key_sum[...] += merged[1]
                r.v_value_sum[...] += merged[2]

            r.v_up[:, lanes(pair + 3, 128)] = (r.v_key_sum[...] * 0.125).astype(BF16)
            r.v_up[:, lanes(pair + 6, 128)] = r.v_value_sum[...].astype(BF16)

    def first_back():
        attended_sum.drain()
        later.inward.wait()
        back_rows(joint_grad, part(r.v_two, wide, 3 * wide))

    inward_done = []

    def inward_grad(index):
        if not inward_done:
            later.first.wait()
        inward_done.append(index)
        reduces[index].drain()
        product = dot(r.v_left[...], part(r.v_up, index * wide, wide)[...])
        grads[inward + index][...] = product.astype(BF16)

    def norm_hop(number, who):
        return push(r.v_norm_sum, r.v_norm_in.at[number], r.nsend.at[number], r.nrecv.at[number], who)

    def first_norm():
        later.again = load(r.w_contract, r.v_one)
        later.active = load(r.active, r.v_grad)
        later.frames.wait()
        norm_back(first_sum, 0, hidden, False)
        for who in (spot.sib, spot.opp):
            pl.semaphore_signal(r.credit.at[6], inc=1, device_id=who, device_id_type=MESH)
        give(hidden, r.frames_out)
        for place in range(6):
            r.v_norm_sum[place : place + 1, :] = jnp.sum(
                r.v_norm_grads[place * 8 : place * 8 + 8, :], axis=0, keepdims=True
            )
        r.v_norm_sum[6:8, :] = jnp.zeros((2, width), F32)
        norm_hop(0, spot.sib).start()

    def norm_step(number, who):
        norm_hop(number, who).wait()
        r.v_norm_sum[...] += r.v_norm_in[number]

    def norm_sib():
        norm_step(0, spot.sib)
        norm_hop(1, spot.opp).start()

    def norm_opp():
        norm_step(1, spot.opp)
        norm_hop(2, spot.part).start()

    def norm_part():
        norm_step(2, spot.part)
        for k in (1, 2, 3):
            norm_hop(2 + k, spot.z_peer(k)).start()

    def norm_peers():
        for k in (1, 2, 3):
            norm_hop(2 + k, spot.z_peer(k)).wait()
        r.v_norm_sum[...] += r.v_norm_in[3] + r.v_norm_in[4] + r.v_norm_in[5]
        give(r.v_norm_sum, r.norm_out)

    def out_product():
        later.again.wait()
        later.active.wait()
        first_sum.drain()
        back_rows(r.v_grad, r.v_one)

    def out_start():
        pl.semaphore_wait(r.credit.at[6], 2)
        out_sum.start()

    def out_done():
        turn_one.drain()

        @pl.loop(0, rows // 16)
        def _(index):
            here = pl.ds(pl.multiple_of(index * 16, 16), 16)
            r.v_branch[here, :] = (out_sum.value(here) + r.v_two_rows[here, :].astype(F32)).astype(BF16)

        give(r.v_branch, r.block_out)

    steps = (
        up, third_back, third_sum.start, third_sum.relay, third_sum.finish,
        *(functools.partial(expand_grad, index) for index in range(4)),
        third_norm, turn_two.finish, crossed_back,
        crossed_sum.start, crossed_sum.relay, crossed_sum.finish,
        back_grad, cross, terms_share.start, terms_share.relay, terms_share.finish,
        second_back, second_sum.start, second_sum.relay, second_sum.finish,
        query_grad, keys_grad, text_start, text_sum.relay, text_done,
        second_norm, turn_one.finish, attended_back,
        attended_sum.start, attended_sum.relay, attended_sum.finish,
        outward_grad, attend, first_back, first_sum.start, first_sum.relay, first_sum.finish,
        *(functools.partial(inward_grad, index) for index in range(3)),
        first_norm, norm_sib, norm_opp, norm_part, norm_peers,
        out_product, out_start, out_sum.relay, out_sum.finish, out_done,
    )
    goals = [r.contract_out.at[:, index * wide : (index + 1) * wide] for index in range(4)]
    goals += [r.expand_out.at[:, index * wide : (index + 1) * wide] for index in range(4)]
    goals += [r.returning_out, r.keying_out, r.querying_out, r.outward_out]
    stores = []

    def store(number):
        goal = goals[number]
        slot = len(stores)
        if slot >= 4:
            stores[slot - 4].wait()
        columns = pl.ds(slot // 2 % 2 * 2 * wide, goal.shape[1])
        stage = r.v_slope.at[pl.ds(slot % 2 * 192, 192), columns]

        def keep(here, value):
            stage[here, :] = value

        reduces[number].finish(keep)
        stores.append(give(stage, goal))

    def inward_copy(kind):
        index = kind * 4 + blk
        src = r.v_left.at[kind * 192 : (kind + 1) * 192, 0:wide]
        place = lax.rem(index, 3)
        lines = pl.ds(pl.multiple_of(place * 192, 192), 192)
        return index // 3, place, src, r.v_right.at[lines, 0:wide]

    def hand_over(kind):
        owner, place, src, dst = inward_copy(kind)

        def keep(here, value):
            src[here, :] = value.astype(BF16)

        reduces[inward + kind].finish(keep)

        @pl.when(owner == blk)
        def _():
            pltpu.make_async_copy(src, dst, r.arecv.at[place]).start()

        @pl.when(owner != blk)
        def _():
            push(src, dst, r.asend.at[kind], r.arecv.at[place], (spot.grp, owner)).start()

    taken = [0] * len(reduces)
    for kind, number, *rest in BACKWARD_ORDER:
        if kind == 5:
            steps[number]()
            continue
        item = reduces[number]
        if kind == 0:
            if number >= inward:
                pl.semaphore_wait(r.credit.at[number - inward], 1)
            item.start()
        elif kind == 1:
            if number < 4 and sum(taken) == 0:
                for copy in later.own:
                    copy.wait()
            if number >= inward and taken[number] == 0:
                pl.semaphore_wait(r.credit.at[3 + number - inward], 3)
            item.take(*rest)
            taken[number] += 1
            if number < 3 and taken[number] == 4:
                pl.semaphore_signal(r.credit.at[number], inc=1, device_id=spot.part, device_id_type=MESH)
        elif kind == 2:
            item.pass_on(*rest)
        elif kind == 3:
            item.cross()
        elif number >= inward:
            hand_over(number - inward)
        else:
            store(number)
            for k in (1, 2, 3) if number < 3 else ():
                pl.semaphore_signal(
                    r.credit.at[3 + number], inc=1, device_id=spot.z_peer(k), device_id_type=MESH
                )
    for copy in stores[-4:]:
        copy.wait()
    for place in range(3):
        here = slice(place * wide, (place + 1) * wide)
        dst = r.v_right.at[place * 192 : (place + 1) * 192, 0:wide]
        home = lax.rem(blk * 3 + place, 4)

        @pl.when(home == blk)
        def _():
            pltpu.make_async_copy(dst, dst, r.arecv.at[place]).wait()

        @pl.when(home != blk)
        def _():
            push(dst, dst, r.asend.at[0], r.arecv.at[place], spot.sib).wait_recv()

        stage = r.v_slope.at[pl.ds(0, 192), pl.ds(place * wide, wide)]

        @pl.loop(0, 192 // 16)
        def _(index):
            lines = pl.ds(pl.multiple_of(index * 16, 16), 16)
            stage[lines, :] = dst[lines, :].astype(F32)

        give(stage, r.inward_out.at[:, here])
    for kind in range(3):
        owner, place, src, dst = inward_copy(kind)

        @pl.when(owner != blk)
        def _():
            push(src, dst, r.asend.at[kind], r.arecv.at[place], (spot.grp, owner)).wait_send()

    for item in reduces[3:]:
        item.drain()
    terms_share.drain()
    text_sum.drain()
    out_sum.drain()
    for copy in copies:
        if all(copy is not item for item in stores):
            copy.wait()


def backward(ahead, frames, text, table, incoming):
    rows, width = frames.shape
    length = rows * lax.axis_size("blk")
    wide = width // lax.axis_size("blk")
    shard = width // lax.axis_size("grp")
    feed = ahead.w_expand.shape[1]
    ids_col, ids_row = ids_of(table)
    out = dict(
        contract_out=((shard, feed), F32),
        expand_out=((shard, feed), F32),
        returning_out=((shard, wide), F32),
        keying_out=((shard, 2 * wide), F32),
        querying_out=((shard, wide), F32),
        outward_out=((shard, wide), F32),
        inward_out=((shard, 3 * wide), F32),
        frames_out=((rows, width), F32),
        block_out=((rows, width), BF16),
        text_out=((TEXT // 4, width), F32),
        norm_out=((8, width), F32),
    )
    square, turned, strip = (length, width), (width, length), (length, wide)
    vmem = dict(
        v_one=((width, feed), BF16),
        v_two=((width, feed), BF16),
        g_contract=((width, feed), BF16),
        g_expand=((width, feed), BF16),
        g_rest=((width, 5 * wide), BF16),
        v_left=(turned, BF16),
        v_right=(turned, BF16),
        v_grad=(square, BF16),
        v_up=(square, BF16),
        v_part=(square, BF16),
        v_slope=(square, F32),
        v_joint=((length, 3 * wide), BF16),
        v_text=((TEXT, 2 * wide), BF16),
        v_terms=((2 * TEXT, width), BF16),
        v_text_part=((TEXT, width), BF16),
        v_text_out=((TEXT // 4, width), F32),
        near_rows=((2, rows, width), BF16),
        far_rows=((rows, width), BF16),
        near_cols=((2, length, wide), BF16),
        far_cols=(strip, BF16),
        near_text=((2, TEXT // 4, width), BF16),
        far_text=((TEXT // 4, width), BF16),
        v_branch=((rows, width), BF16),
        v_rows=((rows, width), BF16),
        v_two_rows=((rows, width), BF16),
        v_norm=((8, width), F32),
        v_norm_grads=((48, width), F32),
        v_norm_sum=((8, width), F32),
        v_norm_in=((6, 8, width), F32),
        v_key_sum=((length, 128), F32),
        v_value_sum=((length, 128), F32),
    )
    vmem.update(
        y_contract=((4, shard, feed), BF16),
        y_expand=((4, shard, feed), BF16),
        y_back=((1, shard, wide), BF16),
        y_keys=((4, shard, 2 * wide), BF16),
        y_query=((4, shard, wide), BF16),
        y_outward=((1, shard, wide), BF16),
        z_contract=((5, shard, feed), BF16),
        z_expand=((5, shard, feed), BF16),
        z_back=((10, shard, wide), BF16),
        z_keys=((5, shard, 2 * wide), BF16),
        z_query=((5, shard, wide), BF16),
        z_outward=((10, shard, wide), BF16),
    )
    sems = dict(
        ysend=(15, 4),
        yrecv=(15, 4),
        zsend=(15, 8),
        zrecv=(15, 10),
        bsend=(7, 3),
        brecv=(7, 3),
        tsend=(2, 3),
        trecv=(2, 3),
        csend=(1, 3),
        crecv=(1, 3),
        nsend=(6,),
        nrecv=(6,),
        asend=(3,),
        arecv=(3,),
        local=(32,),
        stored=(24,),
    )
    inner = dict(text=text, ids_col=ids_col, ids_row=ids_row)
    outer = dict(frames=frames, incoming=incoming, **vars(ahead))
    del outer["aligned"]
    return run_kernel(backward_kernel, 2, inner, outer, out, vmem, sems, dict(credit=(7,)))


def closing_kernel(count, *refs):
    given, out, held, sems = refs[:count], refs[count : 2 * count], refs[2 * count : -1], refs[-1]
    loads = [
        pltpu.make_async_copy(src, dst, sems.at[0, index])
        for index, (src, dst) in enumerate(zip(given, held))
    ]
    stores = [
        pltpu.make_async_copy(src, dst, sems.at[1, index])
        for index, (src, dst) in enumerate(zip(held, out))
    ]
    for copy in loads:
        copy.start()
    for load, store in zip(loads, stores):
        load.wait()
        store.start()
    for copy in stores:
        copy.wait()


def closing(*items):
    anywhere = pl.BlockSpec(memory_space=pl.ANY)
    count = len(items)
    return pl.pallas_call(
        functools.partial(closing_kernel, count),
        out_shape=[jax.ShapeDtypeStruct(item.shape, item.dtype) for item in items],
        in_specs=[anywhere] * count,
        out_specs=[anywhere] * count,
        scratch_shapes=[pltpu.VMEM(item.shape, item.dtype) for item in items]
        + [pltpu.SemaphoreType.DMA((2, count))],
    )(*items)


def tp_shards(
    frames,
    text_states,
    block_table,
    inward,
    outward,
    querying,
    keying,
    returning,
    expand,
    contract,
    gains,
    shifts,
    out_grad,
):
    ahead = forward(
        frames[0],
        text_states[0],
        block_table,
        jnp.pad(jnp.concatenate([gains, shifts], axis=0), ((0, 10), (0, 80))),
        out_grad[0],
        dict(
            inward=inward,
            outward=outward,
            query=querying,
            keys=keying,
            back=returning,
            expand=expand,
            contract=contract.T,
        ),
    )
    done = backward(ahead, frames[0], text_states[0], block_table, out_grad[0])
    share = gains.shape[1]
    place = (lax.axis_index("grp") * lax.axis_size("blk") + lax.axis_index("blk")) * share
    norm_grads = lax.dynamic_slice_in_dim(done.norm_out, place, share, 1)
    (
        contract_grad,
        expand_grad,
        returning_grad,
        keying_grad,
        querying_grad,
        outward_grad,
        inward_grad,
        frames_grad,
        block_out,
        text_grad,
    ) = closing(
        done.contract_out,
        done.expand_out,
        done.returning_out,
        done.keying_out,
        done.querying_out,
        done.outward_out,
        done.inward_out,
        done.frames_out,
        done.block_out,
        done.text_out,
    )
    return (
        block_out[None],
        frames_grad[None],
        text_grad[None],
        inward_grad,
        outward_grad,
        querying_grad,
        keying_grad,
        returning_grad,
        expand_grad,
        contract_grad.T,
        norm_grads[:3],
        norm_grads[3:6],
    )


def solution(mesh):
    small = mesh.shape["grp"] == 8 and mesh.shape["blk"] == 4
    return jax.shard_map(
        tp_shards if small else shards,
        mesh=mesh,
        in_specs=(
            P("grp", "blk", None),
            P("grp", None, None),
            P("grp", None),
            P("grp", "blk"),
            P("grp", "blk"),
            P("grp", "blk"),
            P("grp", "blk"),
            P("grp", "blk"),
            P("grp", "blk"),
            P("blk", "grp"),
            P(None, ("grp", "blk")),
            P(None, ("grp", "blk")),
            P("grp", "blk", None),
        ),
        out_specs=(
            P("grp", "blk", None),
            P("grp", "blk", None),
            P("grp", "blk", None),
            P("grp", "blk"),
            P("grp", "blk"),
            P("grp", "blk"),
            P("grp", "blk"),
            P("grp", "blk"),
            P("grp", "blk"),
            P("blk", "grp"),
            P(None, ("grp", "blk")),
            P(None, ("grp", "blk")),
        ),
        check_vma=False,
    )
```

```python
import functools
import math

import jax
import jax.numpy as jnp
from jax import lax
from jax.experimental import pallas as pl
from jax.experimental.pallas import tpu as pltpu
from jax.sharding import PartitionSpec as P

HEADS = 24
HEAD = 64
TEXT = 64
SEG = 64


def layer_norm(values, gain, shift):
    center = values - jnp.mean(values, axis=-1, keepdims=True)
    spread = jnp.mean(center * center, axis=-1, keepdims=True)
    return center * lax.rsqrt(spread + 1e-05) * gain + shift


def norm_pull(values, gain, shift, incoming):
    unused, pullback = jax.vjp(layer_norm, values, gain, shift)
    return pullback(incoming)


def gelu_slope(upward):
    return (
        0.5 * (1.0 + lax.erf(upward * 0.7071067811865476))
        + upward * jnp.exp(-0.5 * upward * upward) * 0.3989422804014327
    )


def gather_weights(inward, outward, querying, keying, returning, expand, contract, gains, shifts):
    inward, outward, querying, keying, returning, expand, contract, gains, shifts = (
        lax.all_gather(inward, "blk", axis=1, tiled=True),
        lax.all_gather(outward, "blk", axis=1, tiled=True),
        lax.all_gather(querying, "blk", axis=1, tiled=True),
        lax.all_gather(keying, "blk", axis=1, tiled=True),
        lax.all_gather(returning, "blk", axis=1, tiled=True),
        lax.all_gather(expand, "blk", axis=1, tiled=True),
        lax.all_gather(contract, "blk", axis=0, tiled=True),
        lax.all_gather(gains, "blk", axis=1, tiled=True),
        lax.all_gather(shifts, "blk", axis=1, tiled=True),
    )
    return (
        lax.all_gather(inward, "grp", axis=0, tiled=True),
        lax.all_gather(outward, "grp", axis=0, tiled=True),
        lax.all_gather(querying, "grp", axis=0, tiled=True),
        lax.all_gather(keying, "grp", axis=0, tiled=True),
        lax.all_gather(returning, "grp", axis=0, tiled=True),
        lax.all_gather(expand, "grp", axis=0, tiled=True),
        lax.all_gather(contract, "grp", axis=1, tiled=True),
        lax.all_gather(gains, "grp", axis=1, tiled=True),
        lax.all_gather(shifts, "grp", axis=1, tiled=True),
    )


def shards(
    frames,
    text_states,
    block_table,
    inward,
    outward,
    querying,
    keying,
    returning,
    expand,
    contract,
    gains,
    shifts,
    out_grad,
):
    (
        full_inward,
        full_outward,
        full_query,
        full_keys,
        full_return,
        full_expand,
        full_contract,
        full_gains,
        full_shifts,
    ) = gather_weights(
        inward, outward, querying, keying, returning, expand, contract, gains, shifts
    )
    width = frames.shape[2]
    rows = frames.shape[1]
    length = block_table.shape[1] * SEG
    group = lax.axis_size("blk")
    member = lax.axis_index("blk")
    span = math.gcd(length, 512)
    steps = length // span
    gain_rows = full_gains.astype(jnp.float32)
    shift_rows = full_shifts.astype(jnp.float32)
    key_frames = (
        block_table[0][:, None] * SEG + jnp.arange(SEG, dtype=jnp.int32)[None, :]
    ).reshape(length)
    own_frames = lax.dynamic_slice_in_dim(key_frames, member * rows, rows, 0)
    inputs = frames[0].astype(jnp.float32)
    first = layer_norm(inputs, gain_rows[0], shift_rows[0]).astype(jnp.bfloat16)
    joint = jnp.dot(first, full_inward, preferred_element_type=jnp.float32).astype(jnp.bfloat16)
    queries = joint[:, :width].reshape(rows, HEADS, HEAD)
    pairs = lax.all_gather(joint[:, width:], "blk", axis=0, tiled=True)
    pair_blocks = pairs.reshape(steps, span, 2 * width)
    frame_blocks = key_frames.reshape(steps, span)

    def scores_of(block, block_frames):
        keys = block[:, :width].reshape(span, HEADS, HEAD)
        raw = jnp.einsum("qhd,khd->hqk", queries, keys, preferred_element_type=jnp.float32) * 0.125
        allowed = block_frames[None, :] <= own_frames[:, None]
        return jnp.where(allowed[None], raw, -1e30)

    def stat_step(carry, items):
        peak, total = carry
        scores = scores_of(items[0], items[1])
        higher = jnp.maximum(peak, jnp.max(scores, axis=2))
        total = total * jnp.exp(peak - higher) + jnp.sum(
            jnp.exp(scores - higher[:, :, None]), axis=2
        )
        return ((higher, total), None)

    start_peak = jnp.full((HEADS, rows), -1e30, jnp.float32)
    (peak, total), unused = lax.scan(
        stat_step, (start_peak, jnp.zeros((HEADS, rows), jnp.float32)), (pair_blocks, frame_blocks)
    )
    log_total = peak + jnp.log(total)

    def out_step(carry, items):
        weighting = jnp.exp(scores_of(items[0], items[1]) - log_total[:, :, None]).astype(
            jnp.bfloat16
        )
        values = items[0][:, width:].reshape(span, HEADS, HEAD)
        return (
            carry
            + jnp.einsum("hqk,khd->qhd", weighting, values, preferred_element_type=jnp.float32),
            None,
        )

    mixed, unused = lax.scan(
        out_step, jnp.zeros((rows, HEADS, HEAD), jnp.float32), (pair_blocks, frame_blocks)
    )
    attended = mixed.reshape(rows, width).astype(jnp.bfloat16)
    hidden_one = inputs + jnp.dot(attended, full_outward, preferred_element_type=jnp.float32)
    second = layer_norm(hidden_one, gain_rows[1], shift_rows[1]).astype(jnp.bfloat16)
    cross_query = jnp.dot(second, full_query, preferred_element_type=jnp.float32).astype(
        jnp.bfloat16
    )
    cross_heads = cross_query.reshape(rows, HEADS, HEAD)
    text = text_states[0]
    text_pairs = jnp.dot(text, full_keys, preferred_element_type=jnp.float32).astype(jnp.bfloat16)
    text_keys = text_pairs[:, :width].reshape(TEXT, HEADS, HEAD)
    text_values = text_pairs[:, width:].reshape(TEXT, HEADS, HEAD)
    cross_scores = (
        jnp.einsum("qhd,khd->hqk", cross_heads, text_keys, preferred_element_type=jnp.float32)
        * 0.125
    )
    cross_soft = jax.nn.softmax(cross_scores, axis=2)
    cross_weighting = cross_soft.astype(jnp.bfloat16)
    crossed = (
        jnp.einsum("hqk,khd->qhd", cross_weighting, text_values, preferred_element_type=jnp.float32)
        .reshape(rows, width)
        .astype(jnp.bfloat16)
    )
    hidden_two = hidden_one + jnp.dot(crossed, full_return, preferred_element_type=jnp.float32)
    third = layer_norm(hidden_two, gain_rows[2], shift_rows[2]).astype(jnp.bfloat16)
    upward = jnp.dot(third, full_expand, preferred_element_type=jnp.float32)
    activated = jax.nn.gelu(upward, approximate=False).astype(jnp.bfloat16)
    branch = jnp.dot(activated, full_contract, preferred_element_type=jnp.float32)
    block_out = (hidden_two + branch).astype(jnp.bfloat16)[None]
    (
        full_inward,
        full_outward,
        full_query,
        full_keys,
        full_return,
        full_expand,
        full_contract,
        full_gains,
        full_shifts,
    ) = gather_weights(
        inward, outward, querying, keying, returning, expand, contract, gains, shifts
    )
    incoming = out_grad[0].astype(jnp.float32)
    branch_grad = out_grad[0]
    act_grad = jnp.dot(branch_grad, full_contract.T, preferred_element_type=jnp.float32)
    contract_grad = jnp.dot(activated.T, branch_grad, preferred_element_type=jnp.float32)
    up_grad = (act_grad * gelu_slope(upward)).astype(jnp.bfloat16)
    expand_grad = jnp.dot(third.T, up_grad, preferred_element_type=jnp.float32)
    third_grad = jnp.dot(up_grad, full_expand.T, preferred_element_type=jnp.float32)
    two_grad, gain_two, shift_two = norm_pull(hidden_two, gain_rows[2], shift_rows[2], third_grad)
    hidden_two_grad = incoming + two_grad
    branch_two = hidden_two_grad.astype(jnp.bfloat16)
    crossed_grad = jnp.dot(branch_two, full_return.T, preferred_element_type=jnp.float32).astype(
        jnp.bfloat16
    )
    crossed_grad = crossed_grad.reshape(rows, HEADS, HEAD)
    prob_grad = jnp.einsum(
        "qhd,khd->hqk", crossed_grad, text_values, preferred_element_type=jnp.float32
    )
    text_value_grad = jnp.einsum(
        "hqk,qhd->khd", cross_weighting, crossed_grad, preferred_element_type=jnp.float32
    )
    cross_score_grad = (
        cross_soft * (prob_grad - jnp.sum(prob_grad * cross_soft, axis=2, keepdims=True))
    ).astype(jnp.bfloat16)
    cross_query_grad = (
        (
            jnp.einsum(
                "hqk,khd->qhd", cross_score_grad, text_keys, preferred_element_type=jnp.float32
            )
            * 0.125
        )
        .reshape(rows, width)
        .astype(jnp.bfloat16)
    )
    text_key_grad = (
        jnp.einsum(
            "hqk,qhd->khd", cross_score_grad, cross_heads, preferred_element_type=jnp.float32
        )
        * 0.125
    )
    text_terms = jnp.concatenate(
        [text_key_grad.reshape(TEXT, width), text_value_grad.reshape(TEXT, width)], axis=1
    )
    text_share = lax.psum_scatter(
        text_terms.astype(jnp.bfloat16), "blk", scatter_dimension=0, tiled=True
    )
    share = TEXT // group
    text_grad = jnp.dot(text_share, full_keys.T, preferred_element_type=jnp.float32)[None]
    one_grad, gain_one, shift_one = norm_pull(
        hidden_one,
        gain_rows[1],
        shift_rows[1],
        jnp.dot(cross_query_grad, full_query.T, preferred_element_type=jnp.float32),
    )
    hidden_one_grad = hidden_two_grad + one_grad
    branch_one = hidden_one_grad.astype(jnp.bfloat16)
    attended_grad = jnp.dot(branch_one, full_outward.T, preferred_element_type=jnp.float32).astype(
        jnp.bfloat16
    )
    attended_grad = attended_grad.reshape(rows, HEADS, HEAD)
    delta = jnp.sum(attended_grad.astype(jnp.float32) * mixed, axis=2).T

    def back_step(carry, items):
        block = items[0]
        weighting = jnp.exp(scores_of(block, items[1]) - log_total[:, :, None])
        keys = block[:, :width].reshape(span, HEADS, HEAD)
        values = block[:, width:].reshape(span, HEADS, HEAD)
        value_grad = jnp.einsum(
            "hqk,qhd->khd",
            weighting.astype(jnp.bfloat16),
            attended_grad,
            preferred_element_type=jnp.float32,
        )
        weight_grad = jnp.einsum(
            "qhd,khd->hqk", attended_grad, values, preferred_element_type=jnp.float32
        )
        score_grad = (weighting * (weight_grad - delta[:, :, None])).astype(jnp.bfloat16)
        carry = carry + jnp.einsum(
            "hqk,khd->qhd", score_grad, keys, preferred_element_type=jnp.float32
        )
        key_grad = (
            jnp.einsum("hqk,qhd->khd", score_grad, queries, preferred_element_type=jnp.float32)
            * 0.125
        )
        return (
            carry,
            jnp.concatenate(
                [key_grad.reshape(span, width), value_grad.reshape(span, width)], axis=1
            ),
        )

    query_sum, pair_terms = lax.scan(
        back_step, jnp.zeros((rows, HEADS, HEAD), jnp.float32), (pair_blocks, frame_blocks)
    )
    pair_grad = lax.psum_scatter(
        pair_terms.reshape(length, 2 * width).astype(jnp.bfloat16),
        "blk",
        scatter_dimension=0,
        tiled=True,
    )
    joint_grad = jnp.concatenate(
        [(query_sum * 0.125).reshape(rows, width).astype(jnp.bfloat16), pair_grad], axis=1
    )
    zero_grad, gain_zero, shift_zero = norm_pull(
        inputs,
        gain_rows[0],
        shift_rows[0],
        jnp.dot(joint_grad, full_inward.T, preferred_element_type=jnp.float32),
    )
    frames_grad = (hidden_one_grad + zero_grad)[None]
    across = lax.axis_size("grp")
    gains_grad = (
        jnp.stack([gain_zero, gain_one, gain_two])
        .reshape(3, across, group, -1)
        .transpose(0, 2, 1, 3)
        .reshape(3, width)
    )
    shifts_grad = (
        jnp.stack([shift_zero, shift_one, shift_two])
        .reshape(3, across, group, -1)
        .transpose(0, 2, 1, 3)
        .reshape(3, width)
    )
    expand_grad, contract_grad = (
        lax.psum_scatter(
            expand_grad.astype(jnp.bfloat16), "blk", scatter_dimension=1, tiled=True
        ).astype(jnp.float32),
        lax.psum_scatter(
            contract_grad.astype(jnp.bfloat16), "blk", scatter_dimension=0, tiled=True
        ).astype(jnp.float32),
    )
    own_text = lax.dynamic_slice_in_dim(text, member * share, share, 0)
    inward_grad = jnp.dot(first.T, joint_grad, preferred_element_type=jnp.float32)
    outward_grad = jnp.dot(attended.T, branch_one, preferred_element_type=jnp.float32)
    querying_grad = jnp.dot(second.T, cross_query_grad, preferred_element_type=jnp.float32)
    keying_grad = jnp.dot(own_text.T, text_share, preferred_element_type=jnp.float32)
    returning_grad = jnp.dot(crossed.T, branch_two, preferred_element_type=jnp.float32)
    (
        inward_grad,
        outward_grad,
        querying_grad,
        keying_grad,
        returning_grad,
        gains_grad,
        shifts_grad,
    ) = (
        lax.psum_scatter(
            inward_grad.astype(jnp.bfloat16), "blk", scatter_dimension=1, tiled=True
        ).astype(jnp.float32),
        lax.psum_scatter(
            outward_grad.astype(jnp.bfloat16), "blk", scatter_dimension=1, tiled=True
        ).astype(jnp.float32),
        lax.psum_scatter(
            querying_grad.astype(jnp.bfloat16), "blk", scatter_dimension=1, tiled=True
        ).astype(jnp.float32),
        lax.psum_scatter(
            keying_grad.astype(jnp.bfloat16), "blk", scatter_dimension=1, tiled=True
        ).astype(jnp.float32),
        lax.psum_scatter(
            returning_grad.astype(jnp.bfloat16), "blk", scatter_dimension=1, tiled=True
        ).astype(jnp.float32),
        lax.psum_scatter(
            gains_grad.astype(jnp.bfloat16), "blk", scatter_dimension=1, tiled=True
        ).astype(jnp.float32),
        lax.psum_scatter(
            shifts_grad.astype(jnp.bfloat16), "blk", scatter_dimension=1, tiled=True
        ).astype(jnp.float32),
    )
    (
        inward_grad,
        outward_grad,
        querying_grad,
        keying_grad,
        returning_grad,
        expand_grad,
        contract_grad,
        gains_grad,
        shifts_grad,
    ) = (
        lax.psum_scatter(
            inward_grad.astype(jnp.bfloat16), "grp", scatter_dimension=0, tiled=True
        ).astype(jnp.float32),
        lax.psum_scatter(
            outward_grad.astype(jnp.bfloat16), "grp", scatter_dimension=0, tiled=True
        ).astype(jnp.float32),
        lax.psum_scatter(
            querying_grad.astype(jnp.bfloat16), "grp", scatter_dimension=0, tiled=True
        ).astype(jnp.float32),
        lax.psum_scatter(
            keying_grad.astype(jnp.bfloat16), "grp", scatter_dimension=0, tiled=True
        ).astype(jnp.float32),
        lax.psum_scatter(
            returning_grad.astype(jnp.bfloat16), "grp", scatter_dimension=0, tiled=True
        ).astype(jnp.float32),
        lax.psum_scatter(
            expand_grad.astype(jnp.bfloat16), "grp", scatter_dimension=0, tiled=True
        ).astype(jnp.float32),
        lax.psum_scatter(
            contract_grad.astype(jnp.bfloat16), "grp", scatter_dimension=1, tiled=True
        ).astype(jnp.float32),
        lax.psum_scatter(
            gains_grad.astype(jnp.bfloat16), "grp", scatter_dimension=1, tiled=True
        ).astype(jnp.float32),
        lax.psum_scatter(
            shifts_grad.astype(jnp.bfloat16), "grp", scatter_dimension=1, tiled=True
        ).astype(jnp.float32),
    )
    return (
        block_out,
        frames_grad,
        text_grad,
        inward_grad,
        outward_grad,
        querying_grad,
        keying_grad,
        returning_grad,
        expand_grad,
        contract_grad,
        gains_grad,
        shifts_grad,
    )


MESH = pl.DeviceIdType.MESH
BF16, F32 = jnp.bfloat16, jnp.float32


class Bag:
    def __init__(self, **items):
        self.__dict__.update(items)


def named(keys, items):
    return Bag(**dict(zip(keys, items)))


class Spot:
    def __init__(self):
        grp, blk = lax.axis_index("grp"), lax.axis_index("blk")
        self.grp, self.blk = grp, blk
        self.z, self.y = grp // 2, lax.rem(grp, 2)
        self.x, self.core = blk // 2, lax.rem(blk, 2)
        self.sib_blk = self.x * 2 + 1 - self.core
        self.opp_blk = (1 - self.x) * 2 + self.core
        self.sib = (grp, self.sib_blk)
        self.opp = (grp, self.opp_blk)
        self.part = (self.z * 2 + 1 - self.y, blk)
        self.up = ((self.z + 1) * 2 + self.y, blk)
        self.down = ((self.z - 1) * 2 + self.y, blk)

        self.far_blk = (1 - self.x) * 2 + 1 - self.core

    def z_peer(self, k):
        return (lax.rem(self.z + k, 4) * 2 + self.y, self.blk)

    def greet_all(self):
        barrier = pltpu.get_barrier_semaphore()
        peers = [self.z_peer(k) for k in (1, 2, 3)]
        for who in [self.sib, self.opp, (self.grp, self.far_blk), self.part] + peers:
            pl.semaphore_signal(barrier, inc=1, device_id=who, device_id_type=MESH)
        pl.semaphore_wait(barrier, 7)

    def greet(self):
        barrier = pltpu.get_barrier_semaphore()
        for who in (self.sib, self.opp, self.part):
            pl.semaphore_signal(barrier, inc=1, device_id=who, device_id_type=MESH)

        @pl.when(self.z > 0)
        def _():
            pl.semaphore_signal(barrier, inc=1, device_id=self.down, device_id_type=MESH)

        @pl.when(self.z < 3)
        def _():
            pl.semaphore_signal(barrier, inc=1, device_id=self.up, device_id_type=MESH)

        ends = (self.z == 0) | (self.z == 3)

        @pl.when(ends)
        def _():
            pl.semaphore_wait(barrier, 4)

        @pl.when(jnp.logical_not(ends))
        def _():
            pl.semaphore_wait(barrier, 5)


def push(src, dst, send, recv, who):
    return pltpu.make_async_remote_copy(
        src_ref=src, dst_ref=dst, send_sem=send, recv_sem=recv, device_id=who, device_id_type=MESH
    )


class Gather:
    def __init__(self, spot, shard, full, zsend, zrecv, ysend, yrecv, near, spread):
        self.spot, self.shard, self.full = spot, shard, full
        self.zsend, self.zrecv, self.ysend, self.yrecv, self.near = zsend, zrecv, ysend, yrecv, near
        self.spread = spread
        self.size = shard.shape[0]

    def rows(self, z, flip=0):
        spot = self.spot
        row = z * 2 + (1 - spot.y if flip else spot.y)
        return self.full.at[pl.ds(pl.multiple_of(row * self.size, self.size), self.size)]

    def z_copy(self, src, dst, k, side, flip):
        slot = (flip * 2 + side) * 3 + k - 1
        who = self.spot.up if side else self.spot.down
        return push(src, dst, self.zsend.at[slot], self.zrecv.at[slot], who)

    def y_copy(self, src, dst, slot):
        return push(src, dst, self.ysend.at[slot], self.yrecv.at[slot], self.spot.part)

    def launch(self, src, flip):
        spot = self.spot

        @pl.when(spot.z > 0)
        def _():
            self.z_copy(src, self.rows(spot.z, flip), 1, 0, flip).start()

        @pl.when(spot.z < 3)
        def _():
            self.z_copy(src, self.rows(spot.z, flip), 1, 1, flip).start()

    def start(self):
        here = self.rows(self.spot.z)
        self.y_copy(self.shard, here, 0).start()
        self.launch(self.shard, 0)
        pltpu.make_async_copy(self.shard, here, self.near).start()

    def pass_on(self):
        other = self.rows(self.spot.z, 1)
        self.y_copy(other, other, 0).wait_recv()
        self.launch(other, 1)

    def relay(self, k, side, flip):
        spot = self.spot
        src_z = spot.z - k if side else spot.z + k
        block = self.rows(src_z, flip)

        @pl.when(src_z >= 0 if side else src_z <= 3)
        def _():
            self.z_copy(block, block, k, side, flip).wait_recv()
            if k < 3:

                @pl.when(spot.z < 3 if side else spot.z > 0)
                def _():
                    self.z_copy(block, block, k + 1, side, flip).start()

            if not self.spread:
                self.y_copy(block, block, 1 + side * 3 + k - 1).start()

    def finish(self):
        spot = self.spot
        pltpu.make_async_copy(self.shard, self.rows(spot.z), self.near).wait()
        if self.spread:
            return
        self.y_copy(self.shard, self.rows(spot.z, 1), 0).wait_recv()
        for side in (0, 1):
            for k in (1, 2, 3):
                src_z = spot.z - k if side else spot.z + k
                block = self.rows(src_z, 1)

                @pl.when(src_z >= 0 if side else src_z <= 3)
                def _():
                    self.y_copy(block, block, 1 + side * 3 + k - 1).wait_recv()

    def drain(self):
        spot = self.spot
        self.y_copy(self.shard, self.rows(spot.z), 0).wait_send()
        for side in (0, 1):
            for k in (1, 2, 3):
                src_z = spot.z - k if side else spot.z + k
                sent_z = spot.z - k + 1 if side else spot.z + k - 1
                block = self.rows(spot.z)
                if not self.spread:

                    @pl.when(src_z >= 0 if side else src_z <= 3)
                    def _():
                        self.y_copy(block, block, 1 + side * 3 + k - 1).wait_send()

                for flip in (0, 1) if self.spread else (0,):

                    @pl.when((spot.z < 3) & (sent_z >= 0) if side else (spot.z > 0) & (sent_z <= 3))
                    def _():
                        self.z_copy(block, block, k, side, flip).wait_send()


class Share:
    def __init__(self, spot, own, where, send, recv):
        self.spot, self.own, self.where, self.send, self.recv = spot, own, where, send, recv

    def first(self):
        return push(
            self.own, self.where(self.spot.blk), self.send.at[0], self.recv.at[0], self.spot.opp
        )

    def second(self):
        return push(
            self.own, self.where(self.spot.blk), self.send.at[1], self.recv.at[1], self.spot.sib
        )

    def third(self):
        passed = self.where(self.spot.opp_blk)
        return push(passed, passed, self.send.at[2], self.recv.at[2], self.spot.sib)

    def start(self):
        self.first().start()
        self.second().start()

    def relay(self):
        self.first().wait_recv()
        self.third().start()

    def finish(self):
        self.second().wait_recv()
        self.third().wait_recv()

    def drain(self):
        self.first().wait_send()
        self.second().wait_send()
        self.third().wait_send()


def dot(left, right):
    return jnp.dot(left, right, preferred_element_type=F32)


def dot_t(left, right):
    return lax.dot_general(left, right, (((1,), (1,)), ((), ())), preferred_element_type=F32)


def tiles(count, size, body):
    @pl.loop(0, count)
    def _(step):
        body(pl.ds(pl.multiple_of(step * size, size), size))


def norm_block(values, gain, shift):
    center = values - jnp.mean(values, axis=1, keepdims=True)
    spread = jnp.mean(center * center, axis=1, keepdims=True)
    return center * lax.rsqrt(spread + 1e-05) * gain + shift


FORWARD_ORDER = (
    (0, 1), (0, 0), (3, 28), (0, 2), (2, 0, 1, 0, 0), (2, 0, 1, 1, 0), (2, 1, 1, 0, 0),
    (2, 1, 1, 1, 0), (2, 2, 1, 0, 0), (2, 2, 1, 1, 0), (2, 0, 2, 1, 0), (2, 0, 2, 0, 0), (0, 3),
    (3, 29), (2, 1, 2, 1, 0), (3, 31), (2, 2, 2, 0, 0), (2, 2, 2, 1, 0), (2, 1, 2, 0, 0),
    (2, 0, 3, 1, 0), (3, 30), (2, 0, 3, 0, 0), (0, 4), (2, 3, 1, 1, 0), (2, 3, 1, 0, 0),
    (2, 2, 3, 0, 0), (2, 1, 3, 1, 0), (2, 2, 3, 1, 0), (2, 1, 3, 0, 0), (3, 0), (3, 32),
    (2, 4, 1, 1, 0), (2, 3, 2, 0, 0), (2, 3, 2, 1, 0), (2, 4, 1, 0, 0), (0, 5), (2, 4, 2, 1, 0),
    (2, 3, 3, 0, 0), (3, 33), (3, 36), (2, 3, 3, 1, 0), (2, 4, 2, 0, 0), (0, 6), (2, 5, 1, 0, 0),
    (2, 5, 1, 1, 0), (2, 4, 3, 1, 0), (2, 4, 3, 0, 0), (2, 6, 1, 1, 0), (2, 6, 1, 0, 0),
    (2, 5, 2, 1, 0), (2, 5, 2, 0, 0), (0, 7), (0, 8), (2, 6, 2, 1, 0), (2, 6, 2, 0, 0),
    (2, 5, 3, 1, 0), (2, 5, 3, 0, 0), (2, 7, 1, 1, 0), (2, 7, 1, 0, 0), (3, 1), (3, 2), (3, 3),
    (2, 6, 3, 1, 0), (2, 8, 1, 0, 0), (2, 6, 3, 0, 0), (2, 7, 2, 1, 0), (2, 7, 2, 0, 0), (0, 9),
    (2, 8, 1, 1, 0), (0, 10), (2, 7, 3, 1, 0), (2, 8, 2, 0, 0), (3, 4), (2, 9, 1, 1, 0),
    (2, 7, 3, 0, 0), (3, 5), (3, 6), (3, 7), (2, 8, 2, 1, 0), (2, 9, 1, 0, 0), (0, 11), (3, 34),
    (2, 10, 1, 1, 0), (2, 10, 1, 0, 0), (1, 8), (3, 10), (3, 11), (2, 9, 2, 1, 0),
    (2, 8, 3, 0, 0), (3, 8), (3, 9), (3, 12), (3, 13), (2, 8, 3, 1, 0), (2, 9, 2, 0, 0), (3, 14),
    (2, 11, 1, 0, 0), (2, 10, 2, 0, 0), (0, 12), (3, 15), (3, 16), (2, 8, 1, 1, 1), (3, 17),
    (2, 8, 1, 0, 1), (0, 13), (2, 10, 2, 1, 0), (2, 11, 1, 1, 0), (2, 9, 3, 0, 0),
    (2, 9, 3, 1, 0), (2, 11, 2, 0, 0), (2, 12, 1, 1, 0), (3, 18), (2, 10, 3, 0, 0), (3, 19),
    (2, 8, 2, 1, 1), (2, 12, 1, 0, 0), (3, 20), (3, 21), (2, 13, 1, 1, 0), (3, 35),
    (2, 8, 2, 0, 1), (2, 10, 3, 1, 0), (2, 11, 2, 1, 0), (2, 13, 1, 0, 0), (2, 11, 3, 0, 0),
    (2, 12, 2, 1, 0), (3, 22), (2, 12, 2, 0, 0), (3, 23), (2, 8, 3, 1, 1), (3, 24),
    (2, 8, 3, 0, 1), (2, 13, 2, 1, 0), (2, 11, 3, 1, 0), (2, 13, 2, 0, 0), (3, 25),
    (2, 12, 3, 0, 0), (2, 12, 3, 1, 0), (2, 13, 3, 0, 0), (2, 13, 3, 1, 0), (3, 26), (3, 27),
)


def forward_kernel(names, *refs):
    r = named(names, refs)
    spot = Spot()
    rows, width = r.frames.shape
    length = r.x_all.shape[0]
    wide = r.outward.shape[1]
    blk = spot.blk
    outs = []

    def save(src, dst):
        copy = pltpu.make_async_copy(src, dst, r.local.at[len(outs)])
        copy.start()
        outs.append(copy)
        return copy

    def lanes(index, size):
        return pl.ds(pl.multiple_of(index * size, 128), size)

    def row_block(ref):
        return lambda index: ref.at[pl.ds(pl.multiple_of(index * rows, rows), rows)]

    def col_block(ref, size):
        return lambda index: ref.at[:, lanes(index, size)]

    def share(number, own, where):
        return Share(spot, own, where, r.bsend.at[number], r.brecv.at[number])

    gathers = []

    def gather(shard, full, spread):
        wide = full.shape[1] // len(spread)
        first = len(gathers)
        for number, flag in enumerate(spread):
            here = slice(number * wide, (number + 1) * wide)
            sems = (item.at[first + number] for item in (r.zsend, r.zrecv, r.ysend, r.yrecv, r.near))
            gathers.append(Gather(spot, shard.at[:, here], full.at[:, here], *sems, flag))
        return gathers[first:]

    g_norms = gather(r.v_norms, r.v_norm_all, (False,))
    g_outward = gather(r.outward, r.v_outward, (False,))
    g_inward = gather(r.aligned, r.v_inward, (False, False, False))
    g_query = gather(r.query, r.v_query, (False,))
    g_keys = gather(r.keys, r.v_keys, (False,))
    g_back = gather(r.back, r.v_back, (False,))
    g_expand = gather(r.expand, r.v_expand, (True, False))
    g_contract = gather(r.contract, r.v_contract, (False, False, False, False))

    spot.greet()

    def piece(part):
        index = blk * 3 + part
        owner = lax.rem(index, 4)
        return owner, index // 4

    def aligned_copy(part):
        owner, kind = piece(part)
        src = r.inward.at[:, part * wide : (part + 1) * wide]
        return owner, kind, src, r.aligned.at[:, lanes(kind, wide)]

    for part in range(3):
        owner, kind, src, dst = aligned_copy(part)

        @pl.when(owner == blk)
        def _():
            pltpu.make_async_copy(src, dst, r.arecv.at[kind]).start()

        @pl.when(owner != blk)
        def _():
            push(src, dst, r.asend.at[part], r.arecv.at[kind], (spot.grp, owner)).start()

    norm_share = share(0, r.norms, lambda index: r.v_norms.at[pl.ds(index * 16, 16)])
    norm_own = pltpu.make_async_copy(r.norms, r.v_norms.at[pl.ds(blk * 16, 16)], r.near.at[16])
    norm_own.start()
    norm_share.start()
    frame_share = share(1, r.frames, row_block(r.x_all))
    frame_own = pltpu.make_async_copy(r.frames, row_block(r.x_all)(blk), r.near.at[17])
    frame_own.start()
    frame_share.start()
    grad_share = share(2, r.incoming, row_block(r.g_all))
    grad_own = pltpu.make_async_copy(r.incoming, row_block(r.g_all)(blk), r.near.at[18])
    attended_share = share(3, col_block(r.s_attended, wide)(blk), col_block(r.s_attended, wide))
    one_share = share(4, col_block(r.s_one_all, wide)(blk), col_block(r.s_one_all, wide))
    text_share = share(5, col_block(r.s_text, 2 * wide)(blk), col_block(r.s_text, 2 * wide))
    crossed_share = share(6, col_block(r.s_crossed, wide)(blk), col_block(r.s_crossed, wide))
    two_share = share(7, col_block(r.s_two_all, wide)(blk), col_block(r.s_two_all, wide))
    g_outward[0].start()
    for kind in range(3):
        dst = r.aligned.at[:, kind * wide : (kind + 1) * wide]
        home = (kind * 4 + blk) // 3

        @pl.when(home == blk)
        def _():
            pltpu.make_async_copy(dst, dst, r.arecv.at[kind]).wait()

        @pl.when(home != blk)
        def _():
            push(dst, dst, r.asend.at[0], r.arecv.at[kind], spot.sib).wait_recv()

    low = lax.broadcasted_iota(jnp.int32, (1, 128), 1) < 64
    kept = []

    def half(value, part):
        return jnp.where(low if part == 0 else jnp.logical_not(low), value, jnp.zeros_like(value))

    def finish(items):
        for item in items:
            item.finish()

    def turn_over(source, turned):
        def flip(block):
            turned[:, block] = source[block, :].T

        tiles(length // 128, 128, flip)

    def normed(source, index, turned):
        gain = r.v_norm_rows[index : index + 1, :]
        shift = r.v_norm_rows[3 + index : 4 + index, :]

        def body(block):
            result = norm_block(source[block, :].astype(F32), gain, shift).astype(BF16)
            r.a_all[block, :] = result

        tiles(length // 32, 32, body)
        turn_over(r.a_all, turned)

    def side_by_side():
        depth = 8 * 128
        line = lax.broadcasted_iota(jnp.int32, (depth, 384), 0)
        column = lax.broadcasted_iota(jnp.int32, (depth, 384), 1)
        inside = line & 127
        place = jnp.where((inside < 48) & (column == (line >> 7) * 48 + inside), 1.0, 0.0).astype(BF16)
        for pair in range(4):
            parts = [pl.ds(pair * 128 + part * 16, 16) for part in range(8)]
            left = jnp.concatenate([r.v_norm_all[part, :] for part in parts], axis=1)
            r.v_norm_rows[:, pair * 384 : (pair + 1) * 384] = dot(left, place)
        save(r.v_norm_rows, r.norm_all)

    def first_norm():
        finish(g_norms)
        side_by_side()
        normed(r.x_all, 0, r.t_first)
        save(r.t_first, r.first_t)

    def joint():
        finish(g_inward)
        save(r.v_inward, r.w_inward)

        def body(block):
            r.s_joint[:, block] = dot(r.a_all[...], r.v_inward[:, block]).astype(BF16)

        tiles(3, wide, body)
        save(r.s_joint, r.joint)

    def soft(scores):
        power = jnp.exp(scores - jnp.max(scores, axis=1, keepdims=True))
        return (power * (1.0 / jnp.sum(power, axis=1, keepdims=True))).astype(BF16)

    def attend():
        @pl.loop(0, 12)
        def _(step):
            pair, block = step // 4, lax.rem(step, 4)
            here = pl.ds(pl.multiple_of(block * 128, 128), 128)
            query = r.s_joint[here, lanes(pair, 128)]
            key = r.s_joint[:, lanes(pair + 3, 128)]
            value = r.s_joint[:, lanes(pair + 6, 128)]
            keep = r.ids_row[...] <= r.ids_col[here, :]
            results = []
            for part in (0, 1):
                scores = jnp.where(keep, dot_t(half(query, part), key) * 0.125, -1e30)
                results.append(dot(soft(scores), value))
            r.s_attended[here, lanes(blk * 3 + pair, 128)] = jnp.where(low, *results).astype(BF16)

    def hidden_one():
        finish(g_outward)
        save(r.v_outward, r.w_outward)
        own = r.x_all[:, lanes(blk, wide)].astype(F32)
        r.s_one[...] = dot(r.s_attended[...], r.v_outward[...]) + own
        r.s_one_all[:, lanes(blk, wide)] = r.s_one[...].astype(BF16)

    def one_here():
        one_share.finish()
        save(row_block(r.s_one_all)(blk), r.one_rows)

    def text_pairs():
        finish(g_keys)
        save(r.v_keys, r.w_keys)
        r.s_text[:, lanes(blk, 2 * wide)] = dot(r.text[...], r.v_keys[...]).astype(BF16)

    def second_norm():
        normed(r.s_one_all, 1, r.t_second)
        save(r.t_second, r.second_t)

    def cross_query():
        finish(g_query)
        save(r.v_query, r.w_query)
        r.s_query[...] = dot(r.a_all[...], r.v_query[...]).astype(BF16)
        save(r.s_query, r.cross_query)

    def text_here():
        text_share.finish()
        save(r.s_text, r.text_all)

    def cross():
        @pl.loop(0, 3)
        def _(pair):
            query = r.s_query[:, lanes(pair, 128)]
            key = r.s_text[:, lanes(blk * 3 + pair, 128)]
            value = r.s_text[:, lanes(12 + blk * 3 + pair, 128)]
            results = []
            for part in (0, 1):
                results.append(dot(soft(dot_t(half(query, part), key) * 0.125), value))
            r.s_crossed[:, lanes(blk * 3 + pair, 128)] = jnp.where(low, *results).astype(BF16)

    def hidden_two():
        finish(g_back)
        save(r.v_back, r.w_back)
        r.s_one[...] += dot(r.s_crossed[...], r.v_back[...])
        r.s_two_all[:, lanes(blk, wide)] = r.s_one[...].astype(BF16)

    def two_here():
        two_share.finish()
        save(row_block(r.s_two_all)(blk), r.two_rows)

    def third_norm():
        normed(r.s_two_all, 2, r.t_third)
        save(r.t_third, r.third_t)

    def upward():
        finish(g_expand)
        kept.append(save(r.v_expand, r.w_expand))

        def body(block):
            r.s_upward[:, block] = dot(r.a_all[...], r.v_expand[:, block])

        tiles(4, 384, body)

    def gelu():
        def body(block):
            value = r.s_upward[block, :]
            gate = 0.5 + 0.5 * lax.erf(value * 0.7071067811865476)
            r.s_active[block, :] = (value * gate).astype(BF16)
            r.s_slope[block, :] = gate + value * jnp.exp(-0.5 * value * value) * 0.3989422804014327

        tiles(length // 16, 16, body)
        save(r.s_slope, r.slope)
        save(r.s_active, r.active)

    def contract_grad():
        kept[0].wait()
        for item in g_expand:
            item.drain()

        def body(block):
            r.v_expand[:, block] = dot(r.t_grad[...], r.s_active[:, block]).astype(BF16)

        tiles(4, 384, body)
        save(r.v_expand, r.contract_grad)

    def nothing():
        pass

    def frames_here():
        frame_own.wait()
        frame_share.finish()

    def grad_start():
        grad_own.start()
        grad_share.start()

    def grad_here():
        grad_share.finish()
        grad_own.wait()
        save(r.g_all, r.grad_all)

    def attended_over():
        turn_over(r.s_attended, r.t_attended)
        save(r.t_attended, r.attended_t)

    def crossed_over():
        turn_over(r.s_crossed, r.t_crossed)
        save(r.t_crossed, r.crossed_t)

    def grad_over():
        turn_over(r.g_all, r.t_grad)

    steps = (
        first_norm, joint, attend,
        attended_share.start, attended_share.relay, attended_share.finish,
        hidden_one, one_share.start, one_share.relay, one_here,
        text_pairs, text_share.start, text_share.relay, text_here,
        second_norm, cross_query, cross,
        crossed_share.start, crossed_share.relay, crossed_share.finish,
        hidden_two, two_share.start, two_share.relay, two_here,
        third_norm, upward, gelu, contract_grad,
        nothing, frame_share.relay, frames_here, grad_start, grad_share.relay, grad_here,
        attended_over, crossed_over, grad_over,
    )
    for kind, number, *rest in FORWARD_ORDER:
        if kind == 3:
            steps[number]()
            continue
        item = gathers[number]
        if kind == 2:
            item.relay(*rest)
        elif kind == 1:
            item.pass_on()
        elif item is g_norms[0]:
            norm_share.relay()
            norm_own.wait()
            norm_share.finish()
            item.start()
        elif item is not g_outward[0]:
            item.start()
    finish(g_contract)
    save(r.v_contract, r.w_contract)
    for part in range(3):
        owner, kind, src, dst = aligned_copy(part)

        @pl.when(owner != blk)
        def _():
            push(src, dst, r.asend.at[part], r.arecv.at[kind], (spot.grp, owner)).wait_send()

    for item in (
        norm_share, frame_share, grad_share, attended_share, one_share, text_share, crossed_share, two_share,
    ):
        item.drain()
    for item in gathers:
        if item not in g_expand:
            item.drain()
    for copy in outs:
        if copy is not kept[0]:
            copy.wait()


def ids_of(table):
    ids = (table[0][:, None] * SEG + jnp.arange(SEG, dtype=jnp.int32)[None, :]).reshape(-1)
    return ids[:, None], ids[None, :]


def run_kernel(kernel, number, inner, outer, out, vmem, sems, credits):
    anywhere = pl.BlockSpec(memory_space=pl.ANY)
    inside = pl.BlockSpec(memory_space=pltpu.VMEM)
    names = [*inner, *outer, *out, *vmem, *sems, *credits]
    results = pl.pallas_call(
        functools.partial(kernel, names),
        out_shape=[jax.ShapeDtypeStruct(*item) for item in out.values()],
        in_specs=[inside] * len(inner) + [anywhere] * len(outer),
        out_specs=[anywhere] * len(out),
        scratch_shapes=[pltpu.VMEM(*item) for item in vmem.values()]
        + [pltpu.SemaphoreType.DMA(shape) for shape in sems.values()]
        + [pltpu.SemaphoreType.REGULAR(shape) for shape in credits.values()],
        compiler_params=pltpu.CompilerParams(
            collective_id=number, has_side_effects=True, vmem_limit_bytes=60 * 2**20
        ),
    )(*inner.values(), *outer.values())
    return named(out, results)


def forward(frames, text, table, norms, incoming, weights):
    rows, width = frames.shape
    length = rows * lax.axis_size("blk")
    wide = width // lax.axis_size("blk")
    feed = weights["expand"].shape[1]
    ids_col, ids_row = ids_of(table)
    one = ((width, wide), BF16)
    two = ((width, 2 * wide), BF16)
    three = ((width, 3 * wide), BF16)
    four = ((width, feed), BF16)
    square, turned, strip = ((length, width), BF16), ((width, length), BF16), ((length, wide), BF16)
    big = ((length, feed), F32)
    own = ((rows, width), BF16)
    out = dict(
        w_outward=one,
        w_inward=three,
        w_query=one,
        w_keys=two,
        w_back=one,
        w_expand=four,
        w_contract=four,
        first_t=turned,
        second_t=turned,
        third_t=turned,
        attended_t=turned,
        crossed_t=turned,
        contract_grad=four,
        grad_all=square,
        joint=((length, 3 * wide), BF16),
        cross_query=strip,
        text_all=((TEXT, 2 * width), BF16),
        slope=big,
        active=((length, feed), BF16),
        one_rows=own,
        two_rows=own,
        norm_all=((16, width), F32),
        aligned=((width // lax.axis_size("grp"), 3 * wide), BF16),
    )
    vmem = dict(
        v_outward=one,
        v_inward=three,
        v_query=one,
        v_keys=two,
        v_back=one,
        v_expand=four,
        v_contract=four,
        x_all=square,
        g_all=square,
        a_all=square,
        s_attended=square,
        s_one_all=square,
        s_crossed=square,
        s_two_all=square,
        t_first=turned,
        t_second=turned,
        t_third=turned,
        t_attended=turned,
        t_crossed=turned,
        t_grad=turned,
        s_joint=((length, 3 * wide), BF16),
        s_one=((length, wide), F32),
        s_query=strip,
        s_text=((TEXT, 2 * width), BF16),
        s_upward=big,
        s_slope=big,
        s_active=((length, feed), BF16),
        v_norms=((64, 128), BF16),
        v_norm_all=((512, 128), BF16),
        v_norm_rows=((16, width), F32),
    )
    sems = dict(
        zsend=(14, 12),
        zrecv=(14, 12),
        ysend=(14, 7),
        yrecv=(14, 7),
        near=(19,),
        bsend=(8, 3),
        brecv=(8, 3),
        asend=(3,),
        arecv=(3,),
        local=(32,),
    )
    inner = dict(text=text, ids_col=ids_col, ids_row=ids_row)
    outer = dict(frames=frames, norms=norms, incoming=incoming, **weights)
    return run_kernel(forward_kernel, 1, inner, outer, out, vmem, sems, {})


class Reduce:
    def __init__(self, spot, grad, over, along, sems, spread, source=None):
        self.spot, self.grad, self.over, self.along = spot, grad, over, along
        self.ysend, self.yrecv, self.zsend, self.zrecv = sems
        self.spread = spread
        self.source = grad if source is None else source
        self.size, self.cols = over.shape[-2], over.shape[-1]

    def rows(self, z, flip=0, ref=None):
        spot = self.spot
        row = z * 2 + (1 - spot.y if flip else spot.y)
        return (self.grad if ref is None else ref).at[pl.ds(pl.multiple_of(row * self.size, self.size), self.size)]

    def add(self, target, extra):
        step = 16

        @pl.loop(0, self.size // step)
        def _(index):
            here = pl.ds(pl.multiple_of(index * step, step), step)
            target[here, :] = (target[here, :].astype(F32) + extra[here, :].astype(F32)).astype(BF16)

    def y_copy(self, z):
        return push(
            self.rows(z, 1, self.source), self.over.at[z], self.ysend.at[z], self.yrecv.at[z], self.spot.part
        )

    def y_start(self):
        for z in (0, 3, 1, 2):
            self.y_copy(z).start()

    def z_push(self, goal, flip, who, slot):
        index = flip * 5 + slot
        return push(
            self.rows(goal, flip), self.along.at[index], self.zsend.at[flip * 4 + goal],
            self.zrecv.at[index], (who * 2 + self.spot.y, self.spot.blk),
        )

    def onward(self, goal, flip, home):
        who = home + 1 if goal > home else home - 1
        slot = 4 if who == goal and home > goal else goal
        self.z_push(goal, flip, who, slot).start()

    def z_first(self, goal, flip):
        for home in (0, 3):
            if home != goal:

                @pl.when(self.spot.z == home)
                def _():
                    self.onward(goal, flip, home)

    def pass_on(self, goal, flip, home):
        @pl.when(self.spot.z == home)
        def _():
            self.z_push(goal, flip, home, goal).wait_recv()
            self.add(self.rows(goal, flip), self.along.at[flip * 5 + goal])
            self.onward(goal, flip, home)

    def take(self, goal):
        self.y_copy(goal).wait_recv()
        self.add(self.rows(goal), self.over.at[goal])
        self.z_first(goal, 0)

    def start(self):
        if not self.spread:
            return self.y_start()
        for goal in (0, 3, 1, 2):
            for flip in (1, 0):
                self.z_first(goal, flip)

    def slots(self, home):
        return ([home] if home > 0 else []) + ([4] if home < 3 else [])

    def arrive(self, flip):
        for home in range(4):

            @pl.when(self.spot.z == home)
            def _():
                for slot in self.slots(home):
                    self.z_push(home, flip, home, slot).wait_recv()

    def total(self, flip, extra, body):
        own = self.rows(self.spot.z, flip)
        for home in range(4):

            @pl.when(self.spot.z == home)
            def _():
                @pl.loop(0, self.size // 16)
                def _(index):
                    here = pl.ds(pl.multiple_of(index * 16, 16), 16)
                    value = own[here, :].astype(F32)
                    for slot in self.slots(home):
                        value += self.along[flip * 5 + slot, here, :].astype(F32)
                    if extra is not None:
                        value += extra[here, :].astype(F32)
                    body(here, value)

    def cross(self):
        self.arrive(1)
        target = self.rows(self.spot.z, 1)

        def keep(here, value):
            target[here, :] = value.astype(BF16)

        self.total(1, None, keep)
        push(target, self.over.at[0], self.ysend.at[0], self.yrecv.at[0], self.spot.part).start()

    def finish(self, body):
        self.arrive(0)
        if self.spread:
            target = self.rows(self.spot.z, 1)
            push(target, self.over.at[0], self.ysend.at[0], self.yrecv.at[0], self.spot.part).wait_recv()
            self.total(0, self.over.at[0], body)
        else:
            self.total(0, None, body)

    def drain(self):
        z = self.spot.z
        if self.spread:
            target = self.rows(z, 1)
            push(target, self.over.at[0], self.ysend.at[0], self.yrecv.at[0], self.spot.part).wait_send()
        else:
            for goal in range(4):
                self.y_copy(goal).wait_send()
        for flip in (0, 1) if self.spread else (0,):
            for goal in range(4):

                @pl.when(z != goal)
                def _():
                    self.z_push(goal, flip, 0, 0).wait_send()


class BlkSum:
    def __init__(self, spot, piece, near, far, send, recv, step, size):
        self.spot, self.piece, self.near, self.far = spot, piece, near, far
        self.send, self.recv, self.step, self.size = send, recv, step, size

    def to_core(self, x):
        spot = self.spot
        goal = x * 2 + 1 - spot.core
        return push(self.piece(goal), self.near.at[x], self.send.at[x], self.recv.at[x], spot.sib)

    def to_chip(self):
        spot = self.spot
        return push(self.piece(spot.opp_blk), self.far, self.send.at[2], self.recv.at[2], spot.opp)

    def start(self):
        self.to_core(0).start()
        self.to_core(1).start()

    def relay(self):
        spot = self.spot
        for x in (0, 1):
            self.to_core(x).wait_recv()
        target, extra = self.piece(spot.opp_blk), self.near.at[1 - spot.x]

        @pl.loop(0, self.size // self.step)
        def _(index):
            here = pl.ds(pl.multiple_of(index * self.step, self.step), self.step)
            target[here, :] = (target[here, :].astype(F32) + extra[here, :].astype(F32)).astype(BF16)

        self.to_chip().start()

    def finish(self):
        self.to_chip().wait_recv()

    def value(self, here):
        spot = self.spot
        own = self.piece(spot.blk)[here, :].astype(F32)
        return own + self.near[spot.x, here, :].astype(F32) + self.far[here, :].astype(F32)

    def drain(self):
        self.to_core(0).wait_send()
        self.to_core(1).wait_send()
        self.to_chip().wait_send()


class Turn:
    def __init__(self, spot, source, target, send, recv):
        self.spot, self.source, self.target, self.send, self.recv = spot, source, target, send, recv
        self.rows, self.wide = source.shape[0], target.shape[1]

    def copy(self, number):
        spot = self.spot
        goal = (spot.sib_blk, spot.opp_blk, spot.far_blk)[number]
        src = self.source.at[:, pl.ds(pl.multiple_of(goal * self.wide, 128), self.wide)]
        return push(src, self.place(spot.blk), self.send.at[number], self.recv.at[number], (spot.grp, goal))

    def place(self, index):
        return self.target.at[pl.ds(pl.multiple_of(index * self.rows, self.rows), self.rows)]

    def start(self):
        for number in (2, 1, 0):
            self.copy(number).start()
        spot = self.spot
        src = self.source.at[:, pl.ds(pl.multiple_of(spot.blk * self.wide, 128), self.wide)]
        self.place(spot.blk)[...] = src[...]

    def finish(self):
        for number in range(3):
            self.copy(number).wait_recv()

    def drain(self):
        for number in range(3):
            self.copy(number).wait_send()


def t_dot(left, right):
    return lax.dot_general(left, right, (((0,), (0,)), ((), ())), preferred_element_type=F32)


BACKWARD_ORDER = (
    (0, 0), (0, 1), (0, 2), (0, 3), (5, 0), (1, 0, 0), (1, 0, 3), (5, 1), (5, 2), (1, 0, 1),
    (5, 5), (0, 4), (5, 6), (1, 0, 2), (2, 0, 0, 0, 2), (0, 5), (2, 0, 3, 0, 1), (5, 7), (5, 3),
    (5, 8), (0, 6), (0, 7), (1, 1, 0), (2, 0, 1, 0, 2), (1, 1, 3), (2, 0, 0, 0, 1),
    (2, 0, 2, 0, 1), (2, 0, 3, 0, 2), (1, 1, 1), (2, 1, 0, 0, 2), (2, 1, 3, 0, 1), (1, 1, 2),
    (4, 0), (2, 1, 1, 0, 2), (1, 2, 0), (2, 1, 0, 0, 1), (5, 4), (5, 9), (2, 1, 3, 0, 2),
    (2, 1, 2, 0, 1), (1, 2, 3), (2, 2, 0, 0, 2), (1, 2, 1), (2, 2, 3, 0, 1), (1, 2, 2), (4, 1),
    (5, 10), (2, 2, 1, 0, 2), (2, 2, 0, 0, 1), (1, 3, 0), (5, 15), (5, 11), (2, 2, 3, 0, 2),
    (2, 2, 2, 0, 1), (5, 12), (1, 3, 3), (0, 8), (2, 3, 0, 0, 2), (1, 3, 1), (5, 13), (4, 2),
    (2, 3, 3, 0, 1), (2, 3, 0, 0, 1), (2, 8, 0, 1, 2), (2, 8, 3, 1, 1), (2, 8, 0, 0, 2),
    (1, 4, 0), (1, 3, 2), (2, 8, 0, 1, 1), (2, 3, 3, 0, 2), (2, 8, 1, 1, 2), (2, 8, 3, 0, 1),
    (1, 4, 3), (2, 8, 3, 1, 2), (2, 8, 1, 0, 2), (2, 8, 0, 0, 1), (1, 4, 1), (5, 14),
    (2, 8, 3, 0, 2), (1, 4, 2), (5, 16), (5, 17), (2, 8, 2, 1, 1), (5, 20), (2, 8, 2, 0, 1),
    (2, 3, 1, 0, 2), (5, 21), (1, 5, 0), (1, 5, 3), (5, 24), (0, 10), (2, 4, 0, 0, 2), (1, 5, 1),
    (5, 18), (5, 22), (3, 8), (5, 19), (2, 3, 2, 0, 1), (5, 26), (1, 5, 2), (5, 25), (0, 9),
    (5, 27), (2, 4, 3, 0, 1), (2, 4, 1, 0, 2), (2, 4, 0, 0, 1), (1, 6, 0), (4, 3), (1, 6, 3),
    (2, 4, 3, 0, 2), (2, 4, 2, 0, 1), (2, 5, 0, 0, 2), (1, 6, 1), (5, 28), (2, 5, 3, 0, 1),
    (2, 5, 1, 0, 2), (5, 23), (1, 6, 2), (5, 29), (2, 5, 0, 0, 1), (4, 4), (1, 7, 0),
    (2, 5, 3, 0, 2), (2, 5, 2, 0, 1), (2, 6, 0, 0, 2), (1, 7, 3), (2, 6, 1, 0, 2),
    (2, 6, 3, 0, 1), (1, 7, 1), (5, 30), (5, 31), (5, 32), (5, 35), (4, 5), (1, 7, 2), (0, 11),
    (2, 6, 0, 0, 1), (2, 6, 3, 0, 2), (2, 6, 2, 0, 1), (2, 7, 0, 0, 2), (5, 33), (1, 10, 0),
    (2, 7, 3, 0, 1), (2, 7, 1, 0, 2), (1, 10, 3), (4, 6), (2, 7, 0, 0, 1), (1, 10, 1),
    (2, 7, 3, 0, 2), (2, 7, 2, 0, 1), (2, 11, 0, 1, 2), (1, 10, 2), (2, 11, 3, 1, 1),
    (2, 11, 0, 0, 2), (4, 8), (5, 34), (2, 11, 0, 1, 1), (2, 11, 3, 0, 1), (2, 11, 1, 1, 2),
    (5, 36), (2, 11, 3, 1, 2), (2, 10, 1, 0, 2), (2, 11, 3, 0, 2), (2, 10, 0, 0, 2),
    (2, 11, 2, 1, 1), (2, 11, 0, 0, 1), (2, 10, 3, 0, 1), (2, 11, 1, 0, 2), (2, 11, 2, 0, 1),
    (1, 9, 0), (4, 7), (1, 9, 3), (1, 9, 1), (5, 41), (5, 43), (3, 11), (2, 10, 2, 0, 1),
    (0, 12), (5, 37), (5, 38), (5, 42), (2, 10, 3, 0, 2), (2, 10, 0, 0, 1), (0, 13), (0, 14),
    (2, 9, 0, 0, 2), (1, 9, 2), (5, 39), (2, 9, 3, 0, 1), (4, 11), (1, 12, 0), (4, 10),
    (2, 9, 1, 0, 2), (1, 12, 3), (2, 9, 0, 0, 1), (1, 12, 1), (2, 9, 3, 0, 2), (1, 12, 2),
    (2, 9, 2, 0, 1), (2, 12, 0, 0, 2), (5, 40), (5, 44), (2, 12, 3, 0, 1), (1, 13, 0),
    (2, 12, 1, 0, 2), (5, 49), (5, 45), (5, 50), (2, 12, 2, 0, 1), (2, 13, 0, 0, 2), (1, 13, 3),
    (2, 12, 0, 0, 1), (1, 13, 1), (4, 9), (1, 13, 2), (2, 12, 3, 0, 2), (2, 13, 3, 0, 1),
    (5, 51), (5, 46), (2, 13, 1, 0, 2), (1, 14, 0), (2, 13, 0, 0, 1), (1, 14, 3),
    (2, 13, 2, 0, 1), (2, 13, 3, 0, 2), (4, 12), (2, 14, 0, 0, 2), (5, 47), (2, 14, 3, 0, 1),
    (1, 14, 1), (1, 14, 2), (4, 13), (2, 14, 0, 0, 1), (5, 52), (5, 53), (2, 14, 3, 0, 2),
    (2, 14, 2, 0, 1), (2, 14, 1, 0, 2), (5, 48), (4, 14),
)


def backward_kernel(names, *refs):
    r = named(names, refs)
    spot = Spot()
    rows, width = r.frames.shape
    length = r.v_grad.shape[0]
    wide = width // 4
    blk = spot.blk
    spot.greet_all()
    query_part, head_part, turn_part, turned_part = (
        r.v_grad.at[:, index * wide : (index + 1) * wide] for index in range(4)
    )

    def lanes(index, size):
        return pl.ds(pl.multiple_of(index * size, 128), size)

    def part(ref, first, size):
        return ref.at[:, first : first + size]

    def row_piece(ref, size):
        return lambda index: ref.at[pl.ds(pl.multiple_of(index * size, size), size)]

    loads = []

    def load(src, dst):
        copy = pltpu.make_async_copy(src, dst, r.local.at[len(loads)])
        copy.start()
        loads.append(copy)
        return copy

    reduces, grads = [], []

    def reduce(grad, over, along, spread=False, source=None):
        number = len(reduces)
        sems = tuple(item.at[number] for item in (r.ysend, r.yrecv, r.zsend, r.zrecv))
        reduces.append(Reduce(spot, grad, over, along, sems, spread, source))
        grads.append(grad)

    def columns(index, *items):
        here = slice(index * wide, (index + 1) * wide)
        return [item.at[:, here] if len(item.shape) == 2 else item.at[:, :, here] for item in items]

    for index in range(4):
        *items, source = columns(index, r.g_contract, r.y_contract, r.z_contract, r.contract_grad)
        reduce(*items, False, source)
    for index in range(4):
        reduce(*columns(index, r.g_expand, r.y_expand, r.z_expand))
    reduce(part(r.g_rest, 0 * wide, 1 * wide), r.y_back, r.z_back, True)
    reduce(part(r.g_rest, 1 * wide, 2 * wide), r.y_keys, r.z_keys, False)
    reduce(part(r.g_rest, 3 * wide, 1 * wide), r.y_query, r.z_query, False)
    reduce(part(r.g_rest, 4 * wide, 1 * wide), r.y_outward, r.z_outward, True)
    for index in range(3):
        reduce(*columns(index, r.g_contract, r.y_contract, r.z_contract))
    back, keys, query, outward = range(8, 12)
    inward = 12
    load_grad = load(r.grad_all, r.v_grad)
    load_contract = load(r.w_contract, r.v_one)
    load_slope = load(r.slope, r.v_slope)
    later = Bag()
    later.own = [
        load(reduces[0].rows(z, 0, r.contract_grad), reduces[0].rows(z, 0, r.g_contract))
        for z in range(4)
    ]
    cross_query = part(r.v_joint, 0, wide)

    def blk_sum(number, piece, near, far, size):
        return BlkSum(spot, piece, near, far, r.bsend.at[number], r.brecv.at[number], 16, size)

    copies = []

    def give(src, goal):
        copy = pltpu.make_async_copy(src, goal, r.stored.at[len(copies)])
        copy.start()
        copies.append(copy)
        return copy

    def back_rows(left, right):
        def body(block):
            r.v_part[:, block] = dot_t(left[...], right[block, :]).astype(BF16)

        tiles(4, 384, body)

    def back_cols(left, right):
        for core in (1 - spot.core, spot.core):
            for x in (0, 1):
                goal = x * 2 + core
                here = pl.ds(pl.multiple_of(goal * wide, 128), wide)
                mine = pl.ds(pl.multiple_of(goal * wide, wide), wide)
                r.v_part[:, here] = dot_t(left[...], right[mine, :]).astype(BF16)

    def outer(target, left, right):
        def body(block):
            target[block, :] = dot(left[block, :], right[...]).astype(BF16)

        tiles(4, 384, body)

    row_parts = row_piece(r.v_part, rows)

    def col_parts(index):
        return r.v_part.at[:, lanes(index, wide)]

    third_sum = blk_sum(0, row_parts, r.near_rows, r.far_rows, rows)
    crossed_sum = blk_sum(1, col_parts, r.near_cols, r.far_cols, length)
    second_sum = blk_sum(2, row_parts, r.near_rows, r.far_rows, rows)
    attended_sum = blk_sum(3, col_parts, r.near_cols, r.far_cols, length)
    text_rows = TEXT // 4
    text_sum = blk_sum(4, row_piece(r.v_text_part, text_rows), r.near_text, r.far_text, text_rows)
    first_sum = blk_sum(5, row_parts, r.near_rows, r.far_rows, rows)
    out_sum = blk_sum(6, row_parts, r.near_rows, r.far_rows, rows)
    turn_two = Turn(spot, r.v_branch, turn_part, r.tsend.at[0], r.trecv.at[0])
    turn_one = Turn(spot, r.v_branch, turned_part, r.tsend.at[1], r.trecv.at[1])
    terms_share = Share(
        spot,
        r.v_terms.at[:, lanes(blk, wide)],
        lambda index: r.v_terms.at[:, lanes(index, wide)],
        r.csend.at[0],
        r.crecv.at[0],
    )
    hidden = r.v_slope.at[pl.ds(3 * rows, rows)]
    joint_grad = part(r.v_up, 0, 3 * wide)
    own_rows = pl.ds(pl.multiple_of((blk // 2) * TEXT, TEXT), TEXT)
    own_cols = lanes(lax.rem(blk, 2), 2 * wide)
    low = lax.broadcasted_iota(jnp.int32, (1, 128), 1) < 64

    def up():
        load_grad.wait()
        load_contract.wait()
        load_slope.wait()
        later.expand_in = load(r.w_expand, r.v_two)
        later.third_in = load(r.third_t, r.v_left)
        later.norm_in = load(r.norm_all.at[0:8], r.v_norm)
        later.two_in = load(r.two_rows, r.v_two_rows)
        later.incoming_in = load(r.incoming, r.v_rows)
        later.crossed_in = load(r.crossed_t, r.v_right)
        later.query_in = load(r.cross_query, cross_query)
        later.text_in = load(r.text_all.at[:, lanes(blk, wide)], part(r.v_text, 0, wide))
        later.values_in = load(r.text_all.at[:, lanes(blk + 4, wide)], part(r.v_text, wide, wide))

        def body(block):
            product = dot(r.v_grad[...], r.v_one[:, block])
            r.v_up[:, block] = (product * r.v_slope[:, block]).astype(BF16)

        tiles(4, 384, body)
        later.back = load(r.w_back, part(r.v_one, 0, wide))
        later.keys = load(r.w_keys, part(r.v_one, wide, 2 * wide))
        later.outward = load(r.w_outward, part(r.v_one, 3 * wide, wide))

    def third_back():
        later.expand_in.wait()
        back_rows(r.v_up, r.v_two)
        later.query = load(r.w_query, part(r.v_two, 0, wide))
        later.inward = load(r.w_inward, part(r.v_two, wide, 3 * wide))

    expand_done = []

    def expand_grad(index):
        if not expand_done:
            later.third_in.wait()
        expand_done.append(index)
        grads[4 + index][...] = dot(r.v_left[...], part(r.v_up, index * wide, wide)[...]).astype(BF16)
        if len(expand_done) == 4:
            later.second = load(r.second_t, r.v_left)

    def norm_back(total, number, base, keep):
        values = r.v_two_rows if number == 2 else r.v_rows
        gain = r.v_norm[number : number + 1, :]

        @pl.loop(0, rows // 16)
        def _(index):
            here = pl.ds(pl.multiple_of(index * 16, 16), 16)
            incoming = total.value(here)
            value = values[here, :].astype(F32)
            center = value - jnp.mean(value, axis=1, keepdims=True)
            scale = lax.rsqrt(jnp.mean(center * center, axis=1, keepdims=True) + 1e-05)
            normal = center * scale
            scaled = incoming * gain
            mean = jnp.mean(scaled, axis=1, keepdims=True)
            match = jnp.mean(scaled * normal, axis=1, keepdims=True)
            result = base[here, :].astype(F32) + (scaled - mean - normal * match) * scale
            hidden[here, :] = result
            if keep:
                r.v_branch[here, :] = result.astype(BF16)
            for place, term in ((number, incoming * normal), (3 + number, incoming)):
                spread = pl.ds(place * 8, 8)
                r.v_norm_grads[spread, :] += term[0:8, :] + term[8:16, :]

    def third_norm():
        for copy in (later.norm_in, later.two_in, later.incoming_in):
            copy.wait()
        r.v_norm_grads[...] = jnp.zeros_like(r.v_norm_grads)
        norm_back(third_sum, 2, r.v_rows, True)
        later.one = load(r.one_rows, r.v_rows)
        turn_two.start()

    def crossed_back():
        third_sum.drain()
        later.back.wait()
        back_cols(turn_part, part(r.v_one, 0, wide))

    def back_grad():
        later.crossed_in.wait()
        outer(grads[back], r.v_right, turn_part)
        later.attended = load(r.attended_t, r.v_right)

    def merge(total, target):
        @pl.loop(0, length // 16)
        def _(index):
            here = pl.ds(pl.multiple_of(index * 16, 16), 16)
            target[here, :] = total.value(here).astype(BF16)

    def half(value, side):
        return jnp.where(low if side == 0 else jnp.logical_not(low), value, jnp.zeros_like(value))

    def soft(scores):
        power = jnp.exp(scores - jnp.max(scores, axis=1, keepdims=True))
        return power * (1.0 / jnp.sum(power, axis=1, keepdims=True))

    def cross():
        later.query_in.wait()
        later.text_in.wait()
        later.values_in.wait()
        merge(crossed_sum, head_part)

        @pl.loop(0, 3)
        def _(pair):
            query = cross_query[:, lanes(pair, 128)]
            key = r.v_text[:, lanes(pair, 128)]
            value = r.v_text[:, lanes(3 + pair, 128)]
            head_grad = head_part[:, lanes(pair, 128)]
            results = []
            for side in (0, 1):
                weights = soft(dot_t(half(query, side), key) * 0.125)
                slope = dot_t(half(head_grad, side), value)
                score = (weights * (slope - jnp.sum(slope * weights, axis=1, keepdims=True))).astype(BF16)
                results.append(
                    (
                        dot(score, key) * 0.125,
                        t_dot(score, query) * 0.125,
                        t_dot(weights.astype(BF16), head_grad),
                    )
                )
            merged = [jnp.where(low, *item).astype(BF16) for item in zip(*results)]
            query_part[:, lanes(pair, 128)] = merged[0]
            r.v_terms[0:TEXT, lanes(blk * 3 + pair, 128)] = merged[1]
            r.v_terms[TEXT : 2 * TEXT, lanes(blk * 3 + pair, 128)] = merged[2]

        later.joint = load(r.joint, r.v_joint)

    def second_back():
        later.query.wait()
        crossed_sum.drain()
        back_rows(query_part, part(r.v_two, 0, wide))

    def query_grad():
        later.second.wait()
        outer(grads[query], r.v_left, query_part)
        later.first = load(r.first_t, r.v_left)

    def keys_grad():
        def body(block):
            product = t_dot(r.text[:, block], r.v_terms[own_rows, own_cols])
            grads[keys][block, :] = product.astype(BF16)

        tiles(6, 256, body)

    def text_start():
        later.keys.wait()
        terms = r.v_terms[own_rows, own_cols]
        r.v_text_part[...] = dot_t(terms, r.v_one[:, wide : 3 * wide]).astype(BF16)
        text_sum.start()

    def text_done():
        text_sum.finish()
        r.v_text_out[...] = text_sum.value(pl.ds(0, text_rows))
        give(r.v_text_out, r.text_out)

    def second_norm():
        later.one.wait()
        turn_two.drain()
        norm_back(second_sum, 1, hidden, True)
        later.frames = load(r.frames, r.v_rows)
        turn_one.start()

    def attended_back():
        second_sum.drain()
        later.outward.wait()
        back_cols(turned_part, part(r.v_one, 3 * wide, wide))

    def outward_grad():
        later.attended.wait()
        outer(grads[outward], r.v_right, turned_part)

    def attend():
        later.joint.wait()
        merge(attended_sum, head_part)

        @pl.loop(0, 3)
        def _(pair):
            r.v_key_sum[...] = jnp.zeros_like(r.v_key_sum)
            r.v_value_sum[...] = jnp.zeros_like(r.v_value_sum)

            @pl.loop(0, 4)
            def _(block):
                here = pl.ds(pl.multiple_of(block * 128, 128), 128)
                query = r.v_joint[here, lanes(pair, 128)]
                key = r.v_joint[:, lanes(pair + 3, 128)]
                value = r.v_joint[:, lanes(pair + 6, 128)]
                head_grad = head_part[here, lanes(pair, 128)]
                keep = r.ids_row[...] <= r.ids_col[here, :]
                results = []
                for side in (0, 1):
                    weights = soft(jnp.where(keep, dot_t(half(query, side), key) * 0.125, -1e30))
                    slope = dot_t(half(head_grad, side), value)
                    score = weights * (slope - jnp.sum(slope * weights, axis=1, keepdims=True))
                    score = score.astype(BF16)
                    results.append(
                        (dot(score, key), t_dot(score, query), t_dot(weights.astype(BF16), head_grad))
                    )
                merged = [jnp.where(low, *item) for item in zip(*results)]
                r.v_up[here, lanes(pair, 128)] = (merged[0] * 0.125).astype(BF16)
                r.v_key_sum[...] += merged[1]
                r.v_value_sum[...] += merged[2]

            r.v_up[:, lanes(pair + 3, 128)] = (r.v_key_sum[...] * 0.125).astype(BF16)
            r.v_up[:, lanes(pair + 6, 128)] = r.v_value_sum[...].astype(BF16)

    def first_back():
        attended_sum.drain()
        later.inward.wait()
        back_rows(joint_grad, part(r.v_two, wide, 3 * wide))

    inward_done = []

    def inward_grad(index):
        if not inward_done:
            later.first.wait()
        inward_done.append(index)
        reduces[index].drain()
        product = dot(r.v_left[...], part(r.v_up, index * wide, wide)[...])
        grads[inward + index][...] = product.astype(BF16)

    def norm_hop(number, who):
        return push(r.v_norm_sum, r.v_norm_in.at[number], r.nsend.at[number], r.nrecv.at[number], who)

    def first_norm():
        later.again = load(r.w_contract, r.v_one)
        later.active = load(r.active, r.v_grad)
        later.frames.wait()
        norm_back(first_sum, 0, hidden, False)
        for who in (spot.sib, spot.opp):
            pl.semaphore_signal(r.credit.at[6], inc=1, device_id=who, device_id_type=MESH)
        give(hidden, r.frames_out)
        for place in range(6):
            r.v_norm_sum[place : place + 1, :] = jnp.sum(
                r.v_norm_grads[place * 8 : place * 8 + 8, :], axis=0, keepdims=True
            )
        r.v_norm_sum[6:8, :] = jnp.zeros((2, width), F32)
        norm_hop(0, spot.sib).start()

    def norm_step(number, who):
        norm_hop(number, who).wait()
        r.v_norm_sum[...] += r.v_norm_in[number]

    def norm_sib():
        norm_step(0, spot.sib)
        norm_hop(1, spot.opp).start()

    def norm_opp():
        norm_step(1, spot.opp)
        norm_hop(2, spot.part).start()

    def norm_part():
        norm_step(2, spot.part)
        for k in (1, 2, 3):
            norm_hop(2 + k, spot.z_peer(k)).start()

    def norm_peers():
        for k in (1, 2, 3):
            norm_hop(2 + k, spot.z_peer(k)).wait()
        r.v_norm_sum[...] += r.v_norm_in[3] + r.v_norm_in[4] + r.v_norm_in[5]
        give(r.v_norm_sum, r.norm_out)

    def out_product():
        later.again.wait()
        later.active.wait()
        first_sum.drain()
        back_rows(r.v_grad, r.v_one)

    def out_start():
        pl.semaphore_wait(r.credit.at[6], 2)
        out_sum.start()

    def out_done():
        turn_one.drain()

        @pl.loop(0, rows // 16)
        def _(index):
            here = pl.ds(pl.multiple_of(index * 16, 16), 16)
            r.v_branch[here, :] = (out_sum.value(here) + r.v_two_rows[here, :].astype(F32)).astype(BF16)

        give(r.v_branch, r.block_out)

    steps = (
        up, third_back, third_sum.start, third_sum.relay, third_sum.finish,
        *(functools.partial(expand_grad, index) for index in range(4)),
        third_norm, turn_two.finish, crossed_back,
        crossed_sum.start, crossed_sum.relay, crossed_sum.finish,
        back_grad, cross, terms_share.start, terms_share.relay, terms_share.finish,
        second_back, second_sum.start, second_sum.relay, second_sum.finish,
        query_grad, keys_grad, text_start, text_sum.relay, text_done,
        second_norm, turn_one.finish, attended_back,
        attended_sum.start, attended_sum.relay, attended_sum.finish,
        outward_grad, attend, first_back, first_sum.start, first_sum.relay, first_sum.finish,
        *(functools.partial(inward_grad, index) for index in range(3)),
        first_norm, norm_sib, norm_opp, norm_part, norm_peers,
        out_product, out_start, out_sum.relay, out_sum.finish, out_done,
    )
    goals = [r.contract_out.at[:, index * wide : (index + 1) * wide] for index in range(4)]
    goals += [r.expand_out.at[:, index * wide : (index + 1) * wide] for index in range(4)]
    goals += [r.returning_out, r.keying_out, r.querying_out, r.outward_out]
    stores = []

    def store(number):
        goal = goals[number]
        slot = len(stores)
        if slot >= 4:
            stores[slot - 4].wait()
        columns = pl.ds(slot // 2 % 2 * 2 * wide, goal.shape[1])
        stage = r.v_slope.at[pl.ds(slot % 2 * 192, 192), columns]

        def keep(here, value):
            stage[here, :] = value

        reduces[number].finish(keep)
        stores.append(give(stage, goal))

    def inward_copy(kind):
        index = kind * 4 + blk
        src = r.v_left.at[kind * 192 : (kind + 1) * 192, 0:wide]
        place = lax.rem(index, 3)
        lines = pl.ds(pl.multiple_of(place * 192, 192), 192)
        return index // 3, place, src, r.v_right.at[lines, 0:wide]

    def hand_over(kind):
        owner, place, src, dst = inward_copy(kind)

        def keep(here, value):
            src[here, :] = value.astype(BF16)

        reduces[inward + kind].finish(keep)

        @pl.when(owner == blk)
        def _():
            pltpu.make_async_copy(src, dst, r.arecv.at[place]).start()

        @pl.when(owner != blk)
        def _():
            push(src, dst, r.asend.at[kind], r.arecv.at[place], (spot.grp, owner)).start()

    taken = [0] * len(reduces)
    for kind, number, *rest in BACKWARD_ORDER:
        if kind == 5:
            steps[number]()
            continue
        item = reduces[number]
        if kind == 0:
            if number >= inward:
                pl.semaphore_wait(r.credit.at[number - inward], 1)
            item.start()
        elif kind == 1:
            if number < 4 and sum(taken) == 0:
                for copy in later.own:
                    copy.wait()
            if number >= inward and taken[number] == 0:
                pl.semaphore_wait(r.credit.at[3 + number - inward], 3)
            item.take(*rest)
            taken[number] += 1
            if number < 3 and taken[number] == 4:
                pl.semaphore_signal(r.credit.at[number], inc=1, device_id=spot.part, device_id_type=MESH)
        elif kind == 2:
            item.pass_on(*rest)
        elif kind == 3:
            item.cross()
        elif number >= inward:
            hand_over(number - inward)
        else:
            store(number)
            for k in (1, 2, 3) if number < 3 else ():
                pl.semaphore_signal(
                    r.credit.at[3 + number], inc=1, device_id=spot.z_peer(k), device_id_type=MESH
                )
    for copy in stores[-4:]:
        copy.wait()
    for place in range(3):
        here = slice(place * wide, (place + 1) * wide)
        dst = r.v_right.at[place * 192 : (place + 1) * 192, 0:wide]
        home = lax.rem(blk * 3 + place, 4)

        @pl.when(home == blk)
        def _():
            pltpu.make_async_copy(dst, dst, r.arecv.at[place]).wait()

        @pl.when(home != blk)
        def _():
            push(dst, dst, r.asend.at[0], r.arecv.at[place], spot.sib).wait_recv()

        stage = r.v_slope.at[pl.ds(0, 192), pl.ds(place * wide, wide)]

        @pl.loop(0, 192 // 16)
        def _(index):
            lines = pl.ds(pl.multiple_of(index * 16, 16), 16)
            stage[lines, :] = dst[lines, :].astype(F32)

        give(stage, r.inward_out.at[:, here])
    for kind in range(3):
        owner, place, src, dst = inward_copy(kind)

        @pl.when(owner != blk)
        def _():
            push(src, dst, r.asend.at[kind], r.arecv.at[place], (spot.grp, owner)).wait_send()

    for item in reduces[3:]:
        item.drain()
    terms_share.drain()
    text_sum.drain()
    out_sum.drain()
    for copy in copies:
        if all(copy is not item for item in stores):
            copy.wait()


def backward(ahead, frames, text, table, incoming):
    rows, width = frames.shape
    length = rows * lax.axis_size("blk")
    wide = width // lax.axis_size("blk")
    shard = width // lax.axis_size("grp")
    feed = ahead.w_expand.shape[1]
    ids_col, ids_row = ids_of(table)
    out = dict(
        contract_out=((shard, feed), F32),
        expand_out=((shard, feed), F32),
        returning_out=((shard, wide), F32),
        keying_out=((shard, 2 * wide), F32),
        querying_out=((shard, wide), F32),
        outward_out=((shard, wide), F32),
        inward_out=((shard, 3 * wide), F32),
        frames_out=((rows, width), F32),
        block_out=((rows, width), BF16),
        text_out=((TEXT // 4, width), F32),
        norm_out=((8, width), F32),
    )
    square, turned, strip = (length, width), (width, length), (length, wide)
    vmem = dict(
        v_one=((width, feed), BF16),
        v_two=((width, feed), BF16),
        g_contract=((width, feed), BF16),
        g_expand=((width, feed), BF16),
        g_rest=((width, 5 * wide), BF16),
        v_left=(turned, BF16),
        v_right=(turned, BF16),
        v_grad=(square, BF16),
        v_up=(square, BF16),
        v_part=(square, BF16),
        v_slope=(square, F32),
        v_joint=((length, 3 * wide), BF16),
        v_text=((TEXT, 2 * wide), BF16),
        v_terms=((2 * TEXT, width), BF16),
        v_text_part=((TEXT, width), BF16),
        v_text_out=((TEXT // 4, width), F32),
        near_rows=((2, rows, width), BF16),
        far_rows=((rows, width), BF16),
        near_cols=((2, length, wide), BF16),
        far_cols=(strip, BF16),
        near_text=((2, TEXT // 4, width), BF16),
        far_text=((TEXT // 4, width), BF16),
        v_branch=((rows, width), BF16),
        v_rows=((rows, width), BF16),
        v_two_rows=((rows, width), BF16),
        v_norm=((8, width), F32),
        v_norm_grads=((48, width), F32),
        v_norm_sum=((8, width), F32),
        v_norm_in=((6, 8, width), F32),
        v_key_sum=((length, 128), F32),
        v_value_sum=((length, 128), F32),
    )
    vmem.update(
        y_contract=((4, shard, feed), BF16),
        y_expand=((4, shard, feed), BF16),
        y_back=((1, shard, wide), BF16),
        y_keys=((4, shard, 2 * wide), BF16),
        y_query=((4, shard, wide), BF16),
        y_outward=((1, shard, wide), BF16),
        z_contract=((5, shard, feed), BF16),
        z_expand=((5, shard, feed), BF16),
        z_back=((10, shard, wide), BF16),
        z_keys=((5, shard, 2 * wide), BF16),
        z_query=((5, shard, wide), BF16),
        z_outward=((10, shard, wide), BF16),
    )
    sems = dict(
        ysend=(15, 4),
        yrecv=(15, 4),
        zsend=(15, 8),
        zrecv=(15, 10),
        bsend=(7, 3),
        brecv=(7, 3),
        tsend=(2, 3),
        trecv=(2, 3),
        csend=(1, 3),
        crecv=(1, 3),
        nsend=(6,),
        nrecv=(6,),
        asend=(3,),
        arecv=(3,),
        local=(32,),
        stored=(24,),
    )
    inner = dict(text=text, ids_col=ids_col, ids_row=ids_row)
    outer = dict(frames=frames, incoming=incoming, **vars(ahead))
    del outer["aligned"]
    return run_kernel(backward_kernel, 2, inner, outer, out, vmem, sems, dict(credit=(7,)))


def closing_kernel(count, *refs):
    given, out, held, sems = refs[:count], refs[count : 2 * count], refs[2 * count : -1], refs[-1]
    loads = [
        pltpu.make_async_copy(src, dst, sems.at[0, index])
        for index, (src, dst) in enumerate(zip(given, held))
    ]
    stores = [
        pltpu.make_async_copy(src, dst, sems.at[1, index])
        for index, (src, dst) in enumerate(zip(held, out))
    ]
    for copy in loads:
        copy.start()
    for load, store in zip(loads, stores):
        load.wait()
        store.start()
    for copy in stores:
        copy.wait()


def closing(*items):
    anywhere = pl.BlockSpec(memory_space=pl.ANY)
    count = len(items)
    return pl.pallas_call(
        functools.partial(closing_kernel, count),
        out_shape=[jax.ShapeDtypeStruct(item.shape, item.dtype) for item in items],
        in_specs=[anywhere] * count,
        out_specs=[anywhere] * count,
        scratch_shapes=[pltpu.VMEM(item.shape, item.dtype) for item in items]
        + [pltpu.SemaphoreType.DMA((2, count))],
    )(*items)


def tp_shards(
    frames,
    text_states,
    block_table,
    inward,
    outward,
    querying,
    keying,
    returning,
    expand,
    contract,
    gains,
    shifts,
    out_grad,
):
    ahead = forward(
        frames[0],
        text_states[0],
        block_table,
        jnp.pad(jnp.concatenate([gains, shifts], axis=0), ((0, 10), (0, 80))),
        out_grad[0],
        dict(
            inward=inward,
            outward=outward,
            query=querying,
            keys=keying,
            back=returning,
            expand=expand,
            contract=contract.T,
        ),
    )
    done = backward(ahead, frames[0], text_states[0], block_table, out_grad[0])
    share = gains.shape[1]
    place = (lax.axis_index("grp") * lax.axis_size("blk") + lax.axis_index("blk")) * share
    norm_grads = lax.dynamic_slice_in_dim(done.norm_out, place, share, 1)
    (
        contract_grad,
        expand_grad,
        returning_grad,
        keying_grad,
        querying_grad,
        outward_grad,
        inward_grad,
        frames_grad,
        block_out,
        text_grad,
    ) = closing(
        done.contract_out,
        done.expand_out,
        done.returning_out,
        done.keying_out,
        done.querying_out,
        done.outward_out,
        done.inward_out,
        done.frames_out,
        done.block_out,
        done.text_out,
    )
    return (
        block_out[None],
        frames_grad[None],
        text_grad[None],
        inward_grad,
        outward_grad,
        querying_grad,
        keying_grad,
        returning_grad,
        expand_grad,
        contract_grad.T,
        norm_grads[:3],
        norm_grads[3:6],
    )


def solution(mesh):
    small = mesh.shape["grp"] == 8 and mesh.shape["blk"] == 4
    return jax.shard_map(
        tp_shards if small else shards,
        mesh=mesh,
        in_specs=(
            P("grp", "blk", None),
            P("grp", None, None),
            P("grp", None),
            P("grp", "blk"),
            P("grp", "blk"),
            P("grp", "blk"),
            P("grp", "blk"),
            P("grp", "blk"),
            P("grp", "blk"),
            P("blk", "grp"),
            P(None, ("grp", "blk")),
            P(None, ("grp", "blk")),
            P("grp", "blk", None),
        ),
        out_specs=(
            P("grp", "blk", None),
            P("grp", "blk", None),
            P("grp", "blk", None),
            P("grp", "blk"),
            P("grp", "blk"),
            P("grp", "blk"),
            P("grp", "blk"),
            P("grp", "blk"),
            P("grp", "blk"),
            P("blk", "grp"),
            P(None, ("grp", "blk")),
            P(None, ("grp", "blk")),
        ),
        check_vma=False,
    )
```

```python
import functools
import math

import jax
import jax.numpy as jnp
from jax import lax
from jax.experimental import pallas as pl
from jax.experimental.pallas import tpu as pltpu
from jax.sharding import PartitionSpec as P

HEADS = 24
HEAD = 64
TEXT = 64
SEG = 64


def layer_norm(values, gain, shift):
    center = values - jnp.mean(values, axis=-1, keepdims=True)
    spread = jnp.mean(center * center, axis=-1, keepdims=True)
    return center * lax.rsqrt(spread + 1e-05) * gain + shift


def norm_pull(values, gain, shift, incoming):
    unused, pullback = jax.vjp(layer_norm, values, gain, shift)
    return pullback(incoming)


def gelu_slope(upward):
    return (
        0.5 * (1.0 + lax.erf(upward * 0.7071067811865476))
        + upward * jnp.exp(-0.5 * upward * upward) * 0.3989422804014327
    )


def gather_weights(inward, outward, querying, keying, returning, expand, contract, gains, shifts):
    inward, outward, querying, keying, returning, expand, contract, gains, shifts = (
        lax.all_gather(inward, "blk", axis=1, tiled=True),
        lax.all_gather(outward, "blk", axis=1, tiled=True),
        lax.all_gather(querying, "blk", axis=1, tiled=True),
        lax.all_gather(keying, "blk", axis=1, tiled=True),
        lax.all_gather(returning, "blk", axis=1, tiled=True),
        lax.all_gather(expand, "blk", axis=1, tiled=True),
        lax.all_gather(contract, "blk", axis=0, tiled=True),
        lax.all_gather(gains, "blk", axis=1, tiled=True),
        lax.all_gather(shifts, "blk", axis=1, tiled=True),
    )
    return (
        lax.all_gather(inward, "grp", axis=0, tiled=True),
        lax.all_gather(outward, "grp", axis=0, tiled=True),
        lax.all_gather(querying, "grp", axis=0, tiled=True),
        lax.all_gather(keying, "grp", axis=0, tiled=True),
        lax.all_gather(returning, "grp", axis=0, tiled=True),
        lax.all_gather(expand, "grp", axis=0, tiled=True),
        lax.all_gather(contract, "grp", axis=1, tiled=True),
        lax.all_gather(gains, "grp", axis=1, tiled=True),
        lax.all_gather(shifts, "grp", axis=1, tiled=True),
    )


def shards(
    frames,
    text_states,
    block_table,
    inward,
    outward,
    querying,
    keying,
    returning,
    expand,
    contract,
    gains,
    shifts,
    out_grad,
):
    (
        full_inward,
        full_outward,
        full_query,
        full_keys,
        full_return,
        full_expand,
        full_contract,
        full_gains,
        full_shifts,
    ) = gather_weights(
        inward, outward, querying, keying, returning, expand, contract, gains, shifts
    )
    width = frames.shape[2]
    rows = frames.shape[1]
    length = block_table.shape[1] * SEG
    group = lax.axis_size("blk")
    member = lax.axis_index("blk")
    span = math.gcd(length, 512)
    steps = length // span
    gain_rows = full_gains.astype(jnp.float32)
    shift_rows = full_shifts.astype(jnp.float32)
    key_frames = (
        block_table[0][:, None] * SEG + jnp.arange(SEG, dtype=jnp.int32)[None, :]
    ).reshape(length)
    own_frames = lax.dynamic_slice_in_dim(key_frames, member * rows, rows, 0)
    inputs = frames[0].astype(jnp.float32)
    first = layer_norm(inputs, gain_rows[0], shift_rows[0]).astype(jnp.bfloat16)
    joint = jnp.dot(first, full_inward, preferred_element_type=jnp.float32).astype(jnp.bfloat16)
    queries = joint[:, :width].reshape(rows, HEADS, HEAD)
    pairs = lax.all_gather(joint[:, width:], "blk", axis=0, tiled=True)
    pair_blocks = pairs.reshape(steps, span, 2 * width)
    frame_blocks = key_frames.reshape(steps, span)

    def scores_of(block, block_frames):
        keys = block[:, :width].reshape(span, HEADS, HEAD)
        raw = jnp.einsum("qhd,khd->hqk", queries, keys, preferred_element_type=jnp.float32) * 0.125
        allowed = block_frames[None, :] <= own_frames[:, None]
        return jnp.where(allowed[None], raw, -1e30)

    def stat_step(carry, items):
        peak, total = carry
        scores = scores_of(items[0], items[1])
        higher = jnp.maximum(peak, jnp.max(scores, axis=2))
        total = total * jnp.exp(peak - higher) + jnp.sum(
            jnp.exp(scores - higher[:, :, None]), axis=2
        )
        return ((higher, total), None)

    start_peak = jnp.full((HEADS, rows), -1e30, jnp.float32)
    (peak, total), unused = lax.scan(
        stat_step, (start_peak, jnp.zeros((HEADS, rows), jnp.float32)), (pair_blocks, frame_blocks)
    )
    log_total = peak + jnp.log(total)

    def out_step(carry, items):
        weighting = jnp.exp(scores_of(items[0], items[1]) - log_total[:, :, None]).astype(
            jnp.bfloat16
        )
        values = items[0][:, width:].reshape(span, HEADS, HEAD)
        return (
            carry
            + jnp.einsum("hqk,khd->qhd", weighting, values, preferred_element_type=jnp.float32),
            None,
        )

    mixed, unused = lax.scan(
        out_step, jnp.zeros((rows, HEADS, HEAD), jnp.float32), (pair_blocks, frame_blocks)
    )
    attended = mixed.reshape(rows, width).astype(jnp.bfloat16)
    hidden_one = inputs + jnp.dot(attended, full_outward, preferred_element_type=jnp.float32)
    second = layer_norm(hidden_one, gain_rows[1], shift_rows[1]).astype(jnp.bfloat16)
    cross_query = jnp.dot(second, full_query, preferred_element_type=jnp.float32).astype(
        jnp.bfloat16
    )
    cross_heads = cross_query.reshape(rows, HEADS, HEAD)
    text = text_states[0]
    text_pairs = jnp.dot(text, full_keys, preferred_element_type=jnp.float32).astype(jnp.bfloat16)
    text_keys = text_pairs[:, :width].reshape(TEXT, HEADS, HEAD)
    text_values = text_pairs[:, width:].reshape(TEXT, HEADS, HEAD)
    cross_scores = (
        jnp.einsum("qhd,khd->hqk", cross_heads, text_keys, preferred_element_type=jnp.float32)
        * 0.125
    )
    cross_soft = jax.nn.softmax(cross_scores, axis=2)
    cross_weighting = cross_soft.astype(jnp.bfloat16)
    crossed = (
        jnp.einsum("hqk,khd->qhd", cross_weighting, text_values, preferred_element_type=jnp.float32)
        .reshape(rows, width)
        .astype(jnp.bfloat16)
    )
    hidden_two = hidden_one + jnp.dot(crossed, full_return, preferred_element_type=jnp.float32)
    third = layer_norm(hidden_two, gain_rows[2], shift_rows[2]).astype(jnp.bfloat16)
    upward = jnp.dot(third, full_expand, preferred_element_type=jnp.float32)
    activated = jax.nn.gelu(upward, approximate=False).astype(jnp.bfloat16)
    branch = jnp.dot(activated, full_contract, preferred_element_type=jnp.float32)
    block_out = (hidden_two + branch).astype(jnp.bfloat16)[None]
    (
        full_inward,
        full_outward,
        full_query,
        full_keys,
        full_return,
        full_expand,
        full_contract,
        full_gains,
        full_shifts,
    ) = gather_weights(
        inward, outward, querying, keying, returning, expand, contract, gains, shifts
    )
    incoming = out_grad[0].astype(jnp.float32)
    branch_grad = out_grad[0]
    act_grad = jnp.dot(branch_grad, full_contract.T, preferred_element_type=jnp.float32)
    contract_grad = jnp.dot(activated.T, branch_grad, preferred_element_type=jnp.float32)
    up_grad = (act_grad * gelu_slope(upward)).astype(jnp.bfloat16)
    expand_grad = jnp.dot(third.T, up_grad, preferred_element_type=jnp.float32)
    third_grad = jnp.dot(up_grad, full_expand.T, preferred_element_type=jnp.float32)
    two_grad, gain_two, shift_two = norm_pull(hidden_two, gain_rows[2], shift_rows[2], third_grad)
    hidden_two_grad = incoming + two_grad
    branch_two = hidden_two_grad.astype(jnp.bfloat16)
    crossed_grad = jnp.dot(branch_two, full_return.T, preferred_element_type=jnp.float32).astype(
        jnp.bfloat16
    )
    crossed_grad = crossed_grad.reshape(rows, HEADS, HEAD)
    prob_grad = jnp.einsum(
        "qhd,khd->hqk", crossed_grad, text_values, preferred_element_type=jnp.float32
    )
    text_value_grad = jnp.einsum(
        "hqk,qhd->khd", cross_weighting, crossed_grad, preferred_element_type=jnp.float32
    )
    cross_score_grad = (
        cross_soft * (prob_grad - jnp.sum(prob_grad * cross_soft, axis=2, keepdims=True))
    ).astype(jnp.bfloat16)
    cross_query_grad = (
        (
            jnp.einsum(
                "hqk,khd->qhd", cross_score_grad, text_keys, preferred_element_type=jnp.float32
            )
            * 0.125
        )
        .reshape(rows, width)
        .astype(jnp.bfloat16)
    )
    text_key_grad = (
        jnp.einsum(
            "hqk,qhd->khd", cross_score_grad, cross_heads, preferred_element_type=jnp.float32
        )
        * 0.125
    )
    text_terms = jnp.concatenate(
        [text_key_grad.reshape(TEXT, width), text_value_grad.reshape(TEXT, width)], axis=1
    )
    text_share = lax.psum_scatter(
        text_terms.astype(jnp.bfloat16), "blk", scatter_dimension=0, tiled=True
    )
    share = TEXT // group
    text_grad = jnp.dot(text_share, full_keys.T, preferred_element_type=jnp.float32)[None]
    one_grad, gain_one, shift_one = norm_pull(
        hidden_one,
        gain_rows[1],
        shift_rows[1],
        jnp.dot(cross_query_grad, full_query.T, preferred_element_type=jnp.float32),
    )
    hidden_one_grad = hidden_two_grad + one_grad
    branch_one = hidden_one_grad.astype(jnp.bfloat16)
    attended_grad = jnp.dot(branch_one, full_outward.T, preferred_element_type=jnp.float32).astype(
        jnp.bfloat16
    )
    attended_grad = attended_grad.reshape(rows, HEADS, HEAD)
    delta = jnp.sum(attended_grad.astype(jnp.float32) * mixed, axis=2).T

    def back_step(carry, items):
        block = items[0]
        weighting = jnp.exp(scores_of(block, items[1]) - log_total[:, :, None])
        keys = block[:, :width].reshape(span, HEADS, HEAD)
        values = block[:, width:].reshape(span, HEADS, HEAD)
        value_grad = jnp.einsum(
            "hqk,qhd->khd",
            weighting.astype(jnp.bfloat16),
            attended_grad,
            preferred_element_type=jnp.float32,
        )
        weight_grad = jnp.einsum(
            "qhd,khd->hqk", attended_grad, values, preferred_element_type=jnp.float32
        )
        score_grad = (weighting * (weight_grad - delta[:, :, None])).astype(jnp.bfloat16)
        carry = carry + jnp.einsum(
            "hqk,khd->qhd", score_grad, keys, preferred_element_type=jnp.float32
        )
        key_grad = (
            jnp.einsum("hqk,qhd->khd", score_grad, queries, preferred_element_type=jnp.float32)
            * 0.125
        )
        return (
            carry,
            jnp.concatenate(
                [key_grad.reshape(span, width), value_grad.reshape(span, width)], axis=1
            ),
        )

    query_sum, pair_terms = lax.scan(
        back_step, jnp.zeros((rows, HEADS, HEAD), jnp.float32), (pair_blocks, frame_blocks)
    )
    pair_grad = lax.psum_scatter(
        pair_terms.reshape(length, 2 * width).astype(jnp.bfloat16),
        "blk",
        scatter_dimension=0,
        tiled=True,
    )
    joint_grad = jnp.concatenate(
        [(query_sum * 0.125).reshape(rows, width).astype(jnp.bfloat16), pair_grad], axis=1
    )
    zero_grad, gain_zero, shift_zero = norm_pull(
        inputs,
        gain_rows[0],
        shift_rows[0],
        jnp.dot(joint_grad, full_inward.T, preferred_element_type=jnp.float32),
    )
    frames_grad = (hidden_one_grad + zero_grad)[None]
    across = lax.axis_size("grp")
    gains_grad = (
        jnp.stack([gain_zero, gain_one, gain_two])
        .reshape(3, across, group, -1)
        .transpose(0, 2, 1, 3)
        .reshape(3, width)
    )
    shifts_grad = (
        jnp.stack([shift_zero, shift_one, shift_two])
        .reshape(3, across, group, -1)
        .transpose(0, 2, 1, 3)
        .reshape(3, width)
    )
    expand_grad, contract_grad = (
        lax.psum_scatter(
            expand_grad.astype(jnp.bfloat16), "blk", scatter_dimension=1, tiled=True
        ).astype(jnp.float32),
        lax.psum_scatter(
            contract_grad.astype(jnp.bfloat16), "blk", scatter_dimension=0, tiled=True
        ).astype(jnp.float32),
    )
    own_text = lax.dynamic_slice_in_dim(text, member * share, share, 0)
    inward_grad = jnp.dot(first.T, joint_grad, preferred_element_type=jnp.float32)
    outward_grad = jnp.dot(attended.T, branch_one, preferred_element_type=jnp.float32)
    querying_grad = jnp.dot(second.T, cross_query_grad, preferred_element_type=jnp.float32)
    keying_grad = jnp.dot(own_text.T, text_share, preferred_element_type=jnp.float32)
    returning_grad = jnp.dot(crossed.T, branch_two, preferred_element_type=jnp.float32)
    (
        inward_grad,
        outward_grad,
        querying_grad,
        keying_grad,
        returning_grad,
        gains_grad,
        shifts_grad,
    ) = (
        lax.psum_scatter(
            inward_grad.astype(jnp.bfloat16), "blk", scatter_dimension=1, tiled=True
        ).astype(jnp.float32),
        lax.psum_scatter(
            outward_grad.astype(jnp.bfloat16), "blk", scatter_dimension=1, tiled=True
        ).astype(jnp.float32),
        lax.psum_scatter(
            querying_grad.astype(jnp.bfloat16), "blk", scatter_dimension=1, tiled=True
        ).astype(jnp.float32),
        lax.psum_scatter(
            keying_grad.astype(jnp.bfloat16), "blk", scatter_dimension=1, tiled=True
        ).astype(jnp.float32),
        lax.psum_scatter(
            returning_grad.astype(jnp.bfloat16), "blk", scatter_dimension=1, tiled=True
        ).astype(jnp.float32),
        lax.psum_scatter(
            gains_grad.astype(jnp.bfloat16), "blk", scatter_dimension=1, tiled=True
        ).astype(jnp.float32),
        lax.psum_scatter(
            shifts_grad.astype(jnp.bfloat16), "blk", scatter_dimension=1, tiled=True
        ).astype(jnp.float32),
    )
    (
        inward_grad,
        outward_grad,
        querying_grad,
        keying_grad,
        returning_grad,
        expand_grad,
        contract_grad,
        gains_grad,
        shifts_grad,
    ) = (
        lax.psum_scatter(
            inward_grad.astype(jnp.bfloat16), "grp", scatter_dimension=0, tiled=True
        ).astype(jnp.float32),
        lax.psum_scatter(
            outward_grad.astype(jnp.bfloat16), "grp", scatter_dimension=0, tiled=True
        ).astype(jnp.float32),
        lax.psum_scatter(
            querying_grad.astype(jnp.bfloat16), "grp", scatter_dimension=0, tiled=True
        ).astype(jnp.float32),
        lax.psum_scatter(
            keying_grad.astype(jnp.bfloat16), "grp", scatter_dimension=0, tiled=True
        ).astype(jnp.float32),
        lax.psum_scatter(
            returning_grad.astype(jnp.bfloat16), "grp", scatter_dimension=0, tiled=True
        ).astype(jnp.float32),
        lax.psum_scatter(
            expand_grad.astype(jnp.bfloat16), "grp", scatter_dimension=0, tiled=True
        ).astype(jnp.float32),
        lax.psum_scatter(
            contract_grad.astype(jnp.bfloat16), "grp", scatter_dimension=1, tiled=True
        ).astype(jnp.float32),
        lax.psum_scatter(
            gains_grad.astype(jnp.bfloat16), "grp", scatter_dimension=1, tiled=True
        ).astype(jnp.float32),
        lax.psum_scatter(
            shifts_grad.astype(jnp.bfloat16), "grp", scatter_dimension=1, tiled=True
        ).astype(jnp.float32),
    )
    return (
        block_out,
        frames_grad,
        text_grad,
        inward_grad,
        outward_grad,
        querying_grad,
        keying_grad,
        returning_grad,
        expand_grad,
        contract_grad,
        gains_grad,
        shifts_grad,
    )


MESH = pl.DeviceIdType.MESH
BF16, F32 = jnp.bfloat16, jnp.float32


class Bag:
    def __init__(self, **items):
        self.__dict__.update(items)


def named(keys, items):
    return Bag(**dict(zip(keys, items)))


class Spot:
    def __init__(self):
        grp, blk = lax.axis_index("grp"), lax.axis_index("blk")
        self.grp, self.blk = grp, blk
        self.z, self.y = grp // 2, lax.rem(grp, 2)
        self.x, self.core = blk // 2, lax.rem(blk, 2)
        self.sib_blk = self.x * 2 + 1 - self.core
        self.opp_blk = (1 - self.x) * 2 + self.core
        self.sib = (grp, self.sib_blk)
        self.opp = (grp, self.opp_blk)
        self.part = (self.z * 2 + 1 - self.y, blk)
        self.up = ((self.z + 1) * 2 + self.y, blk)
        self.down = ((self.z - 1) * 2 + self.y, blk)

        self.far_blk = (1 - self.x) * 2 + 1 - self.core

    def z_peer(self, k):
        return (lax.rem(self.z + k, 4) * 2 + self.y, self.blk)

    def greet_all(self):
        barrier = pltpu.get_barrier_semaphore()
        peers = [self.z_peer(k) for k in (1, 2, 3)]
        for who in [self.sib, self.opp, (self.grp, self.far_blk), self.part] + peers:
            pl.semaphore_signal(barrier, inc=1, device_id=who, device_id_type=MESH)
        pl.semaphore_wait(barrier, 7)

    def greet(self):
        barrier = pltpu.get_barrier_semaphore()
        for who in (self.sib, self.opp, self.part):
            pl.semaphore_signal(barrier, inc=1, device_id=who, device_id_type=MESH)

        @pl.when(self.z > 0)
        def _():
            pl.semaphore_signal(barrier, inc=1, device_id=self.down, device_id_type=MESH)

        @pl.when(self.z < 3)
        def _():
            pl.semaphore_signal(barrier, inc=1, device_id=self.up, device_id_type=MESH)

        ends = (self.z == 0) | (self.z == 3)

        @pl.when(ends)
        def _():
            pl.semaphore_wait(barrier, 4)

        @pl.when(jnp.logical_not(ends))
        def _():
            pl.semaphore_wait(barrier, 5)


def push(src, dst, send, recv, who):
    return pltpu.make_async_remote_copy(
        src_ref=src, dst_ref=dst, send_sem=send, recv_sem=recv, device_id=who, device_id_type=MESH
    )


class Gather:
    def __init__(self, spot, shard, full, zsend, zrecv, ysend, yrecv, near, spread):
        self.spot, self.shard, self.full = spot, shard, full
        self.zsend, self.zrecv, self.ysend, self.yrecv, self.near = zsend, zrecv, ysend, yrecv, near
        self.spread = spread
        self.size = shard.shape[0]

    def rows(self, z, flip=0):
        spot = self.spot
        row = z * 2 + (1 - spot.y if flip else spot.y)
        return self.full.at[pl.ds(pl.multiple_of(row * self.size, self.size), self.size)]

    def z_copy(self, src, dst, k, side, flip):
        slot = (flip * 2 + side) * 3 + k - 1
        who = self.spot.up if side else self.spot.down
        return push(src, dst, self.zsend.at[slot], self.zrecv.at[slot], who)

    def y_copy(self, src, dst, slot):
        return push(src, dst, self.ysend.at[slot], self.yrecv.at[slot], self.spot.part)

    def launch(self, src, flip):
        spot = self.spot

        @pl.when(spot.z > 0)
        def _():
            self.z_copy(src, self.rows(spot.z, flip), 1, 0, flip).start()

        @pl.when(spot.z < 3)
        def _():
            self.z_copy(src, self.rows(spot.z, flip), 1, 1, flip).start()

    def start(self):
        here = self.rows(self.spot.z)
        self.y_copy(self.shard, here, 0).start()
        self.launch(self.shard, 0)
        pltpu.make_async_copy(self.shard, here, self.near).start()

    def pass_on(self):
        other = self.rows(self.spot.z, 1)
        self.y_copy(other, other, 0).wait_recv()
        self.launch(other, 1)

    def relay(self, k, side, flip):
        spot = self.spot
        src_z = spot.z - k if side else spot.z + k
        block = self.rows(src_z, flip)

        @pl.when(src_z >= 0 if side else src_z <= 3)
        def _():
            self.z_copy(block, block, k, side, flip).wait_recv()
            if k < 3:

                @pl.when(spot.z < 3 if side else spot.z > 0)
                def _():
                    self.z_copy(block, block, k + 1, side, flip).start()

            if not self.spread:
                self.y_copy(block, block, 1 + side * 3 + k - 1).start()

    def finish(self):
        spot = self.spot
        pltpu.make_async_copy(self.shard, self.rows(spot.z), self.near).wait()
        if self.spread:
            return
        self.y_copy(self.shard, self.rows(spot.z, 1), 0).wait_recv()
        for side in (0, 1):
            for k in (1, 2, 3):
                src_z = spot.z - k if side else spot.z + k
                block = self.rows(src_z, 1)

                @pl.when(src_z >= 0 if side else src_z <= 3)
                def _():
                    self.y_copy(block, block, 1 + side * 3 + k - 1).wait_recv()

    def drain(self):
        spot = self.spot
        self.y_copy(self.shard, self.rows(spot.z), 0).wait_send()
        for side in (0, 1):
            for k in (1, 2, 3):
                src_z = spot.z - k if side else spot.z + k
                sent_z = spot.z - k + 1 if side else spot.z + k - 1
                block = self.rows(spot.z)
                if not self.spread:

                    @pl.when(src_z >= 0 if side else src_z <= 3)
                    def _():
                        self.y_copy(block, block, 1 + side * 3 + k - 1).wait_send()

                for flip in (0, 1) if self.spread else (0,):

                    @pl.when((spot.z < 3) & (sent_z >= 0) if side else (spot.z > 0) & (sent_z <= 3))
                    def _():
                        self.z_copy(block, block, k, side, flip).wait_send()


class Share:
    def __init__(self, spot, own, where, send, recv):
        self.spot, self.own, self.where, self.send, self.recv = spot, own, where, send, recv

    def first(self):
        return push(
            self.own, self.where(self.spot.blk), self.send.at[0], self.recv.at[0], self.spot.opp
        )

    def second(self):
        return push(
            self.own, self.where(self.spot.blk), self.send.at[1], self.recv.at[1], self.spot.sib
        )

    def third(self):
        passed = self.where(self.spot.opp_blk)
        return push(passed, passed, self.send.at[2], self.recv.at[2], self.spot.sib)

    def start(self):
        self.first().start()
        self.second().start()

    def relay(self):
        self.first().wait_recv()
        self.third().start()

    def finish(self):
        self.second().wait_recv()
        self.third().wait_recv()

    def drain(self):
        self.first().wait_send()
        self.second().wait_send()
        self.third().wait_send()


def dot(left, right):
    return jnp.dot(left, right, preferred_element_type=F32)


def dot_t(left, right):
    return lax.dot_general(left, right, (((1,), (1,)), ((), ())), preferred_element_type=F32)


def tiles(count, size, body):
    @pl.loop(0, count)
    def _(step):
        body(pl.ds(pl.multiple_of(step * size, size), size))


def norm_block(values, gain, shift):
    center = values - jnp.mean(values, axis=1, keepdims=True)
    spread = jnp.mean(center * center, axis=1, keepdims=True)
    return center * lax.rsqrt(spread + 1e-05) * gain + shift


FORWARD_ORDER = (
    (0, 1), (0, 0), (3, 28), (0, 2), (2, 0, 1, 0, 0), (2, 0, 1, 1, 0), (2, 1, 1, 0, 0),
    (2, 1, 1, 1, 0), (2, 2, 1, 0, 0), (2, 2, 1, 1, 0), (2, 0, 2, 1, 0), (2, 0, 2, 0, 0), (0, 3),
    (3, 29), (2, 1, 2, 1, 0), (3, 31), (2, 2, 2, 0, 0), (2, 2, 2, 1, 0), (2, 1, 2, 0, 0),
    (2, 0, 3, 1, 0), (3, 30), (2, 0, 3, 0, 0), (0, 4), (2, 3, 1, 1, 0), (2, 3, 1, 0, 0),
    (2, 2, 3, 0, 0), (2, 1, 3, 1, 0), (2, 2, 3, 1, 0), (2, 1, 3, 0, 0), (3, 0), (3, 32),
    (2, 4, 1, 1, 0), (2, 3, 2, 0, 0), (2, 3, 2, 1, 0), (2, 4, 1, 0, 0), (0, 5), (2, 4, 2, 1, 0),
    (2, 3, 3, 0, 0), (3, 33), (3, 36), (2, 3, 3, 1, 0), (2, 4, 2, 0, 0), (0, 6), (2, 5, 1, 0, 0),
    (2, 5, 1, 1, 0), (2, 4, 3, 1, 0), (2, 4, 3, 0, 0), (2, 6, 1, 1, 0), (2, 6, 1, 0, 0),
    (2, 5, 2, 1, 0), (2, 5, 2, 0, 0), (0, 7), (0, 8), (2, 6, 2, 1, 0), (2, 6, 2, 0, 0),
    (2, 5, 3, 1, 0), (2, 5, 3, 0, 0), (2, 7, 1, 1, 0), (2, 7, 1, 0, 0), (3, 1), (3, 2), (3, 3),
    (2, 6, 3, 1, 0), (2, 8, 1, 0, 0), (2, 6, 3, 0, 0), (2, 7, 2, 1, 0), (2, 7, 2, 0, 0), (0, 9),
    (2, 8, 1, 1, 0), (0, 10), (2, 7, 3, 1, 0), (2, 8, 2, 0, 0), (3, 4), (2, 9, 1, 1, 0),
    (2, 7, 3, 0, 0), (3, 5), (3, 6), (3, 7), (2, 8, 2, 1, 0), (2, 9, 1, 0, 0), (0, 11), (3, 34),
    (2, 10, 1, 1, 0), (2, 10, 1, 0, 0), (1, 8), (3, 10), (3, 11), (2, 9, 2, 1, 0),
    (2, 8, 3, 0, 0), (3, 8), (3, 9), (3, 12), (3, 13), (2, 8, 3, 1, 0), (2, 9, 2, 0, 0), (3, 14),
    (2, 11, 1, 0, 0), (2, 10, 2, 0, 0), (0, 12), (3, 15), (3, 16), (2, 8, 1, 1, 1), (3, 17),
    (2, 8, 1, 0, 1), (0, 13), (2, 10, 2, 1, 0), (2, 11, 1, 1, 0), (2, 9, 3, 0, 0),
    (2, 9, 3, 1, 0), (2, 11, 2, 0, 0), (2, 12, 1, 1, 0), (3, 18), (2, 10, 3, 0, 0), (3, 19),
    (2, 8, 2, 1, 1), (2, 12, 1, 0, 0), (3, 20), (3, 21), (2, 13, 1, 1, 0), (3, 35),
    (2, 8, 2, 0, 1), (2, 10, 3, 1, 0), (2, 11, 2, 1, 0), (2, 13, 1, 0, 0), (2, 11, 3, 0, 0),
    (2, 12, 2, 1, 0), (3, 22), (2, 12, 2, 0, 0), (3, 23), (2, 8, 3, 1, 1), (3, 24),
    (2, 8, 3, 0, 1), (2, 13, 2, 1, 0), (2, 11, 3, 1, 0), (2, 13, 2, 0, 0), (3, 25),
    (2, 12, 3, 0, 0), (2, 12, 3, 1, 0), (2, 13, 3, 0, 0), (2, 13, 3, 1, 0), (3, 26), (3, 27),
)


def forward_kernel(names, *refs):
    r = named(names, refs)
    spot = Spot()
    rows, width = r.frames.shape
    length = r.x_all.shape[0]
    wide = r.outward.shape[1]
    blk = spot.blk
    outs = []

    def save(src, dst):
        copy = pltpu.make_async_copy(src, dst, r.local.at[len(outs)])
        copy.start()
        outs.append(copy)
        return copy

    def lanes(index, size):
        return pl.ds(pl.multiple_of(index * size, 128), size)

    def row_block(ref):
        return lambda index: ref.at[pl.ds(pl.multiple_of(index * rows, rows), rows)]

    def col_block(ref, size):
        return lambda index: ref.at[:, lanes(index, size)]

    def share(number, own, where):
        return Share(spot, own, where, r.bsend.at[number], r.brecv.at[number])

    gathers = []

    def gather(shard, full, spread):
        wide = full.shape[1] // len(spread)
        first = len(gathers)
        for number, flag in enumerate(spread):
            here = slice(number * wide, (number + 1) * wide)
            sems = (item.at[first + number] for item in (r.zsend, r.zrecv, r.ysend, r.yrecv, r.near))
            gathers.append(Gather(spot, shard.at[:, here], full.at[:, here], *sems, flag))
        return gathers[first:]

    g_norms = gather(r.v_norms, r.v_norm_all, (False,))
    g_outward = gather(r.outward, r.v_outward, (False,))
    g_inward = gather(r.aligned, r.v_inward, (False, False, False))
    g_query = gather(r.query, r.v_query, (False,))
    g_keys = gather(r.keys, r.v_keys, (False,))
    g_back = gather(r.back, r.v_back, (False,))
    g_expand = gather(r.expand, r.v_expand, (True, False))
    g_contract = gather(r.contract, r.v_contract, (False, False, False, False))

    spot.greet()

    def piece(part):
        index = blk * 3 + part
        owner = lax.rem(index, 4)
        return owner, index // 4

    def aligned_copy(part):
        owner, kind = piece(part)
        src = r.inward.at[:, part * wide : (part + 1) * wide]
        return owner, kind, src, r.aligned.at[:, lanes(kind, wide)]

    for part in range(3):
        owner, kind, src, dst = aligned_copy(part)

        @pl.when(owner == blk)
        def _():
            pltpu.make_async_copy(src, dst, r.arecv.at[kind]).start()

        @pl.when(owner != blk)
        def _():
            push(src, dst, r.asend.at[part], r.arecv.at[kind], (spot.grp, owner)).start()

    norm_share = share(0, r.norms, lambda index: r.v_norms.at[pl.ds(index * 16, 16)])
    norm_own = pltpu.make_async_copy(r.norms, r.v_norms.at[pl.ds(blk * 16, 16)], r.near.at[16])
    norm_own.start()
    norm_share.start()
    frame_share = share(1, r.frames, row_block(r.x_all))
    frame_own = pltpu.make_async_copy(r.frames, row_block(r.x_all)(blk), r.near.at[17])
    frame_own.start()
    frame_share.start()
    grad_share = share(2, r.incoming, row_block(r.g_all))
    grad_own = pltpu.make_async_copy(r.incoming, row_block(r.g_all)(blk), r.near.at[18])
    attended_share = share(3, col_block(r.s_attended, wide)(blk), col_block(r.s_attended, wide))
    one_share = share(4, col_block(r.s_one_all, wide)(blk), col_block(r.s_one_all, wide))
    text_share = share(5, col_block(r.s_text, 2 * wide)(blk), col_block(r.s_text, 2 * wide))
    crossed_share = share(6, col_block(r.s_crossed, wide)(blk), col_block(r.s_crossed, wide))
    two_share = share(7, col_block(r.s_two_all, wide)(blk), col_block(r.s_two_all, wide))
    g_outward[0].start()
    for kind in range(3):
        dst = r.aligned.at[:, kind * wide : (kind + 1) * wide]
        home = (kind * 4 + blk) // 3

        @pl.when(home == blk)
        def _():
            pltpu.make_async_copy(dst, dst, r.arecv.at[kind]).wait()

        @pl.when(home != blk)
        def _():
            push(dst, dst, r.asend.at[0], r.arecv.at[kind], spot.sib).wait_recv()

    low = lax.broadcasted_iota(jnp.int32, (1, 128), 1) < 64
    kept = []

    def half(value, part):
        return jnp.where(low if part == 0 else jnp.logical_not(low), value, jnp.zeros_like(value))

    def finish(items):
        for item in items:
            item.finish()

    def turn_over(source, turned):
        def flip(block):
            turned[:, block] = source[block, :].T

        tiles(length // 128, 128, flip)

    def normed(source, index, turned):
        gain = r.v_norm_rows[index : index + 1, :]
        shift = r.v_norm_rows[3 + index : 4 + index, :]

        def body(block):
            result = norm_block(source[block, :].astype(F32), gain, shift).astype(BF16)
            r.a_all[block, :] = result

        tiles(length // 32, 32, body)
        turn_over(r.a_all, turned)

    def side_by_side():
        depth = 8 * 128
        line = lax.broadcasted_iota(jnp.int32, (depth, 384), 0)
        column = lax.broadcasted_iota(jnp.int32, (depth, 384), 1)
        inside = line & 127
        place = jnp.where((inside < 48) & (column == (line >> 7) * 48 + inside), 1.0, 0.0).astype(BF16)
        for pair in range(4):
            parts = [pl.ds(pair * 128 + part * 16, 16) for part in range(8)]
            left = jnp.concatenate([r.v_norm_all[part, :] for part in parts], axis=1)
            r.v_norm_rows[:, pair * 384 : (pair + 1) * 384] = dot(left, place)
        save(r.v_norm_rows, r.norm_all)

    def first_norm():
        finish(g_norms)
        side_by_side()
        normed(r.x_all, 0, r.t_first)
        save(r.t_first, r.first_t)

    def joint():
        finish(g_inward)
        save(r.v_inward, r.w_inward)

        def body(block):
            r.s_joint[:, block] = dot(r.a_all[...], r.v_inward[:, block]).astype(BF16)

        tiles(3, wide, body)
        save(r.s_joint, r.joint)

    def soft(scores):
        power = jnp.exp(scores - jnp.max(scores, axis=1, keepdims=True))
        return (power * (1.0 / jnp.sum(power, axis=1, keepdims=True))).astype(BF16)

    def attend():
        @pl.loop(0, 12)
        def _(step):
            pair, block = step // 4, lax.rem(step, 4)
            here = pl.ds(pl.multiple_of(block * 128, 128), 128)
            query = r.s_joint[here, lanes(pair, 128)]
            key = r.s_joint[:, lanes(pair + 3, 128)]
            value = r.s_joint[:, lanes(pair + 6, 128)]
            keep = r.ids_row[...] <= r.ids_col[here, :]
            results = []
            for part in (0, 1):
                scores = jnp.where(keep, dot_t(half(query, part), key) * 0.125, -1e30)
                results.append(dot(soft(scores), value))
            r.s_attended[here, lanes(blk * 3 + pair, 128)] = jnp.where(low, *results).astype(BF16)

    def hidden_one():
        finish(g_outward)
        save(r.v_outward, r.w_outward)
        own = r.x_all[:, lanes(blk, wide)].astype(F32)
        r.s_one[...] = dot(r.s_attended[...], r.v_outward[...]) + own
        r.s_one_all[:, lanes(blk, wide)] = r.s_one[...].astype(BF16)

    def one_here():
        one_share.finish()
        save(row_block(r.s_one_all)(blk), r.one_rows)

    def text_pairs():
        finish(g_keys)
        save(r.v_keys, r.w_keys)
        r.s_text[:, lanes(blk, 2 * wide)] = dot(r.text[...], r.v_keys[...]).astype(BF16)

    def second_norm():
        normed(r.s_one_all, 1, r.t_second)
        save(r.t_second, r.second_t)

    def cross_query():
        finish(g_query)
        save(r.v_query, r.w_query)
        r.s_query[...] = dot(r.a_all[...], r.v_query[...]).astype(BF16)
        save(r.s_query, r.cross_query)

    def text_here():
        text_share.finish()
        save(r.s_text, r.text_all)

    def cross():
        @pl.loop(0, 3)
        def _(pair):
            query = r.s_query[:, lanes(pair, 128)]
            key = r.s_text[:, lanes(blk * 3 + pair, 128)]
            value = r.s_text[:, lanes(12 + blk * 3 + pair, 128)]
            results = []
            for part in (0, 1):
                results.append(dot(soft(dot_t(half(query, part), key) * 0.125), value))
            r.s_crossed[:, lanes(blk * 3 + pair, 128)] = jnp.where(low, *results).astype(BF16)

    def hidden_two():
        finish(g_back)
        save(r.v_back, r.w_back)
        r.s_one[...] += dot(r.s_crossed[...], r.v_back[...])
        r.s_two_all[:, lanes(blk, wide)] = r.s_one[...].astype(BF16)

    def two_here():
        two_share.finish()
        save(row_block(r.s_two_all)(blk), r.two_rows)

    def third_norm():
        normed(r.s_two_all, 2, r.t_third)
        save(r.t_third, r.third_t)

    def upward():
        finish(g_expand)
        kept.append(save(r.v_expand, r.w_expand))

        def body(block):
            r.s_upward[:, block] = dot(r.a_all[...], r.v_expand[:, block])

        tiles(4, 384, body)

    def gelu():
        def body(block):
            value = r.s_upward[block, :]
            gate = 0.5 + 0.5 * lax.erf(value * 0.7071067811865476)
            r.s_active[block, :] = (value * gate).astype(BF16)
            r.s_slope[block, :] = gate + value * jnp.exp(-0.5 * value * value) * 0.3989422804014327

        tiles(length // 16, 16, body)
        save(r.s_slope, r.slope)
        save(r.s_active, r.active)

    def contract_grad():
        kept[0].wait()
        for item in g_expand:
            item.drain()

        def body(block):
            r.v_expand[:, block] = dot(r.t_grad[...], r.s_active[:, block]).astype(BF16)

        tiles(4, 384, body)
        save(r.v_expand, r.contract_grad)

    def nothing():
        pass

    def frames_here():
        frame_own.wait()
        frame_share.finish()

    def grad_start():
        grad_own.start()
        grad_share.start()

    def grad_here():
        grad_share.finish()
        grad_own.wait()
        save(r.g_all, r.grad_all)

    def attended_over():
        turn_over(r.s_attended, r.t_attended)
        save(r.t_attended, r.attended_t)

    def crossed_over():
        turn_over(r.s_crossed, r.t_crossed)
        save(r.t_crossed, r.crossed_t)

    def grad_over():
        turn_over(r.g_all, r.t_grad)

    steps = (
        first_norm, joint, attend,
        attended_share.start, attended_share.relay, attended_share.finish,
        hidden_one, one_share.start, one_share.relay, one_here,
        text_pairs, text_share.start, text_share.relay, text_here,
        second_norm, cross_query, cross,
        crossed_share.start, crossed_share.relay, crossed_share.finish,
        hidden_two, two_share.start, two_share.relay, two_here,
        third_norm, upward, gelu, contract_grad,
        nothing, frame_share.relay, frames_here, grad_start, grad_share.relay, grad_here,
        attended_over, crossed_over, grad_over,
    )
    for kind, number, *rest in FORWARD_ORDER:
        if kind == 3:
            steps[number]()
            continue
        item = gathers[number]
        if kind == 2:
            item.relay(*rest)
        elif kind == 1:
            item.pass_on()
        elif item is g_norms[0]:
            norm_share.relay()
            norm_own.wait()
            norm_share.finish()
            item.start()
        elif item is not g_outward[0]:
            item.start()
    finish(g_contract)
    save(r.v_contract, r.w_contract)
    for part in range(3):
        owner, kind, src, dst = aligned_copy(part)

        @pl.when(owner != blk)
        def _():
            push(src, dst, r.asend.at[part], r.arecv.at[kind], (spot.grp, owner)).wait_send()

    for item in (
        norm_share, frame_share, grad_share, attended_share, one_share, text_share, crossed_share, two_share,
    ):
        item.drain()
    for item in gathers:
        if item not in g_expand:
            item.drain()
    for copy in outs:
        if copy is not kept[0]:
            copy.wait()


def ids_of(table):
    ids = (table[0][:, None] * SEG + jnp.arange(SEG, dtype=jnp.int32)[None, :]).reshape(-1)
    return ids[:, None], ids[None, :]


def run_kernel(kernel, number, inner, outer, out, vmem, sems, credits):
    anywhere = pl.BlockSpec(memory_space=pl.ANY)
    inside = pl.BlockSpec(memory_space=pltpu.VMEM)
    names = [*inner, *outer, *out, *vmem, *sems, *credits]
    results = pl.pallas_call(
        functools.partial(kernel, names),
        out_shape=[jax.ShapeDtypeStruct(*item) for item in out.values()],
        in_specs=[inside] * len(inner) + [anywhere] * len(outer),
        out_specs=[anywhere] * len(out),
        scratch_shapes=[pltpu.VMEM(*item) for item in vmem.values()]
        + [pltpu.SemaphoreType.DMA(shape) for shape in sems.values()]
        + [pltpu.SemaphoreType.REGULAR(shape) for shape in credits.values()],
        compiler_params=pltpu.CompilerParams(
            collective_id=number, has_side_effects=True, vmem_limit_bytes=60 * 2**20
        ),
    )(*inner.values(), *outer.values())
    return named(out, results)


def forward(frames, text, table, norms, incoming, weights):
    rows, width = frames.shape
    length = rows * lax.axis_size("blk")
    wide = width // lax.axis_size("blk")
    feed = weights["expand"].shape[1]
    ids_col, ids_row = ids_of(table)
    one = ((width, wide), BF16)
    two = ((width, 2 * wide), BF16)
    three = ((width, 3 * wide), BF16)
    four = ((width, feed), BF16)
    square, turned, strip = ((length, width), BF16), ((width, length), BF16), ((length, wide), BF16)
    big = ((length, feed), F32)
    own = ((rows, width), BF16)
    out = dict(
        w_outward=one,
        w_inward=three,
        w_query=one,
        w_keys=two,
        w_back=one,
        w_expand=four,
        w_contract=four,
        first_t=turned,
        second_t=turned,
        third_t=turned,
        attended_t=turned,
        crossed_t=turned,
        contract_grad=four,
        grad_all=square,
        joint=((length, 3 * wide), BF16),
        cross_query=strip,
        text_all=((TEXT, 2 * width), BF16),
        slope=big,
        active=((length, feed), BF16),
        one_rows=own,
        two_rows=own,
        norm_all=((16, width), F32),
        aligned=((width // lax.axis_size("grp"), 3 * wide), BF16),
    )
    vmem = dict(
        v_outward=one,
        v_inward=three,
        v_query=one,
        v_keys=two,
        v_back=one,
        v_expand=four,
        v_contract=four,
        x_all=square,
        g_all=square,
        a_all=square,
        s_attended=square,
        s_one_all=square,
        s_crossed=square,
        s_two_all=square,
        t_first=turned,
        t_second=turned,
        t_third=turned,
        t_attended=turned,
        t_crossed=turned,
        t_grad=turned,
        s_joint=((length, 3 * wide), BF16),
        s_one=((length, wide), F32),
        s_query=strip,
        s_text=((TEXT, 2 * width), BF16),
        s_upward=big,
        s_slope=big,
        s_active=((length, feed), BF16),
        v_norms=((64, 128), BF16),
        v_norm_all=((512, 128), BF16),
        v_norm_rows=((16, width), F32),
    )
    sems = dict(
        zsend=(14, 12),
        zrecv=(14, 12),
        ysend=(14, 7),
        yrecv=(14, 7),
        near=(19,),
        bsend=(8, 3),
        brecv=(8, 3),
        asend=(3,),
        arecv=(3,),
        local=(32,),
    )
    inner = dict(text=text, ids_col=ids_col, ids_row=ids_row)
    outer = dict(frames=frames, norms=norms, incoming=incoming, **weights)
    return run_kernel(forward_kernel, 1, inner, outer, out, vmem, sems, {})


class Reduce:
    def __init__(self, spot, grad, over, along, sems, spread, source=None):
        self.spot, self.grad, self.over, self.along = spot, grad, over, along
        self.ysend, self.yrecv, self.zsend, self.zrecv = sems
        self.spread = spread
        self.source = grad if source is None else source
        self.size, self.cols = over.shape[-2], over.shape[-1]

    def rows(self, z, flip=0, ref=None):
        spot = self.spot
        row = z * 2 + (1 - spot.y if flip else spot.y)
        return (self.grad if ref is None else ref).at[pl.ds(pl.multiple_of(row * self.size, self.size), self.size)]

    def add(self, target, extra):
        step = 16

        @pl.loop(0, self.size // step)
        def _(index):
            here = pl.ds(pl.multiple_of(index * step, step), step)
            target[here, :] = (target[here, :].astype(F32) + extra[here, :].astype(F32)).astype(BF16)

    def y_copy(self, z):
        return push(
            self.rows(z, 1, self.source), self.over.at[z], self.ysend.at[z], self.yrecv.at[z], self.spot.part
        )

    def y_start(self):
        for z in (0, 3, 1, 2):
            self.y_copy(z).start()

    def z_push(self, goal, flip, who, slot):
        index = flip * 5 + slot
        return push(
            self.rows(goal, flip), self.along.at[index], self.zsend.at[flip * 4 + goal],
            self.zrecv.at[index], (who * 2 + self.spot.y, self.spot.blk),
        )

    def onward(self, goal, flip, home):
        who = home + 1 if goal > home else home - 1
        slot = 4 if who == goal and home > goal else goal
        self.z_push(goal, flip, who, slot).start()

    def z_first(self, goal, flip):
        for home in (0, 3):
            if home != goal:

                @pl.when(self.spot.z == home)
                def _():
                    self.onward(goal, flip, home)

    def pass_on(self, goal, flip, home):
        @pl.when(self.spot.z == home)
        def _():
            self.z_push(goal, flip, home, goal).wait_recv()
            self.add(self.rows(goal, flip), self.along.at[flip * 5 + goal])
            self.onward(goal, flip, home)

    def take(self, goal):
        self.y_copy(goal).wait_recv()
        self.add(self.rows(goal), self.over.at[goal])
        self.z_first(goal, 0)

    def start(self):
        if not self.spread:
            return self.y_start()
        for goal in (0, 3, 1, 2):
            for flip in (1, 0):
                self.z_first(goal, flip)

    def slots(self, home):
        return ([home] if home > 0 else []) + ([4] if home < 3 else [])

    def arrive(self, flip):
        for home in range(4):

            @pl.when(self.spot.z == home)
            def _():
                for slot in self.slots(home):
                    self.z_push(home, flip, home, slot).wait_recv()

    def total(self, flip, extra, body):
        own = self.rows(self.spot.z, flip)
        for home in range(4):

            @pl.when(self.spot.z == home)
            def _():
                @pl.loop(0, self.size // 16)
                def _(index):
                    here = pl.ds(pl.multiple_of(index * 16, 16), 16)
                    value = own[here, :].astype(F32)
                    for slot in self.slots(home):
                        value += self.along[flip * 5 + slot, here, :].astype(F32)
                    if extra is not None:
                        value += extra[here, :].astype(F32)
                    body(here, value)

    def cross(self):
        self.arrive(1)
        target = self.rows(self.spot.z, 1)

        def keep(here, value):
            target[here, :] = value.astype(BF16)

        self.total(1, None, keep)
        push(target, self.over.at[0], self.ysend.at[0], self.yrecv.at[0], self.spot.part).start()

    def finish(self, body):
        self.arrive(0)
        if self.spread:
            target = self.rows(self.spot.z, 1)
            push(target, self.over.at[0], self.ysend.at[0], self.yrecv.at[0], self.spot.part).wait_recv()
            self.total(0, self.over.at[0], body)
        else:
            self.total(0, None, body)

    def drain(self):
        z = self.spot.z
        if self.spread:
            target = self.rows(z, 1)
            push(target, self.over.at[0], self.ysend.at[0], self.yrecv.at[0], self.spot.part).wait_send()
        else:
            for goal in range(4):
                self.y_copy(goal).wait_send()
        for flip in (0, 1) if self.spread else (0,):
            for goal in range(4):

                @pl.when(z != goal)
                def _():
                    self.z_push(goal, flip, 0, 0).wait_send()


class BlkSum:
    def __init__(self, spot, piece, near, far, send, recv, step, size):
        self.spot, self.piece, self.near, self.far = spot, piece, near, far
        self.send, self.recv, self.step, self.size = send, recv, step, size

    def to_core(self, x):
        spot = self.spot
        goal = x * 2 + 1 - spot.core
        return push(self.piece(goal), self.near.at[x], self.send.at[x], self.recv.at[x], spot.sib)

    def to_chip(self):
        spot = self.spot
        return push(self.piece(spot.opp_blk), self.far, self.send.at[2], self.recv.at[2], spot.opp)

    def start(self):
        self.to_core(0).start()
        self.to_core(1).start()

    def relay(self):
        spot = self.spot
        for x in (0, 1):
            self.to_core(x).wait_recv()
        target, extra = self.piece(spot.opp_blk), self.near.at[1 - spot.x]

        @pl.loop(0, self.size // self.step)
        def _(index):
            here = pl.ds(pl.multiple_of(index * self.step, self.step), self.step)
            target[here, :] = (target[here, :].astype(F32) + extra[here, :].astype(F32)).astype(BF16)

        self.to_chip().start()

    def finish(self):
        self.to_chip().wait_recv()

    def value(self, here):
        spot = self.spot
        own = self.piece(spot.blk)[here, :].astype(F32)
        return own + self.near[spot.x, here, :].astype(F32) + self.far[here, :].astype(F32)

    def drain(self):
        self.to_core(0).wait_send()
        self.to_core(1).wait_send()
        self.to_chip().wait_send()


class Turn:
    def __init__(self, spot, source, target, send, recv):
        self.spot, self.source, self.target, self.send, self.recv = spot, source, target, send, recv
        self.rows, self.wide = source.shape[0], target.shape[1]

    def copy(self, number):
        spot = self.spot
        goal = (spot.sib_blk, spot.opp_blk, spot.far_blk)[number]
        src = self.source.at[:, pl.ds(pl.multiple_of(goal * self.wide, 128), self.wide)]
        return push(src, self.place(spot.blk), self.send.at[number], self.recv.at[number], (spot.grp, goal))

    def place(self, index):
        return self.target.at[pl.ds(pl.multiple_of(index * self.rows, self.rows), self.rows)]

    def start(self):
        for number in (2, 1, 0):
            self.copy(number).start()
        spot = self.spot
        src = self.source.at[:, pl.ds(pl.multiple_of(spot.blk * self.wide, 128), self.wide)]
        self.place(spot.blk)[...] = src[...]

    def finish(self):
        for number in range(3):
            self.copy(number).wait_recv()

    def drain(self):
        for number in range(3):
            self.copy(number).wait_send()


def t_dot(left, right):
    return lax.dot_general(left, right, (((0,), (0,)), ((), ())), preferred_element_type=F32)


BACKWARD_ORDER = (
    (0, 0), (0, 1), (0, 2), (0, 3), (5, 0), (1, 0, 0), (1, 0, 3), (5, 1), (5, 2), (1, 0, 1),
    (5, 5), (0, 4), (5, 6), (1, 0, 2), (2, 0, 0, 0, 2), (5, 7), (2, 0, 3, 0, 1), (0, 5), (0, 6),
    (5, 3), (1, 1, 0), (5, 8), (0, 7), (2, 0, 1, 0, 2), (1, 1, 3), (2, 0, 0, 0, 1),
    (2, 0, 2, 0, 1), (2, 0, 3, 0, 2), (1, 1, 1), (2, 1, 3, 0, 1), (2, 1, 0, 0, 2), (1, 1, 2),
    (4, 0), (2, 1, 1, 0, 2), (1, 2, 0), (2, 1, 0, 0, 1), (5, 4), (2, 1, 3, 0, 2),
    (2, 1, 2, 0, 1), (1, 2, 3), (5, 9), (2, 2, 0, 0, 2), (1, 2, 1), (4, 1), (2, 2, 3, 0, 1),
    (1, 2, 2), (2, 2, 0, 0, 1), (2, 2, 1, 0, 2), (1, 3, 0), (2, 2, 3, 0, 2), (2, 2, 2, 0, 1),
    (5, 10), (1, 3, 3), (5, 15), (5, 11), (5, 12), (2, 3, 0, 0, 2), (1, 3, 1), (0, 8), (4, 2),
    (5, 13), (2, 3, 3, 0, 1), (1, 3, 2), (2, 3, 1, 0, 2), (2, 3, 0, 0, 1), (1, 4, 0),
    (2, 8, 0, 1, 2), (2, 8, 3, 1, 1), (2, 3, 3, 0, 2), (1, 4, 3), (2, 8, 0, 0, 2),
    (2, 8, 3, 0, 1), (1, 4, 1), (2, 8, 0, 1, 1), (2, 8, 3, 1, 2), (2, 8, 1, 1, 2), (1, 4, 2),
    (2, 8, 3, 0, 2), (5, 14), (2, 8, 1, 0, 2), (5, 16), (2, 8, 2, 1, 1), (5, 17), (5, 20),
    (5, 21), (1, 5, 0), (1, 5, 3), (5, 24), (2, 8, 0, 0, 1), (0, 10), (2, 8, 2, 0, 1), (1, 5, 1),
    (5, 22), (2, 3, 2, 0, 1), (5, 18), (1, 5, 2), (3, 8), (2, 4, 3, 0, 1), (2, 4, 0, 0, 2),
    (5, 19), (5, 26), (1, 6, 0), (5, 25), (0, 9), (5, 27), (2, 4, 1, 0, 2), (1, 6, 3), (4, 3),
    (2, 4, 0, 0, 1), (2, 4, 2, 0, 1), (1, 6, 1), (2, 4, 3, 0, 2), (5, 28), (2, 5, 3, 0, 1),
    (2, 5, 0, 0, 2), (1, 6, 2), (5, 23), (2, 5, 1, 0, 2), (2, 5, 0, 0, 1), (2, 5, 2, 0, 1),
    (2, 5, 3, 0, 2), (5, 29), (1, 7, 0), (1, 7, 3), (2, 6, 0, 0, 2), (2, 6, 3, 0, 1), (1, 7, 1),
    (4, 4), (4, 5), (2, 6, 1, 0, 2), (2, 6, 3, 0, 2), (2, 6, 0, 0, 1), (2, 6, 2, 0, 1), (5, 30),
    (5, 31), (5, 32), (1, 7, 2), (5, 35), (2, 7, 0, 0, 2), (2, 7, 3, 0, 1), (1, 10, 0), (0, 11),
    (5, 33), (2, 7, 1, 0, 2), (1, 10, 3), (1, 10, 1), (4, 6), (2, 7, 0, 0, 1), (2, 7, 3, 0, 2),
    (2, 7, 2, 0, 1), (1, 10, 2), (2, 11, 3, 1, 1), (2, 10, 0, 0, 2), (2, 11, 0, 1, 2), (4, 7),
    (4, 8), (2, 11, 3, 1, 2), (2, 11, 0, 0, 2), (2, 11, 3, 0, 1), (2, 11, 3, 0, 2),
    (2, 10, 0, 0, 1), (5, 34), (2, 11, 1, 1, 2), (2, 11, 0, 1, 1), (5, 36), (2, 11, 1, 0, 2),
    (2, 11, 2, 1, 1), (2, 10, 3, 0, 1), (2, 10, 1, 0, 2), (1, 9, 0), (1, 9, 3), (5, 37), (3, 11),
    (2, 11, 0, 0, 1), (2, 11, 2, 0, 1), (5, 38), (2, 10, 2, 0, 1), (2, 9, 0, 0, 2), (5, 41),
    (2, 9, 3, 0, 1), (0, 12), (1, 9, 1), (2, 10, 3, 0, 2), (5, 42), (0, 13), (5, 39), (5, 43),
    (0, 14), (1, 9, 2), (4, 11), (2, 9, 1, 0, 2), (1, 12, 0), (4, 10), (2, 9, 0, 0, 1),
    (1, 12, 3), (2, 9, 2, 0, 1), (2, 9, 3, 0, 2), (2, 12, 0, 0, 2), (2, 12, 3, 0, 1), (1, 12, 1),
    (1, 12, 2), (2, 12, 1, 0, 2), (5, 40), (5, 44), (2, 12, 0, 0, 1), (2, 12, 2, 0, 1), (5, 49),
    (5, 50), (5, 45), (1, 13, 0), (2, 13, 0, 0, 2), (2, 12, 3, 0, 2), (1, 13, 3), (1, 13, 1),
    (2, 13, 1, 0, 2), (2, 13, 3, 0, 1), (4, 9), (1, 13, 2), (5, 51), (2, 13, 0, 0, 1),
    (2, 13, 2, 0, 1), (5, 46), (2, 13, 3, 0, 2), (1, 14, 0), (4, 12), (2, 14, 0, 0, 2),
    (1, 14, 3), (2, 14, 3, 0, 1), (1, 14, 1), (2, 14, 0, 0, 1), (2, 14, 1, 0, 2), (5, 47),
    (2, 14, 3, 0, 2), (1, 14, 2), (2, 14, 2, 0, 1), (4, 13), (5, 52), (5, 53), (4, 14), (5, 48),
)


def backward_kernel(names, *refs):
    r = named(names, refs)
    spot = Spot()
    rows, width = r.frames.shape
    length = r.v_grad.shape[0]
    wide = width // 4
    blk = spot.blk
    spot.greet_all()
    query_part, head_part, turn_part, turned_part = (
        r.v_grad.at[:, index * wide : (index + 1) * wide] for index in range(4)
    )

    def lanes(index, size):
        return pl.ds(pl.multiple_of(index * size, 128), size)

    def part(ref, first, size):
        return ref.at[:, first : first + size]

    def row_piece(ref, size):
        return lambda index: ref.at[pl.ds(pl.multiple_of(index * size, size), size)]

    loads = []

    def load(src, dst):
        copy = pltpu.make_async_copy(src, dst, r.local.at[len(loads)])
        copy.start()
        loads.append(copy)
        return copy

    reduces, grads = [], []

    def reduce(grad, over, along, spread=False, source=None):
        number = len(reduces)
        sems = tuple(item.at[number] for item in (r.ysend, r.yrecv, r.zsend, r.zrecv))
        reduces.append(Reduce(spot, grad, over, along, sems, spread, source))
        grads.append(grad)

    def columns(index, *items):
        here = slice(index * wide, (index + 1) * wide)
        return [item.at[:, here] if len(item.shape) == 2 else item.at[:, :, here] for item in items]

    for index in range(4):
        *items, source = columns(index, r.g_contract, r.y_contract, r.z_contract, r.contract_grad)
        reduce(*items, False, source)
    for index in range(4):
        reduce(*columns(index, r.g_expand, r.y_expand, r.z_expand))
    reduce(part(r.g_rest, 0 * wide, 1 * wide), r.y_back, r.z_back, True)
    reduce(part(r.g_rest, 1 * wide, 2 * wide), r.y_keys, r.z_keys, False)
    reduce(part(r.g_rest, 3 * wide, 1 * wide), r.y_query, r.z_query, False)
    reduce(part(r.g_rest, 4 * wide, 1 * wide), r.y_outward, r.z_outward, True)
    for index in range(3):
        reduce(*columns(index, r.g_contract, r.y_contract, r.z_contract))
    back, keys, query, outward = range(8, 12)
    inward = 12
    load_grad = load(r.grad_all, r.v_grad)
    load_contract = load(r.w_contract, r.v_one)
    load_slope = load(r.slope, r.v_slope)
    later = Bag()
    later.own = [
        load(reduces[0].rows(z, 0, r.contract_grad), reduces[0].rows(z, 0, r.g_contract))
        for z in range(4)
    ]
    cross_query = part(r.v_joint, 0, wide)

    def blk_sum(number, piece, near, far, size):
        return BlkSum(spot, piece, near, far, r.bsend.at[number], r.brecv.at[number], 16, size)

    copies = []

    def give(src, goal):
        copy = pltpu.make_async_copy(src, goal, r.stored.at[len(copies)])
        copy.start()
        copies.append(copy)
        return copy

    def back_rows(left, right):
        def body(block):
            r.v_part[:, block] = dot_t(left[...], right[block, :]).astype(BF16)

        tiles(4, 384, body)

    def back_cols(left, right):
        for core in (1 - spot.core, spot.core):
            for x in (0, 1):
                goal = x * 2 + core
                here = pl.ds(pl.multiple_of(goal * wide, 128), wide)
                mine = pl.ds(pl.multiple_of(goal * wide, wide), wide)
                r.v_part[:, here] = dot_t(left[...], right[mine, :]).astype(BF16)

    def outer(target, left, right):
        def body(block):
            target[block, :] = dot(left[block, :], right[...]).astype(BF16)

        tiles(4, 384, body)

    row_parts = row_piece(r.v_part, rows)

    def col_parts(index):
        return r.v_part.at[:, lanes(index, wide)]

    third_sum = blk_sum(0, row_parts, r.near_rows, r.far_rows, rows)
    crossed_sum = blk_sum(1, col_parts, r.near_cols, r.far_cols, length)
    second_sum = blk_sum(2, row_parts, r.near_rows, r.far_rows, rows)
    attended_sum = blk_sum(3, col_parts, r.near_cols, r.far_cols, length)
    text_rows = TEXT // 4
    text_sum = blk_sum(4, row_piece(r.v_text_part, text_rows), r.near_text, r.far_text, text_rows)
    first_sum = blk_sum(5, row_parts, r.near_rows, r.far_rows, rows)
    out_sum = blk_sum(6, row_parts, r.near_rows, r.far_rows, rows)
    turn_two = Turn(spot, r.v_branch, turn_part, r.tsend.at[0], r.trecv.at[0])
    turn_one = Turn(spot, r.v_branch, turned_part, r.tsend.at[1], r.trecv.at[1])
    terms_share = Share(
        spot,
        r.v_terms.at[:, lanes(blk, wide)],
        lambda index: r.v_terms.at[:, lanes(index, wide)],
        r.csend.at[0],
        r.crecv.at[0],
    )
    hidden = r.v_slope.at[pl.ds(3 * rows, rows)]
    joint_grad = part(r.v_up, 0, 3 * wide)
    own_rows = pl.ds(pl.multiple_of((blk // 2) * TEXT, TEXT), TEXT)
    own_cols = lanes(lax.rem(blk, 2), 2 * wide)
    low = lax.broadcasted_iota(jnp.int32, (1, 128), 1) < 64

    def up():
        load_grad.wait()
        load_contract.wait()
        load_slope.wait()
        later.expand_in = load(r.w_expand, r.v_two)
        later.third_in = load(r.third_t, r.v_left)
        later.norm_in = load(r.norm_all.at[0:8], r.v_norm)
        later.two_in = load(r.two_rows, r.v_two_rows)
        later.incoming_in = load(r.incoming, r.v_rows)
        later.crossed_in = load(r.crossed_t, r.v_right)
        later.query_in = load(r.cross_query, cross_query)
        later.text_in = load(r.text_all.at[:, lanes(blk, wide)], part(r.v_text, 0, wide))
        later.values_in = load(r.text_all.at[:, lanes(blk + 4, wide)], part(r.v_text, wide, wide))

        def body(block):
            product = dot(r.v_grad[...], r.v_one[:, block])
            r.v_up[:, block] = (product * r.v_slope[:, block]).astype(BF16)

        tiles(4, 384, body)
        later.back = load(r.w_back, part(r.v_one, 0, wide))
        later.keys = load(r.w_keys, part(r.v_one, wide, 2 * wide))
        later.outward = load(r.w_outward, part(r.v_one, 3 * wide, wide))

    def third_back():
        later.expand_in.wait()
        back_rows(r.v_up, r.v_two)
        later.query = load(r.w_query, part(r.v_two, 0, wide))
        later.inward = load(r.w_inward, part(r.v_two, wide, 3 * wide))

    expand_done = []

    def expand_grad(index):
        if not expand_done:
            later.third_in.wait()
        expand_done.append(index)
        grads[4 + index][...] = dot(r.v_left[...], part(r.v_up, index * wide, wide)[...]).astype(BF16)
        if len(expand_done) == 4:
            later.second = load(r.second_t, r.v_left)

    def norm_back(total, number, base, keep):
        values = r.v_two_rows if number == 2 else r.v_rows
        gain = r.v_norm[number : number + 1, :]

        @pl.loop(0, rows // 16)
        def _(index):
            here = pl.ds(pl.multiple_of(index * 16, 16), 16)
            incoming = total.value(here)
            value = values[here, :].astype(F32)
            center = value - jnp.mean(value, axis=1, keepdims=True)
            scale = lax.rsqrt(jnp.mean(center * center, axis=1, keepdims=True) + 1e-05)
            normal = center * scale
            scaled = incoming * gain
            mean = jnp.mean(scaled, axis=1, keepdims=True)
            match = jnp.mean(scaled * normal, axis=1, keepdims=True)
            result = base[here, :].astype(F32) + (scaled - mean - normal * match) * scale
            hidden[here, :] = result
            if keep:
                r.v_branch[here, :] = result.astype(BF16)
            for place, term in ((number, incoming * normal), (3 + number, incoming)):
                spread = pl.ds(place * 8, 8)
                r.v_norm_grads[spread, :] += term[0:8, :] + term[8:16, :]

    def third_norm():
        for copy in (later.norm_in, later.two_in, later.incoming_in):
            copy.wait()
        r.v_norm_grads[...] = jnp.zeros_like(r.v_norm_grads)
        norm_back(third_sum, 2, r.v_rows, True)
        later.one = load(r.one_rows, r.v_rows)
        turn_two.start()

    def crossed_back():
        third_sum.drain()
        later.back.wait()
        back_cols(turn_part, part(r.v_one, 0, wide))

    def back_grad():
        later.crossed_in.wait()
        outer(grads[back], r.v_right, turn_part)
        later.attended = load(r.attended_t, r.v_right)

    def merge(total, target):
        @pl.loop(0, length // 16)
        def _(index):
            here = pl.ds(pl.multiple_of(index * 16, 16), 16)
            target[here, :] = total.value(here).astype(BF16)

    def half(value, side):
        return jnp.where(low if side == 0 else jnp.logical_not(low), value, jnp.zeros_like(value))

    def soft(scores):
        power = jnp.exp(scores - jnp.max(scores, axis=1, keepdims=True))
        return power * (1.0 / jnp.sum(power, axis=1, keepdims=True))

    def cross():
        later.query_in.wait()
        later.text_in.wait()
        later.values_in.wait()
        merge(crossed_sum, head_part)

        @pl.loop(0, 3)
        def _(pair):
            query = cross_query[:, lanes(pair, 128)]
            key = r.v_text[:, lanes(pair, 128)]
            value = r.v_text[:, lanes(3 + pair, 128)]
            head_grad = head_part[:, lanes(pair, 128)]
            results = []
            for side in (0, 1):
                weights = soft(dot_t(half(query, side), key) * 0.125)
                slope = dot_t(half(head_grad, side), value)
                score = (weights * (slope - jnp.sum(slope * weights, axis=1, keepdims=True))).astype(BF16)
                results.append(
                    (
                        dot(score, key) * 0.125,
                        t_dot(score, query) * 0.125,
                        t_dot(weights.astype(BF16), head_grad),
                    )
                )
            merged = [jnp.where(low, *item).astype(BF16) for item in zip(*results)]
            query_part[:, lanes(pair, 128)] = merged[0]
            r.v_terms[0:TEXT, lanes(blk * 3 + pair, 128)] = merged[1]
            r.v_terms[TEXT : 2 * TEXT, lanes(blk * 3 + pair, 128)] = merged[2]

        later.joint = load(r.joint, r.v_joint)

    def second_back():
        later.query.wait()
        crossed_sum.drain()
        back_rows(query_part, part(r.v_two, 0, wide))

    def query_grad():
        later.second.wait()
        outer(grads[query], r.v_left, query_part)
        later.first = load(r.first_t, r.v_left)

    def keys_grad():
        def body(block):
            product = t_dot(r.text[:, block], r.v_terms[own_rows, own_cols])
            grads[keys][block, :] = product.astype(BF16)

        tiles(6, 256, body)

    def text_start():
        later.keys.wait()
        terms = r.v_terms[own_rows, own_cols]
        r.v_text_part[...] = dot_t(terms, r.v_one[:, wide : 3 * wide]).astype(BF16)
        text_sum.start()

    def text_done():
        text_sum.finish()
        r.v_text_out[...] = text_sum.value(pl.ds(0, text_rows))
        give(r.v_text_out, r.text_out)

    def second_norm():
        later.one.wait()
        turn_two.drain()
        norm_back(second_sum, 1, hidden, True)
        later.frames = load(r.frames, r.v_rows)
        turn_one.start()

    def attended_back():
        second_sum.drain()
        later.outward.wait()
        back_cols(turned_part, part(r.v_one, 3 * wide, wide))

    def outward_grad():
        later.attended.wait()
        outer(grads[outward], r.v_right, turned_part)

    def attend():
        later.joint.wait()
        merge(attended_sum, head_part)

        @pl.loop(0, 3)
        def _(pair):
            r.v_key_sum[...] = jnp.zeros_like(r.v_key_sum)
            r.v_value_sum[...] = jnp.zeros_like(r.v_value_sum)

            @pl.loop(0, 4)
            def _(block):
                here = pl.ds(pl.multiple_of(block * 128, 128), 128)
                query = r.v_joint[here, lanes(pair, 128)]
                key = r.v_joint[:, lanes(pair + 3, 128)]
                value = r.v_joint[:, lanes(pair + 6, 128)]
                head_grad = head_part[here, lanes(pair, 128)]
                keep = r.ids_row[...] <= r.ids_col[here, :]
                results = []
                for side in (0, 1):
                    weights = soft(jnp.where(keep, dot_t(half(query, side), key) * 0.125, -1e30))
                    slope = dot_t(half(head_grad, side), value)
                    score = weights * (slope - jnp.sum(slope * weights, axis=1, keepdims=True))
                    score = score.astype(BF16)
                    results.append(
                        (dot(score, key), t_dot(score, query), t_dot(weights.astype(BF16), head_grad))
                    )
                merged = [jnp.where(low, *item) for item in zip(*results)]
                r.v_up[here, lanes(pair, 128)] = (merged[0] * 0.125).astype(BF16)
                r.v_key_sum[...] += merged[1]
                r.v_value_sum[...] += merged[2]

            r.v_up[:, lanes(pair + 3, 128)] = (r.v_key_sum[...] * 0.125).astype(BF16)
            r.v_up[:, lanes(pair + 6, 128)] = r.v_value_sum[...].astype(BF16)

    def first_back():
        attended_sum.drain()
        later.inward.wait()
        back_rows(joint_grad, part(r.v_two, wide, 3 * wide))

    inward_done = []

    def inward_grad(index):
        if not inward_done:
            later.first.wait()
        inward_done.append(index)
        reduces[index].drain()
        product = dot(r.v_left[...], part(r.v_up, index * wide, wide)[...])
        grads[inward + index][...] = product.astype(BF16)

    def norm_hop(number, who):
        return push(r.v_norm_sum, r.v_norm_in.at[number], r.nsend.at[number], r.nrecv.at[number], who)

    def first_norm():
        later.again = load(r.w_contract, r.v_one)
        later.active = load(r.active, r.v_grad)
        later.frames.wait()
        norm_back(first_sum, 0, hidden, False)
        for who in (spot.sib, spot.opp):
            pl.semaphore_signal(r.credit.at[6], inc=1, device_id=who, device_id_type=MESH)
        give(hidden, r.frames_out)
        for place in range(6):
            r.v_norm_sum[place : place + 1, :] = jnp.sum(
                r.v_norm_grads[place * 8 : place * 8 + 8, :], axis=0, keepdims=True
            )
        r.v_norm_sum[6:8, :] = jnp.zeros((2, width), F32)
        norm_hop(0, spot.sib).start()

    def norm_step(number, who):
        norm_hop(number, who).wait()
        r.v_norm_sum[...] += r.v_norm_in[number]

    def norm_sib():
        norm_step(0, spot.sib)
        norm_hop(1, spot.opp).start()

    def norm_opp():
        norm_step(1, spot.opp)
        norm_hop(2, spot.part).start()

    def norm_part():
        norm_step(2, spot.part)
        for k in (1, 2, 3):
            norm_hop(2 + k, spot.z_peer(k)).start()

    def norm_peers():
        for k in (1, 2, 3):
            norm_hop(2 + k, spot.z_peer(k)).wait()
        r.v_norm_sum[...] += r.v_norm_in[3] + r.v_norm_in[4] + r.v_norm_in[5]
        give(r.v_norm_sum, r.norm_out)

    def out_product():
        later.again.wait()
        later.active.wait()
        first_sum.drain()
        back_rows(r.v_grad, r.v_one)

    def out_start():
        pl.semaphore_wait(r.credit.at[6], 2)
        out_sum.start()

    def out_done():
        turn_one.drain()

        @pl.loop(0, rows // 16)
        def _(index):
            here = pl.ds(pl.multiple_of(index * 16, 16), 16)
            r.v_branch[here, :] = (out_sum.value(here) + r.v_two_rows[here, :].astype(F32)).astype(BF16)

        give(r.v_branch, r.block_out)

    steps = (
        up, third_back, third_sum.start, third_sum.relay, third_sum.finish,
        *(functools.partial(expand_grad, index) for index in range(4)),
        third_norm, turn_two.finish, crossed_back,
        crossed_sum.start, crossed_sum.relay, crossed_sum.finish,
        back_grad, cross, terms_share.start, terms_share.relay, terms_share.finish,
        second_back, second_sum.start, second_sum.relay, second_sum.finish,
        query_grad, keys_grad, text_start, text_sum.relay, text_done,
        second_norm, turn_one.finish, attended_back,
        attended_sum.start, attended_sum.relay, attended_sum.finish,
        outward_grad, attend, first_back, first_sum.start, first_sum.relay, first_sum.finish,
        *(functools.partial(inward_grad, index) for index in range(3)),
        first_norm, norm_sib, norm_opp, norm_part, norm_peers,
        out_product, out_start, out_sum.relay, out_sum.finish, out_done,
    )
    goals = [r.contract_out.at[:, index * wide : (index + 1) * wide] for index in range(4)]
    goals += [r.expand_out.at[:, index * wide : (index + 1) * wide] for index in range(4)]
    goals += [r.returning_out, r.keying_out, r.querying_out, r.outward_out]
    stores = []

    def store(number):
        goal = goals[number]
        slot = len(stores)
        if slot >= 4:
            stores[slot - 4].wait()
        columns = pl.ds(slot // 2 % 2 * 2 * wide, goal.shape[1])
        stage = r.v_slope.at[pl.ds(slot % 2 * 192, 192), columns]

        def keep(here, value):
            stage[here, :] = value

        reduces[number].finish(keep)
        stores.append(give(stage, goal))

    def inward_copy(kind):
        index = kind * 4 + blk
        src = r.v_left.at[kind * 192 : (kind + 1) * 192, 0:wide]
        place = lax.rem(index, 3)
        lines = pl.ds(pl.multiple_of(place * 192, 192), 192)
        return index // 3, place, src, r.v_right.at[lines, 0:wide]

    def hand_over(kind):
        owner, place, src, dst = inward_copy(kind)

        def keep(here, value):
            src[here, :] = value.astype(BF16)

        reduces[inward + kind].finish(keep)

        @pl.when(owner == blk)
        def _():
            pltpu.make_async_copy(src, dst, r.arecv.at[place]).start()

        @pl.when(owner != blk)
        def _():
            push(src, dst, r.asend.at[kind], r.arecv.at[place], (spot.grp, owner)).start()

    taken = [0] * len(reduces)
    for kind, number, *rest in BACKWARD_ORDER:
        if kind == 5:
            steps[number]()
            continue
        item = reduces[number]
        if kind == 0:
            if number >= inward:
                pl.semaphore_wait(r.credit.at[number - inward], 1)
            item.start()
        elif kind == 1:
            if number < 4 and sum(taken) == 0:
                for copy in later.own:
                    copy.wait()
            if number >= inward and taken[number] == 0:
                pl.semaphore_wait(r.credit.at[3 + number - inward], 3)
            item.take(*rest)
            taken[number] += 1
            if number < 3 and taken[number] == 4:
                pl.semaphore_signal(r.credit.at[number], inc=1, device_id=spot.part, device_id_type=MESH)
        elif kind == 2:
            item.pass_on(*rest)
        elif kind == 3:
            item.cross()
        elif number >= inward:
            hand_over(number - inward)
        else:
            store(number)
            for k in (1, 2, 3) if number < 3 else ():
                pl.semaphore_signal(
                    r.credit.at[3 + number], inc=1, device_id=spot.z_peer(k), device_id_type=MESH
                )
    for copy in stores[-4:]:
        copy.wait()
    for place in range(3):
        here = slice(place * wide, (place + 1) * wide)
        dst = r.v_right.at[place * 192 : (place + 1) * 192, 0:wide]
        home = lax.rem(blk * 3 + place, 4)

        @pl.when(home == blk)
        def _():
            pltpu.make_async_copy(dst, dst, r.arecv.at[place]).wait()

        @pl.when(home != blk)
        def _():
            push(dst, dst, r.asend.at[0], r.arecv.at[place], spot.sib).wait_recv()

        stage = r.v_slope.at[pl.ds(0, 192), pl.ds(place * wide, wide)]

        @pl.loop(0, 192 // 16)
        def _(index):
            lines = pl.ds(pl.multiple_of(index * 16, 16), 16)
            stage[lines, :] = dst[lines, :].astype(F32)

        give(stage, r.inward_out.at[:, here])
    for kind in range(3):
        owner, place, src, dst = inward_copy(kind)

        @pl.when(owner != blk)
        def _():
            push(src, dst, r.asend.at[kind], r.arecv.at[place], (spot.grp, owner)).wait_send()

    for item in reduces[3:]:
        item.drain()
    terms_share.drain()
    text_sum.drain()
    out_sum.drain()
    for copy in copies:
        if all(copy is not item for item in stores):
            copy.wait()


def backward(ahead, frames, text, table, incoming):
    rows, width = frames.shape
    length = rows * lax.axis_size("blk")
    wide = width // lax.axis_size("blk")
    shard = width // lax.axis_size("grp")
    feed = ahead.w_expand.shape[1]
    ids_col, ids_row = ids_of(table)
    out = dict(
        contract_out=((shard, feed), F32),
        expand_out=((shard, feed), F32),
        returning_out=((shard, wide), F32),
        keying_out=((shard, 2 * wide), F32),
        querying_out=((shard, wide), F32),
        outward_out=((shard, wide), F32),
        inward_out=((shard, 3 * wide), F32),
        frames_out=((rows, width), F32),
        block_out=((rows, width), BF16),
        text_out=((TEXT // 4, width), F32),
        norm_out=((8, width), F32),
    )
    square, turned, strip = (length, width), (width, length), (length, wide)
    vmem = dict(
        v_one=((width, feed), BF16),
        v_two=((width, feed), BF16),
        g_contract=((width, feed), BF16),
        g_expand=((width, feed), BF16),
        g_rest=((width, 5 * wide), BF16),
        v_left=(turned, BF16),
        v_right=(turned, BF16),
        v_grad=(square, BF16),
        v_up=(square, BF16),
        v_part=(square, BF16),
        v_slope=(square, F32),
        v_joint=((length, 3 * wide), BF16),
        v_text=((TEXT, 2 * wide), BF16),
        v_terms=((2 * TEXT, width), BF16),
        v_text_part=((TEXT, width), BF16),
        v_text_out=((TEXT // 4, width), F32),
        near_rows=((2, rows, width), BF16),
        far_rows=((rows, width), BF16),
        near_cols=((2, length, wide), BF16),
        far_cols=(strip, BF16),
        near_text=((2, TEXT // 4, width), BF16),
        far_text=((TEXT // 4, width), BF16),
        v_branch=((rows, width), BF16),
        v_rows=((rows, width), BF16),
        v_two_rows=((rows, width), BF16),
        v_norm=((8, width), F32),
        v_norm_grads=((48, width), F32),
        v_norm_sum=((8, width), F32),
        v_norm_in=((6, 8, width), F32),
        v_key_sum=((length, 128), F32),
        v_value_sum=((length, 128), F32),
    )
    vmem.update(
        y_contract=((4, shard, feed), BF16),
        y_expand=((4, shard, feed), BF16),
        y_back=((1, shard, wide), BF16),
        y_keys=((4, shard, 2 * wide), BF16),
        y_query=((4, shard, wide), BF16),
        y_outward=((1, shard, wide), BF16),
        z_contract=((5, shard, feed), BF16),
        z_expand=((5, shard, feed), BF16),
        z_back=((10, shard, wide), BF16),
        z_keys=((5, shard, 2 * wide), BF16),
        z_query=((5, shard, wide), BF16),
        z_outward=((10, shard, wide), BF16),
    )
    sems = dict(
        ysend=(15, 4),
        yrecv=(15, 4),
        zsend=(15, 8),
        zrecv=(15, 10),
        bsend=(7, 3),
        brecv=(7, 3),
        tsend=(2, 3),
        trecv=(2, 3),
        csend=(1, 3),
        crecv=(1, 3),
        nsend=(6,),
        nrecv=(6,),
        asend=(3,),
        arecv=(3,),
        local=(32,),
        stored=(24,),
    )
    inner = dict(text=text, ids_col=ids_col, ids_row=ids_row)
    outer = dict(frames=frames, incoming=incoming, **vars(ahead))
    del outer["aligned"]
    return run_kernel(backward_kernel, 2, inner, outer, out, vmem, sems, dict(credit=(7,)))


def closing_kernel(count, *refs):
    given, out, held, sems = refs[:count], refs[count : 2 * count], refs[2 * count : -1], refs[-1]
    loads = [
        pltpu.make_async_copy(src, dst, sems.at[0, index])
        for index, (src, dst) in enumerate(zip(given, held))
    ]
    stores = [
        pltpu.make_async_copy(src, dst, sems.at[1, index])
        for index, (src, dst) in enumerate(zip(held, out))
    ]
    for copy in loads:
        copy.start()
    for load, store in zip(loads, stores):
        load.wait()
        store.start()
    for copy in stores:
        copy.wait()


def closing(*items):
    anywhere = pl.BlockSpec(memory_space=pl.ANY)
    count = len(items)
    return pl.pallas_call(
        functools.partial(closing_kernel, count),
        out_shape=[jax.ShapeDtypeStruct(item.shape, item.dtype) for item in items],
        in_specs=[anywhere] * count,
        out_specs=[anywhere] * count,
        scratch_shapes=[pltpu.VMEM(item.shape, item.dtype) for item in items]
        + [pltpu.SemaphoreType.DMA((2, count))],
    )(*items)


def tp_shards(
    frames,
    text_states,
    block_table,
    inward,
    outward,
    querying,
    keying,
    returning,
    expand,
    contract,
    gains,
    shifts,
    out_grad,
):
    ahead = forward(
        frames[0],
        text_states[0],
        block_table,
        jnp.pad(jnp.concatenate([gains, shifts], axis=0), ((0, 10), (0, 80))),
        out_grad[0],
        dict(
            inward=inward,
            outward=outward,
            query=querying,
            keys=keying,
            back=returning,
            expand=expand,
            contract=contract.T,
        ),
    )
    done = backward(ahead, frames[0], text_states[0], block_table, out_grad[0])
    share = gains.shape[1]
    place = (lax.axis_index("grp") * lax.axis_size("blk") + lax.axis_index("blk")) * share
    norm_grads = lax.dynamic_slice_in_dim(done.norm_out, place, share, 1)
    (
        contract_grad,
        expand_grad,
        returning_grad,
        keying_grad,
        querying_grad,
        outward_grad,
        inward_grad,
        frames_grad,
        block_out,
        text_grad,
    ) = closing(
        done.contract_out,
        done.expand_out,
        done.returning_out,
        done.keying_out,
        done.querying_out,
        done.outward_out,
        done.inward_out,
        done.frames_out,
        done.block_out,
        done.text_out,
    )
    return (
        block_out[None],
        frames_grad[None],
        text_grad[None],
        inward_grad,
        outward_grad,
        querying_grad,
        keying_grad,
        returning_grad,
        expand_grad,
        contract_grad.T,
        norm_grads[:3],
        norm_grads[3:6],
    )


def solution(mesh):
    small = mesh.shape["grp"] == 8 and mesh.shape["blk"] == 4
    return jax.shard_map(
        tp_shards if small else shards,
        mesh=mesh,
        in_specs=(
            P("grp", "blk", None),
            P("grp", None, None),
            P("grp", None),
            P("grp", "blk"),
            P("grp", "blk"),
            P("grp", "blk"),
            P("grp", "blk"),
            P("grp", "blk"),
            P("grp", "blk"),
            P("blk", "grp"),
            P(None, ("grp", "blk")),
            P(None, ("grp", "blk")),
            P("grp", "blk", None),
        ),
        out_specs=(
            P("grp", "blk", None),
            P("grp", "blk", None),
            P("grp", "blk", None),
            P("grp", "blk"),
            P("grp", "blk"),
            P("grp", "blk"),
            P("grp", "blk"),
            P("grp", "blk"),
            P("grp", "blk"),
            P("blk", "grp"),
            P(None, ("grp", "blk")),
            P(None, ("grp", "blk")),
        ),
        check_vma=False,
    )
```
